32 devices in a mesh: dp: 2 (over core), tensor: 16 (over z, y, x).
Axes of the slice: x: 2, y: 2, z: 4, core: 2. Of those that a mesh axis runs over, the one named last changes fastest.
Arguments:
- sequence_entries: float32 [8192, 1024], P(('dp', 'tensor')), may hold values from -6 to 6
- running_dividend: float32 [4, 1024], P('dp', 'tensor'), may hold values from -6 to 6
- running_divisor: float32 [4, 1024], P('dp', 'tensor'), may hold values from 1 to 4
- running_exponent: float32 [4, 1024], P('dp', 'tensor'), may hold values from -1 to 2
- preceding_attend: bfloat16 [4, 1024], P('dp'), may hold values from -6 to 6
- preceding_feedforward: bfloat16 [4, 1024], P('dp'), may hold values from -6 to 6
- first_norm_factor: float32 [1024], replicated, may hold values from 0.5 to 1.5
- first_norm_shift: float32 [1024], replicated, may hold values from -3 to 3
- attend_fading: float32 [1024], replicated, may hold values from -6.2 to -2.3
- instant_reward: float32 [1024], replicated, may hold values from -1 to 1
- attend_kshare: float32 [1024], replicated, may hold values from 0.05 to 0.95
- attend_vshare: float32 [1024], replicated, may hold values from 0.05 to 0.95
- attend_rshare: float32 [1024], replicated, may hold values from 0.05 to 0.95
- attend_kmatrix: bfloat16 [1024, 1024], P('dp', 'tensor'), may hold values from -0.1875 to 0.1875
- attend_vmatrix: bfloat16 [1024, 1024], P('dp', 'tensor'), may hold values from -0.1875 to 0.1875
- attend_rmatrix: bfloat16 [1024, 1024], P('dp', 'tensor'), may hold values from -0.1875 to 0.1875
- attend_omatrix: bfloat16 [1024, 1024], P('dp', 'tensor'), may hold values from -0.75 to 0.75
- second_norm_factor: float32 [1024], replicated, may hold values from 0.5 to 1.5
- second_norm_shift: float32 [1024], replicated, may hold values from -3 to 3
- feedforward_kshare: float32 [1024], replicated, may hold values from 0.05 to 0.95
- feedforward_rshare: float32 [1024], replicated, may hold values from 0.05 to 0.95
- feedforward_kmatrix: bfloat16 [1024, 4096], P('dp', 'tensor'), may hold values from -0.1875 to 0.1875
- feedforward_vmatrix: bfloat16 [1024, 4096], P('dp', 'tensor'), may hold values from -0.09375 to 0.09375
- feedforward_rmatrix: bfloat16 [1024, 1024], P('dp', 'tensor'), may hold values from -0.1875 to 0.1875
- upstream_gradient: float32 [8192, 1024], P(('dp', 'tensor')), may hold values from -6 to 6
Outputs:
- block_out: float32 [8192, 1024], P(('dp', 'tensor'))
- tokens_grad: float32 [8192, 1024], P(('dp', 'tensor'))
- state_num_grad: float32 [4, 1024], P('dp', 'tensor')
- state_den_grad: float32 [4, 1024], P('dp', 'tensor')
- state_top_grad: float32 [4, 1024], P('dp', 'tensor')
- prev_time_grad: float32 [4, 1024], P('dp')
- prev_channel_grad: float32 [4, 1024], P('dp')
- norm1_gain_grad: float32 [1024], replicated
- norm1_bias_grad: float32 [1024], replicated
- time_decay_grad: float32 [1024], replicated
- time_first_grad: float32 [1024], replicated
- time_mix_key_grad: float32 [1024], replicated
- time_mix_value_grad: float32 [1024], replicated
- time_mix_recept_grad: float32 [1024], replicated
- key_weight_grad: float32 [1024, 1024], P('dp', 'tensor')
- value_weight_grad: float32 [1024, 1024], P('dp', 'tensor')
- recept_weight_grad: float32 [1024, 1024], P('dp', 'tensor')
- out_weight_grad: float32 [1024, 1024], P('dp', 'tensor')
- norm2_gain_grad: float32 [1024], replicated
- norm2_bias_grad: float32 [1024], replicated
- chan_mix_key_grad: float32 [1024], replicated
- chan_mix_recept_grad: float32 [1024], replicated
- chan_key_weight_grad: float32 [1024, 4096], P('dp', 'tensor')
- chan_value_weight_grad: float32 [1024, 4096], P('dp', 'tensor')
- chan_recept_weight_grad: float32 [1024, 1024], P('dp', 'tensor')
The draws below stay inside these ranges and needn't reach their ends.
All inputs are finite; a program needn't handle non-finite values.
Results may differ from the reference program's by a relative error of at most 0.02.
Values may be sent and summed in bfloat16 or wider, within the bound.
A program may use at most 384 MiB of HBM per device.

```python
import math
import jax
import jax.numpy as jnp
from jax import lax

MODEL_DIM = 1024
FF = 4096
SEGMENT = 2048
SPAN_LENGTH = 64
BATCH = 4
TOKENS = 8192


def block_scale(key, extent, shards, low, top_value):
    def one(dim, blocks):
        heights = jax.random.uniform(jax.random.fold_in(jax.random.fold_in(key, 6), dim), (blocks,), jnp.float32, low / len(shards), top_value / len(shards))
        return jnp.repeat(jnp.exp(heights), extent[dim] // blocks).reshape((-1,) + (1,) * (len(extent) - dim - 1))

    factor_of = one(*shards[0])
    for cut in shards[1:]:
        factor_of = factor_of * one(*cut)
    return factor_of


def normal_values(stream_key, shape, width, reach, shards=(), kind=jnp.bfloat16):
    entries = jax.random.normal(stream_key, shape, jnp.float32) * width
    if len(shards) > 0:
        entries = block_scale(stream_key, shape, shards, -0.22, 0.18) * entries
    return jnp.clip(entries, min=-reach, max=reach).astype(kind)


def setup_inputs(seed: int = 0) -> dict:
    seeds = jax.random.split(jax.random.key(seed), 26)
    sequence_entries = normal_values(seeds[0], (TOKENS, MODEL_DIM), 1.0, 6.0, ((0, 32),), jnp.float32)
    running_dividend = normal_values(seeds[1], (BATCH, MODEL_DIM), 1.0, 6.0, ((0, 2), (1, 16)), jnp.float32)
    running_divisor = jnp.clip(jnp.exp(math.log(4.0) - 1.3862944 * jax.random.uniform(seeds[2], (BATCH, MODEL_DIM), jnp.float32) ** block_scale(seeds[2], (BATCH, MODEL_DIM), ((0, 2), (1, 16)), -0.2, 0.2)), 1.0, 4.0)
    running_exponent = jnp.clip(-1.0 + 3.0 * jax.random.uniform(seeds[3], (BATCH, MODEL_DIM), jnp.float32) ** block_scale(seeds[3], (BATCH, MODEL_DIM), ((0, 2), (1, 16)), -0.2, 0.2), -1.0, 2.0)
    preceding_attend = normal_values(seeds[4], (BATCH, MODEL_DIM), 1.0, 6.0, ((0, 2),))
    preceding_feedforward = normal_values(seeds[5], (BATCH, MODEL_DIM), 1.0, 6.0, ((0, 2),))
    first_norm_factor = jnp.clip(1.0 + 0.1 * jax.random.normal(seeds[6], (MODEL_DIM,), jnp.float32), 0.5, 1.5)
    first_norm_shift = normal_values(seeds[7], (MODEL_DIM,), 0.3, 3.0, (), jnp.float32)
    attend_fading = jnp.clip(jax.random.uniform(seeds[8], (MODEL_DIM,), jnp.float32, -6.2, -2.3), -6.2, -2.3)
    instant_reward = jnp.clip(jax.random.uniform(seeds[9], (MODEL_DIM,), jnp.float32, -1.0, 1.0), -1.0, 1.0)
    attend_kshare = jnp.clip(jax.random.uniform(seeds[10], (MODEL_DIM,), jnp.float32, 0.05, 0.95), 0.05, 0.95)
    attend_vshare = jnp.clip(jax.random.uniform(seeds[11], (MODEL_DIM,), jnp.float32, 0.05, 0.95), 0.05, 0.95)
    attend_rshare = jnp.clip(jax.random.uniform(seeds[12], (MODEL_DIM,), jnp.float32, 0.05, 0.95), 0.05, 0.95)
    attend_kmatrix = normal_values(seeds[13], (MODEL_DIM, MODEL_DIM), MODEL_DIM ** -0.5, 0.1875, ((0, 2), (1, 16)))
    attend_vmatrix = normal_values(seeds[14], (MODEL_DIM, MODEL_DIM), MODEL_DIM ** -0.5, 0.1875, ((0, 2), (1, 16)))
    attend_rmatrix = normal_values(seeds[15], (MODEL_DIM, MODEL_DIM), MODEL_DIM ** -0.5, 0.1875, ((0, 2), (1, 16)))
    attend_omatrix = normal_values(seeds[16], (MODEL_DIM, MODEL_DIM), (MODEL_DIM // 16) ** -0.5, 0.75, ((0, 2), (1, 16)))
    second_norm_factor = jnp.clip(1.0 + 0.1 * jax.random.normal(seeds[17], (MODEL_DIM,), jnp.float32), 0.5, 1.5)
    second_norm_shift = normal_values(seeds[18], (MODEL_DIM,), 0.3, 3.0, (), jnp.float32)
    feedforward_kshare = jnp.clip(jax.random.uniform(seeds[19], (MODEL_DIM,), jnp.float32, 0.05, 0.95), 0.05, 0.95)
    feedforward_rshare = jnp.clip(jax.random.uniform(seeds[20], (MODEL_DIM,), jnp.float32, 0.05, 0.95), 0.05, 0.95)
    feedforward_kmatrix = normal_values(seeds[21], (MODEL_DIM, FF), MODEL_DIM ** -0.5, 0.1875, ((0, 2), (1, 16)))
    feedforward_vmatrix = normal_values(seeds[22], (MODEL_DIM, FF), FF ** -0.5, 0.09375, ((0, 2), (1, 16)))
    feedforward_rmatrix = normal_values(seeds[23], (MODEL_DIM, MODEL_DIM), MODEL_DIM ** -0.5, 0.1875, ((0, 2), (1, 16)))
    upstream_gradient = normal_values(seeds[24], (TOKENS, MODEL_DIM), 1.0, 6.0, ((0, 32),), jnp.float32)
    return {"sequence_entries": sequence_entries, "running_dividend": running_dividend, "running_divisor": running_divisor, "running_exponent": running_exponent, "preceding_attend": preceding_attend, "preceding_feedforward": preceding_feedforward, "first_norm_factor": first_norm_factor, "first_norm_shift": first_norm_shift, "attend_fading": attend_fading, "instant_reward": instant_reward, "attend_kshare": attend_kshare, "attend_vshare": attend_vshare, "attend_rshare": attend_rshare, "attend_kmatrix": attend_kmatrix, "attend_vmatrix": attend_vmatrix, "attend_rmatrix": attend_rmatrix, "attend_omatrix": attend_omatrix, "second_norm_factor": second_norm_factor, "second_norm_shift": second_norm_shift, "feedforward_kshare": feedforward_kshare, "feedforward_rshare": feedforward_rshare, "feedforward_kmatrix": feedforward_kmatrix, "feedforward_vmatrix": feedforward_vmatrix, "feedforward_rmatrix": feedforward_rmatrix, "upstream_gradient": upstream_gradient}


epsilon = 1e-05

@jax.custom_vjp
def low(v):
    return lax.optimization_barrier(v.astype(jnp.bfloat16)).astype(jnp.float32)

@jax.custom_vjp
def lower_backward(v):
    return v

def low_keep(v):
    return (low(v), None)

def low_pass(kept, grad):
    return (grad,)

def back_keep(v):
    return (v, None)

def back_low(kept, grad):
    return (low(grad),)
low.defvjp(low_keep, low_pass)
lower_backward.defvjp(back_keep, back_low)

def layer_norm(vals_matrix, gain, offset):
    center = vals_matrix - lax.optimization_barrier(jnp.mean(vals_matrix, axis=-1, keepdims=True))
    spread = lax.optimization_barrier(jnp.mean(center * center, axis=-1, keepdims=True))
    return center * lax.rsqrt(spread + epsilon) * gain + offset

def span_blend(running_bundle, pieces):
    running_dividend, running_divisor, running_exponent, fading_rates, reward_terms = running_bundle
    span_keys_matrix, span_values = pieces
    length = span_keys_matrix.shape[0]
    places = jnp.arange(length)
    offsets = places.astype(span_keys_matrix.dtype)
    distance = offsets[:, None] - 1.0 - offsets[None, :]
    earlier = span_keys_matrix[None, :, :] - distance[:, :, None] * fading_rates[None, None, :]
    instant_entry = reward_terms[None, :] + span_keys_matrix
    before_mask = (places[None, :] < places[:, None])[:, :, None]
    same_mask = (places[None, :] == places[:, None])[:, :, None]
    scores = jnp.where(before_mask, earlier, jnp.where(same_mask, instant_entry[None, :, :], -1e+30))
    carried = running_exponent[None, :] - offsets[:, None] * fading_rates[None, :]
    highest = jnp.maximum(lax.optimization_barrier(jnp.max(scores, axis=1)), carried)
    weights = jnp.exp(scores - highest[:, None, :])
    kept_weight = jnp.exp(carried - highest)
    numerator = lax.optimization_barrier(jnp.sum(weights * span_values[None, :, :], axis=1)) + kept_weight * running_dividend[None, :]
    denominator = lax.optimization_barrier(jnp.sum(weights, axis=1)) + kept_weight * running_divisor[None, :]
    result_matrix = numerator / denominator
    tail_scores = span_keys_matrix - (length - 1.0 - offsets)[:, None] * fading_rates[None, :]
    old_score = running_exponent - length * fading_rates
    updated_exponent = jnp.maximum(lax.optimization_barrier(jnp.max(tail_scores, axis=0)), old_score)
    tail_weight = jnp.exp(tail_scores - updated_exponent[None, :])
    old_weight = jnp.exp(old_score - updated_exponent)
    updated_dividend = lax.optimization_barrier(jnp.sum(tail_weight * span_values, axis=0)) + old_weight * running_dividend
    updated_divisor = lax.optimization_barrier(jnp.sum(tail_weight, axis=0)) + old_weight * running_divisor
    return ((updated_dividend, updated_divisor, updated_exponent, fading_rates, reward_terms), result_matrix)

def recurrent_average(whole_keys_matrix, whole_vals_matrix, fading_rates, reward_terms, running_dividend, running_divisor, running_exponent):
    length, feature_count = whole_keys_matrix.shape
    span_sequence = length // SPAN_LENGTH
    final_recurrent, result_matrix = lax.scan(jax.checkpoint(span_blend), (running_dividend, running_divisor, running_exponent, fading_rates, reward_terms), (whole_keys_matrix.reshape(span_sequence, SPAN_LENGTH, feature_count), whole_vals_matrix.reshape(span_sequence, SPAN_LENGTH, feature_count)))
    return result_matrix.reshape(length, feature_count)

def earlier_rows(token_rows, previous):
    return jnp.concatenate([previous[:, None, :], token_rows[:, :-1, :]], axis=1)

def attend_prefix(array):
    cluster_sequence, length, feature_indices = array.shape
    return jnp.transpose(array, (1, 0, 2)).reshape(length, cluster_sequence * feature_indices)

def batch_major(array, cluster_sequence):
    length, feature_count = array.shape
    return jnp.transpose(array.reshape(length, cluster_sequence, feature_count // cluster_sequence), (1, 0, 2))

def apply_projection(left, right, form):
    return jnp.einsum(form, left, right, precision=lax.Precision.HIGHEST)

def block_forward(parameters, sequence_entries, running_dividend, running_divisor, running_exponent, preceding_attend, preceding_feedforward):
    first_norm_factor, first_norm_shift, attend_fading, instant_reward, attend_kshare, attend_vshare, attend_rshare, attend_kmatrix, attend_vmatrix, attend_rmatrix, attend_omatrix, second_norm_factor, second_norm_shift, feedforward_kshare, feedforward_rshare, feedforward_kmatrix, feedforward_vmatrix, feedforward_rmatrix = parameters
    cluster_sequence = preceding_attend.shape[0]
    token_rows = sequence_entries.reshape(cluster_sequence, SEGMENT, MODEL_DIM)
    normed_first = low(layer_norm(token_rows, first_norm_factor, first_norm_shift))
    before_first = earlier_rows(normed_first, preceding_attend)
    key_in = low(normed_first * attend_kshare + before_first * (1.0 - attend_kshare))
    value_in = low(normed_first * attend_vshare + before_first * (1.0 - attend_vshare))
    recept_in = low(normed_first * attend_rshare + before_first * (1.0 - attend_rshare))
    keys_matrix = lower_backward(apply_projection(key_in, attend_kmatrix, 'gld,de->gle'))
    vals_matrix = lower_backward(apply_projection(value_in, attend_vmatrix, 'gld,de->gle'))
    recept_pre = lower_backward(apply_projection(recept_in, attend_rmatrix, 'gld,de->gle'))
    fading_rates = jnp.tile(jnp.exp(attend_fading), cluster_sequence)
    reward_terms = jnp.tile(instant_reward, cluster_sequence)
    blended_source = recurrent_average(attend_prefix(keys_matrix), attend_prefix(vals_matrix), fading_rates, reward_terms, running_dividend.reshape(-1), running_divisor.reshape(-1), running_exponent.reshape(-1))
    blended_source = batch_major(blended_source, cluster_sequence)
    gated_output = low(jax.nn.sigmoid(recept_pre) * blended_source)
    attention_output = lower_backward(apply_projection(gated_output, attend_omatrix, 'iub,tb->iut'))
    middle = token_rows + attention_output
    normed_second = low(layer_norm(middle, second_norm_factor, second_norm_shift))
    before_second = earlier_rows(normed_second, preceding_feedforward)
    chan_key_in = low(normed_second * feedforward_kshare + before_second * (1.0 - feedforward_kshare))
    chan_rec_in = low(normed_second * feedforward_rshare + before_second * (1.0 - feedforward_rshare))
    hidden = lower_backward(apply_projection(chan_key_in, feedforward_kmatrix, 'gld,df->glf'))
    squared = low(jnp.square(jax.nn.relu(hidden)))
    chan_values = lower_backward(apply_projection(squared, feedforward_vmatrix, 'glf,df->gld'))
    chan_gate = jax.nn.sigmoid(lower_backward(apply_projection(chan_rec_in, feedforward_rmatrix, 'gld,de->gle')))
    result = middle + chan_gate * chan_values
    return result.reshape(cluster_sequence * SEGMENT, MODEL_DIM)

def reference(sequence_entries, running_dividend, running_divisor, running_exponent, preceding_attend, preceding_feedforward, first_norm_factor, first_norm_shift, attend_fading, instant_reward, attend_kshare, attend_vshare, attend_rshare, attend_kmatrix, attend_vmatrix, attend_rmatrix, attend_omatrix, second_norm_factor, second_norm_shift, feedforward_kshare, feedforward_rshare, feedforward_kmatrix, feedforward_vmatrix, feedforward_rmatrix, upstream_gradient):
    parameters = tuple((element.astype(jnp.float32) for element in (first_norm_factor, first_norm_shift, attend_fading, instant_reward, attend_kshare, attend_vshare, attend_rshare, attend_kmatrix, attend_vmatrix, attend_rmatrix, attend_omatrix, second_norm_factor, second_norm_shift, feedforward_kshare, feedforward_rshare, feedforward_kmatrix, feedforward_vmatrix, feedforward_rmatrix)))
    group = 2
    count = BATCH // group
    token_groups = sequence_entries.astype(jnp.float32).reshape(count, group * SEGMENT, MODEL_DIM)
    cot_groups = upstream_gradient.astype(jnp.float32).reshape(count, group * SEGMENT, MODEL_DIM)
    num_groups = running_dividend.astype(jnp.float32).reshape(count, group, MODEL_DIM)
    den_groups = running_divisor.astype(jnp.float32).reshape(count, group, MODEL_DIM)
    top_groups = running_exponent.astype(jnp.float32).reshape(count, group, MODEL_DIM)
    ptime_groups = preceding_attend.astype(jnp.float32).reshape(count, group, MODEL_DIM)
    pchan_groups = preceding_feedforward.astype(jnp.float32).reshape(count, group, MODEL_DIM)

    def one_group(totals, pieces):
        tok_piece, num_piece, den_piece, top_piece, ptime_piece, pchan_piece, cot_piece = pieces
        result, pull = jax.vjp(block_forward, parameters, tok_piece, num_piece, den_piece, top_piece, ptime_piece, pchan_piece)
        grads = pull(cot_piece)
        updated = jax.tree.map(lambda running, extra: running + extra, totals, grads[0])
        return (updated, (result, grads[1], grads[2], grads[3], grads[4], grads[5], grads[6]))
    starting = jax.tree.map(jnp.zeros_like, parameters)
    totals, stacked = lax.scan(one_group, starting, (token_groups, num_groups, den_groups, top_groups, ptime_groups, pchan_groups, cot_groups))
    block_out = stacked[0].reshape(TOKENS, MODEL_DIM)
    tokens_grad = stacked[1].reshape(TOKENS, MODEL_DIM)
    num_grad = stacked[2].reshape(BATCH, MODEL_DIM)
    den_grad = stacked[3].reshape(BATCH, MODEL_DIM)
    top_grad = stacked[4].reshape(BATCH, MODEL_DIM)
    ptime_grad = stacked[5].reshape(BATCH, MODEL_DIM)
    pchan_grad = stacked[6].reshape(BATCH, MODEL_DIM)
    return (block_out, tokens_grad, num_grad, den_grad, top_grad, ptime_grad, pchan_grad, totals[0], totals[1], totals[2], totals[3], totals[4], totals[5], totals[6], totals[7], totals[8], totals[9], totals[10], totals[11], totals[12], totals[13], totals[14], totals[15], totals[16], totals[17])
```

```python
import functools

import jax
import jax.numpy as jnp
from jax import lax
from jax.experimental import pallas as pl
from jax.experimental.pallas import tpu as pltpu
from jax.sharding import PartitionSpec as P

EPS = 1e-05
STEP = 16
NEG = -1e30


def norm_stats(x):
    center = x - jnp.mean(x, axis=-1, keepdims=True)
    scale = lax.rsqrt(jnp.mean(center * center, axis=-1, keepdims=True) + EPS)
    return center * scale, scale


def norm_back(g, s, scale, gain):
    q = g * gain
    gx = (q - jnp.mean(q, axis=-1, keepdims=True) - s * jnp.mean(q * s, axis=-1, keepdims=True)) * scale
    return gx, jnp.sum(g * s, axis=0), jnp.sum(g, axis=0)


def blended(now, before, mix):
    return (now.astype(jnp.float32) * mix + before.astype(jnp.float32) * (1.0 - mix)).astype(jnp.bfloat16)


def dot_nt(x, y):
    return lax.dot_general(x, y, (((1,), (1,)), ((), ())), preferred_element_type=jnp.float32)


def dot_nn(x, y):
    return lax.dot_general(x, y, (((1,), (0,)), ((), ())), preferred_element_type=jnp.float32)


def dot_tn(x, y):
    return lax.dot_general(x, y, (((0,), (0,)), ((), ())), preferred_element_type=jnp.float32)


LANES = 128
VMEM = pl.BlockSpec(memory_space=pltpu.VMEM)


def scan_groups(width):
    blocks = width // LANES
    size = 4 if blocks % 4 == 0 else 1
    return [range(g, g + size) for g in range(0, blocks, size)]


def lane(c):
    return slice(c * LANES, (c + 1) * LANES)


def wkv_forward_body(k_ref, v_ref, r_ref, w_ref, u_ref, a0_ref, b0_ref, m0_ref,
                     g_ref, kb, vb, yb, mb, ab, bb, sm, sa, sb):
    rows, width = k_ref.shape
    chunks = rows // STEP
    for c in range(width // LANES):
        kb[c] = k_ref[:, lane(c)]
        vb[c] = v_ref[:, lane(c)]

    for group in scan_groups(width):
        m = [jnp.full((chunks, LANES), NEG, jnp.float32) for _ in group]
        a = [jnp.zeros((chunks, LANES), jnp.float32) for _ in group]
        b = [jnp.zeros((chunks, LANES), jnp.float32) for _ in group]
        for j in range(STEP):
            at = pl.ds(j, chunks, stride=STEP)
            for i, c in enumerate(group):
                k = kb[c, at, :]
                mw = m[i] - w_ref[:, lane(c)]
                m[i] = jnp.maximum(mw, k)
                keep = jnp.exp(mw - m[i])
                take = jnp.exp(k - m[i])
                a[i] = keep * a[i] + take * vb[c, at, :]
                b[i] = keep * b[i] + take
        for i, c in enumerate(group):
            sm[:, lane(c)] = m[i]
            sa[:, lane(c)] = a[i]
            sb[:, lane(c)] = b[i]

    w = w_ref[...]
    m, a, b = m0_ref[...], a0_ref[...], b0_ref[...]
    for s in range(chunks):
        me, ae, be = sm[s:s + 1, :], sa[s:s + 1, :], sb[s:s + 1, :]
        sm[s:s + 1, :] = m
        sa[s:s + 1, :] = a
        sb[s:s + 1, :] = b
        mw = m - float(STEP) * w
        m = jnp.maximum(mw, me)
        keep = jnp.exp(mw - m)
        take = jnp.exp(me - m)
        a = keep * a + take * ae
        b = keep * b + take * be

    for group in scan_groups(width):
        m = [sm[:, lane(c)] for c in group]
        a = [sa[:, lane(c)] for c in group]
        b = [sb[:, lane(c)] for c in group]
        for j in range(STEP):
            at = pl.ds(j, chunks, stride=STEP)
            for i, c in enumerate(group):
                k = kb[c, at, :]
                v = vb[c, at, :]
                mb[c, at, :] = m[i]
                ab[c, at, :] = a[i]
                bb[c, at, :] = b[i]
                uk = u_ref[:, lane(c)] + k
                p = jnp.maximum(m[i], uk)
                alpha = jnp.exp(m[i] - p)
                beta = jnp.exp(uk - p)
                yb[c, at, :] = (alpha * a[i] + beta * v) / (alpha * b[i] + beta)
                mw = m[i] - w_ref[:, lane(c)]
                m[i] = jnp.maximum(mw, k)
                keep = jnp.exp(mw - m[i])
                take = jnp.exp(k - m[i])
                a[i] = keep * a[i] + take * v
                b[i] = keep * b[i] + take
    for c in range(width // LANES):
        g_ref[:, lane(c)] = (jax.nn.sigmoid(r_ref[:, lane(c)]) * yb[c]).astype(jnp.bfloat16)


def wkv_forward(k, v, r, w, u, a0, b0, m0):
    rows, width = k.shape
    block = jax.ShapeDtypeStruct((width // LANES, rows, LANES), jnp.float32)
    chunks = rows // STEP
    return pl.pallas_call(
        wkv_forward_body,
        out_shape=(jax.ShapeDtypeStruct((rows, width), jnp.bfloat16),) + (block,) * 6,
        in_specs=[VMEM] * 8,
        out_specs=[VMEM] * 7,
        scratch_shapes=[pltpu.VMEM((chunks, width), jnp.float32)] * 3,
        compiler_params=pltpu.CompilerParams(vmem_limit_bytes=40 * 2**20),
        cost_estimate=pl.CostEstimate(flops=60 * rows * width, transcendentals=7 * rows * width, bytes_accessed=36 * rows * width),
        name="wkv_forward",
    )(k, v, r, w, u, a0, b0, m0)


def wkv_carry_body(r_ref, gg_ref, kb, yb, mb, bb, w_ref, u_ref, gyb, ca_ref, cb_ref, lc_ref, la_ref, lb_ref, lg_ref):
    rows, width = r_ref.shape
    chunks = rows // STEP
    for c in range(width // LANES):
        gyb[c] = gg_ref[:, lane(c)] * jax.nn.sigmoid(r_ref[:, lane(c)])
    for group in scan_groups(width):
        ga = [jnp.zeros((chunks, LANES), jnp.float32) for _ in group]
        gb = [jnp.zeros((chunks, LANES), jnp.float32) for _ in group]
        end = [None for _ in group]
        for j in reversed(range(STEP)):
            at = pl.ds(j, chunks, stride=STEP)
            for i, c in enumerate(group):
                w = w_ref[:, lane(c)]
                k = kb[c, at, :]
                m = mb[c, at, :]
                uk = u_ref[:, lane(c)] + k
                p = jnp.maximum(m, uk)
                alpha = jnp.exp(m - p)
                beta = jnp.exp(uk - p)
                gn = gyb[c, at, :] / (alpha * bb[c, at, :] + beta)
                gd = -gn * yb[c, at, :]
                mw = m - w
                mn = jnp.maximum(mw, k)
                if j == STEP - 1:
                    end[i] = mn
                keep = jnp.exp(mw - mn)
                ga[i] = alpha * gn + keep * ga[i]
                gb[i] = alpha * gd + keep * gb[i]
                if j == 0:
                    lc_ref[:, lane(c)] = m - float(STEP) * w - end[i]
        for i, c in enumerate(group):
            ca_ref[:, lane(c)] = ga[i]
            cb_ref[:, lane(c)] = gb[i]
    ga = jnp.zeros((1, width), jnp.float32)
    gb = jnp.zeros((1, width), jnp.float32)
    lg = jnp.zeros((1, width), jnp.float32)
    for s in reversed(range(chunks)):
        keep = jnp.exp(lc_ref[s:s + 1, :])
        ga = ca_ref[s:s + 1, :] + keep * ga
        gb = cb_ref[s:s + 1, :] + keep * gb
        lg = lg + lc_ref[s:s + 1, :]
    la_ref[...] = ga
    lb_ref[...] = gb
    lg_ref[...] = lg


def wkv_carry(r, gg, kb, yb, mb, bb, w, u):
    rows, width = r.shape
    chunks = rows // STEP
    small = jax.ShapeDtypeStruct((chunks, width), jnp.float32)
    row = jax.ShapeDtypeStruct((1, width), jnp.float32)
    block = jax.ShapeDtypeStruct((width // LANES, rows, LANES), jnp.float32)
    return pl.pallas_call(
        wkv_carry_body,
        out_shape=(block, small, small, small, row, row, row),
        in_specs=[VMEM] * 8,
        out_specs=[VMEM] * 7,
        compiler_params=pltpu.CompilerParams(vmem_limit_bytes=40 * 2**20),
        cost_estimate=pl.CostEstimate(flops=40 * rows * width, transcendentals=5 * rows * width, bytes_accessed=28 * rows * width),
        name="wkv_carry",
    )(r, gg, kb, yb, mb, bb, w, u)


def wkv_backward_body(r_ref, gg_ref, kb, vb, yb, mb, ab, bb, gyb, w_ref, u_ref, ca_ref, cb_ref, lc_ref, ea_ref, eb_ref,
                      gk_ref, gv_ref, gr_ref, gu_ref, gw_ref, ta, tb, fk, fv):
    rows, width = r_ref.shape
    chunks = rows // STEP
    ga, gb = ea_ref[...], eb_ref[...]
    for s in reversed(range(chunks)):
        ta[s:s + 1, :] = ga
        tb[s:s + 1, :] = gb
        keep = jnp.exp(lc_ref[s:s + 1, :])
        ga = ca_ref[s:s + 1, :] + keep * ga
        gb = cb_ref[s:s + 1, :] + keep * gb
    for group in scan_groups(width):
        ga = [ta[:, lane(c)] for c in group]
        gb = [tb[:, lane(c)] for c in group]
        gu = [jnp.zeros((chunks, LANES), jnp.float32) for _ in group]
        gw = [jnp.zeros((chunks, LANES), jnp.float32) for _ in group]
        for j in reversed(range(STEP)):
            at = pl.ds(j, chunks, stride=STEP)
            for i, c in enumerate(group):
                k = kb[c, at, :]
                v = vb[c, at, :]
                m = mb[c, at, :]
                uk = u_ref[:, lane(c)] + k
                p = jnp.maximum(m, uk)
                alpha = jnp.exp(m - p)
                beta = jnp.exp(uk - p)
                b = bb[c, at, :]
                gn = gyb[c, at, :] / (alpha * b + beta)
                gd = -gn * yb[c, at, :]
                mw = m - w_ref[:, lane(c)]
                mn = jnp.maximum(mw, k)
                keep = jnp.exp(mw - mn)
                take = jnp.exp(k - mn)
                now = beta * (gn * v + gd)
                fv[c, at, :] = beta * gn + take * ga[i]
                fk[c, at, :] = now + take * (ga[i] * v + gb[i])
                gu[i] = gu[i] + now
                gw[i] = gw[i] + keep * (ga[i] * ab[c, at, :] + gb[i] * b)
                ga[i] = alpha * gn + keep * ga[i]
                gb[i] = alpha * gd + keep * gb[i]
        for i, c in enumerate(group):
            gu_ref[:, lane(c)] = jnp.sum(gu[i], axis=0, keepdims=True)
            gw_ref[:, lane(c)] = -jnp.sum(gw[i], axis=0, keepdims=True)
    for c in range(width // LANES):
        gk_ref[:, lane(c)] = fk[c].astype(jnp.bfloat16)
        gv_ref[:, lane(c)] = fv[c].astype(jnp.bfloat16)
        sig = jax.nn.sigmoid(r_ref[:, lane(c)])
        gr_ref[:, lane(c)] = (gg_ref[:, lane(c)] * yb[c] * sig * (1.0 - sig)).astype(jnp.bfloat16)


def wkv_backward(r, gg, kb, vb, yb, mb, ab, bb, gyb, w, u, ca, cb, lc, ea, eb):
    rows, width = r.shape
    chunks = rows // STEP
    low = jax.ShapeDtypeStruct((rows, width), jnp.bfloat16)
    row = jax.ShapeDtypeStruct((1, width), jnp.float32)
    return pl.pallas_call(
        wkv_backward_body,
        out_shape=(low, low, low, row, row),
        in_specs=[VMEM] * 16,
        out_specs=[VMEM] * 5,
        scratch_shapes=[pltpu.VMEM((chunks, width), jnp.float32)] * 2 + [pltpu.VMEM((width // LANES, rows, LANES), jnp.float32)] * 2,
        compiler_params=pltpu.CompilerParams(vmem_limit_bytes=40 * 2**20),
        cost_estimate=pl.CostEstimate(flops=80 * rows * width, transcendentals=6 * rows * width, bytes_accessed=44 * rows * width),
        name="wkv_backward",
    )(r, gg, kb, vb, yb, mb, ab, bb, gyb, w, u, ca, cb, lc, ea, eb)


def local(nd, nt, x, num, den, top, prev_a, prev_f, n1g, n1b, fading, reward, mk, mv, mr, wk, wv, wr, wo, n2g, n2b, ck, cr,
          fk, fv, fr, up):
    rows, dim = x.shape
    seqs = prev_a.shape[0]
    span = nt // seqs
    tp = lax.axis_index("tensor")
    dp = lax.axis_index("dp")
    seq = tp // span
    pos = tp % span
    part = dim // nd
    head = num.shape[1]
    ahead = [(i, i + 1) for i in range(nt - 1)]
    behind = [(i + 1, i) for i in range(nt - 1)]

    def gather(shard):
        whole = lax.all_gather(shard.T, ("dp", "tensor"), axis=0, tiled=True)
        return whole.reshape(nd, nt * shard.shape[1], shard.shape[0])

    whole_k, whole_v, whole_r, whole_o = gather(wk), gather(wv), gather(wr), gather(wo)
    whole_fk, whole_fv, whole_fr = gather(fk), gather(fv), gather(fr)
    states = lax.all_gather(jnp.stack([num, den, top]), "tensor", axis=2, tiled=True)

    def into(left, whole):
        total = dot_nt(left[:, :part], whole[0])
        for d in range(1, nd):
            total = total + dot_nt(left[:, d * part:(d + 1) * part], whole[d])
        return total

    def outof(left, whole):
        return jnp.concatenate([dot_nn(left, whole[d]) for d in range(nd)], axis=1)

    def weight_grad(cols, ins):
        both = dot_tn(cols, ins).astype(jnp.bfloat16)
        return jnp.stack([both[:, d * part:(d + 1) * part] for d in range(nd)])

    def prior(rows_now, previous):
        halo = lax.ppermute(rows_now[-1:, :], "tensor", ahead)
        mine = lax.dynamic_slice_in_dim(previous, seq, 1, 0)
        first = jnp.where(pos == 0, mine, halo)
        return jnp.concatenate([first, rows_now[:-1, :]], axis=0)

    def pushed(back):
        halo = lax.ppermute(back[:1, :], "tensor", behind)
        last = jnp.where(pos == span - 1, 0.0, halo)
        return jnp.concatenate([back[1:, :], last], axis=0)

    s1, scale1 = norm_stats(x)
    first = (s1 * n1g + n1b).astype(jnp.bfloat16)
    before = prior(first, prev_a)
    key_in, value_in, recept_in = blended(first, before, mk), blended(first, before, mv), blended(first, before, mr)
    keys, vals, recept = into(key_in, whole_k), into(value_in, whole_v), into(recept_in, whole_r)

    w = jnp.exp(fading)
    steps = jnp.arange(rows, dtype=jnp.float32)[:, None]
    tail = keys - (rows - 1.0 - steps) * w
    m_loc = jnp.max(tail, axis=0)
    e_loc = jnp.exp(tail - m_loc)
    sent = jnp.stack([jnp.sum(e_loc * vals, axis=0), jnp.sum(e_loc, axis=0), m_loc])
    got = lax.all_gather(sent, "tensor", axis=0)
    mine = lax.dynamic_slice_in_dim(got, seq * span, span, 0)
    start = lax.dynamic_index_in_dim(states, seq, 1, keepdims=False)
    a, b, m = start[0], start[1], start[2]
    for i in range(span - 1):
        on = i < pos
        mw = m - rows * w
        mn = jnp.maximum(mw, mine[i, 2])
        keep, take = jnp.exp(mw - mn), jnp.exp(mine[i, 2] - mn)
        a = jnp.where(on, keep * a + take * mine[i, 0], a)
        b = jnp.where(on, keep * b + take * mine[i, 1], b)
        m = jnp.where(on, mn, m)
    wr_, ur_ = w[None, :], reward[None, :]
    gated, kb, vb, yb, mb, ab, bb = wkv_forward(keys, vals, recept, wr_, ur_, a[None, :], b[None, :], m[None, :])
    middle = x + outof(gated, whole_o)

    s2, scale2 = norm_stats(middle)
    second = (s2 * n2g + n2b).astype(jnp.bfloat16)
    before2 = prior(second, prev_f)
    chan_key = blended(second, before2, ck)
    chan_rec = blended(second, before2, cr)
    hidden = jnp.maximum(into(chan_key, whole_fk), 0.0)
    squared = jnp.square(hidden).astype(jnp.bfloat16)
    chan_values = outof(squared, whole_fv)
    gate = jax.nn.sigmoid(into(chan_rec, whole_fr))
    result = middle + gate * chan_values

    g_values = (up * gate).astype(jnp.bfloat16)
    g_gate = (up * chan_values * gate * (1.0 - gate)).astype(jnp.bfloat16)
    grad_fr = weight_grad(g_gate, chan_rec)
    g_rec_in = outof(g_gate, whole_fr)
    g_squared = into(g_values, whole_fv)
    grad_fv = weight_grad(squared, g_values)
    g_hidden = (g_squared * 2.0 * hidden).astype(jnp.bfloat16)
    grad_fk = weight_grad(g_hidden, chan_key)
    g_key_in = outof(g_hidden, whole_fk)
    diff2 = second.astype(jnp.float32) - before2.astype(jnp.float32)
    grad_ck = jnp.sum(g_key_in * diff2, axis=0)
    grad_cr = jnp.sum(g_rec_in * diff2, axis=0)
    back2 = g_key_in * (1.0 - ck) + g_rec_in * (1.0 - cr)
    g_second = g_key_in * ck + g_rec_in * cr + pushed(back2)
    g_mid, grad_g2, grad_b2 = norm_back(g_second, s2, scale2, n2g)
    g_middle = up + g_mid
    g_attn = g_middle.astype(jnp.bfloat16)
    g_gated = into(g_attn, whole_o)
    grad_o = weight_grad(gated, g_attn)

    gyb, ca, cb, lc, la, lb, lg = wkv_carry(recept, g_gated, kb, yb, mb, bb, wr_, ur_)
    sent = jnp.concatenate([la, lb, lg], axis=0)
    got = lax.all_gather(sent, "tensor", axis=0)

    def chain(items, steps_on):
        ga = jnp.zeros((dim,), jnp.float32)
        gb = jnp.zeros((dim,), jnp.float32)
        for i in reversed(range(span)):
            keep = jnp.exp(items[i, 2])
            na, nb = items[i, 0] + keep * ga, items[i, 1] + keep * gb
            if steps_on is None:
                ga, gb = na, nb
            else:
                on = i > steps_on
                ga, gb = jnp.where(on, na, ga), jnp.where(on, nb, gb)
        return ga, gb

    ea, eb = chain(lax.dynamic_slice_in_dim(got, seq * span, span, 0), pos)
    own = lax.dynamic_slice_in_dim(got, tp * head, head, 2)
    nums, dens = [], []
    for s in range(seqs):
        ga, gb = jnp.zeros((head,), jnp.float32), jnp.zeros((head,), jnp.float32)
        for i in reversed(range(span)):
            keep = jnp.exp(own[s * span + i, 2])
            ga, gb = own[s * span + i, 0] + keep * ga, own[s * span + i, 1] + keep * gb
        nums.append(ga)
        dens.append(gb)
    grad_num, grad_den = jnp.stack(nums), jnp.stack(dens)
    grad_top = grad_num * num + grad_den * den

    g_keys, g_vals, g_recept, gu, gw = wkv_backward(
        recept, g_gated, kb, vb, yb, mb, ab, bb, gyb, wr_, ur_, ca, cb, lc, ea[None, :], eb[None, :])
    grad_k, grad_v, grad_r = weight_grad(g_keys, key_in), weight_grad(g_vals, value_in), weight_grad(g_recept, recept_in)
    diff1 = first.astype(jnp.float32) - before.astype(jnp.float32)
    in_k, in_v, in_r = outof(g_keys, whole_k), outof(g_vals, whole_v), outof(g_recept, whole_r)
    grad_mk, grad_mv, grad_mr = jnp.sum(in_k * diff1, axis=0), jnp.sum(in_v * diff1, axis=0), jnp.sum(in_r * diff1, axis=0)
    back1 = in_k * (1.0 - mk) + in_v * (1.0 - mv) + in_r * (1.0 - mr)
    g_first = in_k * mk + in_v * mv + in_r * mr + pushed(back1)
    g_tok, grad_g1, grad_b1 = norm_back(g_first, s1, scale1, n1g)
    tokens_grad = g_middle + g_tok

    def scatter(stack):
        cols = stack.shape[1]
        mine = lax.psum_scatter(stack.reshape(nd * cols, part), "dp", scatter_dimension=0, tiled=True)
        mine = lax.psum_scatter(mine, "tensor", scatter_dimension=0, tiled=True)
        return mine.astype(jnp.float32).T

    out_k, out_v, out_r, out_o = scatter(grad_k), scatter(grad_v), scatter(grad_r), scatter(grad_o)
    out_fk, out_fv, out_fr = scatter(grad_fk), scatter(grad_fv), scatter(grad_fr)

    vectors = jnp.stack([grad_g1, grad_b1, gw[0] * w, gu[0], grad_mk, grad_mv, grad_mr, grad_g2, grad_b2, grad_ck, grad_cr])
    lead = jnp.where(pos == 0, 1.0, 0.0)
    slots = jnp.zeros((2, nd, seqs, dim), jnp.float32)
    pair = (jnp.stack([back1[0], back2[0]]) * lead)[:, None, None, :]
    slots = lax.dynamic_update_slice(slots, pair, (0, dp, seq, 0))
    vectors, slots = lax.psum((vectors, slots), ("dp", "tensor"))
    prevs = lax.dynamic_index_in_dim(slots, dp, axis=1, keepdims=False)
    return (result, tokens_grad, grad_num, grad_den, grad_top, prevs[0], prevs[1],
            vectors[0], vectors[1], vectors[2], vectors[3], vectors[4], vectors[5], vectors[6],
            out_k, out_v, out_r, out_o, vectors[7], vectors[8], vectors[9], vectors[10], out_fk, out_fv, out_fr)


def solution(mesh):
    nd, nt = mesh.shape["dp"], mesh.shape["tensor"]
    rows, both, lead, one = P(("dp", "tensor"), None), P("dp", "tensor"), P("dp", None), P()
    return jax.shard_map(
        functools.partial(local, nd, nt),
        mesh=mesh,
        in_specs=(rows, both, both, both, lead, lead) + (one,) * 7 + (both,) * 4 + (one,) * 4 + (both,) * 3 + (rows,),
        out_specs=(rows, rows, both, both, both, lead, lead) + (one,) * 7 + (both,) * 4 + (one,) * 4 + (both,) * 3,
        check_vma=False,
    )
```

```python
import functools

import jax
import jax.numpy as jnp
from jax import lax
from jax.experimental import pallas as pl
from jax.experimental.pallas import tpu as pltpu
from jax.sharding import PartitionSpec as P

EPS = 1e-05
STEP = 16
NEG = -1e30


def norm_stats(x):
    center = x - jnp.mean(x, axis=-1, keepdims=True)
    scale = lax.rsqrt(jnp.mean(center * center, axis=-1, keepdims=True) + EPS)
    return center * scale, scale


def norm_back(g, s, scale, gain):
    q = g * gain
    gx = (q - jnp.mean(q, axis=-1, keepdims=True) - s * jnp.mean(q * s, axis=-1, keepdims=True)) * scale
    return gx, jnp.sum(g * s, axis=0), jnp.sum(g, axis=0)


def blended(now, before, mix):
    return (now.astype(jnp.float32) * mix + before.astype(jnp.float32) * (1.0 - mix)).astype(jnp.bfloat16)


def dot_nt(x, y):
    return lax.dot_general(x, y, (((1,), (1,)), ((), ())), preferred_element_type=jnp.float32)


def dot_nn(x, y):
    return lax.dot_general(x, y, (((1,), (0,)), ((), ())), preferred_element_type=jnp.float32)


def dot_tn(x, y):
    return lax.dot_general(x, y, (((0,), (0,)), ((), ())), preferred_element_type=jnp.float32)


LANES = 128
VMEM = pl.BlockSpec(memory_space=pltpu.VMEM)


def scan_groups(width):
    blocks = width // LANES
    size = 4 if blocks % 4 == 0 else 1
    return [range(g, g + size) for g in range(0, blocks, size)]


def lane(c):
    return slice(c * LANES, (c + 1) * LANES)


def wkv_forward_body(k_ref, v_ref, r_ref, w_ref, u_ref, a0_ref, b0_ref, m0_ref,
                     g_ref, kb, vb, yb, mb, ab, bb, sm, sa, sb):
    rows, width = k_ref.shape
    chunks = rows // STEP
    for c in range(width // LANES):
        kb[c] = k_ref[:, lane(c)]
        vb[c] = v_ref[:, lane(c)]

    for group in scan_groups(width):
        m = [jnp.full((chunks, LANES), NEG, jnp.float32) for _ in group]
        a = [jnp.zeros((chunks, LANES), jnp.float32) for _ in group]
        b = [jnp.zeros((chunks, LANES), jnp.float32) for _ in group]
        for j in range(STEP):
            at = pl.ds(j, chunks, stride=STEP)
            for i, c in enumerate(group):
                k = kb[c, at, :]
                mw = m[i] - w_ref[:, lane(c)]
                m[i] = jnp.maximum(mw, k)
                keep = jnp.exp(mw - m[i])
                take = jnp.exp(k - m[i])
                a[i] = keep * a[i] + take * vb[c, at, :]
                b[i] = keep * b[i] + take
        for i, c in enumerate(group):
            sm[:, lane(c)] = m[i]
            sa[:, lane(c)] = a[i]
            sb[:, lane(c)] = b[i]

    w = w_ref[...]
    m, a, b = m0_ref[...], a0_ref[...], b0_ref[...]
    for s in range(chunks):
        me, ae, be = sm[s:s + 1, :], sa[s:s + 1, :], sb[s:s + 1, :]
        sm[s:s + 1, :] = m
        sa[s:s + 1, :] = a
        sb[s:s + 1, :] = b
        mw = m - float(STEP) * w
        m = jnp.maximum(mw, me)
        keep = jnp.exp(mw - m)
        take = jnp.exp(me - m)
        a = keep * a + take * ae
        b = keep * b + take * be

    for group in scan_groups(width):
        m = [sm[:, lane(c)] for c in group]
        a = [sa[:, lane(c)] for c in group]
        b = [sb[:, lane(c)] for c in group]
        for j in range(STEP):
            at = pl.ds(j, chunks, stride=STEP)
            for i, c in enumerate(group):
                k = kb[c, at, :]
                v = vb[c, at, :]
                mb[c, at, :] = m[i]
                ab[c, at, :] = a[i]
                bb[c, at, :] = b[i]
                uk = u_ref[:, lane(c)] + k
                p = jnp.maximum(m[i], uk)
                alpha = jnp.exp(m[i] - p)
                beta = jnp.exp(uk - p)
                yb[c, at, :] = (alpha * a[i] + beta * v) / (alpha * b[i] + beta)
                mw = m[i] - w_ref[:, lane(c)]
                m[i] = jnp.maximum(mw, k)
                keep = jnp.exp(mw - m[i])
                take = jnp.exp(k - m[i])
                a[i] = keep * a[i] + take * v
                b[i] = keep * b[i] + take
    for c in range(width // LANES):
        g_ref[:, lane(c)] = (jax.nn.sigmoid(r_ref[:, lane(c)]) * yb[c]).astype(jnp.bfloat16)


def wkv_forward(k, v, r, w, u, a0, b0, m0):
    rows, width = k.shape
    block = jax.ShapeDtypeStruct((width // LANES, rows, LANES), jnp.float32)
    chunks = rows // STEP
    return pl.pallas_call(
        wkv_forward_body,
        out_shape=(jax.ShapeDtypeStruct((rows, width), jnp.bfloat16),) + (block,) * 6,
        in_specs=[VMEM] * 8,
        out_specs=[VMEM] * 7,
        scratch_shapes=[pltpu.VMEM((chunks, width), jnp.float32)] * 3,
        compiler_params=pltpu.CompilerParams(vmem_limit_bytes=40 * 2**20),
        cost_estimate=pl.CostEstimate(flops=60 * rows * width, transcendentals=7 * rows * width, bytes_accessed=36 * rows * width),
        name="wkv_forward",
    )(k, v, r, w, u, a0, b0, m0)


def wkv_carry_body(r_ref, gg_ref, kb, yb, mb, bb, w_ref, u_ref, gyb, ca_ref, cb_ref, lc_ref, la_ref, lb_ref, lg_ref):
    rows, width = r_ref.shape
    chunks = rows // STEP
    for c in range(width // LANES):
        gyb[c] = gg_ref[:, lane(c)] * jax.nn.sigmoid(r_ref[:, lane(c)])
    for group in scan_groups(width):
        ga = [jnp.zeros((chunks, LANES), jnp.float32) for _ in group]
        gb = [jnp.zeros((chunks, LANES), jnp.float32) for _ in group]
        end = [None for _ in group]
        for j in reversed(range(STEP)):
            at = pl.ds(j, chunks, stride=STEP)
            for i, c in enumerate(group):
                w = w_ref[:, lane(c)]
                k = kb[c, at, :]
                m = mb[c, at, :]
                uk = u_ref[:, lane(c)] + k
                p = jnp.maximum(m, uk)
                alpha = jnp.exp(m - p)
                beta = jnp.exp(uk - p)
                gn = gyb[c, at, :] / (alpha * bb[c, at, :] + beta)
                gd = -gn * yb[c, at, :]
                mw = m - w
                mn = jnp.maximum(mw, k)
                if j == STEP - 1:
                    end[i] = mn
                keep = jnp.exp(mw - mn)
                ga[i] = alpha * gn + keep * ga[i]
                gb[i] = alpha * gd + keep * gb[i]
                if j == 0:
                    lc_ref[:, lane(c)] = m - float(STEP) * w - end[i]
        for i, c in enumerate(group):
            ca_ref[:, lane(c)] = ga[i]
            cb_ref[:, lane(c)] = gb[i]
    ga = jnp.zeros((1, width), jnp.float32)
    gb = jnp.zeros((1, width), jnp.float32)
    lg = jnp.zeros((1, width), jnp.float32)
    for s in reversed(range(chunks)):
        keep = jnp.exp(lc_ref[s:s + 1, :])
        ga = ca_ref[s:s + 1, :] + keep * ga
        gb = cb_ref[s:s + 1, :] + keep * gb
        lg = lg + lc_ref[s:s + 1, :]
    la_ref[...] = ga
    lb_ref[...] = gb
    lg_ref[...] = lg


def wkv_carry(r, gg, kb, yb, mb, bb, w, u):
    rows, width = r.shape
    chunks = rows // STEP
    small = jax.ShapeDtypeStruct((chunks, width), jnp.float32)
    row = jax.ShapeDtypeStruct((1, width), jnp.float32)
    block = jax.ShapeDtypeStruct((width // LANES, rows, LANES), jnp.float32)
    return pl.pallas_call(
        wkv_carry_body,
        out_shape=(block, small, small, small, row, row, row),
        in_specs=[VMEM] * 8,
        out_specs=[VMEM] * 7,
        compiler_params=pltpu.CompilerParams(vmem_limit_bytes=40 * 2**20),
        cost_estimate=pl.CostEstimate(flops=40 * rows * width, transcendentals=5 * rows * width, bytes_accessed=28 * rows * width),
        name="wkv_carry",
    )(r, gg, kb, yb, mb, bb, w, u)


def wkv_backward_body(r_ref, gg_ref, kb, vb, yb, mb, ab, bb, gyb, w_ref, u_ref, ca_ref, cb_ref, lc_ref, ea_ref, eb_ref,
                      gk_ref, gv_ref, gr_ref, gu_ref, gw_ref, ta, tb, fk, fv):
    rows, width = r_ref.shape
    chunks = rows // STEP
    ga, gb = ea_ref[...], eb_ref[...]
    for s in reversed(range(chunks)):
        ta[s:s + 1, :] = ga
        tb[s:s + 1, :] = gb
        keep = jnp.exp(lc_ref[s:s + 1, :])
        ga = ca_ref[s:s + 1, :] + keep * ga
        gb = cb_ref[s:s + 1, :] + keep * gb
    for group in scan_groups(width):
        ga = [ta[:, lane(c)] for c in group]
        gb = [tb[:, lane(c)] for c in group]
        gu = [jnp.zeros((chunks, LANES), jnp.float32) for _ in group]
        gw = [jnp.zeros((chunks, LANES), jnp.float32) for _ in group]
        for j in reversed(range(STEP)):
            at = pl.ds(j, chunks, stride=STEP)
            for i, c in enumerate(group):
                k = kb[c, at, :]
                v = vb[c, at, :]
                m = mb[c, at, :]
                uk = u_ref[:, lane(c)] + k
                p = jnp.maximum(m, uk)
                alpha = jnp.exp(m - p)
                beta = jnp.exp(uk - p)
                b = bb[c, at, :]
                gn = gyb[c, at, :] / (alpha * b + beta)
                gd = -gn * yb[c, at, :]
                mw = m - w_ref[:, lane(c)]
                mn = jnp.maximum(mw, k)
                keep = jnp.exp(mw - mn)
                take = jnp.exp(k - mn)
                now = beta * (gn * v + gd)
                fv[c, at, :] = beta * gn + take * ga[i]
                fk[c, at, :] = now + take * (ga[i] * v + gb[i])
                gu[i] = gu[i] + now
                gw[i] = gw[i] + keep * (ga[i] * ab[c, at, :] + gb[i] * b)
                ga[i] = alpha * gn + keep * ga[i]
                gb[i] = alpha * gd + keep * gb[i]
        for i, c in enumerate(group):
            gu_ref[:, lane(c)] = jnp.sum(gu[i], axis=0, keepdims=True)
            gw_ref[:, lane(c)] = -jnp.sum(gw[i], axis=0, keepdims=True)
    for c in range(width // LANES):
        gk_ref[:, lane(c)] = fk[c].astype(jnp.bfloat16)
        gv_ref[:, lane(c)] = fv[c].astype(jnp.bfloat16)
        sig = jax.nn.sigmoid(r_ref[:, lane(c)])
        gr_ref[:, lane(c)] = (gg_ref[:, lane(c)] * yb[c] * sig * (1.0 - sig)).astype(jnp.bfloat16)


def wkv_backward(r, gg, kb, vb, yb, mb, ab, bb, gyb, w, u, ca, cb, lc, ea, eb):
    rows, width = r.shape
    chunks = rows // STEP
    low = jax.ShapeDtypeStruct((rows, width), jnp.bfloat16)
    row = jax.ShapeDtypeStruct((1, width), jnp.float32)
    return pl.pallas_call(
        wkv_backward_body,
        out_shape=(low, low, low, row, row),
        in_specs=[VMEM] * 16,
        out_specs=[VMEM] * 5,
        scratch_shapes=[pltpu.VMEM((chunks, width), jnp.float32)] * 2 + [pltpu.VMEM((width // LANES, rows, LANES), jnp.float32)] * 2,
        compiler_params=pltpu.CompilerParams(vmem_limit_bytes=40 * 2**20),
        cost_estimate=pl.CostEstimate(flops=80 * rows * width, transcendentals=6 * rows * width, bytes_accessed=44 * rows * width),
        name="wkv_backward",
    )(r, gg, kb, vb, yb, mb, ab, bb, gyb, w, u, ca, cb, lc, ea, eb)


MESH = pl.DeviceIdType.MESH
HBM = pl.BlockSpec(memory_space=pltpu.HBM)


def place(nd, nz):
    d = lax.axis_index("dp")
    t = lax.axis_index("tensor")
    return d, t // 4, lax.rem(t // 2, 2), lax.rem(t, 2)


def spot(d, z, y, x):
    return (d, z * 4 + y * 2 + x)


def partners(nd, nz, d, z, y, x):
    out = [spot(lax.rem(d + i, nd), z, y, x) for i in range(1, nd)]
    out += [spot(d, lax.rem(z + i, nz), y, x) for i in range(1, nz)]
    return out + [spot(d, z, 1 - y, x), spot(d, z, y, 1 - x)]


def meet(others):
    barrier = pltpu.get_barrier_semaphore()
    for other in others:
        pl.semaphore_signal(barrier, inc=1, device_id=other, device_id_type=MESH)
    pl.semaphore_wait(barrier, len(others))


def send(src, dst, send_sem, recv_sem, to):
    return pltpu.make_async_remote_copy(src_ref=src, dst_ref=dst, send_sem=send_sem, recv_sem=recv_sem, device_id=to, device_id_type=MESH)


def gather_body(nd, nz, pieces, lag, count, *refs):
    ins, outs = refs[:count], refs[count:2 * count]
    loc, zs, zr, as_, ar, bs, br, ds, dr = refs[2 * count:]
    d, z, y, x = place(nd, nz)
    meet(partners(nd, nz, d, z, y, x))

    def own(p):
        a, at, n = pieces[p]
        return pltpu.make_async_copy(ins[a].at[at:at + n], outs[a].at[d, z, y, x, at:at + n], loc.at[p])

    def along_z(p, i, source):
        a, at, n = pieces[p]
        return send(ins[a].at[at:at + n], outs[a].at[d, source, y, x, at:at + n], zs.at[p, i - 1], zr.at[p, i - 1],
                    spot(d, lax.rem(z + i, nz), y, x))

    def first_pair(p, mine):
        a, at, n = pieces[p]
        if p % 2 == 0:
            part = outs[a].at[d, :, y if mine else 1 - y, x, at:at + n]
            to = spot(d, z, 1 - y, x)
        else:
            part = outs[a].at[d, :, y, x if mine else 1 - x, at:at + n]
            to = spot(d, z, y, 1 - x)
        return send(part, part, as_.at[p], ar.at[p], to)

    def second_pair(p, mine):
        a, at, n = pieces[p]
        if p % 2 == 0:
            part = outs[a].at[d, :, :, x if mine else 1 - x, at:at + n]
            to = spot(d, z, y, 1 - x)
        else:
            part = outs[a].at[d, :, y if mine else 1 - y, :, at:at + n]
            to = spot(d, z, 1 - y, x)
        return send(part, part, bs.at[p], br.at[p], to)

    def along_d(p, i, source):
        a, at, n = pieces[p]
        part = outs[a].at[source, :, :, :, at:at + n]
        return send(part, part, ds.at[p, i - 1], dr.at[p, i - 1], spot(lax.rem(d + i, nd), z, y, x))

    total = len(pieces)
    for step in range(total + 3 * lag):
        p = step
        if p < total:
            own(p).start()
            for i in range(1, nz):
                along_z(p, i, z).start()
        p = step - lag
        if 0 <= p < total:
            own(p).wait()
            for i in range(1, nz):
                along_z(p, i, lax.rem(z - i + nz, nz)).wait_recv()
            first_pair(p, True).start()
        p = step - 2 * lag
        if 0 <= p < total:
            first_pair(p, False).wait_recv()
            second_pair(p, True).start()
        p = step - 3 * lag
        if 0 <= p < total:
            second_pair(p, False).wait_recv()
            for i in range(1, nd):
                along_d(p, i, d).start()
    for p in range(total):
        for i in range(1, nd):
            along_d(p, i, lax.rem(d - i + nd, nd)).wait_recv()
        for i in range(1, nz):
            along_z(p, i, z).wait_send()
        first_pair(p, True).wait_send()
        second_pair(p, True).wait_send()
        for i in range(1, nd):
            along_d(p, i, d).wait_send()


def gather_weights(nd, nt, shards, unit, lag=1, space=None):
    nz = nt // 4
    pieces = []
    for a, s in enumerate(shards):
        pieces += [(a, at, min(unit, s.shape[0])) for at in range(0, s.shape[0], unit)]
    n = len(pieces)
    dma = pltpu.SemaphoreType.DMA
    outs = pl.pallas_call(
        functools.partial(gather_body, nd, nz, pieces, lag, len(shards)),
        out_shape=tuple(jax.ShapeDtypeStruct((nd, nz, 2, 2) + s.shape, s.dtype) for s in shards),
        in_specs=[HBM] * len(shards),
        out_specs=[space or HBM] * len(shards),
        scratch_shapes=[dma((n,)), dma((n, nz - 1)), dma((n, nz - 1)), dma((n,)), dma((n,)), dma((n,)), dma((n,)),
                        dma((n, nd - 1)), dma((n, nd - 1))],
        compiler_params=pltpu.CompilerParams(collective_id=0, has_side_effects=True, vmem_limit_bytes=58 * 2**20),
        name="gather_weights",
    )(*shards)
    return [o.reshape(nd, nt * s.shape[0], s.shape[1]) for o, s in zip(outs, shards)]


def add_tiles(dst, src, tiles):
    @pl.loop(0, tiles)
    def _(i):
        dst[i] = (dst[i].astype(jnp.float32) + src[i].astype(jnp.float32)).astype(dst.dtype)


def scatter_body(nd, nz, chunks, rc, part, lag, ahead, count, *refs):
    grads, vec = refs[:count], refs[count]
    out, vout, own, sib, ra, rb, rz, vd, v1, vx, v2, vy, v3, vz, loc, ds, dr, as_, ar, bs, br, zs, zr, vs, vr = refs[count + 1:]
    d, z, y, x = place(nd, nz)
    meet(partners(nd, nz, d, z, y, x))
    f32 = jnp.float32

    def load(c):
        a, at = chunks[c]
        return pltpu.make_async_copy(grads[a].at[d, :, :, :, at:at + rc], own.at[c], loc.at[c])

    def along_d(c, i):
        a, at = chunks[c]
        to = lax.rem(d + i, nd)
        return send(grads[a].at[to, :, :, :, at:at + rc], sib.at[i - 1, c], ds.at[i - 1, c], dr.at[i - 1, c], spot(to, z, y, x))

    def first_pair(c):
        if c % 2 == 0:
            return send(own.at[c, :, :, 1 - x], ra.at[c], as_.at[c], ar.at[c], spot(d, z, y, 1 - x))
        return send(own.at[c, :, 1 - y], ra.at[c], as_.at[c], ar.at[c], spot(d, z, 1 - y, x))

    def second_pair(c):
        if c % 2 == 0:
            return send(own.at[c, :, 1 - y, x], rb.at[c], bs.at[c], br.at[c], spot(d, z, 1 - y, x))
        return send(own.at[c, :, y, 1 - x], rb.at[c], bs.at[c], br.at[c], spot(d, z, y, 1 - x))

    def along_z(c, i):
        to = lax.rem(z + i, nz)
        return send(own.at[c, to, y, x], rz.at[i - 1, c], zs.at[i - 1, c], zr.at[i - 1, c], spot(d, to, y, x))

    total = len(chunks)
    top = vd.shape[1]

    def vec_d(i):
        to = lax.rem(d + i, nd)
        return send(vec.at[:top], vd.at[d], vs.at[i - 1], vr.at[i - 1], spot(to, z, y, x))

    def vec_x():
        return send(v1, vx, vs.at[nd - 1], vr.at[nd - 1], spot(d, z, y, 1 - x))

    def vec_y():
        return send(v2, vy, vs.at[nd], vr.at[nd], spot(d, z, 1 - y, x))

    def vec_z(i):
        return send(v3, vz.at[z], vs.at[nd + i], vr.at[nd + i], spot(d, lax.rem(z + i, nz), y, x))

    def vec_step(step):
        if step == 0:
            vd[d] = vec[:top]
            for i in range(1, nd):
                vec_d(i).start()
        elif step == 1:
            for i in range(1, nd):
                vec_d(i).wait()
            acc = vd[0]
            for i in range(1, nd):
                acc = acc + vd[i]
            v1[:top] = acc
            v1[top:] = vec[top:]
            vec_x().start()
        elif step == 2:
            vec_x().wait()
            v2[...] = v1[...] + vx[...]
            vec_y().start()
        elif step == 3:
            vec_y().wait()
            v3[...] = v2[...] + vy[...]
            vz[z] = v3[...]
            for i in range(1, nz):
                vec_z(i).start()
        elif step == 4:
            for i in range(1, nz):
                vec_z(i).wait()
            acc = vz[0]
            for i in range(1, nz):
                acc = acc + vz[i]
            vout[...] = acc

    def begin(c):
        load(c).start()
        for i in range(1, nd):
            along_d(c, i).start()

    for c in range(min(ahead, total)):
        begin(c)
    for step in range(total + 3 * lag):
        c = step
        if c + ahead < total:
            begin(c + ahead)
        if step % 2 == 0:
            vec_step(step // 2)
        if c < total:
            load(c).wait()
            for i in range(1, nd):
                along_d(c, i).wait_recv()

            @pl.loop(0, nz)
            def _(b):
                for q in range(4):
                    acc = own[c, b, q // 2, q % 2].astype(f32)
                    for i in range(1, nd):
                        acc = acc + sib[i - 1, c, b, q // 2, q % 2].astype(f32)
                    own[c, b, q // 2, q % 2] = acc.astype(jnp.bfloat16)
            first_pair(c).start()
        c = step - lag
        if 0 <= c < total:
            first_pair(c).wait_recv()

            @pl.loop(0, nz)
            def _(b):
                for q in range(2):
                    at = (b, q, x) if c % 2 == 0 else (b, y, q)
                    own[(c,) + at] = (own[(c,) + at].astype(f32) + ra[c, b, q].astype(f32)).astype(jnp.bfloat16)
            second_pair(c).start()
        c = step - 2 * lag
        if 0 <= c < total:
            second_pair(c).wait_recv()

            @pl.loop(0, nz)
            def _(b):
                own[c, b, y, x] = (own[c, b, y, x].astype(f32) + rb[c, b].astype(f32)).astype(jnp.bfloat16)
            for i in range(1, nz):
                along_z(c, i).start()
        c = step - 3 * lag
        if 0 <= c < total:
            for i in range(1, nz):
                along_z(c, i).wait_recv()
            acc = own[c, z, y, x].astype(f32)
            for i in range(1, nz):
                acc = acc + rz[i - 1, c].astype(f32)
            out[c * rc:(c + 1) * rc] = acc
    for c in range(total):
        for i in range(1, nd):
            along_d(c, i).wait_send()
        first_pair(c).wait_send()
        second_pair(c).wait_send()
        for i in range(1, nz):
            along_z(c, i).wait_send()


def scatter_grads(nd, nt, grads, vec, top, rc, lag=2, ahead=3):
    nz = nt // 4
    part = grads[0].shape[2]
    split = [g.reshape(nd, nz, 2, 2, g.shape[1] // nt, part) for g in grads]
    chunks = []
    for a, g in enumerate(split):
        chunks += [(a, at) for at in range(0, g.shape[4], rc)]
    n = len(chunks)
    dma = pltpu.SemaphoreType.DMA
    bf = jnp.bfloat16
    wide = vec.shape[1]

    def vv(shape):
        return pltpu.VMEM(shape, jnp.float32)

    return pl.pallas_call(
        functools.partial(scatter_body, nd, nz, chunks, rc, part, lag, ahead, len(grads)),
        out_shape=(jax.ShapeDtypeStruct((n * rc, part), jnp.float32), jax.ShapeDtypeStruct(vec.shape, vec.dtype)),
        in_specs=[HBM] * len(grads) + [VMEM],
        out_specs=[VMEM, VMEM],
        scratch_shapes=[pltpu.VMEM((n, nz, 2, 2, rc, part), bf), pltpu.VMEM((nd - 1, n, nz, 2, 2, rc, part), bf),
                        pltpu.VMEM((n, nz, 2, rc, part), bf), pltpu.VMEM((n, nz, rc, part), bf), pltpu.VMEM((nz - 1, n, rc, part), bf),
                        vv((nd, top, wide)), vv(vec.shape), vv(vec.shape), vv(vec.shape), vv(vec.shape), vv(vec.shape), vv((nz,) + vec.shape),
                        dma((n,)), dma((nd - 1, n)), dma((nd - 1, n)), dma((n,)), dma((n,)), dma((n,)), dma((n,)),
                        dma((nz - 1, n)), dma((nz - 1, n)), dma((nd + nz,)), dma((nd + nz,))],
        compiler_params=pltpu.CompilerParams(collective_id=1, has_side_effects=True, vmem_limit_bytes=58 * 2**20),
        name="scatter_grads",
    )(*split, vec)


def local(nd, nt, x, num, den, top, prev_a, prev_f, n1g, n1b, fading, reward, mk, mv, mr, wk, wv, wr, wo, n2g, n2b, ck, cr,
          fk, fv, fr, up):
    rows, dim = x.shape
    seqs = prev_a.shape[0]
    span = nt // seqs
    tp = lax.axis_index("tensor")
    dp = lax.axis_index("dp")
    seq = tp // span
    pos = tp % span
    part = dim // nd
    head = num.shape[1]
    ahead = [(i, i + 1) for i in range(nt - 1)]
    behind = [(i + 1, i) for i in range(nt - 1)]

    whole_k, whole_v, whole_r, whole_o, whole_fk, whole_fv, whole_fr = gather_weights(
        nd, nt, [s.T for s in (wk, wv, wr, wo, fk, fv, fr)], 32, 2)
    states = lax.all_gather(jnp.stack([num, den, top]), "tensor", axis=2, tiled=True)

    def into(left, whole):
        total = dot_nt(left[:, :part], whole[0])
        for d in range(1, nd):
            total = total + dot_nt(left[:, d * part:(d + 1) * part], whole[d])
        return total

    def outof(left, whole):
        return jnp.concatenate([dot_nn(left, whole[d]) for d in range(nd)], axis=1)

    def weight_grad(cols, ins):
        both = dot_tn(cols, ins).astype(jnp.bfloat16)
        return jnp.stack([both[:, d * part:(d + 1) * part] for d in range(nd)])

    def prior(rows_now, previous):
        halo = lax.ppermute(rows_now[-1:, :], "tensor", ahead)
        mine = lax.dynamic_slice_in_dim(previous, seq, 1, 0)
        first = jnp.where(pos == 0, mine, halo)
        return jnp.concatenate([first, rows_now[:-1, :]], axis=0)

    def pushed(back):
        halo = lax.ppermute(back[:1, :], "tensor", behind)
        last = jnp.where(pos == span - 1, 0.0, halo)
        return jnp.concatenate([back[1:, :], last], axis=0)

    s1, scale1 = norm_stats(x)
    first = (s1 * n1g + n1b).astype(jnp.bfloat16)
    before = prior(first, prev_a)
    key_in, value_in, recept_in = blended(first, before, mk), blended(first, before, mv), blended(first, before, mr)
    keys, vals, recept = into(key_in, whole_k), into(value_in, whole_v), into(recept_in, whole_r)

    w = jnp.exp(fading)
    steps = jnp.arange(rows, dtype=jnp.float32)[:, None]
    tail = keys - (rows - 1.0 - steps) * w
    m_loc = jnp.max(tail, axis=0)
    e_loc = jnp.exp(tail - m_loc)
    sent = jnp.stack([jnp.sum(e_loc * vals, axis=0), jnp.sum(e_loc, axis=0), m_loc])
    got = lax.all_gather(sent, "tensor", axis=0)
    mine = lax.dynamic_slice_in_dim(got, seq * span, span, 0)
    start = lax.dynamic_index_in_dim(states, seq, 1, keepdims=False)
    a, b, m = start[0], start[1], start[2]
    for i in range(span - 1):
        on = i < pos
        mw = m - rows * w
        mn = jnp.maximum(mw, mine[i, 2])
        keep, take = jnp.exp(mw - mn), jnp.exp(mine[i, 2] - mn)
        a = jnp.where(on, keep * a + take * mine[i, 0], a)
        b = jnp.where(on, keep * b + take * mine[i, 1], b)
        m = jnp.where(on, mn, m)
    wr_, ur_ = w[None, :], reward[None, :]
    gated, kb, vb, yb, mb, ab, bb = wkv_forward(keys, vals, recept, wr_, ur_, a[None, :], b[None, :], m[None, :])
    middle = x + outof(gated, whole_o)

    s2, scale2 = norm_stats(middle)
    second = (s2 * n2g + n2b).astype(jnp.bfloat16)
    before2 = prior(second, prev_f)
    chan_key = blended(second, before2, ck)
    chan_rec = blended(second, before2, cr)
    hidden = jnp.maximum(into(chan_key, whole_fk), 0.0)
    squared = jnp.square(hidden).astype(jnp.bfloat16)
    chan_values = outof(squared, whole_fv)
    gate = jax.nn.sigmoid(into(chan_rec, whole_fr))
    result = middle + gate * chan_values

    g_values = (up * gate).astype(jnp.bfloat16)
    g_gate = (up * chan_values * gate * (1.0 - gate)).astype(jnp.bfloat16)
    grad_fr = weight_grad(g_gate, chan_rec)
    g_rec_in = outof(g_gate, whole_fr)
    g_squared = into(g_values, whole_fv)
    grad_fv = weight_grad(squared, g_values)
    g_hidden = (g_squared * 2.0 * hidden).astype(jnp.bfloat16)
    grad_fk = weight_grad(g_hidden, chan_key)
    g_key_in = outof(g_hidden, whole_fk)
    diff2 = second.astype(jnp.float32) - before2.astype(jnp.float32)
    grad_ck = jnp.sum(g_key_in * diff2, axis=0)
    grad_cr = jnp.sum(g_rec_in * diff2, axis=0)
    back2 = g_key_in * (1.0 - ck) + g_rec_in * (1.0 - cr)
    g_second = g_key_in * ck + g_rec_in * cr + pushed(back2)
    g_mid, grad_g2, grad_b2 = norm_back(g_second, s2, scale2, n2g)
    g_middle = up + g_mid
    g_attn = g_middle.astype(jnp.bfloat16)
    g_gated = into(g_attn, whole_o)
    grad_o = weight_grad(gated, g_attn)

    gyb, ca, cb, lc, la, lb, lg = wkv_carry(recept, g_gated, kb, yb, mb, bb, wr_, ur_)
    sent = jnp.concatenate([la, lb, lg], axis=0)
    got = lax.all_gather(sent, "tensor", axis=0)

    def chain(items, steps_on):
        ga = jnp.zeros((dim,), jnp.float32)
        gb = jnp.zeros((dim,), jnp.float32)
        for i in reversed(range(span)):
            keep = jnp.exp(items[i, 2])
            na, nb = items[i, 0] + keep * ga, items[i, 1] + keep * gb
            if steps_on is None:
                ga, gb = na, nb
            else:
                on = i > steps_on
                ga, gb = jnp.where(on, na, ga), jnp.where(on, nb, gb)
        return ga, gb

    ea, eb = chain(lax.dynamic_slice_in_dim(got, seq * span, span, 0), pos)
    own = lax.dynamic_slice_in_dim(got, tp * head, head, 2)
    nums, dens = [], []
    for s in range(seqs):
        ga, gb = jnp.zeros((head,), jnp.float32), jnp.zeros((head,), jnp.float32)
        for i in reversed(range(span)):
            keep = jnp.exp(own[s * span + i, 2])
            ga, gb = own[s * span + i, 0] + keep * ga, own[s * span + i, 1] + keep * gb
        nums.append(ga)
        dens.append(gb)
    grad_num, grad_den = jnp.stack(nums), jnp.stack(dens)
    grad_top = grad_num * num + grad_den * den

    g_keys, g_vals, g_recept, gu, gw = wkv_backward(
        recept, g_gated, kb, vb, yb, mb, ab, bb, gyb, wr_, ur_, ca, cb, lc, ea[None, :], eb[None, :])
    grad_k, grad_v, grad_r = weight_grad(g_keys, key_in), weight_grad(g_vals, value_in), weight_grad(g_recept, recept_in)
    diff1 = first.astype(jnp.float32) - before.astype(jnp.float32)
    in_k, in_v, in_r = outof(g_keys, whole_k), outof(g_vals, whole_v), outof(g_recept, whole_r)
    grad_mk, grad_mv, grad_mr = jnp.sum(in_k * diff1, axis=0), jnp.sum(in_v * diff1, axis=0), jnp.sum(in_r * diff1, axis=0)
    back1 = in_k * (1.0 - mk) + in_v * (1.0 - mv) + in_r * (1.0 - mr)
    g_first = in_k * mk + in_v * mv + in_r * mr + pushed(back1)
    g_tok, grad_g1, grad_b1 = norm_back(g_first, s1, scale1, n1g)
    tokens_grad = g_middle + g_tok

    vectors = jnp.stack([grad_g1, grad_b1, gw[0] * w, gu[0], grad_mk, grad_mv, grad_mr, grad_g2, grad_b2, grad_ck, grad_cr])
    lead = jnp.where(pos == 0, 1.0, 0.0)
    pair = (jnp.stack([back1[0], back2[0]]) * lead)[:, None, :]
    slots = lax.dynamic_update_slice(jnp.zeros((2, seqs, dim), jnp.float32), pair, (0, seq, 0)).reshape(2 * seqs, dim)
    tail_rows = -(-2 * seqs // 8) * 8
    vec = jnp.concatenate([vectors, jnp.zeros((5, dim), jnp.float32), slots, jnp.zeros((tail_rows - 2 * seqs, dim), jnp.float32)])
    unit = sum(s.shape[1] for s in (wk, wv, wr, wo, fk, fv, fr)) // 26
    summed, vectors = scatter_grads(nd, nt, [grad_k, grad_v, grad_r, grad_o, grad_fk, grad_fv, grad_fr], vec, 16, unit)
    prevs = vectors[16:16 + 2 * seqs].reshape(2, seqs, dim)
    outs, at = [], 0
    for s in (wk, wv, wr, wo, fk, fv, fr):
        outs.append(summed[at:at + s.shape[1]].T)
        at += s.shape[1]
    out_k, out_v, out_r, out_o, out_fk, out_fv, out_fr = outs
    return (result, tokens_grad, grad_num, grad_den, grad_top, prevs[0], prevs[1],
            vectors[0], vectors[1], vectors[2], vectors[3], vectors[4], vectors[5], vectors[6],
            out_k, out_v, out_r, out_o, vectors[7], vectors[8], vectors[9], vectors[10], out_fk, out_fv, out_fr)


def solution(mesh):
    nd, nt = mesh.shape["dp"], mesh.shape["tensor"]
    rows, both, lead, one = P(("dp", "tensor"), None), P("dp", "tensor"), P("dp", None), P()
    return jax.shard_map(
        functools.partial(local, nd, nt),
        mesh=mesh,
        in_specs=(rows, both, both, both, lead, lead) + (one,) * 7 + (both,) * 4 + (one,) * 4 + (both,) * 3 + (rows,),
        out_specs=(rows, rows, both, both, both, lead, lead) + (one,) * 7 + (both,) * 4 + (one,) * 4 + (both,) * 3,
        check_vma=False,
    )
```

```python
import functools

import jax
import jax.numpy as jnp
from jax import lax
from jax.experimental import pallas as pl
from jax.experimental.pallas import tpu as pltpu
from jax.sharding import PartitionSpec as P

EPS = 1e-05
STEP = 16
NEG = -1e30


def norm_stats(x):
    center = x - jnp.mean(x, axis=-1, keepdims=True)
    scale = lax.rsqrt(jnp.mean(center * center, axis=-1, keepdims=True) + EPS)
    return center * scale, scale


def norm_back(g, s, scale, gain):
    q = g * gain
    gx = (q - jnp.mean(q, axis=-1, keepdims=True) - s * jnp.mean(q * s, axis=-1, keepdims=True)) * scale
    return gx, jnp.sum(g * s, axis=0), jnp.sum(g, axis=0)


def blended(now, before, mix):
    return (now.astype(jnp.float32) * mix + before.astype(jnp.float32) * (1.0 - mix)).astype(jnp.bfloat16)


def dot_nt(x, y):
    return lax.dot_general(x, y, (((1,), (1,)), ((), ())), preferred_element_type=jnp.float32)


def dot_nn(x, y):
    return lax.dot_general(x, y, (((1,), (0,)), ((), ())), preferred_element_type=jnp.float32)


def dot_tn(x, y):
    return lax.dot_general(x, y, (((0,), (0,)), ((), ())), preferred_element_type=jnp.float32)


LANES = 128
VMEM = pl.BlockSpec(memory_space=pltpu.VMEM)


def scan_groups(width):
    blocks = width // LANES
    size = 4 if blocks % 4 == 0 else 1
    return [range(g, g + size) for g in range(0, blocks, size)]


def lane(c):
    return slice(c * LANES, (c + 1) * LANES)


def wkv_carry_body(r_ref, gg_ref, kb, yb, mb, bb, w_ref, u_ref, gyb, ca_ref, cb_ref, lc_ref, la_ref, lb_ref, lg_ref):
    rows, width = r_ref.shape
    chunks = rows // STEP
    for c in range(width // LANES):
        gyb[c] = gg_ref[:, lane(c)] * jax.nn.sigmoid(r_ref[:, lane(c)])
    for group in scan_groups(width):
        ga = [jnp.zeros((chunks, LANES), jnp.float32) for _ in group]
        gb = [jnp.zeros((chunks, LANES), jnp.float32) for _ in group]
        end = [None for _ in group]
        for j in reversed(range(STEP)):
            at = pl.ds(j, chunks, stride=STEP)
            for i, c in enumerate(group):
                w = w_ref[:, lane(c)]
                k = kb[c, at, :]
                m = mb[c, at, :]
                uk = u_ref[:, lane(c)] + k
                p = jnp.maximum(m, uk)
                alpha = jnp.exp(m - p)
                beta = jnp.exp(uk - p)
                gn = gyb[c, at, :] / (alpha * bb[c, at, :] + beta)
                gd = -gn * yb[c, at, :]
                mw = m - w
                mn = jnp.maximum(mw, k)
                if j == STEP - 1:
                    end[i] = mn
                keep = jnp.exp(mw - mn)
                ga[i] = alpha * gn + keep * ga[i]
                gb[i] = alpha * gd + keep * gb[i]
                if j == 0:
                    lc_ref[:, lane(c)] = m - float(STEP) * w - end[i]
        for i, c in enumerate(group):
            ca_ref[:, lane(c)] = ga[i]
            cb_ref[:, lane(c)] = gb[i]
    ga = jnp.zeros((1, width), jnp.float32)
    gb = jnp.zeros((1, width), jnp.float32)
    lg = jnp.zeros((1, width), jnp.float32)
    for s in reversed(range(chunks)):
        keep = jnp.exp(lc_ref[s:s + 1, :])
        ga = ca_ref[s:s + 1, :] + keep * ga
        gb = cb_ref[s:s + 1, :] + keep * gb
        lg = lg + lc_ref[s:s + 1, :]
    la_ref[...] = ga
    lb_ref[...] = gb
    lg_ref[...] = lg


def wkv_carry(r, gg, kb, yb, mb, bb, w, u):
    rows, width = r.shape
    chunks = rows // STEP
    small = jax.ShapeDtypeStruct((chunks, width), jnp.float32)
    row = jax.ShapeDtypeStruct((1, width), jnp.float32)
    block = jax.ShapeDtypeStruct((width // LANES, rows, LANES), jnp.float32)
    return pl.pallas_call(
        wkv_carry_body,
        out_shape=(block, small, small, small, row, row, row),
        in_specs=[VMEM] * 8,
        out_specs=[VMEM] * 7,
        compiler_params=pltpu.CompilerParams(vmem_limit_bytes=40 * 2**20),
        cost_estimate=pl.CostEstimate(flops=40 * rows * width, transcendentals=5 * rows * width, bytes_accessed=28 * rows * width),
        name="wkv_carry",
    )(r, gg, kb, yb, mb, bb, w, u)


def wkv_backward_body(r_ref, gg_ref, kb, vb, yb, mb, ab, bb, gyb, w_ref, u_ref, ca_ref, cb_ref, lc_ref, ea_ref, eb_ref,
                      gk_ref, gv_ref, gr_ref, gu_ref, gw_ref, ta, tb, fk, fv):
    rows, width = r_ref.shape
    chunks = rows // STEP
    ga, gb = ea_ref[...], eb_ref[...]
    for s in reversed(range(chunks)):
        ta[s:s + 1, :] = ga
        tb[s:s + 1, :] = gb
        keep = jnp.exp(lc_ref[s:s + 1, :])
        ga = ca_ref[s:s + 1, :] + keep * ga
        gb = cb_ref[s:s + 1, :] + keep * gb
    for group in scan_groups(width):
        ga = [ta[:, lane(c)] for c in group]
        gb = [tb[:, lane(c)] for c in group]
        gu = [jnp.zeros((chunks, LANES), jnp.float32) for _ in group]
        gw = [jnp.zeros((chunks, LANES), jnp.float32) for _ in group]
        for j in reversed(range(STEP)):
            at = pl.ds(j, chunks, stride=STEP)
            for i, c in enumerate(group):
                k = kb[c, at, :]
                v = vb[c, at, :]
                m = mb[c, at, :]
                uk = u_ref[:, lane(c)] + k
                p = jnp.maximum(m, uk)
                alpha = jnp.exp(m - p)
                beta = jnp.exp(uk - p)
                b = bb[c, at, :]
                gn = gyb[c, at, :] / (alpha * b + beta)
                gd = -gn * yb[c, at, :]
                mw = m - w_ref[:, lane(c)]
                mn = jnp.maximum(mw, k)
                keep = jnp.exp(mw - mn)
                take = jnp.exp(k - mn)
                now = beta * (gn * v + gd)
                fv[c, at, :] = beta * gn + take * ga[i]
                fk[c, at, :] = now + take * (ga[i] * v + gb[i])
                gu[i] = gu[i] + now
                gw[i] = gw[i] + keep * (ga[i] * ab[c, at, :] + gb[i] * b)
                ga[i] = alpha * gn + keep * ga[i]
                gb[i] = alpha * gd + keep * gb[i]
        for i, c in enumerate(group):
            gu_ref[:, lane(c)] = jnp.sum(gu[i], axis=0, keepdims=True)
            gw_ref[:, lane(c)] = -jnp.sum(gw[i], axis=0, keepdims=True)
    for c in range(width // LANES):
        gk_ref[:, lane(c)] = fk[c].astype(jnp.bfloat16)
        gv_ref[:, lane(c)] = fv[c].astype(jnp.bfloat16)
        sig = jax.nn.sigmoid(r_ref[:, lane(c)])
        gr_ref[:, lane(c)] = (gg_ref[:, lane(c)] * yb[c] * sig * (1.0 - sig)).astype(jnp.bfloat16)


def wkv_backward(r, gg, kb, vb, yb, mb, ab, bb, gyb, w, u, ca, cb, lc, ea, eb):
    rows, width = r.shape
    chunks = rows // STEP
    low = jax.ShapeDtypeStruct((rows, width), jnp.bfloat16)
    row = jax.ShapeDtypeStruct((1, width), jnp.float32)
    return pl.pallas_call(
        wkv_backward_body,
        out_shape=(low, low, low, row, row),
        in_specs=[VMEM] * 16,
        out_specs=[VMEM] * 5,
        scratch_shapes=[pltpu.VMEM((chunks, width), jnp.float32)] * 2 + [pltpu.VMEM((width // LANES, rows, LANES), jnp.float32)] * 2,
        compiler_params=pltpu.CompilerParams(vmem_limit_bytes=40 * 2**20),
        cost_estimate=pl.CostEstimate(flops=80 * rows * width, transcendentals=6 * rows * width, bytes_accessed=44 * rows * width),
        name="wkv_backward",
    )(r, gg, kb, vb, yb, mb, ab, bb, gyb, w, u, ca, cb, lc, ea, eb)


MESH = pl.DeviceIdType.MESH
HBM = pl.BlockSpec(memory_space=pltpu.HBM)


def place(nd, nz):
    d = lax.axis_index("dp")
    t = lax.axis_index("tensor")
    return d, t // 4, lax.rem(t // 2, 2), lax.rem(t, 2)


def spot(d, z, y, x):
    return (d, z * 4 + y * 2 + x)


def partners(nd, nz, d, z, y, x):
    out = [spot(lax.rem(d + i, nd), z, y, x) for i in range(1, nd)]
    out += [spot(d, lax.rem(z + i, nz), y, x) for i in range(1, nz)]
    return out + [spot(d, z, 1 - y, x), spot(d, z, y, 1 - x)]


def meet(others):
    barrier = pltpu.get_barrier_semaphore()
    for other in others:
        pl.semaphore_signal(barrier, inc=1, device_id=other, device_id_type=MESH)
    pl.semaphore_wait(barrier, len(others))


def send(src, dst, send_sem, recv_sem, to):
    return pltpu.make_async_remote_copy(src_ref=src, dst_ref=dst, send_sem=send_sem, recv_sem=recv_sem, device_id=to, device_id_type=MESH)


def rowwise_norm(x):
    center = x - jnp.mean(x, axis=-1, keepdims=True)
    return center * lax.rsqrt(jnp.mean(center * center, axis=-1, keepdims=True) + EPS)


def scan_ends(kb, vb, w_ref, sm, sa, sb, width, chunks):
    for group in scan_groups(width):
        m = [jnp.full((chunks, LANES), NEG, jnp.float32) for _ in group]
        a = [jnp.zeros((chunks, LANES), jnp.float32) for _ in group]
        b = [jnp.zeros((chunks, LANES), jnp.float32) for _ in group]
        for j in range(STEP):
            at = pl.ds(j, chunks, stride=STEP)
            for i, c in enumerate(group):
                k = kb[c, at, :]
                mw = m[i] - w_ref[:, lane(c)]
                m[i] = jnp.maximum(mw, k)
                keep = jnp.exp(mw - m[i])
                take = jnp.exp(k - m[i])
                a[i] = keep * a[i] + take * vb[c, at, :]
                b[i] = keep * b[i] + take
        for i, c in enumerate(group):
            sm[:, lane(c)] = m[i]
            sa[:, lane(c)] = a[i]
            sb[:, lane(c)] = b[i]


def join(m, a, b, decay, me, ae, be):
    mw = m - decay
    mn = jnp.maximum(mw, me)
    keep = jnp.exp(mw - mn)
    take = jnp.exp(me - mn)
    return mn, keep * a + take * ae, keep * b + take * be


def scan_rows(kb, vb, yb, mb, ab, bb, w_ref, u_ref, sm, sa, sb, width, chunks):
    for group in scan_groups(width):
        m = [sm[:, lane(c)] for c in group]
        a = [sa[:, lane(c)] for c in group]
        b = [sb[:, lane(c)] for c in group]
        for j in range(STEP):
            at = pl.ds(j, chunks, stride=STEP)
            for i, c in enumerate(group):
                k = kb[c, at, :]
                v = vb[c, at, :]
                mb[c, at, :] = m[i]
                ab[c, at, :] = a[i]
                bb[c, at, :] = b[i]
                uk = u_ref[:, lane(c)] + k
                p = jnp.maximum(m[i], uk)
                alpha = jnp.exp(m[i] - p)
                beta = jnp.exp(uk - p)
                yb[c, at, :] = (alpha * a[i] + beta * v) / (alpha * b[i] + beta)
                m[i], a[i], b[i] = step_state(m[i], a[i], b[i], w_ref[:, lane(c)], k, v)


def step_state(m, a, b, w, k, v):
    mw = m - w
    mn = jnp.maximum(mw, k)
    keep = jnp.exp(mw - mn)
    take = jnp.exp(k - mn)
    return mn, keep * a + take * v, keep * b + take


def interleave(work, step, first, total, last):
    at = first
    for i, piece in enumerate(work):
        piece()
        goal = first + (last - first) * (i + 1) // len(work)
        while at < goal:
            step(at)
            at += 1
    while at < total:
        step(at)
        at += 1


def forward_body(nd, nz, seqs, pieces, lag, count, *refs):
    ins, refs = refs[:count], refs[count:]
    x_ref, n1g, n1b, mk, mv, mr, w_ref, u_ref, n2g, n2b, ck, cr, prev_a, prev_f = refs[:14]
    outs, refs = refs[14:14 + count], refs[14 + count:]
    first, before, gated, chan_key, chan_rec, r_ref, middle, diff2, kb, vb, yb, mb, ab, bb = refs[:14]
    (key_in, value_in, recept_in, wbuf, sbuf, init, sm, sa, sb, halo, xs, xr, second,
     loc, zs, zr, as_, ar, bs, br, ds, dr, hs, hr, es, er, ws) = refs[14:]
    d, z, y, x = place(nd, nz)
    rows, dim = x_ref.shape
    part = dim // nd
    chunks = rows // STEP
    nt = 4 * nz
    span = nt // seqs
    t = lax.axis_index("tensor")
    seq = t // span
    pos = lax.rem(t, span)
    f32 = jnp.float32

    def mate(i):
        return (d, seq * span + lax.rem(pos + i, span))

    meet(partners(nd, nz, d, z, y, x) + [mate(i) for i in range(1, span)])

    def own(p):
        a, at, n = pieces[p]
        return pltpu.make_async_copy(ins[a].at[at:at + n], outs[a].at[d, z, y, x, at:at + n], loc.at[p])

    def along_z(p, i, source):
        a, at, n = pieces[p]
        return send(ins[a].at[at:at + n], outs[a].at[d, source, y, x, at:at + n], zs.at[p, i - 1], zr.at[p, i - 1],
                    spot(d, lax.rem(z + i, nz), y, x))

    def first_pair(p, mine):
        a, at, n = pieces[p]
        if p % 2 == 0:
            block = outs[a].at[d, :, y if mine else 1 - y, x, at:at + n]
            to = spot(d, z, 1 - y, x)
        else:
            block = outs[a].at[d, :, y, x if mine else 1 - x, at:at + n]
            to = spot(d, z, y, 1 - x)
        return send(block, block, as_.at[p], ar.at[p], to)

    def second_pair(p, mine):
        a, at, n = pieces[p]
        if p % 2 == 0:
            block = outs[a].at[d, :, :, x if mine else 1 - x, at:at + n]
            to = spot(d, z, y, 1 - x)
        else:
            block = outs[a].at[d, :, y if mine else 1 - y, :, at:at + n]
            to = spot(d, z, 1 - y, x)
        return send(block, block, bs.at[p], br.at[p], to)

    def along_d(p, i, source):
        a, at, n = pieces[p]
        block = outs[a].at[source, :, :, :, at:at + n]
        return send(block, block, ds.at[p, i - 1], dr.at[p, i - 1], spot(lax.rem(d + i, nd), z, y, x))

    total = len(pieces)
    arrived = set()

    def gather_step(step):
        p = step
        if p < total:
            own(p).start()
            for i in range(1, nz):
                along_z(p, i, z).start()
        p = step - lag
        if 0 <= p < total:
            own(p).wait()
            for i in range(1, nz):
                along_z(p, i, lax.rem(z - i + nz, nz)).wait_recv()
            first_pair(p, True).start()
        p = step - 2 * lag
        if 0 <= p < total:
            first_pair(p, False).wait_recv()
            second_pair(p, True).start()
        p = step - 3 * lag
        if 0 <= p < total:
            second_pair(p, False).wait_recv()
            for i in range(1, nd):
                along_d(p, i, d).start()

    def have(array):
        for p in range(total):
            if pieces[p][0] == array and p not in arrived:
                arrived.add(p)
                for i in range(1, nd):
                    along_d(p, i, lax.rem(d - i + nd, nd)).wait_recv()

    def fetch(array, slot):
        return pltpu.make_async_copy(outs[array], wbuf.at[slot], ws.at[slot])

    def norm_first():
        @pl.loop(0, rows // 32)
        def _(i):
            at = pl.ds(pl.multiple_of(i * 32, 32), 32)
            first[at, :] = (rowwise_norm(x_ref[at, :]) * n1g[...] + n1b[...]).astype(jnp.bfloat16)
        pass_last(first, 0, 1).start()

    def pass_last(rows_ref, slot, to):
        return send(rows_ref.at[rows - 16:rows], halo.at[slot], hs.at[slot], hr.at[slot], mate(to))

    def shifted(rows_ref, slot, prev, cols):
        now = rows_ref[:, cols].astype(f32)
        edge = jnp.where(pos == 0, prev[:, cols], halo[slot, :, cols].astype(f32)[15:16, :])
        top = lax.broadcasted_iota(jnp.int32, now.shape, 0) == 0
        return now, jnp.where(top, edge, pltpu.roll(now, 1, 0))

    def mix_first():
        pass_last(first, 0, 1).wait()

        @pl.loop(0, dim // LANES)
        def _(c):
            cols = pl.ds(pl.multiple_of(c * LANES, LANES), LANES)
            now, old = shifted(first, 0, prev_a, cols)
            before[:, cols] = old.astype(jnp.bfloat16)
            for mix, dst in ((mk, key_in), (mv, value_in), (mr, recept_in)):
                dst[:, cols] = (now * mix[:, cols] + old * (1.0 - mix[:, cols])).astype(jnp.bfloat16)

    def project(array, slot, left, store):
        def run():
            fetch(array, slot).wait()
            wide = min(256, dim)
            per = 4 * nz * pieces_rows[array] // (dim // wide)
            weights = wbuf.at[slot].reshape(nd, dim, part)
            for n in range(dim // wide):
                acc = dot_nt(left[:, :part], weights[0, n * wide:(n + 1) * wide])
                for e in range(1, nd):
                    acc = acc + dot_nt(left[:, e * part:(e + 1) * part], weights[e, n * wide:(n + 1) * wide])
                store(n, wide, acc)
        return run

    pieces_rows = [s.shape[0] for s in ins]

    def into_blocks(dst):
        def store(n, wide, acc):
            for q in range(wide // LANES):
                dst[n * (wide // LANES) + q] = acc[:, lane(q)]
        return store

    def into_rows(n, wide, acc):
        r_ref[:, n * wide:(n + 1) * wide] = acc

    def get_kv():
        have(1)
        fetch(1, 0).start()
        have(2)
        fetch(2, 1).start()

    def get_r():
        have(3)
        fetch(3, 0).start()
        have(0)
        copy = pltpu.make_async_copy(outs[0].at[d], sbuf, ws.at[2])
        copy.start()
        copy.wait()
        head = dim // nt
        per = LANES // head
        for c in range(dim // LANES):
            cells = []
            for q in range(per):
                b = c * per + q
                cells.append(sbuf[b // 4, (b // 2) % 2, b % 2][:, :head])
            init[:, lane(c)] = jnp.concatenate(cells, axis=1)

    def get_o():
        have(4)
        fetch(4, 1).start()

    def initial(j):
        got = init[j:j + 1, :]
        for s in range(1, seqs):
            got = jnp.where(seq == s, init[3 * s + j:3 * s + j + 1, :], got)
        return got

    def share(i):
        return send(xs, xr.at[i - 1], es.at[i - 1], er.at[i - 1], mate(i))

    def summarize():
        scan_ends(kb, vb, w_ref, sm, sa, sb, dim, chunks)
        lead = pos == 0
        m = jnp.where(lead, initial(2), NEG)
        a = jnp.where(lead, initial(0), 0.0)
        b = jnp.where(lead, initial(1), 0.0)
        decay = float(STEP) * w_ref[...]
        for s in range(chunks):
            m, a, b = join(m, a, b, decay, sm[s:s + 1, :], sa[s:s + 1, :], sb[s:s + 1, :])
        xs[0:1, :] = a
        xs[1:2, :] = b
        xs[2:3, :] = m
        xs[3:8, :] = jnp.zeros((5, dim), f32)
        for i in range(1, span):
            share(i).start()

    def carry_in():
        for i in range(1, span):
            share(i).wait()
        m = jnp.where(pos == 0, initial(2), NEG)
        a = jnp.where(pos == 0, initial(0), 0.0)
        b = jnp.where(pos == 0, initial(1), 0.0)
        decay = float(rows) * w_ref[...]
        for i in range(span - 1, 0, -1):
            on = i <= pos
            mn, an, bn = join(m, a, b, decay, xr[i - 1, 2:3, :], xr[i - 1, 0:1, :], xr[i - 1, 1:2, :])
            m, a, b = jnp.where(on, mn, m), jnp.where(on, an, a), jnp.where(on, bn, b)
        decay = float(STEP) * w_ref[...]
        for s in range(chunks):
            me, ae, be = sm[s:s + 1, :], sa[s:s + 1, :], sb[s:s + 1, :]
            sm[s:s + 1, :] = m
            sa[s:s + 1, :] = a
            sb[s:s + 1, :] = b
            m, a, b = join(m, a, b, decay, me, ae, be)

    def scan():
        scan_rows(kb, vb, yb, mb, ab, bb, w_ref, u_ref, sm, sa, sb, dim, chunks)
        for c in range(dim // LANES):
            gated[:, lane(c)] = (jax.nn.sigmoid(r_ref[:, lane(c)]) * yb[c]).astype(jnp.bfloat16)

    def attend_out():
        fetch(4, 1).wait()
        weights = wbuf.at[1].reshape(nd, dim, part)
        wide = min(256, part)
        for e in range(nd):
            for n in range(part // wide):
                at = slice(e * part + n * wide, e * part + (n + 1) * wide)
                middle[:, at] = x_ref[:, at] + dot_nn(gated[...], weights[e, :, n * wide:(n + 1) * wide])

    def norm_second():
        @pl.loop(0, rows // 32)
        def _(i):
            at = pl.ds(pl.multiple_of(i * 32, 32), 32)
            second[at, :] = (rowwise_norm(middle[at, :]) * n2g[...] + n2b[...]).astype(jnp.bfloat16)
        pass_last(second, 1, 1).start()

    def mix_second():
        pass_last(second, 1, 1).wait()

        @pl.loop(0, dim // LANES)
        def _(c):
            cols = pl.ds(pl.multiple_of(c * LANES, LANES), LANES)
            now, old = shifted(second, 1, prev_f, cols)
            diff2[:, cols] = now - old
            for mix, dst in ((ck, chan_key), (cr, chan_rec)):
                dst[:, cols] = (now * mix[:, cols] + old * (1.0 - mix[:, cols])).astype(jnp.bfloat16)

    steps = total + 3 * lag
    gather_step(0)
    gather_step(1)
    norm_first()
    gather_step(2)
    mix_first()
    ready = 1 + max(p for p in range(total) if pieces[p][0] <= 4) + 3 * lag
    for s in range(3, ready):
        gather_step(s)
    work = [get_kv, project(1, 0, key_in, into_blocks(kb)), project(2, 1, value_in, into_blocks(vb)), get_r, get_o, summarize,
            project(3, 0, recept_in, into_rows), carry_in, scan, attend_out, norm_second, mix_second]
    interleave(work, gather_step, ready, steps, min(steps, ready + 10))
    for a in range(count):
        have(a)
    for p in range(total):
        for i in range(1, nz):
            along_z(p, i, z).wait_send()
        first_pair(p, True).wait_send()
        second_pair(p, True).wait_send()
        for i in range(1, nd):
            along_d(p, i, d).wait_send()


def forward_block(nd, nt, shards, vectors, seqs, rows, unit, lag):
    nz = nt // 4
    span = nt // seqs
    dim = shards[1].shape[0] * nt
    part = dim // nd
    pieces = []
    for a, s in enumerate(shards):
        pieces += [(a, at, min(unit, s.shape[0])) for at in range(0, s.shape[0], unit)]
    n = len(pieces)
    dma = pltpu.SemaphoreType.DMA
    bf, f32 = jnp.bfloat16, jnp.float32
    low = jax.ShapeDtypeStruct((rows, dim), bf)
    full = jax.ShapeDtypeStruct((rows, dim), f32)
    block = jax.ShapeDtypeStruct((dim // LANES, rows, LANES), f32)
    chunks = rows // STEP
    per = shards[1].shape[0]
    got = pl.pallas_call(
        functools.partial(forward_body, nd, nz, seqs, pieces, lag, len(shards)),
        out_shape=tuple(jax.ShapeDtypeStruct((nd, nz, 2, 2) + s.shape, s.dtype) for s in shards)
        + (low,) * 5 + (full,) * 3 + (block,) * 6,
        in_specs=[HBM] * len(shards) + [VMEM] * len(vectors),
        out_specs=[HBM] * len(shards) + [VMEM] * 14,
        scratch_shapes=[pltpu.VMEM((rows, dim), bf)] * 3
        + [pltpu.VMEM((2, nd, nz, 2, 2, per, part), bf), pltpu.VMEM((nz, 2, 2) + shards[0].shape, f32), pltpu.VMEM((shards[0].shape[0], dim), f32)]
        + [pltpu.VMEM((chunks, dim), f32)] * 3
        + [pltpu.VMEM((2, 16, dim), bf), pltpu.VMEM((8, dim), f32), pltpu.VMEM((span - 1, 8, dim), f32), pltpu.VMEM((rows, dim), bf)]
        + [dma((n,)), dma((n, nz - 1)), dma((n, nz - 1)), dma((n,)), dma((n,)), dma((n,)), dma((n,)),
           dma((n, nd - 1)), dma((n, nd - 1)), dma((2,)), dma((2,)), dma((span - 1,)), dma((span - 1,)), dma((3,))],
        compiler_params=pltpu.CompilerParams(collective_id=0, has_side_effects=True, vmem_limit_bytes=58 * 2**20),
        name="forward_block",
    )(*shards, *vectors)
    weights = [o.reshape(nd, nt * s.shape[0], s.shape[1]) for o, s in zip(got[1:len(shards)], shards[1:])]
    return weights, got[len(shards):]


def add_tiles(dst, src, tiles):
    @pl.loop(0, tiles)
    def _(i):
        dst[i] = (dst[i].astype(jnp.float32) + src[i].astype(jnp.float32)).astype(dst.dtype)


def scatter_body(nd, nz, chunks, rc, part, lag, ahead, count, *refs):
    grads, vec = refs[:count], refs[count]
    out, vout, own, sib, ra, rb, rz, vd, v1, vx, v2, vy, v3, vz, loc, ds, dr, as_, ar, bs, br, zs, zr, vs, vr = refs[count + 1:]
    d, z, y, x = place(nd, nz)
    meet(partners(nd, nz, d, z, y, x))
    f32 = jnp.float32

    def load(c):
        a, at = chunks[c]
        return pltpu.make_async_copy(grads[a].at[:, :, :, at:at + rc, pl.ds(pl.multiple_of(d * part, part), part)], own.at[c], loc.at[c])

    def along_d(c, i):
        a, at = chunks[c]
        to = lax.rem(d + i, nd)
        return send(grads[a].at[:, :, :, at:at + rc, pl.ds(pl.multiple_of(to * part, part), part)], sib.at[i - 1, c], ds.at[i - 1, c], dr.at[i - 1, c], spot(to, z, y, x))

    def first_pair(c):
        if c % 2 == 0:
            return send(own.at[c, :, :, 1 - x], ra.at[c], as_.at[c], ar.at[c], spot(d, z, y, 1 - x))
        return send(own.at[c, :, 1 - y], ra.at[c], as_.at[c], ar.at[c], spot(d, z, 1 - y, x))

    def second_pair(c):
        if c % 2 == 0:
            return send(own.at[c, :, 1 - y, x], rb.at[c], bs.at[c], br.at[c], spot(d, z, 1 - y, x))
        return send(own.at[c, :, y, 1 - x], rb.at[c], bs.at[c], br.at[c], spot(d, z, y, 1 - x))

    def along_z(c, i):
        to = lax.rem(z + i, nz)
        return send(own.at[c, to, y, x], rz.at[i - 1, c], zs.at[i - 1, c], zr.at[i - 1, c], spot(d, to, y, x))

    total = len(chunks)
    top = vd.shape[1]

    def vec_d(i):
        to = lax.rem(d + i, nd)
        return send(vec.at[:top], vd.at[d], vs.at[i - 1], vr.at[i - 1], spot(to, z, y, x))

    def vec_x():
        return send(v1, vx, vs.at[nd - 1], vr.at[nd - 1], spot(d, z, y, 1 - x))

    def vec_y():
        return send(v2, vy, vs.at[nd], vr.at[nd], spot(d, z, 1 - y, x))

    def vec_z(i):
        return send(v3, vz.at[z], vs.at[nd + i], vr.at[nd + i], spot(d, lax.rem(z + i, nz), y, x))

    def vec_step(step):
        if step == 0:
            vd[d] = vec[:top]
            for i in range(1, nd):
                vec_d(i).start()
        elif step == 1:
            for i in range(1, nd):
                vec_d(i).wait()
            acc = vd[0]
            for i in range(1, nd):
                acc = acc + vd[i]
            v1[:top] = acc
            v1[top:] = vec[top:]
            vec_x().start()
        elif step == 2:
            vec_x().wait()
            v2[...] = v1[...] + vx[...]
            vec_y().start()
        elif step == 3:
            vec_y().wait()
            v3[...] = v2[...] + vy[...]
            vz[z] = v3[...]
            for i in range(1, nz):
                vec_z(i).start()
        elif step == 4:
            for i in range(1, nz):
                vec_z(i).wait()
            acc = vz[0]
            for i in range(1, nz):
                acc = acc + vz[i]
            vout[...] = acc

    def begin(c):
        load(c).start()
        for i in range(1, nd):
            along_d(c, i).start()

    for c in range(min(ahead, total)):
        begin(c)
    for step in range(total + 3 * lag):
        c = step
        if c + ahead < total:
            begin(c + ahead)
        if step % 2 == 0:
            vec_step(step // 2)
        if c < total:
            load(c).wait()
            for i in range(1, nd):
                along_d(c, i).wait_recv()

            @pl.loop(0, nz)
            def _(b):
                for q in range(4):
                    acc = own[c, b, q // 2, q % 2].astype(f32)
                    for i in range(1, nd):
                        acc = acc + sib[i - 1, c, b, q // 2, q % 2].astype(f32)
                    own[c, b, q // 2, q % 2] = acc.astype(jnp.bfloat16)
            first_pair(c).start()
        c = step - lag
        if 0 <= c < total:
            first_pair(c).wait_recv()

            @pl.loop(0, nz)
            def _(b):
                for q in range(2):
                    at = (b, q, x) if c % 2 == 0 else (b, y, q)
                    own[(c,) + at] = (own[(c,) + at].astype(f32) + ra[c, b, q].astype(f32)).astype(jnp.bfloat16)
            second_pair(c).start()
        c = step - 2 * lag
        if 0 <= c < total:
            second_pair(c).wait_recv()

            @pl.loop(0, nz)
            def _(b):
                own[c, b, y, x] = (own[c, b, y, x].astype(f32) + rb[c, b].astype(f32)).astype(jnp.bfloat16)
            for i in range(1, nz):
                along_z(c, i).start()
        c = step - 3 * lag
        if 0 <= c < total:
            for i in range(1, nz):
                along_z(c, i).wait_recv()
            acc = own[c, z, y, x].astype(f32)
            for i in range(1, nz):
                acc = acc + rz[i - 1, c].astype(f32)
            out[c * rc:(c + 1) * rc] = acc
    for c in range(total):
        for i in range(1, nd):
            along_d(c, i).wait_send()
        first_pair(c).wait_send()
        second_pair(c).wait_send()
        for i in range(1, nz):
            along_z(c, i).wait_send()


def scatter_grads(nd, nt, grads, vec, top, rc, lag=2, ahead=3):
    nz = nt // 4
    part = grads[0].shape[1] // nd
    split = [g.reshape(nz, 2, 2, g.shape[0] // nt, g.shape[1]) for g in grads]
    chunks = []
    for a, g in enumerate(split):
        chunks += [(a, at) for at in range(0, g.shape[3], rc)]
    n = len(chunks)
    dma = pltpu.SemaphoreType.DMA
    bf = jnp.bfloat16
    wide = vec.shape[1]

    def vv(shape):
        return pltpu.VMEM(shape, jnp.float32)

    return pl.pallas_call(
        functools.partial(scatter_body, nd, nz, chunks, rc, part, lag, ahead, len(grads)),
        out_shape=(jax.ShapeDtypeStruct((n * rc, part), jnp.float32), jax.ShapeDtypeStruct(vec.shape, vec.dtype)),
        in_specs=[HBM] * len(grads) + [VMEM],
        out_specs=[VMEM, VMEM],
        scratch_shapes=[pltpu.VMEM((n, nz, 2, 2, rc, part), bf), pltpu.VMEM((nd - 1, n, nz, 2, 2, rc, part), bf),
                        pltpu.VMEM((n, nz, 2, rc, part), bf), pltpu.VMEM((n, nz, rc, part), bf), pltpu.VMEM((nz - 1, n, rc, part), bf),
                        vv((nd, top, wide)), vv(vec.shape), vv(vec.shape), vv(vec.shape), vv(vec.shape), vv(vec.shape), vv((nz,) + vec.shape),
                        dma((n,)), dma((nd - 1, n)), dma((nd - 1, n)), dma((n,)), dma((n,)), dma((n,)), dma((n,)),
                        dma((nz - 1, n)), dma((nz - 1, n)), dma((nd + nz,)), dma((nd + nz,))],
        compiler_params=pltpu.CompilerParams(collective_id=1, has_side_effects=True, vmem_limit_bytes=58 * 2**20),
        name="scatter_grads",
    )(*split, vec)


def local(nd, nt, x, num, den, top, prev_a, prev_f, n1g, n1b, fading, reward, mk, mv, mr, wk, wv, wr, wo, n2g, n2b, ck, cr,
          fk, fv, fr, up):
    rows, dim = x.shape
    seqs = prev_a.shape[0]
    span = nt // seqs
    tp = lax.axis_index("tensor")
    dp = lax.axis_index("dp")
    seq = tp // span
    pos = tp % span
    part = dim // nd
    head = num.shape[1]
    behind = [(i + 1, i) for i in range(nt - 1)]

    def into(left, whole):
        total = dot_nt(left[:, :part], whole[0])
        for d in range(1, nd):
            total = total + dot_nt(left[:, d * part:(d + 1) * part], whole[d])
        return total

    def outof(left, whole):
        return jnp.concatenate([dot_nn(left, whole[d]) for d in range(nd)], axis=1)

    def weight_grad(cols, ins):
        return dot_tn(cols, ins).astype(jnp.bfloat16)

    def pushed(back):
        halo = lax.ppermute(back[:1, :], "tensor", behind)
        last = jnp.where(pos == span - 1, 0.0, halo)
        return jnp.concatenate([back[1:, :], last], axis=0)

    def line(v):
        return v.astype(jnp.float32).reshape(1, dim)

    w = jnp.exp(fading)
    packed = jnp.stack([num, den, top], axis=1).reshape(3 * seqs, head)
    packed = jnp.pad(packed, ((0, -3 * seqs % 8), (0, LANES - head)))
    shards = [packed] + [s.T for s in (wk, wv, wr, wo, fr, fk, fv)]
    mine_a = lax.dynamic_slice_in_dim(prev_a, seq, 1, 0)
    mine_f = lax.dynamic_slice_in_dim(prev_f, seq, 1, 0)
    vectors = [x] + [line(v) for v in (n1g, n1b, mk, mv, mr, w, reward, n2g, n2b, ck, cr, mine_a, mine_f)]
    weights, saved = forward_block(nd, nt, shards, vectors, seqs, rows, 32, 2)
    whole_k, whole_v, whole_r, whole_o, whole_fr, whole_fk, whole_fv = weights
    first, before, gated, chan_key, chan_rec, recept, middle, diff2, kb, vb, yb, mb, ab, bb = saved
    wr_, ur_ = w[None, :], reward[None, :]
    s1, scale1 = norm_stats(x)
    s2, scale2 = norm_stats(middle)
    key_in, value_in, recept_in = blended(first, before, mk), blended(first, before, mv), blended(first, before, mr)

    hidden = jnp.maximum(into(chan_key, whole_fk), 0.0)
    squared = jnp.square(hidden).astype(jnp.bfloat16)
    chan_values = outof(squared, whole_fv)
    gate = jax.nn.sigmoid(into(chan_rec, whole_fr))
    result = middle + gate * chan_values

    g_values = (up * gate).astype(jnp.bfloat16)
    g_gate = (up * chan_values * gate * (1.0 - gate)).astype(jnp.bfloat16)
    grad_fr = weight_grad(g_gate, chan_rec)
    g_rec_in = outof(g_gate, whole_fr)
    g_squared = into(g_values, whole_fv)
    grad_fv = weight_grad(squared, g_values)
    g_hidden = (g_squared * 2.0 * hidden).astype(jnp.bfloat16)
    grad_fk = weight_grad(g_hidden, chan_key)
    g_key_in = outof(g_hidden, whole_fk)
    grad_ck = jnp.sum(g_key_in * diff2, axis=0)
    grad_cr = jnp.sum(g_rec_in * diff2, axis=0)
    back2 = g_key_in * (1.0 - ck) + g_rec_in * (1.0 - cr)
    g_second = g_key_in * ck + g_rec_in * cr + pushed(back2)
    g_mid, grad_g2, grad_b2 = norm_back(g_second, s2, scale2, n2g)
    g_middle = up + g_mid
    g_attn = g_middle.astype(jnp.bfloat16)
    g_gated = into(g_attn, whole_o)
    grad_o = weight_grad(gated, g_attn)

    gyb, ca, cb, lc, la, lb, lg = wkv_carry(recept, g_gated, kb, yb, mb, bb, wr_, ur_)
    sent = jnp.concatenate([la, lb, lg], axis=0)
    got = lax.all_gather(sent, "tensor", axis=0)

    def chain(items, steps_on):
        ga = jnp.zeros((dim,), jnp.float32)
        gb = jnp.zeros((dim,), jnp.float32)
        for i in reversed(range(span)):
            keep = jnp.exp(items[i, 2])
            na, nb = items[i, 0] + keep * ga, items[i, 1] + keep * gb
            if steps_on is None:
                ga, gb = na, nb
            else:
                on = i > steps_on
                ga, gb = jnp.where(on, na, ga), jnp.where(on, nb, gb)
        return ga, gb

    ea, eb = chain(lax.dynamic_slice_in_dim(got, seq * span, span, 0), pos)
    own = lax.dynamic_slice_in_dim(got, tp * head, head, 2)
    nums, dens = [], []
    for s in range(seqs):
        ga, gb = jnp.zeros((head,), jnp.float32), jnp.zeros((head,), jnp.float32)
        for i in reversed(range(span)):
            keep = jnp.exp(own[s * span + i, 2])
            ga, gb = own[s * span + i, 0] + keep * ga, own[s * span + i, 1] + keep * gb
        nums.append(ga)
        dens.append(gb)
    grad_num, grad_den = jnp.stack(nums), jnp.stack(dens)
    grad_top = grad_num * num + grad_den * den

    g_keys, g_vals, g_recept, gu, gw = wkv_backward(
        recept, g_gated, kb, vb, yb, mb, ab, bb, gyb, wr_, ur_, ca, cb, lc, ea[None, :], eb[None, :])
    grad_k, grad_v, grad_r = weight_grad(g_keys, key_in), weight_grad(g_vals, value_in), weight_grad(g_recept, recept_in)
    diff1 = first.astype(jnp.float32) - before.astype(jnp.float32)
    in_k, in_v, in_r = outof(g_keys, whole_k), outof(g_vals, whole_v), outof(g_recept, whole_r)
    grad_mk, grad_mv, grad_mr = jnp.sum(in_k * diff1, axis=0), jnp.sum(in_v * diff1, axis=0), jnp.sum(in_r * diff1, axis=0)
    back1 = in_k * (1.0 - mk) + in_v * (1.0 - mv) + in_r * (1.0 - mr)
    g_first = in_k * mk + in_v * mv + in_r * mr + pushed(back1)
    g_tok, grad_g1, grad_b1 = norm_back(g_first, s1, scale1, n1g)
    tokens_grad = g_middle + g_tok

    vectors = jnp.stack([grad_g1, grad_b1, gw[0] * w, gu[0], grad_mk, grad_mv, grad_mr, grad_g2, grad_b2, grad_ck, grad_cr])
    lead = jnp.where(pos == 0, 1.0, 0.0)
    pair = (jnp.stack([back1[0], back2[0]]) * lead)[:, None, :]
    slots = lax.dynamic_update_slice(jnp.zeros((2, seqs, dim), jnp.float32), pair, (0, seq, 0)).reshape(2 * seqs, dim)
    tail_rows = -(-2 * seqs // 8) * 8
    vec = jnp.concatenate([vectors, jnp.zeros((5, dim), jnp.float32), slots, jnp.zeros((tail_rows - 2 * seqs, dim), jnp.float32)])
    unit = sum(s.shape[1] for s in (wk, wv, wr, wo, fk, fv, fr)) // 26
    summed, vectors = scatter_grads(nd, nt, [grad_k, grad_v, grad_r, grad_o, grad_fk, grad_fv, grad_fr], vec, 16, unit)
    prevs = vectors[16:16 + 2 * seqs].reshape(2, seqs, dim)
    outs, at = [], 0
    for s in (wk, wv, wr, wo, fk, fv, fr):
        outs.append(summed[at:at + s.shape[1]].T)
        at += s.shape[1]
    out_k, out_v, out_r, out_o, out_fk, out_fv, out_fr = outs
    return (result, tokens_grad, grad_num, grad_den, grad_top, prevs[0], prevs[1],
            vectors[0], vectors[1], vectors[2], vectors[3], vectors[4], vectors[5], vectors[6],
            out_k, out_v, out_r, out_o, vectors[7], vectors[8], vectors[9], vectors[10], out_fk, out_fv, out_fr)


def solution(mesh):
    nd, nt = mesh.shape["dp"], mesh.shape["tensor"]
    rows, both, lead, one = P(("dp", "tensor"), None), P("dp", "tensor"), P("dp", None), P()
    return jax.shard_map(
        functools.partial(local, nd, nt),
        mesh=mesh,
        in_specs=(rows, both, both, both, lead, lead) + (one,) * 7 + (both,) * 4 + (one,) * 4 + (both,) * 3 + (rows,),
        out_specs=(rows, rows, both, both, both, lead, lead) + (one,) * 7 + (both,) * 4 + (one,) * 4 + (both,) * 3,
        check_vma=False,
    )
```

```python
import functools

import jax
import jax.numpy as jnp
from jax import lax
from jax.experimental import pallas as pl
from jax.experimental.pallas import tpu as pltpu
from jax.sharding import PartitionSpec as P

EPS = 1e-05
STEP = 16
NEG = -1e30


def norm_stats(x):
    center = x - jnp.mean(x, axis=-1, keepdims=True)
    scale = lax.rsqrt(jnp.mean(center * center, axis=-1, keepdims=True) + EPS)
    return center * scale, scale


def norm_back(g, s, scale, gain):
    q = g * gain
    gx = (q - jnp.mean(q, axis=-1, keepdims=True) - s * jnp.mean(q * s, axis=-1, keepdims=True)) * scale
    return gx, jnp.sum(g * s, axis=0), jnp.sum(g, axis=0)


def blended(now, before, mix):
    return (now.astype(jnp.float32) * mix + before.astype(jnp.float32) * (1.0 - mix)).astype(jnp.bfloat16)


def dot_nt(x, y):
    return lax.dot_general(x, y, (((1,), (1,)), ((), ())), preferred_element_type=jnp.float32)


def dot_nn(x, y):
    return lax.dot_general(x, y, (((1,), (0,)), ((), ())), preferred_element_type=jnp.float32)


def dot_tn(x, y):
    return lax.dot_general(x, y, (((0,), (0,)), ((), ())), preferred_element_type=jnp.float32)


LANES = 128
VMEM = pl.BlockSpec(memory_space=pltpu.VMEM)


def scan_groups(width):
    blocks = width // LANES
    size = 4 if blocks % 4 == 0 else 1
    return [range(g, g + size) for g in range(0, blocks, size)]


def lane(c):
    return slice(c * LANES, (c + 1) * LANES)


MESH = pl.DeviceIdType.MESH
HBM = pl.BlockSpec(memory_space=pltpu.HBM)


def place(nd, nz):
    d = lax.axis_index("dp")
    t = lax.axis_index("tensor")
    return d, t // 4, lax.rem(t // 2, 2), lax.rem(t, 2)


def spot(d, z, y, x):
    return (d, z * 4 + y * 2 + x)


def partners(nd, nz, d, z, y, x):
    out = [spot(lax.rem(d + i, nd), z, y, x) for i in range(1, nd)]
    out += [spot(d, lax.rem(z + i, nz), y, x) for i in range(1, nz)]
    return out + [spot(d, z, 1 - y, x), spot(d, z, y, 1 - x)]


def meet(others):
    barrier = pltpu.get_barrier_semaphore()
    for other in others:
        pl.semaphore_signal(barrier, inc=1, device_id=other, device_id_type=MESH)
    pl.semaphore_wait(barrier, len(others))


def send(src, dst, send_sem, recv_sem, to):
    return pltpu.make_async_remote_copy(src_ref=src, dst_ref=dst, send_sem=send_sem, recv_sem=recv_sem, device_id=to, device_id_type=MESH)


def rowwise_norm(x):
    center = x - jnp.mean(x, axis=-1, keepdims=True)
    return center * lax.rsqrt(jnp.mean(center * center, axis=-1, keepdims=True) + EPS)


def scan_ends(kb, vb, w_ref, sm, sa, sb, width, chunks):
    for group in scan_groups(width):
        m = [jnp.full((chunks, LANES), NEG, jnp.float32) for _ in group]
        a = [jnp.zeros((chunks, LANES), jnp.float32) for _ in group]
        b = [jnp.zeros((chunks, LANES), jnp.float32) for _ in group]
        for j in range(STEP):
            at = pl.ds(j, chunks, stride=STEP)
            for i, c in enumerate(group):
                k = kb[c, at, :]
                mw = m[i] - w_ref[:, lane(c)]
                m[i] = jnp.maximum(mw, k)
                keep = jnp.exp(mw - m[i])
                take = jnp.exp(k - m[i])
                a[i] = keep * a[i] + take * vb[c, at, :]
                b[i] = keep * b[i] + take
        for i, c in enumerate(group):
            sm[:, lane(c)] = m[i]
            sa[:, lane(c)] = a[i]
            sb[:, lane(c)] = b[i]


def join(m, a, b, decay, me, ae, be):
    mw = m - decay
    mn = jnp.maximum(mw, me)
    keep = jnp.exp(mw - mn)
    take = jnp.exp(me - mn)
    return mn, keep * a + take * ae, keep * b + take * be


def scan_rows(kb, vb, yb, mb, ab, bb, w_ref, u_ref, sm, sa, sb, width, chunks):
    for group in scan_groups(width):
        m = [sm[:, lane(c)] for c in group]
        a = [sa[:, lane(c)] for c in group]
        b = [sb[:, lane(c)] for c in group]
        for j in range(STEP):
            at = pl.ds(j, chunks, stride=STEP)
            for i, c in enumerate(group):
                k = kb[c, at, :]
                v = vb[c, at, :]
                mb[c, at, :] = m[i]
                ab[c, at, :] = a[i]
                bb[c, at, :] = b[i]
                uk = u_ref[:, lane(c)] + k
                p = jnp.maximum(m[i], uk)
                alpha = jnp.exp(m[i] - p)
                beta = jnp.exp(uk - p)
                yb[c, at, :] = (alpha * a[i] + beta * v) / (alpha * b[i] + beta)
                m[i], a[i], b[i] = step_state(m[i], a[i], b[i], w_ref[:, lane(c)], k, v)


def step_state(m, a, b, w, k, v):
    mw = m - w
    mn = jnp.maximum(mw, k)
    keep = jnp.exp(mw - mn)
    take = jnp.exp(k - mn)
    return mn, keep * a + take * v, keep * b + take


def interleave(work, step, first, total, last):
    at = first
    for i, piece in enumerate(work):
        piece()
        goal = first + (last - first) * (i + 1) // len(work)
        while at < goal:
            step(at)
            at += 1
    while at < total:
        step(at)
        at += 1


def forward_body(nd, nz, seqs, pieces, lag, count, *refs):
    ins, refs = refs[:count], refs[count:]
    x_ref, n1g, n1b, mk, mv, mr, w_ref, u_ref, n2g, n2b, ck, cr, prev_a, prev_f = refs[:14]
    outs, refs = refs[14:14 + count], refs[14 + count:]
    first, before, gated, chan_key, chan_rec, r_ref, middle, diff2, kb, vb, yb, mb, ab, bb = refs[:14]
    (key_in, value_in, recept_in, wbuf, sbuf, init, sm, sa, sb, halo, xs, xr, second,
     loc, zs, zr, as_, ar, bs, br, ds, dr, hs, hr, es, er, ws) = refs[14:]
    d, z, y, x = place(nd, nz)
    rows, dim = x_ref.shape
    part = dim // nd
    chunks = rows // STEP
    nt = 4 * nz
    span = nt // seqs
    t = lax.axis_index("tensor")
    seq = t // span
    pos = lax.rem(t, span)
    f32 = jnp.float32

    def mate(i):
        return (d, seq * span + lax.rem(pos + i, span))

    meet(partners(nd, nz, d, z, y, x) + [mate(i) for i in range(1, span)])

    def own(p):
        a, at, n = pieces[p]
        return pltpu.make_async_copy(ins[a].at[at:at + n], outs[a].at[d, z, y, x, at:at + n], loc.at[p])

    def along_z(p, i, source):
        a, at, n = pieces[p]
        return send(ins[a].at[at:at + n], outs[a].at[d, source, y, x, at:at + n], zs.at[p, i - 1], zr.at[p, i - 1],
                    spot(d, lax.rem(z + i, nz), y, x))

    def first_pair(p, mine):
        a, at, n = pieces[p]
        if p % 2 == 0:
            block = outs[a].at[d, :, y if mine else 1 - y, x, at:at + n]
            to = spot(d, z, 1 - y, x)
        else:
            block = outs[a].at[d, :, y, x if mine else 1 - x, at:at + n]
            to = spot(d, z, y, 1 - x)
        return send(block, block, as_.at[p], ar.at[p], to)

    def second_pair(p, mine):
        a, at, n = pieces[p]
        if p % 2 == 0:
            block = outs[a].at[d, :, :, x if mine else 1 - x, at:at + n]
            to = spot(d, z, y, 1 - x)
        else:
            block = outs[a].at[d, :, y if mine else 1 - y, :, at:at + n]
            to = spot(d, z, 1 - y, x)
        return send(block, block, bs.at[p], br.at[p], to)

    def along_d(p, i, source):
        a, at, n = pieces[p]
        block = outs[a].at[source, :, :, :, at:at + n]
        return send(block, block, ds.at[p, i - 1], dr.at[p, i - 1], spot(lax.rem(d + i, nd), z, y, x))

    total = len(pieces)
    arrived = set()

    def gather_step(step):
        p = step
        if p < total:
            own(p).start()
            for i in range(1, nz):
                along_z(p, i, z).start()
        p = step - lag
        if 0 <= p < total:
            own(p).wait()
            for i in range(1, nz):
                along_z(p, i, lax.rem(z - i + nz, nz)).wait_recv()
            first_pair(p, True).start()
        p = step - 2 * lag
        if 0 <= p < total:
            first_pair(p, False).wait_recv()
            second_pair(p, True).start()
        p = step - 3 * lag
        if 0 <= p < total:
            second_pair(p, False).wait_recv()
            for i in range(1, nd):
                along_d(p, i, d).start()

    def have(array):
        for p in range(total):
            if pieces[p][0] == array and p not in arrived:
                arrived.add(p)
                for i in range(1, nd):
                    along_d(p, i, lax.rem(d - i + nd, nd)).wait_recv()

    def fetch(array, slot):
        return pltpu.make_async_copy(outs[array], wbuf.at[slot], ws.at[slot])

    def norm_first():
        @pl.loop(0, rows // 32)
        def _(i):
            at = pl.ds(pl.multiple_of(i * 32, 32), 32)
            first[at, :] = (rowwise_norm(x_ref[at, :]) * n1g[...] + n1b[...]).astype(jnp.bfloat16)
        pass_last(first, 0, 1).start()

    def pass_last(rows_ref, slot, to):
        return send(rows_ref.at[rows - 16:rows], halo.at[slot], hs.at[slot], hr.at[slot], mate(to))

    def shifted(rows_ref, slot, prev, cols):
        now = rows_ref[:, cols].astype(f32)
        edge = jnp.where(pos == 0, prev[:, cols], halo[slot, :, cols].astype(f32)[15:16, :])
        top = lax.broadcasted_iota(jnp.int32, now.shape, 0) == 0
        return now, jnp.where(top, edge, pltpu.roll(now, 1, 0))

    def mix_first():
        pass_last(first, 0, 1).wait()

        @pl.loop(0, dim // LANES)
        def _(c):
            cols = pl.ds(pl.multiple_of(c * LANES, LANES), LANES)
            now, old = shifted(first, 0, prev_a, cols)
            before[:, cols] = old.astype(jnp.bfloat16)
            for mix, dst in ((mk, key_in), (mv, value_in), (mr, recept_in)):
                dst[:, cols] = (now * mix[:, cols] + old * (1.0 - mix[:, cols])).astype(jnp.bfloat16)

    def project(array, slot, left, store):
        def run():
            fetch(array, slot).wait()
            wide = min(256, dim)
            per = 4 * nz * pieces_rows[array] // (dim // wide)
            weights = wbuf.at[slot].reshape(nd, dim, part)
            for n in range(dim // wide):
                acc = dot_nt(left[:, :part], weights[0, n * wide:(n + 1) * wide])
                for e in range(1, nd):
                    acc = acc + dot_nt(left[:, e * part:(e + 1) * part], weights[e, n * wide:(n + 1) * wide])
                store(n, wide, acc)
        return run

    pieces_rows = [s.shape[0] for s in ins]

    def into_blocks(dst):
        def store(n, wide, acc):
            for q in range(wide // LANES):
                dst[n * (wide // LANES) + q] = acc[:, lane(q)]
        return store

    def into_rows(n, wide, acc):
        r_ref[:, n * wide:(n + 1) * wide] = acc

    def get_kv():
        have(1)
        fetch(1, 0).start()
        have(2)
        fetch(2, 1).start()

    def get_r():
        have(3)
        fetch(3, 0).start()
        have(0)
        copy = pltpu.make_async_copy(outs[0].at[d], sbuf, ws.at[2])
        copy.start()
        copy.wait()
        head = dim // nt
        per = LANES // head
        for c in range(dim // LANES):
            cells = []
            for q in range(per):
                b = c * per + q
                cells.append(sbuf[b // 4, (b // 2) % 2, b % 2][:, :head])
            init[:, lane(c)] = jnp.concatenate(cells, axis=1)

    def get_o():
        have(4)
        fetch(4, 1).start()

    def initial(j):
        got = init[j:j + 1, :]
        for s in range(1, seqs):
            got = jnp.where(seq == s, init[3 * s + j:3 * s + j + 1, :], got)
        return got

    def share(i):
        return send(xs, xr.at[i - 1], es.at[i - 1], er.at[i - 1], mate(i))

    def summarize():
        scan_ends(kb, vb, w_ref, sm, sa, sb, dim, chunks)
        lead = pos == 0
        m = jnp.where(lead, initial(2), NEG)
        a = jnp.where(lead, initial(0), 0.0)
        b = jnp.where(lead, initial(1), 0.0)
        decay = float(STEP) * w_ref[...]
        for s in range(chunks):
            m, a, b = join(m, a, b, decay, sm[s:s + 1, :], sa[s:s + 1, :], sb[s:s + 1, :])
        xs[0:1, :] = a
        xs[1:2, :] = b
        xs[2:3, :] = m
        xs[3:8, :] = jnp.zeros((5, dim), f32)
        for i in range(1, span):
            share(i).start()

    def carry_in():
        for i in range(1, span):
            share(i).wait()
        m = jnp.where(pos == 0, initial(2), NEG)
        a = jnp.where(pos == 0, initial(0), 0.0)
        b = jnp.where(pos == 0, initial(1), 0.0)
        decay = float(rows) * w_ref[...]
        for i in range(span - 1, 0, -1):
            on = i <= pos
            mn, an, bn = join(m, a, b, decay, xr[i - 1, 2:3, :], xr[i - 1, 0:1, :], xr[i - 1, 1:2, :])
            m, a, b = jnp.where(on, mn, m), jnp.where(on, an, a), jnp.where(on, bn, b)
        decay = float(STEP) * w_ref[...]
        for s in range(chunks):
            me, ae, be = sm[s:s + 1, :], sa[s:s + 1, :], sb[s:s + 1, :]
            sm[s:s + 1, :] = m
            sa[s:s + 1, :] = a
            sb[s:s + 1, :] = b
            m, a, b = join(m, a, b, decay, me, ae, be)

    def scan():
        scan_rows(kb, vb, yb, mb, ab, bb, w_ref, u_ref, sm, sa, sb, dim, chunks)
        for c in range(dim // LANES):
            gated[:, lane(c)] = (jax.nn.sigmoid(r_ref[:, lane(c)]) * yb[c]).astype(jnp.bfloat16)

    def attend_out():
        fetch(4, 1).wait()
        weights = wbuf.at[1].reshape(nd, dim, part)
        wide = min(256, part)
        for e in range(nd):
            for n in range(part // wide):
                at = slice(e * part + n * wide, e * part + (n + 1) * wide)
                middle[:, at] = x_ref[:, at] + dot_nn(gated[...], weights[e, :, n * wide:(n + 1) * wide])

    def norm_second():
        @pl.loop(0, rows // 32)
        def _(i):
            at = pl.ds(pl.multiple_of(i * 32, 32), 32)
            second[at, :] = (rowwise_norm(middle[at, :]) * n2g[...] + n2b[...]).astype(jnp.bfloat16)
        pass_last(second, 1, 1).start()

    def mix_second():
        pass_last(second, 1, 1).wait()

        @pl.loop(0, dim // LANES)
        def _(c):
            cols = pl.ds(pl.multiple_of(c * LANES, LANES), LANES)
            now, old = shifted(second, 1, prev_f, cols)
            diff2[:, cols] = now - old
            for mix, dst in ((ck, chan_key), (cr, chan_rec)):
                dst[:, cols] = (now * mix[:, cols] + old * (1.0 - mix[:, cols])).astype(jnp.bfloat16)

    steps = total + 3 * lag
    gather_step(0)
    gather_step(1)
    norm_first()
    gather_step(2)
    mix_first()
    ready = 1 + max(p for p in range(total) if pieces[p][0] <= 4) + 3 * lag
    for s in range(3, ready):
        gather_step(s)
    work = [get_kv, project(1, 0, key_in, into_blocks(kb)), project(2, 1, value_in, into_blocks(vb)), get_r, get_o, summarize,
            project(3, 0, recept_in, into_rows), carry_in, scan, attend_out, norm_second, mix_second]
    interleave(work, gather_step, ready, steps, min(steps, ready + 10))
    for a in range(count):
        have(a)
    for p in range(total):
        for i in range(1, nz):
            along_z(p, i, z).wait_send()
        first_pair(p, True).wait_send()
        second_pair(p, True).wait_send()
        for i in range(1, nd):
            along_d(p, i, d).wait_send()


def forward_block(nd, nt, shards, vectors, seqs, rows, unit, lag):
    nz = nt // 4
    span = nt // seqs
    dim = shards[1].shape[0] * nt
    part = dim // nd
    pieces = []
    for a, s in enumerate(shards):
        pieces += [(a, at, min(unit, s.shape[0])) for at in range(0, s.shape[0], unit)]
    n = len(pieces)
    dma = pltpu.SemaphoreType.DMA
    bf, f32 = jnp.bfloat16, jnp.float32
    low = jax.ShapeDtypeStruct((rows, dim), bf)
    full = jax.ShapeDtypeStruct((rows, dim), f32)
    block = jax.ShapeDtypeStruct((dim // LANES, rows, LANES), f32)
    chunks = rows // STEP
    per = shards[1].shape[0]
    got = pl.pallas_call(
        functools.partial(forward_body, nd, nz, seqs, pieces, lag, len(shards)),
        out_shape=tuple(jax.ShapeDtypeStruct((nd, nz, 2, 2) + s.shape, s.dtype) for s in shards)
        + (low,) * 5 + (full,) * 3 + (block,) * 6,
        in_specs=[HBM] * len(shards) + [VMEM] * len(vectors),
        out_specs=[HBM] * len(shards) + [VMEM] * 14,
        scratch_shapes=[pltpu.VMEM((rows, dim), bf)] * 3
        + [pltpu.VMEM((2, nd, nz, 2, 2, per, part), bf), pltpu.VMEM((nz, 2, 2) + shards[0].shape, f32), pltpu.VMEM((shards[0].shape[0], dim), f32)]
        + [pltpu.VMEM((chunks, dim), f32)] * 3
        + [pltpu.VMEM((2, 16, dim), bf), pltpu.VMEM((8, dim), f32), pltpu.VMEM((span - 1, 8, dim), f32), pltpu.VMEM((rows, dim), bf)]
        + [dma((n,)), dma((n, nz - 1)), dma((n, nz - 1)), dma((n,)), dma((n,)), dma((n,)), dma((n,)),
           dma((n, nd - 1)), dma((n, nd - 1)), dma((2,)), dma((2,)), dma((span - 1,)), dma((span - 1,)), dma((3,))],
        compiler_params=pltpu.CompilerParams(collective_id=0, has_side_effects=True, vmem_limit_bytes=58 * 2**20),
        name="forward_block",
    )(*shards, *vectors)
    weights = [o.reshape(nd, nt * s.shape[0], s.shape[1]) for o, s in zip(got[1:len(shards)], shards[1:])]
    return weights, got[len(shards):]


def carry_rows(r_ref, gg, kb, yb, mb, bb, w_ref, u_ref, gyb, ca, cb, lc, width, chunks):
    for c in range(width // LANES):
        gyb[c] = gg[:, lane(c)] * jax.nn.sigmoid(r_ref[:, lane(c)])
    for group in scan_groups(width):
        ga = [jnp.zeros((chunks, LANES), jnp.float32) for _ in group]
        gb = [jnp.zeros((chunks, LANES), jnp.float32) for _ in group]
        end = [None for _ in group]
        for j in reversed(range(STEP)):
            at = pl.ds(j, chunks, stride=STEP)
            for i, c in enumerate(group):
                w = w_ref[:, lane(c)]
                k = kb[c, at, :]
                m = mb[c, at, :]
                uk = u_ref[:, lane(c)] + k
                p = jnp.maximum(m, uk)
                alpha = jnp.exp(m - p)
                gn = gyb[c, at, :] / (alpha * bb[c, at, :] + jnp.exp(uk - p))
                gd = -gn * yb[c, at, :]
                mw = m - w
                mn = jnp.maximum(mw, k)
                if j == STEP - 1:
                    end[i] = mn
                keep = jnp.exp(mw - mn)
                ga[i] = alpha * gn + keep * ga[i]
                gb[i] = alpha * gd + keep * gb[i]
                if j == 0:
                    lc[:, lane(c)] = m - float(STEP) * w - end[i]
        for i, c in enumerate(group):
            ca[:, lane(c)] = ga[i]
            cb[:, lane(c)] = gb[i]


def back_rows(kb, vb, yb, mb, ab, bb, gyb, w_ref, u_ref, ta, tb, fk, fv, vec, width, chunks):
    for group in scan_groups(width):
        ga = [ta[:, lane(c)] for c in group]
        gb = [tb[:, lane(c)] for c in group]
        gu = [jnp.zeros((chunks, LANES), jnp.float32) for _ in group]
        gw = [jnp.zeros((chunks, LANES), jnp.float32) for _ in group]
        for j in reversed(range(STEP)):
            at = pl.ds(j, chunks, stride=STEP)
            for i, c in enumerate(group):
                k = kb[c, at, :]
                v = vb[c, at, :]
                m = mb[c, at, :]
                uk = u_ref[:, lane(c)] + k
                p = jnp.maximum(m, uk)
                alpha = jnp.exp(m - p)
                beta = jnp.exp(uk - p)
                b = bb[c, at, :]
                gn = gyb[c, at, :] / (alpha * b + beta)
                gd = -gn * yb[c, at, :]
                mw = m - w_ref[:, lane(c)]
                mn = jnp.maximum(mw, k)
                keep = jnp.exp(mw - mn)
                take = jnp.exp(k - mn)
                now = beta * (gn * v + gd)
                fv[c, at, :] = beta * gn + take * ga[i]
                fk[c, at, :] = now + take * (ga[i] * v + gb[i])
                gu[i] = gu[i] + now
                gw[i] = gw[i] + keep * (ga[i] * ab[c, at, :] + gb[i] * b)
                ga[i] = alpha * gn + keep * ga[i]
                gb[i] = alpha * gd + keep * gb[i]
        for i, c in enumerate(group):
            vec[2:3, lane(c)] = -jnp.sum(gw[i], axis=0, keepdims=True) * w_ref[:, lane(c)]
            vec[3:4, lane(c)] = jnp.sum(gu[i], axis=0, keepdims=True)


def backward_body(nd, nz, seqs, chunks_of, rc, part, lag, *refs):
    gfr, gfk, gfv, wk, wv, wr, wo, gk_in, gr_in, diff_in = refs[:10]
    (middle, x_ref, up, first, before, gated, r_ref, kb, vb, yb, mb, ab, bb,
     n1g, mk, mv, mr, w_ref, u_ref, n2g, ck, cr) = refs[10:32]
    (outk, outv, outr, outo, outfr, outfk, outfv, tok, vout, go, gk, gv, gr, land) = refs[32:46]
    (own, slots, ra, rb, rz, t0, t2, t3, t4, l0, l1, l2, l3, l4, wbuf, ca, cb, lc, ta, tb, xs, xr, hs_buf, hr_buf,
     vec, vd, v1, vx, v2, vy, v3, vz,
     gstage, loc, ds, dr, cs, as_, ar, bs, br, zs, zr, vs, vr, hs, hr, es, er, ws, gs) = refs[46:]
    grads = [gfr, gfk, gfv, go, gk, gv, gr]
    outs = [outfr, outfk, outfv, outo, outk, outv, outr]
    d, z, y, x = place(nd, nz)
    rows, dim = x_ref.shape
    chunks = rows // STEP
    nt = 4 * nz
    span = nt // seqs
    t = lax.axis_index("tensor")
    seq = t // span
    pos = lax.rem(t, span)
    f32, bf = jnp.float32, jnp.bfloat16
    top = vd.shape[1]
    total = len(chunks_of)

    def mate(i):
        return (d, seq * span + lax.rem(pos + i, span))

    def load_block(src, dst, c, sem):
        return pltpu.make_async_copy(src.at[:, c * LANES:(c + 1) * LANES], dst.at[c], sem.at[c])

    blocks = dim // LANES
    for c in range(blocks):
        load_block(gk_in, t2, c, ws.at[0]).start()
        load_block(gr_in, t3, c, ws.at[1]).start()
        load_block(diff_in, t4, c, ws.at[2]).start()
    meet(partners(nd, nz, d, z, y, x) + [mate(i) for i in range(1, span)])

    def view(g):
        return g.reshape(nz, 2, 2, g.shape[0] // nt, dim)

    def load(c):
        a, at = chunks_of[c]
        return pltpu.make_async_copy(view(grads[a]).at[:, :, :, at:at + rc, pl.ds(pl.multiple_of(d * part, part), part)], own.at[c], loc.at[c])

    def along_d(c, i):
        a, at = chunks_of[c]
        to = lax.rem(d + i, nd)
        return send(view(grads[a]).at[:, :, :, at:at + rc, pl.ds(pl.multiple_of(to * part, part), part)], land.at[i - 1, c],
                    ds.at[i - 1, c], dr.at[i - 1, c], spot(to, z, y, x))

    def bring(c, i):
        return pltpu.make_async_copy(land.at[i - 1, c], slots.at[c % 2, i - 1], cs.at[c % 2, i - 1])

    def first_pair(c):
        if c % 2 == 0:
            return send(own.at[c, :, :, 1 - x], ra.at[c], as_.at[c], ar.at[c], spot(d, z, y, 1 - x))
        return send(own.at[c, :, 1 - y], ra.at[c], as_.at[c], ar.at[c], spot(d, z, 1 - y, x))

    def second_pair(c):
        if c % 2 == 0:
            return send(own.at[c, :, 1 - y, x], rb.at[c], bs.at[c], br.at[c], spot(d, z, 1 - y, x))
        return send(own.at[c, :, y, 1 - x], rb.at[c], bs.at[c], br.at[c], spot(d, z, y, 1 - x))

    def along_z(c, i):
        to = lax.rem(z + i, nz)
        return send(own.at[c, to, y, x], rz.at[i - 1, c], zs.at[i - 1, c], zr.at[i - 1, c], spot(d, to, y, x))

    def scatter_step(step):
        c = step
        if c < total:
            load(c).start()
            for i in range(1, nd):
                along_d(c, i).start()
        c = step - 2
        if 0 <= c < total:
            for i in range(1, nd):
                along_d(c, i).wait_recv()
                bring(c, i).start()
        c = step - 3
        if 0 <= c < total:
            load(c).wait()
            for i in range(1, nd):
                bring(c, i).wait()

            @pl.loop(0, nz)
            def _(b):
                for q in range(4):
                    acc = own[c, b, q // 2, q % 2].astype(f32)
                    for i in range(1, nd):
                        acc = acc + slots[c % 2, i - 1, b, q // 2, q % 2].astype(f32)
                    own[c, b, q // 2, q % 2] = acc.astype(bf)
            first_pair(c).start()
        c = step - 3 - lag
        if 0 <= c < total:
            first_pair(c).wait_recv()

            @pl.loop(0, nz)
            def _(b):
                for q in range(2):
                    at = (b, q, x) if c % 2 == 0 else (b, y, q)
                    own[(c,) + at] = (own[(c,) + at].astype(f32) + ra[c, b, q].astype(f32)).astype(bf)
            second_pair(c).start()
        c = step - 3 - 2 * lag
        if 0 <= c < total:
            second_pair(c).wait_recv()

            @pl.loop(0, nz)
            def _(b):
                own[c, b, y, x] = (own[c, b, y, x].astype(f32) + rb[c, b].astype(f32)).astype(bf)
            for i in range(1, nz):
                along_z(c, i).start()
        c = step - 3 - 3 * lag
        if 0 <= c < total:
            for i in range(1, nz):
                along_z(c, i).wait_recv()
            acc = own[c, z, y, x].astype(f32)
            for i in range(1, nz):
                acc = acc + rz[i - 1, c].astype(f32)
            a, at = chunks_of[c]
            outs[a][:, at:at + rc] = acc.T

    steps = total + 3 + 3 * lag

    def vec_d(i):
        return send(vec.at[:top], vd.at[d], vs.at[i - 1], vr.at[i - 1], spot(lax.rem(d + i, nd), z, y, x))

    def vec_x():
        return send(v1, vx, vs.at[nd - 1], vr.at[nd - 1], spot(d, z, y, 1 - x))

    def vec_y():
        return send(v2, vy, vs.at[nd], vr.at[nd], spot(d, z, 1 - y, x))

    def vec_z(i):
        return send(v3, vz.at[z], vs.at[nd + i], vr.at[nd + i], spot(d, lax.rem(z + i, nz), y, x))

    def vec_step(step):
        if step == 0:
            vd[d] = vec[:top]
            for i in range(1, nd):
                vec_d(i).start()
        elif step == 1:
            for i in range(1, nd):
                vec_d(i).wait()
            acc = vd[0]
            for i in range(1, nd):
                acc = acc + vd[i]
            v1[:top] = acc
            v1[top:] = vec[top:]
            vec_x().start()
        elif step == 2:
            vec_x().wait()
            v2[...] = v1[...] + vx[...]
            vec_y().start()
        elif step == 3:
            vec_y().wait()
            v3[...] = v2[...] + vy[...]
            vz[z] = v3[...]
            for i in range(1, nz):
                vec_z(i).start()
        elif step == 4:
            for i in range(1, nz):
                vec_z(i).wait()
            acc = vz[0]
            for i in range(1, nz):
                acc = acc + vz[i]
            vout[...] = acc

    lead = pos == 0

    def keep_lead(group, row):
        for s in range(seqs):
            at = top + group * seqs + s
            vec[at:at + 1, :] = jnp.where(jnp.logical_and(lead, seq == s), row, 0.0)

    def pass_first(slot):
        return send(hs_buf.at[slot], hr_buf.at[slot], hs.at[slot], hr.at[slot], mate(span - 1))

    def pulled(back, slot, cols):
        edge = jnp.where(pos == span - 1, 0.0, hr_buf[slot, 0:1, cols])
        last = lax.broadcasted_iota(jnp.int32, back.shape, 0) == rows - 1
        return jnp.where(last, edge, pltpu.roll(back, rows - 1, 0))

    def start_second():
        vec[...] = jnp.zeros(vec.shape, f32)
        for c in range(blocks):
            for i, (src, dst) in enumerate(((gk_in, t2), (gr_in, t3), (diff_in, t4))):
                load_block(src, dst, c, ws.at[i]).wait()
        for c in range(blocks):
            hs_buf[0, :, lane(c)] = t2[c, 0:8, :] * (1.0 - ck[:, lane(c)]) + t3[c, 0:8, :] * (1.0 - cr[:, lane(c)])
        pass_first(0).start()
        keep_lead(1, hs_buf[0, 0:1, :])

        @pl.loop(0, blocks)
        def _(c):
            cols = pl.ds(pl.multiple_of(c * LANES, LANES), LANES)
            vec[9:10, cols] = jnp.sum(t2[c] * t4[c], axis=0, keepdims=True)
            vec[10:11, cols] = jnp.sum(t3[c] * t4[c], axis=0, keepdims=True)

    def second_grad():
        pass_first(0).wait()

        @pl.loop(0, blocks)
        def _(c):
            cols = pl.ds(pl.multiple_of(c * LANES, LANES), LANES)
            key, rec = t2[c], t3[c]
            back = key * (1.0 - ck[:, cols]) + rec * (1.0 - cr[:, cols])
            t0[:, cols] = key * ck[:, cols] + rec * cr[:, cols] + pulled(back, 0, cols)

    def norm_grad(src, gain, base, dst, row, low):
        @pl.loop(0, rows // 32)
        def _(i):
            at = pl.ds(pl.multiple_of(i * 32, 32), 32)
            raw = src[at, :]
            center = raw - jnp.mean(raw, axis=-1, keepdims=True)
            scale = lax.rsqrt(jnp.mean(center * center, axis=-1, keepdims=True) + EPS)
            s = center * scale
            g = t0[at, :]
            q = g * gain[...]
            out = base[at, :] + (q - jnp.mean(q, axis=-1, keepdims=True) - s * jnp.mean(q * s, axis=-1, keepdims=True)) * scale
            dst[at, :] = out
            if low is not None:
                low[at, :] = out.astype(bf)
            vec[row:row + 1, :] += jnp.sum(g * s, axis=0, keepdims=True)
            vec[row + 1:row + 2, :] += jnp.sum(g, axis=0, keepdims=True)

    def norm_second_grad():
        fetch(wo).start()
        norm_grad(middle, n2g, up, tok, 7, l0)

    def fetch(src):
        return pltpu.make_async_copy(src, wbuf, gs.at[2])

    weights = wbuf
    wide = min(256, part)

    def gated_grad():
        fetch(wo).wait()
        for n in range(dim // wide):
            acc = dot_nt(l0[:, :part], weights[0, n * wide:(n + 1) * wide])
            for e in range(1, nd):
                acc = acc + dot_nt(l0[:, e * part:(e + 1) * part], weights[e, n * wide:(n + 1) * wide])
            t0[:, n * wide:(n + 1) * wide] = acc

    busy = [None, None]
    half = dim // 2
    broad = min(512, dim)

    def settle(h):
        if busy[h] is not None:
            busy[h].wait()
            busy[h] = None

    def weight_grad(cols_ref, ins_ref, dst):
        for h in range(2):
            settle(h)
            for n in range(half // wide):
                at = h * half + n * wide
                for m in range(dim // broad):
                    gstage[h, n * wide:(n + 1) * wide, m * broad:(m + 1) * broad] = dot_tn(
                        cols_ref[:, at:at + wide], ins_ref[:, m * broad:(m + 1) * broad]).astype(bf)
            busy[h] = pltpu.make_async_copy(gstage.at[h], dst.at[h * half:(h + 1) * half], gs.at[h])
            busy[h].start()

    def share(i):
        return send(xs, xr.at[i - 1], es.at[i - 1], er.at[i - 1], mate(i))

    def chain(ga, gb, keep_ends):
        for s in reversed(range(chunks)):
            if keep_ends:
                ta[s:s + 1, :] = ga
                tb[s:s + 1, :] = gb
            keep = jnp.exp(lc[s:s + 1, :])
            ga = ca[s:s + 1, :] + keep * ga
            gb = cb[s:s + 1, :] + keep * gb
        return ga, gb

    def carry_out():
        carry_rows(r_ref, t0, kb, yb, mb, bb, w_ref, u_ref, t2, ca, cb, lc, dim, chunks)
        zero = jnp.zeros((1, dim), f32)
        ga, gb = chain(zero, zero, False)
        lg = lc[0:1, :]
        for s in range(1, chunks):
            lg = lg + lc[s:s + 1, :]
        xs[0:1, :] = ga
        xs[1:2, :] = gb
        xs[2:3, :] = lg
        xs[3:8, :] = jnp.zeros((5, dim), f32)
        for i in range(1, span):
            share(i).start()

    def scan_back():
        for i in range(1, span):
            share(i).wait()
        ga, gb = jnp.zeros((1, dim), f32), jnp.zeros((1, dim), f32)
        for i in range(span - 1, 0, -1):
            on = pos + i < span
            slot = span - i - 1
            keep = jnp.exp(xr[slot, 2:3, :])
            ga = jnp.where(on, xr[slot, 0:1, :] + keep * ga, ga)
            gb = jnp.where(on, xr[slot, 1:2, :] + keep * gb, gb)
        ga, gb = chain(ga, gb, True)
        keep_lead(2, ga)
        keep_lead(3, gb)
        back_rows(kb, vb, yb, mb, ab, bb, t2, w_ref, u_ref, ta, tb, t3, t4, vec, dim, chunks)

    def round_grads():
        for c in range(blocks):
            l1[:, lane(c)] = t3[c].astype(bf)
            l2[:, lane(c)] = t4[c].astype(bf)
            sig = jax.nn.sigmoid(r_ref[:, lane(c)])
            l3[:, lane(c)] = (t0[:, lane(c)] * yb[c] * sig * (1.0 - sig)).astype(bf)

    def mixed_in(mix):
        for c in range(blocks):
            l4[:, lane(c)] = (first[:, lane(c)].astype(f32) * mix[:, lane(c)]
                              + before[:, lane(c)].astype(f32) * (1.0 - mix[:, lane(c)])).astype(bf)

    def grad_of(mix, cols_ref, dst):
        def run():
            mixed_in(mix)
            weight_grad(cols_ref, l4, dst)
        return run

    def input_grad(whole, low, mix, row, initial):
        def run():
            fetch(whole).start()
            fetch(whole).wait()
            for e in range(nd):
                for n in range(part // wide):
                    at = e * part + n * wide
                    got = dot_nn(low[...], weights[e, :, n * wide:(n + 1) * wide])
                    for q in range(wide // LANES):
                        c = at // LANES + q
                        g = got[:, lane(q)]
                        diff = first[:, lane(c)].astype(f32) - before[:, lane(c)].astype(f32)
                        vec[row:row + 1, lane(c)] = jnp.sum(g * diff, axis=0, keepdims=True)
                        stay, back = g * mix[:, lane(c)], g * (1.0 - mix[:, lane(c)])
                        t3[c] = stay if initial else t3[c] + stay
                        t4[c] = back if initial else t4[c] + back
        return run

    def start_first():
        for c in range(blocks):
            hs_buf[1, :, lane(c)] = t4[c, 0:8, :]
        pass_first(1).start()
        keep_lead(0, hs_buf[1, 0:1, :])

    def first_grad():
        pass_first(1).wait()

        @pl.loop(0, blocks)
        def _(c):
            cols = pl.ds(pl.multiple_of(c * LANES, LANES), LANES)
            t0[:, cols] = t3[c] + pulled(t4[c], 1, cols)
        norm_grad(x_ref, n1g, tok, tok, 0, None)

    def out_grad():
        weight_grad(gated, l0, go)

    work = [start_second, second_grad, norm_second_grad, gated_grad, carry_out, out_grad, scan_back, round_grads,
            grad_of(mk, l1, gk), grad_of(mv, l2, gv), grad_of(mr, l3, gr),
            lambda: (settle(0), settle(1)), input_grad(wk, l1, mk, 4, True), input_grad(wv, l2, mv, 5, False),
            input_grad(wr, l3, mr, 6, False), start_first, first_grad]
    ready = min(c for c in range(total) if chunks_of[c][0] == 3)
    scatter_step(0)
    scatter_step(1)
    scatter_step(2)
    interleave(work, scatter_step, 3, ready, ready)
    for s in range(ready, steps):
        if (s - ready) % 2 == 0:
            vec_step((s - ready) // 2)
        scatter_step(s)
    for c in range(total):
        for i in range(1, nd):
            along_d(c, i).wait_send()
        first_pair(c).wait_send()
        second_pair(c).wait_send()
        for i in range(1, nz):
            along_z(c, i).wait_send()


def backward_block(nd, nt, head, wide_head, operands, vec_rows, top, seqs, rc, lag):
    nz = nt // 4
    span = nt // seqs
    rows, dim = operands[11].shape
    part = dim // nd
    chunks_of = []
    for a, cl in enumerate((head, wide_head, wide_head, head, head, head, head)):
        chunks_of += [(a, at) for at in range(0, cl, rc)]
    n = len(chunks_of)
    chunks = rows // STEP
    dma = pltpu.SemaphoreType.DMA
    bf, f32 = jnp.bfloat16, jnp.float32

    def vv(*shape):
        return pltpu.VMEM(shape, f32)

    def lv(*shape):
        return pltpu.VMEM(shape, bf)

    def shard(cl):
        return jax.ShapeDtypeStruct((part, cl), f32)

    square = jax.ShapeDtypeStruct((dim, dim), bf)
    vec = (vec_rows, dim)
    blocks = dim // LANES
    return pl.pallas_call(
        functools.partial(backward_body, nd, nz, seqs, chunks_of, rc, part, lag),
        out_shape=(shard(head),) * 5 + (shard(wide_head),) * 2
        + (jax.ShapeDtypeStruct((rows, dim), f32), jax.ShapeDtypeStruct(vec, f32)) + (square,) * 4
        + (jax.ShapeDtypeStruct((nd - 1, n, nz, 2, 2, rc, part), bf),),
        in_specs=[HBM] * 10 + [VMEM] * 22,
        out_specs=[VMEM] * 9 + [HBM] * 5,
        scratch_shapes=[lv(n, nz, 2, 2, rc, part), lv(2, nd - 1, nz, 2, 2, rc, part), lv(n, nz, 2, rc, part), lv(n, nz, rc, part),
                        lv(nz - 1, n, rc, part), vv(rows, dim)] + [vv(blocks, rows, LANES)] * 3 + [lv(rows, dim)] * 5
        + [lv(nd, dim, part)] + [vv(chunks, dim)] * 5 + [vv(8, dim), vv(span - 1, 8, dim), vv(2, 8, dim), vv(2, 8, dim)]
        + [vv(*vec), vv(nd, top, dim)] + [vv(*vec)] * 5 + [vv(nz, *vec), lv(2, dim // 2, dim)]
        + [dma((n,)), dma((nd - 1, n)), dma((nd - 1, n)), dma((2, nd - 1)), dma((n,)), dma((n,)), dma((n,)), dma((n,)),
           dma((nz - 1, n)), dma((nz - 1, n)), dma((nd + nz,)), dma((nd + nz,)), dma((2,)), dma((2,)),
           dma((span - 1,)), dma((span - 1,)), dma((3, blocks)), dma((3,))],
        compiler_params=pltpu.CompilerParams(collective_id=1, has_side_effects=True, vmem_limit_bytes=60 * 2**20),
        name="backward_block",
    )(*operands)


def local(nd, nt, x, num, den, top, prev_a, prev_f, n1g, n1b, fading, reward, mk, mv, mr, wk, wv, wr, wo, n2g, n2b, ck, cr,
          fk, fv, fr, up):
    rows, dim = x.shape
    seqs = prev_a.shape[0]
    span = nt // seqs
    tp = lax.axis_index("tensor")
    dp = lax.axis_index("dp")
    seq = tp // span
    pos = tp % span
    part = dim // nd
    head = num.shape[1]
    behind = [(i + 1, i) for i in range(nt - 1)]

    def into(left, whole):
        total = dot_nt(left[:, :part], whole[0])
        for d in range(1, nd):
            total = total + dot_nt(left[:, d * part:(d + 1) * part], whole[d])
        return total

    def outof(left, whole):
        return jnp.concatenate([dot_nn(left, whole[d]) for d in range(nd)], axis=1)

    def weight_grad(cols, ins):
        return dot_tn(cols, ins).astype(jnp.bfloat16)

    def line(v):
        return v.astype(jnp.float32).reshape(1, dim)

    w = jnp.exp(fading)
    packed = jnp.stack([num, den, top], axis=1).reshape(3 * seqs, head)
    packed = jnp.pad(packed, ((0, -3 * seqs % 8), (0, LANES - head)))
    shards = [packed] + [s.T for s in (wk, wv, wr, wo, fr, fk, fv)]
    mine_a = lax.dynamic_slice_in_dim(prev_a, seq, 1, 0)
    mine_f = lax.dynamic_slice_in_dim(prev_f, seq, 1, 0)
    vectors = [x] + [line(v) for v in (n1g, n1b, mk, mv, mr, w, reward, n2g, n2b, ck, cr, mine_a, mine_f)]
    weights, saved = forward_block(nd, nt, shards, vectors, seqs, rows, 32, 2)
    whole_k, whole_v, whole_r, whole_o, whole_fr, whole_fk, whole_fv = weights
    first, before, gated, chan_key, chan_rec, recept, middle, diff2, kb, vb, yb, mb, ab, bb = saved
    hidden = jnp.maximum(into(chan_key, whole_fk), 0.0)
    squared = jnp.square(hidden).astype(jnp.bfloat16)
    chan_values = outof(squared, whole_fv)
    gate = jax.nn.sigmoid(into(chan_rec, whole_fr))
    result = middle + gate * chan_values

    g_values = (up * gate).astype(jnp.bfloat16)
    g_gate = (up * chan_values * gate * (1.0 - gate)).astype(jnp.bfloat16)
    grad_fr = weight_grad(g_gate, chan_rec)
    g_rec_in = outof(g_gate, whole_fr)
    g_squared = into(g_values, whole_fv)
    grad_fv = weight_grad(squared, g_values)
    g_hidden = (g_squared * 2.0 * hidden).astype(jnp.bfloat16)
    grad_fk = weight_grad(g_hidden, chan_key)
    g_key_in = outof(g_hidden, whole_fk)
    top = 16
    vec_rows = top + -(-4 * seqs // 8) * 8
    operands = [grad_fr, grad_fk, grad_fv, whole_k, whole_v, whole_r, whole_o, g_key_in, g_rec_in, diff2,
                middle, x, up, first, before, gated, recept, kb, vb, yb, mb, ab, bb]
    operands += [line(v) for v in (n1g, mk, mv, mr, w, reward, n2g, ck, cr)]
    got = backward_block(nd, nt, head, fk.shape[1], operands, vec_rows, top, seqs, (5 * head + 2 * fk.shape[1]) // 26, 2)
    out_k, out_v, out_r, out_o, out_fr, out_fk, out_fv, tokens_grad, vectors = got[:9]
    slots = vectors[top:top + 4 * seqs].reshape(4, seqs, dim)
    prevs = slots[:2]
    states = lax.dynamic_slice_in_dim(slots[2:], tp * head, head, 2)
    grad_num, grad_den = states[0], states[1]
    grad_top = grad_num * num + grad_den * den
    return (result, tokens_grad, grad_num, grad_den, grad_top, prevs[0], prevs[1],
            vectors[0], vectors[1], vectors[2], vectors[3], vectors[4], vectors[5], vectors[6],
            out_k, out_v, out_r, out_o, vectors[7], vectors[8], vectors[9], vectors[10], out_fk, out_fv, out_fr)


def solution(mesh):
    nd, nt = mesh.shape["dp"], mesh.shape["tensor"]
    rows, both, lead, one = P(("dp", "tensor"), None), P("dp", "tensor"), P("dp", None), P()
    return jax.shard_map(
        functools.partial(local, nd, nt),
        mesh=mesh,
        in_specs=(rows, both, both, both, lead, lead) + (one,) * 7 + (both,) * 4 + (one,) * 4 + (both,) * 3 + (rows,),
        out_specs=(rows, rows, both, both, both, lead, lead) + (one,) * 7 + (both,) * 4 + (one,) * 4 + (both,) * 3,
        check_vma=False,
    )
```

```python
import functools

import jax
import jax.numpy as jnp
from jax import lax
from jax.experimental import pallas as pl
from jax.experimental.pallas import tpu as pltpu
from jax.sharding import PartitionSpec as P

EPS = 1e-05
STEP = 16
NEG = -1e30


def norm_stats(x):
    center = x - jnp.mean(x, axis=-1, keepdims=True)
    scale = lax.rsqrt(jnp.mean(center * center, axis=-1, keepdims=True) + EPS)
    return center * scale, scale


def norm_back(g, s, scale, gain):
    q = g * gain
    gx = (q - jnp.mean(q, axis=-1, keepdims=True) - s * jnp.mean(q * s, axis=-1, keepdims=True)) * scale
    return gx, jnp.sum(g * s, axis=0), jnp.sum(g, axis=0)


def blended(now, before, mix):
    return (now.astype(jnp.float32) * mix + before.astype(jnp.float32) * (1.0 - mix)).astype(jnp.bfloat16)


def dot_nt(x, y):
    return lax.dot_general(x, y, (((1,), (1,)), ((), ())), preferred_element_type=jnp.float32)


def dot_nn(x, y):
    return lax.dot_general(x, y, (((1,), (0,)), ((), ())), preferred_element_type=jnp.float32)


def dot_tn(x, y):
    return lax.dot_general(x, y, (((0,), (0,)), ((), ())), preferred_element_type=jnp.float32)


LANES = 128
VMEM = pl.BlockSpec(memory_space=pltpu.VMEM)


def scan_groups(width):
    blocks = width // LANES
    size = 4 if blocks % 4 == 0 else 1
    return [range(g, g + size) for g in range(0, blocks, size)]


def lane(c):
    return slice(c * LANES, (c + 1) * LANES)


MESH = pl.DeviceIdType.MESH
HBM = pl.BlockSpec(memory_space=pltpu.HBM)


def place(nd, nz):
    d = lax.axis_index("dp")
    t = lax.axis_index("tensor")
    return d, t // 4, lax.rem(t // 2, 2), lax.rem(t, 2)


def spot(d, z, y, x):
    return (d, z * 4 + y * 2 + x)


def partners(nd, nz, d, z, y, x):
    out = [spot(lax.rem(d + i, nd), z, y, x) for i in range(1, nd)]
    out += [spot(d, lax.rem(z + i, nz), y, x) for i in range(1, nz)]
    return out + [spot(d, z, 1 - y, x), spot(d, z, y, 1 - x)]


def meet(others):
    barrier = pltpu.get_barrier_semaphore()
    for other in others:
        pl.semaphore_signal(barrier, inc=1, device_id=other, device_id_type=MESH)
    pl.semaphore_wait(barrier, len(others))


def send(src, dst, send_sem, recv_sem, to):
    return pltpu.make_async_remote_copy(src_ref=src, dst_ref=dst, send_sem=send_sem, recv_sem=recv_sem, device_id=to, device_id_type=MESH)


def rowwise_norm(x):
    center = x - jnp.mean(x, axis=-1, keepdims=True)
    return center * lax.rsqrt(jnp.mean(center * center, axis=-1, keepdims=True) + EPS)


def scan_ends(kb, vb, w_ref, sm, sa, sb, width, chunks):
    for group in scan_groups(width):
        m = [jnp.full((chunks, LANES), NEG, jnp.float32) for _ in group]
        a = [jnp.zeros((chunks, LANES), jnp.float32) for _ in group]
        b = [jnp.zeros((chunks, LANES), jnp.float32) for _ in group]
        for j in range(STEP):
            at = pl.ds(j, chunks, stride=STEP)
            for i, c in enumerate(group):
                k = kb[c, at, :]
                mw = m[i] - w_ref[:, lane(c)]
                m[i] = jnp.maximum(mw, k)
                keep = jnp.exp(mw - m[i])
                take = jnp.exp(k - m[i])
                a[i] = keep * a[i] + take * vb[c, at, :]
                b[i] = keep * b[i] + take
        for i, c in enumerate(group):
            sm[:, lane(c)] = m[i]
            sa[:, lane(c)] = a[i]
            sb[:, lane(c)] = b[i]


def join(m, a, b, decay, me, ae, be):
    mw = m - decay
    mn = jnp.maximum(mw, me)
    keep = jnp.exp(mw - mn)
    take = jnp.exp(me - mn)
    return mn, keep * a + take * ae, keep * b + take * be


def scan_rows(kb, vb, yb, mb, ab, bb, w_ref, u_ref, sm, sa, sb, width, chunks):
    for group in scan_groups(width):
        m = [sm[:, lane(c)] for c in group]
        a = [sa[:, lane(c)] for c in group]
        b = [sb[:, lane(c)] for c in group]
        for j in range(STEP):
            at = pl.ds(j, chunks, stride=STEP)
            for i, c in enumerate(group):
                k = kb[c, at, :]
                v = vb[c, at, :]
                mb[c, at, :] = m[i]
                ab[c, at, :] = a[i]
                bb[c, at, :] = b[i]
                uk = u_ref[:, lane(c)] + k
                p = jnp.maximum(m[i], uk)
                alpha = jnp.exp(m[i] - p)
                beta = jnp.exp(uk - p)
                yb[c, at, :] = (alpha * a[i] + beta * v) / (alpha * b[i] + beta)
                m[i], a[i], b[i] = step_state(m[i], a[i], b[i], w_ref[:, lane(c)], k, v)


def step_state(m, a, b, w, k, v):
    mw = m - w
    mn = jnp.maximum(mw, k)
    keep = jnp.exp(mw - mn)
    take = jnp.exp(k - mn)
    return mn, keep * a + take * v, keep * b + take


def interleave(work, step, first, total, last):
    at = first
    for i, piece in enumerate(work):
        piece()
        goal = first + (last - first) * (i + 1) // len(work)
        while at < goal:
            step(at)
            at += 1
    while at < total:
        step(at)
        at += 1


def forward_body(nd, nz, seqs, pieces, lag, count, *refs):
    ins, refs = refs[:count], refs[count:]
    x_ref, up, n1g, n1b, mk, mv, mr, w_ref, u_ref, n2g, n2b, ck, cr, prev_a, prev_f = refs[:15]
    outs, refs = refs[15:15 + count], refs[15 + count:]
    first, before, gated, chan_rec, chan_keys, g_values, gate, r_ref, middle, diff2, kb, vb, yb, mb, ab, bb = refs[:16]
    (key_in, value_in, recept_in, wbuf, sbuf, init, sm, sa, sb, halo, xs, xr, second,
     loc, zs, zr, as_, ar, bs, br, ds, dr, hs, hr, es, er, ws, ps, pr) = refs[16:]
    d, z, y, x = place(nd, nz)
    rows, dim = x_ref.shape
    part = dim // nd
    chunks = rows // STEP
    nt = 4 * nz
    span = nt // seqs
    t = lax.axis_index("tensor")
    seq = t // span
    pos = lax.rem(t, span)
    f32 = jnp.float32

    def mate(i):
        return (d, seq * span + lax.rem(pos + i, span))

    meet(partners(nd, nz, d, z, y, x) + [mate(i) for i in range(1, span)])

    def cell(a, source_d, source_z, source_y, source_x, at, n):
        if half_of(a):
            return outs[a].at[source_d, source_z, source_y, at:at + n]
        return outs[a].at[source_d, source_z, source_y, source_x, at:at + n]

    def half_of(a):
        return a >= 6

    def by_y_first(p):
        a = pieces[p][0]
        return a in (0, 4, 5) or half_of(a) or p % 2 == 0

    def own(p):
        a, at, n = pieces[p]
        return pltpu.make_async_copy(ins[a].at[at:at + n], cell(a, d, z, y, x, at, n), loc.at[p])

    def along_z(p, i, source):
        a, at, n = pieces[p]
        return send(ins[a].at[at:at + n], cell(a, d, source, y, x, at, n), zs.at[p, i - 1], zr.at[p, i - 1],
                    spot(d, lax.rem(z + i, nz), y, x))

    every = slice(None)

    def first_pair(p, mine):
        a, at, n = pieces[p]
        if by_y_first(p):
            block = cell(a, d, every, y if mine else 1 - y, x, at, n)
            to = spot(d, z, 1 - y, x)
        else:
            block = cell(a, d, every, y, x if mine else 1 - x, at, n)
            to = spot(d, z, y, 1 - x)
        return send(block, block, as_.at[p], ar.at[p], to)

    def second_pair(p, mine):
        a, at, n = pieces[p]
        if by_y_first(p):
            block = cell(a, d, every, every, x if mine else 1 - x, at, n)
            to = spot(d, z, y, 1 - x)
        else:
            block = cell(a, d, every, y if mine else 1 - y, every, at, n)
            to = spot(d, z, 1 - y, x)
        return send(block, block, bs.at[p], br.at[p], to)

    def along_d(p, i, source):
        a, at, n = pieces[p]
        block = cell(a, source, every, every, every, at, n)
        return send(block, block, ds.at[p, i - 1], dr.at[p, i - 1], spot(lax.rem(d + i, nd), z, y, x))

    total = len(pieces)
    arrived = set()

    def gather_step(step):
        p = step
        if p < total:
            own(p).start()
            for i in range(1, nz):
                along_z(p, i, z).start()
        p = step - lag
        if 0 <= p < total:
            own(p).wait()
            for i in range(1, nz):
                along_z(p, i, lax.rem(z - i + nz, nz)).wait_recv()
            first_pair(p, True).start()
        p = step - 2 * lag
        if 0 <= p < total:
            first_pair(p, False).wait_recv()
            if half_of(pieces[p][0]):
                for i in range(1, nd):
                    along_d(p, i, d).start()
            else:
                second_pair(p, True).start()
        p = step - 3 * lag
        if 0 <= p < total and not half_of(pieces[p][0]):
            second_pair(p, False).wait_recv()
            for i in range(1, nd):
                along_d(p, i, d).start()

    def have(array):
        for p in range(total):
            if pieces[p][0] == array and p not in arrived:
                arrived.add(p)
                for i in range(1, nd):
                    along_d(p, i, lax.rem(d - i + nd, nd)).wait_recv()

    def fetch(array, slot):
        return pltpu.make_async_copy(outs[array], wbuf.at[slot], ws.at[slot])

    def norm_first():
        @pl.loop(0, rows // 32)
        def _(i):
            at = pl.ds(pl.multiple_of(i * 32, 32), 32)
            first[at, :] = (rowwise_norm(x_ref[at, :]) * n1g[...] + n1b[...]).astype(jnp.bfloat16)
        pass_last(first, 0, 1).start()

    def pass_last(rows_ref, slot, to):
        return send(rows_ref.at[rows - 16:rows], halo.at[slot], hs.at[slot], hr.at[slot], mate(to))

    def shifted(rows_ref, slot, prev, cols):
        now = rows_ref[:, cols].astype(f32)
        edge = jnp.where(pos == 0, prev[:, cols], halo[slot, :, cols].astype(f32)[15:16, :])
        top = lax.broadcasted_iota(jnp.int32, now.shape, 0) == 0
        return now, jnp.where(top, edge, pltpu.roll(now, 1, 0))

    def mix_first():
        pass_last(first, 0, 1).wait()

        @pl.loop(0, dim // LANES)
        def _(c):
            cols = pl.ds(pl.multiple_of(c * LANES, LANES), LANES)
            now, old = shifted(first, 0, prev_a, cols)
            before[:, cols] = old.astype(jnp.bfloat16)
            for mix, dst in ((mk, key_in), (mv, value_in), (mr, recept_in)):
                dst[:, cols] = (now * mix[:, cols] + old * (1.0 - mix[:, cols])).astype(jnp.bfloat16)

    def project(array, slot, left, store):
        def run():
            fetch(array, slot).wait()
            wide = min(256, dim)
            weights = wbuf.at[slot].reshape(nd, dim, part)
            for n in range(dim // wide):
                acc = dot_nt(left[:, :part], weights[0, n * wide:(n + 1) * wide])
                for e in range(1, nd):
                    acc = acc + dot_nt(left[:, e * part:(e + 1) * part], weights[e, n * wide:(n + 1) * wide])
                store(n, wide, acc)
        return run

    def into_blocks(dst):
        def store(n, wide, acc):
            for q in range(wide // LANES):
                dst[n * (wide // LANES) + q] = acc[:, lane(q)]
        return store

    def into_rows(n, wide, acc):
        r_ref[:, n * wide:(n + 1) * wide] = acc

    def get_kv():
        have(1)
        fetch(1, 0).start()
        have(2)
        fetch(2, 1).start()

    def get_r():
        have(3)
        fetch(3, 0).start()
        have(0)
        copy = pltpu.make_async_copy(outs[0].at[d], sbuf, ws.at[2])
        copy.start()
        copy.wait()
        head = dim // nt
        per = LANES // head
        for c in range(dim // LANES):
            cells = []
            for q in range(per):
                b = c * per + q
                cells.append(sbuf[b // 4, (b // 2) % 2, b % 2][:, :head])
            init[:, lane(c)] = jnp.concatenate(cells, axis=1)

    def get_o():
        have(4)
        fetch(4, 1).start()

    def initial(j):
        got = init[j:j + 1, :]
        for s in range(1, seqs):
            got = jnp.where(seq == s, init[3 * s + j:3 * s + j + 1, :], got)
        return got

    def share(i):
        return send(xs, xr.at[i - 1], es.at[i - 1], er.at[i - 1], mate(i))

    def summarize():
        scan_ends(kb, vb, w_ref, sm, sa, sb, dim, chunks)
        lead = pos == 0
        m = jnp.where(lead, initial(2), NEG)
        a = jnp.where(lead, initial(0), 0.0)
        b = jnp.where(lead, initial(1), 0.0)
        decay = float(STEP) * w_ref[...]
        for s in range(chunks):
            m, a, b = join(m, a, b, decay, sm[s:s + 1, :], sa[s:s + 1, :], sb[s:s + 1, :])
        xs[0:1, :] = a
        xs[1:2, :] = b
        xs[2:3, :] = m
        xs[3:8, :] = jnp.zeros((5, dim), f32)
        for i in range(1, span):
            share(i).start()

    def carry_in():
        for i in range(1, span):
            share(i).wait()
        m = jnp.where(pos == 0, initial(2), NEG)
        a = jnp.where(pos == 0, initial(0), 0.0)
        b = jnp.where(pos == 0, initial(1), 0.0)
        decay = float(rows) * w_ref[...]
        for i in range(span - 1, 0, -1):
            on = i <= pos
            mn, an, bn = join(m, a, b, decay, xr[i - 1, 2:3, :], xr[i - 1, 0:1, :], xr[i - 1, 1:2, :])
            m, a, b = jnp.where(on, mn, m), jnp.where(on, an, a), jnp.where(on, bn, b)
        decay = float(STEP) * w_ref[...]
        for s in range(chunks):
            me, ae, be = sm[s:s + 1, :], sa[s:s + 1, :], sb[s:s + 1, :]
            sm[s:s + 1, :] = m
            sa[s:s + 1, :] = a
            sb[s:s + 1, :] = b
            m, a, b = join(m, a, b, decay, me, ae, be)

    def scan():
        scan_rows(kb, vb, yb, mb, ab, bb, w_ref, u_ref, sm, sa, sb, dim, chunks)
        for c in range(dim // LANES):
            gated[:, lane(c)] = (jax.nn.sigmoid(r_ref[:, lane(c)]) * yb[c]).astype(jnp.bfloat16)

    def attend_out():
        fetch(4, 1).wait()
        weights = wbuf.at[1].reshape(nd, dim, part)
        wide = min(256, part)
        for e in range(nd):
            for n in range(part // wide):
                at = slice(e * part + n * wide, e * part + (n + 1) * wide)
                middle[:, at] = x_ref[:, at] + dot_nn(gated[...], weights[e, :, n * wide:(n + 1) * wide])

    def norm_second():
        @pl.loop(0, rows // 32)
        def _(i):
            at = pl.ds(pl.multiple_of(i * 32, 32), 32)
            second[at, :] = (rowwise_norm(middle[at, :]) * n2g[...] + n2b[...]).astype(jnp.bfloat16)
        pass_last(second, 1, 1).start()

    def mix_second():
        pass_last(second, 1, 1).wait()

        @pl.loop(0, dim // LANES)
        def _(c):
            cols = pl.ds(pl.multiple_of(c * LANES, LANES), LANES)
            now, old = shifted(second, 1, prev_f, cols)
            diff2[:, cols] = now - old
            chan_keys[x, :, cols] = (now * ck[:, cols] + old * (1.0 - ck[:, cols])).astype(jnp.bfloat16)
            chan_rec[:, cols] = (now * cr[:, cols] + old * (1.0 - cr[:, cols])).astype(jnp.bfloat16)
        pair_up(chan_keys, 0, x).start()

    def pair_up(both, slot, source):
        return send(both.at[source], both.at[source], ps.at[slot], pr.at[slot], spot(d, z, y, 1 - x))

    def get_fr():
        have(5)
        fetch(5, 0).start()

    def gate_rows(n, wide, acc):
        at = slice(n * wide, (n + 1) * wide)
        got = jax.nn.sigmoid(acc)
        gate[:, at] = got
        g_values[x, :, at] = (up[:, at] * got).astype(jnp.bfloat16)

    def values_grad():
        project(5, 0, chan_rec, gate_rows)()
        pair_up(g_values, 1, x).start()

    steps = total + 3 * lag
    gather_step(0)
    gather_step(1)
    norm_first()
    gather_step(2)
    mix_first()
    ready = 1 + max(p for p in range(total) if pieces[p][0] <= 2) + 3 * lag
    for s in range(3, ready):
        gather_step(s)
    work = [get_kv, project(1, 0, key_in, into_blocks(kb)), project(2, 1, value_in, into_blocks(vb)), get_r, get_o, summarize,
            project(3, 0, recept_in, into_rows), carry_in, scan, get_fr, attend_out, norm_second, mix_second, values_grad]
    last = {3: 3, 4: 4, 9: 5}
    at = ready
    for i, piece in enumerate(work):
        need = 0
        if i in last:
            need = 1 + max(p for p in range(total) if pieces[p][0] <= last[i]) + 3 * lag
        while at < min(steps, max(need, ready + i)):
            gather_step(at)
            at += 1
        piece()
    while at < steps:
        gather_step(at)
        at += 1
    for a in range(count):
        have(a)
    for p in range(total):
        for i in range(1, nz):
            along_z(p, i, z).wait_send()
        first_pair(p, True).wait_send()
        if not half_of(pieces[p][0]):
            second_pair(p, True).wait_send()
        for i in range(1, nd):
            along_d(p, i, d).wait_send()
    for slot, both in enumerate((chan_keys, g_values)):
        pair_up(both, slot, x).wait_send()
        pair_up(both, slot, 1 - x).wait_recv()


def forward_block(nd, nt, shards, vectors, seqs, rows, unit, lag):
    nz = nt // 4
    span = nt // seqs
    dim = shards[1].shape[0] * nt
    part = dim // nd
    pieces = []
    for a, s in enumerate(shards):
        pieces += [(a, at, min(unit, s.shape[0])) for at in range(0, s.shape[0], unit)]
    n = len(pieces)
    dma = pltpu.SemaphoreType.DMA
    bf, f32 = jnp.bfloat16, jnp.float32
    low = jax.ShapeDtypeStruct((rows, dim), bf)
    full = jax.ShapeDtypeStruct((rows, dim), f32)
    twice = jax.ShapeDtypeStruct((2, rows, dim), bf)
    block = jax.ShapeDtypeStruct((dim // LANES, rows, LANES), f32)
    chunks = rows // STEP
    per = shards[1].shape[0]
    got = pl.pallas_call(
        functools.partial(forward_body, nd, nz, seqs, pieces, lag, len(shards)),
        out_shape=tuple(jax.ShapeDtypeStruct(((nd, nz, 2, 2) if a < 6 else (nd, nz, 2)) + s.shape, s.dtype) for a, s in enumerate(shards))
        + (low,) * 4 + (twice,) * 2 + (full,) * 4 + (block,) * 6,
        in_specs=[HBM] * len(shards) + [VMEM] * len(vectors),
        out_specs=[HBM] * len(shards) + [VMEM] * 16,
        scratch_shapes=[pltpu.VMEM((rows, dim), bf)] * 3
        + [pltpu.VMEM((2, nd, nz, 2, 2, per, part), bf), pltpu.VMEM((nz, 2, 2) + shards[0].shape, f32), pltpu.VMEM((shards[0].shape[0], dim), f32)]
        + [pltpu.VMEM((chunks, dim), f32)] * 3
        + [pltpu.VMEM((2, 16, dim), bf), pltpu.VMEM((8, dim), f32), pltpu.VMEM((span - 1, 8, dim), f32), pltpu.VMEM((rows, dim), bf)]
        + [dma((n,)), dma((n, nz - 1)), dma((n, nz - 1)), dma((n,)), dma((n,)), dma((n,)), dma((n,)),
           dma((n, nd - 1)), dma((n, nd - 1)), dma((2,)), dma((2,)), dma((span - 1,)), dma((span - 1,)), dma((3,)), dma((2,)), dma((2,))],
        compiler_params=pltpu.CompilerParams(collective_id=0, has_side_effects=True, vmem_limit_bytes=58 * 2**20),
        name="forward_block",
    )(*shards, *vectors)
    weights = [o.reshape(nd, -1, s.shape[1]) for o, s in zip(got[1:len(shards)], shards[1:])]
    return weights, got[len(shards):]


def carry_rows(r_ref, gg, kb, yb, mb, bb, w_ref, u_ref, gyb, ca, cb, lc, width, chunks):
    for c in range(width // LANES):
        gyb[c] = gg[:, lane(c)] * jax.nn.sigmoid(r_ref[:, lane(c)])
    for group in scan_groups(width):
        ga = [jnp.zeros((chunks, LANES), jnp.float32) for _ in group]
        gb = [jnp.zeros((chunks, LANES), jnp.float32) for _ in group]
        end = [None for _ in group]
        for j in reversed(range(STEP)):
            at = pl.ds(j, chunks, stride=STEP)
            for i, c in enumerate(group):
                w = w_ref[:, lane(c)]
                k = kb[c, at, :]
                m = mb[c, at, :]
                uk = u_ref[:, lane(c)] + k
                p = jnp.maximum(m, uk)
                alpha = jnp.exp(m - p)
                gn = gyb[c, at, :] / (alpha * bb[c, at, :] + jnp.exp(uk - p))
                gd = -gn * yb[c, at, :]
                mw = m - w
                mn = jnp.maximum(mw, k)
                if j == STEP - 1:
                    end[i] = mn
                keep = jnp.exp(mw - mn)
                ga[i] = alpha * gn + keep * ga[i]
                gb[i] = alpha * gd + keep * gb[i]
                if j == 0:
                    lc[:, lane(c)] = m - float(STEP) * w - end[i]
        for i, c in enumerate(group):
            ca[:, lane(c)] = ga[i]
            cb[:, lane(c)] = gb[i]


def back_rows(kb, vb, yb, mb, ab, bb, gyb, w_ref, u_ref, ta, tb, fk, fv, vec, width, chunks):
    for group in scan_groups(width):
        ga = [ta[:, lane(c)] for c in group]
        gb = [tb[:, lane(c)] for c in group]
        gu = [jnp.zeros((chunks, LANES), jnp.float32) for _ in group]
        gw = [jnp.zeros((chunks, LANES), jnp.float32) for _ in group]
        for j in reversed(range(STEP)):
            at = pl.ds(j, chunks, stride=STEP)
            for i, c in enumerate(group):
                k = kb[c, at, :]
                v = vb[c, at, :]
                m = mb[c, at, :]
                uk = u_ref[:, lane(c)] + k
                p = jnp.maximum(m, uk)
                alpha = jnp.exp(m - p)
                beta = jnp.exp(uk - p)
                b = bb[c, at, :]
                gn = gyb[c, at, :] / (alpha * b + beta)
                gd = -gn * yb[c, at, :]
                mw = m - w_ref[:, lane(c)]
                mn = jnp.maximum(mw, k)
                keep = jnp.exp(mw - mn)
                take = jnp.exp(k - mn)
                now = beta * (gn * v + gd)
                fv[c, at, :] = beta * gn + take * ga[i]
                fk[c, at, :] = now + take * (ga[i] * v + gb[i])
                gu[i] = gu[i] + now
                gw[i] = gw[i] + keep * (ga[i] * ab[c, at, :] + gb[i] * b)
                ga[i] = alpha * gn + keep * ga[i]
                gb[i] = alpha * gd + keep * gb[i]
        for i, c in enumerate(group):
            vec[2:3, lane(c)] = -jnp.sum(gw[i], axis=0, keepdims=True) * w_ref[:, lane(c)]
            vec[3:4, lane(c)] = jnp.sum(gu[i], axis=0, keepdims=True)


def backward_body(nd, nz, seqs, chunks_of, rc, part, lag, *refs):
    gfk, gfv, wk, wv, wr, wo, wfr, values_in, keys_in, diff_in = refs[:10]
    (middle, x_ref, up, first, before, gated, chan_rec, gate, r_ref, kb, vb, yb, mb, ab, bb,
     n1g, mk, mv, mr, w_ref, u_ref, n2g, ck, cr) = refs[10:34]
    (outk, outv, outr, outo, outfr, outfk, outfv, result, tok, vout, gfr, go, gk, gv, gr, landf, landa) = refs[34:51]
    (ownf, owna, slots, raf, raa, rba, rzf, rza, pout, pin, t0, t2, t3, t4, l0, l1, l2, l3, l4, wbuf, ca, cb, lc, ta, tb, xs, xr, hs_buf, hr_buf,
     vec, vd, v1, vx, v2, vy, v3, vz,
     gstage, loc, ds, dr, cs, as_, ar, bs, br, zs, zr, vs, vr, hs, hr, es, er, ws, gs, ps, pr) = refs[51:]
    grads = [gfv, gfk, gfr, go, gk, gv, gr]
    outs = [outfv, outfk, outfr, outo, outk, outv, outr]
    d, z, y, x = place(nd, nz)
    rows, dim = x_ref.shape
    chunks = rows // STEP
    nt = 4 * nz
    span = nt // seqs
    t = lax.axis_index("tensor")
    seq = t // span
    pos = lax.rem(t, span)
    f32, bf = jnp.float32, jnp.bfloat16
    top = vd.shape[1]
    total = len(chunks_of)

    def mate(i):
        return (d, seq * span + lax.rem(pos + i, span))

    def load_block(src, dst, c, sem):
        return pltpu.make_async_copy(src.at[:, c * LANES:(c + 1) * LANES], dst.at[c], sem.at[c])

    blocks = dim // LANES

    def load_all(src, dst, i):
        for c in range(blocks):
            load_block(src, dst, c, ws.at[i]).start()

    def wait_all(src, dst, i):
        for c in range(blocks):
            load_block(src, dst, c, ws.at[i]).wait()

    load_all(values_in.at[1 - x], t3, 0)
    load_all(keys_in.at[1 - x], t4, 1)
    meet(partners(nd, nz, d, z, y, x) + [mate(i) for i in range(1, span)])

    half_count = sum(1 for c in chunks_of if c[0] < 2)

    def half_of(c):
        return c < half_count

    def mine_of(c):
        return ownf.at[c] if half_of(c) else owna.at[c - half_count]

    def slab(c, source):
        a, at = chunks_of[c]
        lanes = pl.ds(pl.multiple_of(source * part, part), part)
        if half_of(c):
            g = grads[a].reshape(nz, 2, grads[a].shape[0] // (2 * nz), dim)
            return g.at[:, :, at:at + 2 * rc, lanes]
        g = grads[a].reshape(nz, 2, 2, grads[a].shape[0] // nt, dim)
        return g.at[:, :, :, at:at + rc, lanes]

    def load(c):
        return pltpu.make_async_copy(slab(c, d), mine_of(c), loc.at[c])

    def landing(c, i):
        return landf.at[i - 1, c] if half_of(c) else landa.at[i - 1, c - half_count]

    def slot_of(c, i):
        full = slots.at[c % 2, i - 1]
        return full.reshape(nz, 2, 2 * rc, part) if half_of(c) else full

    def along_d(c, i):
        to = lax.rem(d + i, nd)
        return send(slab(c, to), landing(c, i), ds.at[i - 1, c], dr.at[i - 1, c], spot(to, z, y, x))

    def bring(c, i):
        return pltpu.make_async_copy(landing(c, i), slot_of(c, i), cs.at[c % 2, i - 1])

    def by_x_first(c):
        return not half_of(c) and (chunks_of[c][0] < 4 or c % 2 == 0)

    def got_first(c):
        return raf.at[c] if half_of(c) else raa.at[c - half_count]

    def first_pair(c):
        own = mine_of(c)
        if half_of(c):
            return send(own.at[:, 1 - y], got_first(c), as_.at[c], ar.at[c], spot(d, z, 1 - y, x))
        if by_x_first(c):
            return send(own.at[:, :, 1 - x], got_first(c), as_.at[c], ar.at[c], spot(d, z, y, 1 - x))
        return send(own.at[:, 1 - y], got_first(c), as_.at[c], ar.at[c], spot(d, z, 1 - y, x))

    def second_pair(c):
        own, dst = mine_of(c), rba.at[c - half_count]
        if by_x_first(c):
            return send(own.at[:, 1 - y, x], dst, bs.at[c], br.at[c], spot(d, z, 1 - y, x))
        return send(own.at[:, y, 1 - x], dst, bs.at[c], br.at[c], spot(d, z, y, 1 - x))

    def got_z(c, i):
        return rzf.at[i - 1, c] if half_of(c) else rza.at[i - 1, c - half_count]

    def along_z(c, i):
        own = mine_of(c)
        to = lax.rem(z + i, nz)
        return send(own.at[to, y] if half_of(c) else own.at[to, y, x], got_z(c, i), zs.at[i - 1, c], zr.at[i - 1, c], spot(d, to, y, x))

    def add_into(dst, at, *terms):
        acc = dst[at].astype(f32)
        for src, place_at in terms:
            acc = acc + src[place_at].astype(f32)
        dst[at] = acc.astype(bf)

    def scatter_step(step):
        c = step
        if c < total:
            load(c).start()
            for i in range(1, nd):
                along_d(c, i).start()
        c = step - 2
        if 0 <= c < total:
            for i in range(1, nd):
                along_d(c, i).wait_recv()
                bring(c, i).start()
        c = step - 3
        if 0 <= c < total:
            load(c).wait()
            for i in range(1, nd):
                bring(c, i).wait()
            own = mine_of(c)

            @pl.loop(0, nz)
            def _(b):
                for q in range(2 if half_of(c) else 4):
                    at = (b, q) if half_of(c) else (b, q // 2, q % 2)
                    add_into(own, at, *[(slot_of(c, i), at) for i in range(1, nd)])
            first_pair(c).start()
        c = step - 3 - lag
        if 0 <= c < total:
            first_pair(c).wait_recv()
            own, got = mine_of(c), got_first(c)

            @pl.loop(0, nz)
            def _(b):
                if half_of(c):
                    add_into(own, (b, y), (got, (b,)))
                else:
                    for q in range(2):
                        add_into(own, (b, q, x) if by_x_first(c) else (b, y, q), (got, (b, q)))
            if half_of(c):
                for i in range(1, nz):
                    along_z(c, i).start()
            else:
                second_pair(c).start()
        c = step - 3 - 2 * lag
        if 0 <= c < total:
            if half_of(c):
                finish(c)
            else:
                second_pair(c).wait_recv()
                own, got = mine_of(c), rba.at[c - half_count]

                @pl.loop(0, nz)
                def _(b):
                    add_into(own, (b, y, x), (got, (b,)))
                for i in range(1, nz):
                    along_z(c, i).start()
        c = step - 3 - 3 * lag
        if 0 <= c < total and not half_of(c):
            finish(c)

    def finish(c):
        for i in range(1, nz):
            along_z(c, i).wait_recv()
        own = mine_of(c)
        acc = (own[z, y] if half_of(c) else own[z, y, x]).astype(f32)
        for i in range(1, nz):
            acc = acc + got_z(c, i)[...].astype(f32)
        a, at = chunks_of[c]
        outs[a][:, at:at + acc.shape[0]] = acc.T

    steps = total + 3 + 3 * lag

    def vec_d(i):
        return send(vec.at[:top], vd.at[d], vs.at[i - 1], vr.at[i - 1], spot(lax.rem(d + i, nd), z, y, x))

    def vec_x():
        return send(v1, vx, vs.at[nd - 1], vr.at[nd - 1], spot(d, z, y, 1 - x))

    def vec_y():
        return send(v2, vy, vs.at[nd], vr.at[nd], spot(d, z, 1 - y, x))

    def vec_z(i):
        return send(v3, vz.at[z], vs.at[nd + i], vr.at[nd + i], spot(d, lax.rem(z + i, nz), y, x))

    def vec_step(step):
        if step == 0:
            vd[d] = vec[:top]
            for i in range(1, nd):
                vec_d(i).start()
        elif step == 1:
            for i in range(1, nd):
                vec_d(i).wait()
            acc = vd[0]
            for i in range(1, nd):
                acc = acc + vd[i]
            v1[:top] = acc
            v1[top:] = vec[top:]
            vec_x().start()
        elif step == 2:
            vec_x().wait()
            v2[...] = v1[...] + vx[...]
            vec_y().start()
        elif step == 3:
            vec_y().wait()
            v3[...] = v2[...] + vy[...]
            vz[z] = v3[...]
            for i in range(1, nz):
                vec_z(i).start()
        elif step == 4:
            for i in range(1, nz):
                vec_z(i).wait()
            acc = vz[0]
            for i in range(1, nz):
                acc = acc + vz[i]
            vout[...] = acc

    lead = pos == 0

    def keep_lead(group, row):
        for s in range(seqs):
            at = top + group * seqs + s
            vec[at:at + 1, :] = jnp.where(jnp.logical_and(lead, seq == s), row, 0.0)

    def pass_first(slot):
        return send(hs_buf.at[slot], hr_buf.at[slot], hs.at[slot], hr.at[slot], mate(span - 1))

    def pulled(back, slot, cols):
        edge = jnp.where(pos == span - 1, 0.0, hr_buf[slot, 0:1, cols])
        last = lax.broadcasted_iota(jnp.int32, back.shape, 0) == rows - 1
        return jnp.where(last, edge, pltpu.roll(back, rows - 1, 0))

    def partial(slot):
        return send(pout.at[slot], pin.at[slot], ps.at[slot], pr.at[slot], spot(d, z, y, 1 - x))

    def send_partials():
        for slot, src, buf in ((0, values_in, t3), (1, keys_in, t4)):
            wait_all(src.at[1 - x], buf, slot)

            @pl.loop(0, blocks)
            def _(c):
                pout[slot, c] = buf[c].astype(bf)
            partial(slot).start()
        load_all(values_in.at[x], t3, 0)
        load_all(keys_in.at[x], t2, 1)
        load_all(diff_in, t4, 2)
        vec[...] = jnp.zeros(vec.shape, f32)

    def block_result():
        fetch(wfr).start()
        wait_all(values_in.at[x], t3, 0)
        partial(0).wait()

        @pl.loop(0, blocks)
        def _(c):
            cols = pl.ds(pl.multiple_of(c * LANES, LANES), LANES)
            values = t3[c] + pin[0, c].astype(f32)
            open_ = gate[:, cols]
            result[:, cols] = middle[:, cols] + open_ * values
            l0[:, cols] = (up[:, cols] * values * open_ * (1.0 - open_)).astype(bf)

    def recept_grad():
        weight_grad(l0, chan_rec, gfr)

    def recept_input():
        fetch(wfr).wait()
        for e in range(nd):
            for n in range(part // wide):
                got = dot_nn(l0[...], weights[e, :, n * wide:(n + 1) * wide])
                for q in range(wide // LANES):
                    t3[(e * part + n * wide) // LANES + q] = got[:, lane(q)]

    def start_second():
        wait_all(keys_in.at[x], t2, 1)
        wait_all(diff_in, t4, 2)
        partial(1).wait()
        for c in range(blocks):
            t2[c] = t2[c] + pin[1, c].astype(f32)
        for c in range(blocks):
            hs_buf[0, :, lane(c)] = t2[c, 0:8, :] * (1.0 - ck[:, lane(c)]) + t3[c, 0:8, :] * (1.0 - cr[:, lane(c)])
        pass_first(0).start()
        keep_lead(1, hs_buf[0, 0:1, :])

        @pl.loop(0, blocks)
        def _(c):
            cols = pl.ds(pl.multiple_of(c * LANES, LANES), LANES)
            vec[9:10, cols] = jnp.sum(t2[c] * t4[c], axis=0, keepdims=True)
            vec[10:11, cols] = jnp.sum(t3[c] * t4[c], axis=0, keepdims=True)

    def second_grad():
        pass_first(0).wait()

        @pl.loop(0, blocks)
        def _(c):
            cols = pl.ds(pl.multiple_of(c * LANES, LANES), LANES)
            key, rec = t2[c], t3[c]
            back = key * (1.0 - ck[:, cols]) + rec * (1.0 - cr[:, cols])
            t0[:, cols] = key * ck[:, cols] + rec * cr[:, cols] + pulled(back, 0, cols)

    def norm_grad(src, gain, base, dst, row, low):
        @pl.loop(0, rows // 32)
        def _(i):
            at = pl.ds(pl.multiple_of(i * 32, 32), 32)
            raw = src[at, :]
            center = raw - jnp.mean(raw, axis=-1, keepdims=True)
            scale = lax.rsqrt(jnp.mean(center * center, axis=-1, keepdims=True) + EPS)
            s = center * scale
            g = t0[at, :]
            q = g * gain[...]
            out = base[at, :] + (q - jnp.mean(q, axis=-1, keepdims=True) - s * jnp.mean(q * s, axis=-1, keepdims=True)) * scale
            dst[at, :] = out
            if low is not None:
                low[at, :] = out.astype(bf)
            vec[row:row + 1, :] += jnp.sum(g * s, axis=0, keepdims=True)
            vec[row + 1:row + 2, :] += jnp.sum(g, axis=0, keepdims=True)

    def norm_second_grad():
        fetch(wo).start()
        norm_grad(middle, n2g, up, tok, 7, l0)

    def fetch(src):
        return pltpu.make_async_copy(src, wbuf, gs.at[2])

    weights = wbuf
    wide = min(256, part)

    def gated_grad():
        fetch(wo).wait()
        for n in range(dim // wide):
            acc = dot_nt(l0[:, :part], weights[0, n * wide:(n + 1) * wide])
            for e in range(1, nd):
                acc = acc + dot_nt(l0[:, e * part:(e + 1) * part], weights[e, n * wide:(n + 1) * wide])
            t0[:, n * wide:(n + 1) * wide] = acc

    busy = [None, None]
    half = dim // 2
    broad = min(512, dim)

    def settle(h):
        if busy[h] is not None:
            busy[h].wait()
            busy[h] = None

    def weight_grad(cols_ref, ins_ref, dst):
        for h in range(2):
            settle(h)
            for n in range(half // wide):
                at = h * half + n * wide
                for m in range(dim // broad):
                    gstage[h, n * wide:(n + 1) * wide, m * broad:(m + 1) * broad] = dot_tn(
                        cols_ref[:, at:at + wide], ins_ref[:, m * broad:(m + 1) * broad]).astype(bf)
            busy[h] = pltpu.make_async_copy(gstage.at[h], dst.at[h * half:(h + 1) * half], gs.at[h])
            busy[h].start()

    def share(i):
        return send(xs, xr.at[i - 1], es.at[i - 1], er.at[i - 1], mate(i))

    def chain(ga, gb, keep_ends):
        for s in reversed(range(chunks)):
            if keep_ends:
                ta[s:s + 1, :] = ga
                tb[s:s + 1, :] = gb
            keep = jnp.exp(lc[s:s + 1, :])
            ga = ca[s:s + 1, :] + keep * ga
            gb = cb[s:s + 1, :] + keep * gb
        return ga, gb

    def carry_out():
        carry_rows(r_ref, t0, kb, yb, mb, bb, w_ref, u_ref, t2, ca, cb, lc, dim, chunks)
        zero = jnp.zeros((1, dim), f32)
        ga, gb = chain(zero, zero, False)
        lg = lc[0:1, :]
        for s in range(1, chunks):
            lg = lg + lc[s:s + 1, :]
        xs[0:1, :] = ga
        xs[1:2, :] = gb
        xs[2:3, :] = lg
        xs[3:8, :] = jnp.zeros((5, dim), f32)
        for i in range(1, span):
            share(i).start()

    def scan_back():
        for i in range(1, span):
            share(i).wait()
        ga, gb = jnp.zeros((1, dim), f32), jnp.zeros((1, dim), f32)
        for i in range(span - 1, 0, -1):
            on = pos + i < span
            slot = span - i - 1
            keep = jnp.exp(xr[slot, 2:3, :])
            ga = jnp.where(on, xr[slot, 0:1, :] + keep * ga, ga)
            gb = jnp.where(on, xr[slot, 1:2, :] + keep * gb, gb)
        ga, gb = chain(ga, gb, True)
        keep_lead(2, ga)
        keep_lead(3, gb)
        back_rows(kb, vb, yb, mb, ab, bb, t2, w_ref, u_ref, ta, tb, t3, t4, vec, dim, chunks)

    def round_grads():
        for c in range(blocks):
            l1[:, lane(c)] = t3[c].astype(bf)
            l2[:, lane(c)] = t4[c].astype(bf)
            sig = jax.nn.sigmoid(r_ref[:, lane(c)])
            l3[:, lane(c)] = (t0[:, lane(c)] * yb[c] * sig * (1.0 - sig)).astype(bf)

    def mixed_in(mix):
        for c in range(blocks):
            l4[:, lane(c)] = (first[:, lane(c)].astype(f32) * mix[:, lane(c)]
                              + before[:, lane(c)].astype(f32) * (1.0 - mix[:, lane(c)])).astype(bf)

    def grad_of(mix, cols_ref, dst):
        def run():
            mixed_in(mix)
            weight_grad(cols_ref, l4, dst)
        return run

    def input_grad(whole, low, mix, row, initial):
        def run():
            fetch(whole).start()
            fetch(whole).wait()
            for e in range(nd):
                for n in range(part // wide):
                    at = e * part + n * wide
                    got = dot_nn(low[...], weights[e, :, n * wide:(n + 1) * wide])
                    for q in range(wide // LANES):
                        c = at // LANES + q
                        g = got[:, lane(q)]
                        diff = first[:, lane(c)].astype(f32) - before[:, lane(c)].astype(f32)
                        vec[row:row + 1, lane(c)] = jnp.sum(g * diff, axis=0, keepdims=True)
                        stay, back = g * mix[:, lane(c)], g * (1.0 - mix[:, lane(c)])
                        t3[c] = stay if initial else t3[c] + stay
                        t4[c] = back if initial else t4[c] + back
        return run

    def start_first():
        for c in range(blocks):
            hs_buf[1, :, lane(c)] = t4[c, 0:8, :]
        pass_first(1).start()
        keep_lead(0, hs_buf[1, 0:1, :])

    def first_grad():
        pass_first(1).wait()

        @pl.loop(0, blocks)
        def _(c):
            cols = pl.ds(pl.multiple_of(c * LANES, LANES), LANES)
            t0[:, cols] = t3[c] + pulled(t4[c], 1, cols)
        norm_grad(x_ref, n1g, tok, tok, 0, None)

    def out_grad():
        weight_grad(gated, l0, go)

    first_of = [min(c for c in range(total) if chunks_of[c][0] == a) for a in range(7)]
    plan = [(send_partials, None), (block_result, None), (recept_grad, 2), (recept_input, None), (start_second, None), (second_grad, None),
            (norm_second_grad, None), (gated_grad, None), (carry_out, None), (out_grad, 3), (scan_back, None), (round_grads, None),
            (grad_of(mk, l1, gk), 4), (grad_of(mv, l2, gv), 5), (grad_of(mr, l3, gr), 6),
            (input_grad(wk, l1, mk, 4, True), None), (input_grad(wv, l2, mv, 5, False), None), (input_grad(wr, l3, mr, 6, False), None),
            (start_first, None), (first_grad, None)]
    pace = [0, 4, 5, 6, 7, 8, 9, 10, 10, 11, 12, 12, 13, 14, 16, 18, 19, 20, 21, 22]
    at, done = 0, set()

    def advance(goal):
        nonlocal at
        while at < goal:
            if at < total and chunks_of[at][0] >= 2:
                a = chunks_of[at][0]
                if a not in done:
                    return
                if at == first_of[a]:
                    settle(0)
                    settle(1)
            scatter_step(at)
            at += 1

    for (piece, array), goal in zip(plan, pace):
        advance(goal)
        piece()
        if array is not None:
            done.add(array)
    tail = 0
    while at < steps or tail < 10:
        if tail < 10 and tail % 2 == 0:
            vec_step(tail // 2)
        tail += 1
        advance(min(steps, at + 1))
    settle(0)
    settle(1)
    for c in range(total):
        for i in range(1, nd):
            along_d(c, i).wait_send()
        first_pair(c).wait_send()
        if not half_of(c):
            second_pair(c).wait_send()
        for i in range(1, nz):
            along_z(c, i).wait_send()


def backward_block(nd, nt, head, wide_head, operands, vec_rows, top, seqs, rc, lag):
    nz = nt // 4
    span = nt // seqs
    rows, dim = operands[10].shape
    part = dim // nd
    chunks_of = []
    for a, cl in enumerate((wide_head, wide_head, head, head, head, head, head)):
        size = rc if a > 1 else 2 * rc
        chunks_of += [(a, at) for at in range(0, cl, size)]
    n = len(chunks_of)
    nf = sum(1 for c in chunks_of if c[0] < 2)
    na = n - nf
    chunks = rows // STEP
    dma = pltpu.SemaphoreType.DMA
    bf, f32 = jnp.bfloat16, jnp.float32

    def vv(*shape):
        return pltpu.VMEM(shape, f32)

    def lv(*shape):
        return pltpu.VMEM(shape, bf)

    def shard(cl):
        return jax.ShapeDtypeStruct((part, cl), f32)

    square = jax.ShapeDtypeStruct((dim, dim), bf)
    vec = (vec_rows, dim)
    blocks = dim // LANES
    full = jax.ShapeDtypeStruct((rows, dim), f32)
    return pl.pallas_call(
        functools.partial(backward_body, nd, nz, seqs, chunks_of, rc, part, lag),
        out_shape=(shard(head),) * 5 + (shard(wide_head),) * 2 + (full, full, jax.ShapeDtypeStruct(vec, f32)) + (square,) * 5
        + (jax.ShapeDtypeStruct((nd - 1, nf, nz, 2, 2 * rc, part), bf), jax.ShapeDtypeStruct((nd - 1, na, nz, 2, 2, rc, part), bf)),
        in_specs=[HBM] * 10 + [VMEM] * 24,
        out_specs=[VMEM] * 10 + [HBM] * 7,
        scratch_shapes=[lv(nf, nz, 2, 2 * rc, part), lv(na, nz, 2, 2, rc, part), lv(2, nd - 1, nz, 2, 2, rc, part),
                        lv(nf, nz, 2 * rc, part), lv(na, nz, 2, rc, part), lv(na, nz, rc, part),
                        lv(nz - 1, nf, 2 * rc, part), lv(nz - 1, na, rc, part), lv(2, blocks, rows, LANES), lv(2, blocks, rows, LANES),
                        vv(rows, dim)] + [vv(blocks, rows, LANES)] * 3 + [lv(rows, dim)] * 5
        + [lv(nd, dim, part)] + [vv(chunks, dim)] * 5 + [vv(8, dim), vv(span - 1, 8, dim), vv(2, 8, dim), vv(2, 8, dim)]
        + [vv(*vec), vv(nd, top, dim)] + [vv(*vec)] * 5 + [vv(nz, *vec), lv(2, dim // 2, dim)]
        + [dma((n,)), dma((nd - 1, n)), dma((nd - 1, n)), dma((2, nd - 1)), dma((n,)), dma((n,)), dma((n,)), dma((n,)),
           dma((nz - 1, n)), dma((nz - 1, n)), dma((nd + nz,)), dma((nd + nz,)), dma((2,)), dma((2,)),
           dma((span - 1,)), dma((span - 1,)), dma((3, blocks)), dma((3,)), dma((2,)), dma((2,))],
        compiler_params=pltpu.CompilerParams(collective_id=1, has_side_effects=True, vmem_limit_bytes=60 * 2**20),
        name="backward_block",
    )(*operands)


def local(nd, nt, x, num, den, top, prev_a, prev_f, n1g, n1b, fading, reward, mk, mv, mr, wk, wv, wr, wo, n2g, n2b, ck, cr,
          fk, fv, fr, up):
    rows, dim = x.shape
    seqs = prev_a.shape[0]
    span = nt // seqs
    tp = lax.axis_index("tensor")
    dp = lax.axis_index("dp")
    seq = tp // span
    pos = tp % span
    part = dim // nd
    head = num.shape[1]
    behind = [(i + 1, i) for i in range(nt - 1)]

    def into(left, whole):
        total = dot_nt(left[:, :part], whole[0])
        for d in range(1, nd):
            total = total + dot_nt(left[:, d * part:(d + 1) * part], whole[d])
        return total

    def outof(left, whole):
        return jnp.concatenate([dot_nn(left, whole[d]) for d in range(nd)], axis=1)

    def weight_grad(cols, ins):
        return dot_tn(cols, ins).astype(jnp.bfloat16)

    def line(v):
        return v.astype(jnp.float32).reshape(1, dim)

    w = jnp.exp(fading)
    packed = jnp.stack([num, den, top], axis=1).reshape(3 * seqs, head)
    packed = jnp.pad(packed, ((0, -3 * seqs % 8), (0, LANES - head)))
    shards = [packed] + [s.T for s in (wk, wv, wr, wo, fr, fk, fv)]
    mine_a = lax.dynamic_slice_in_dim(prev_a, seq, 1, 0)
    mine_f = lax.dynamic_slice_in_dim(prev_f, seq, 1, 0)
    vectors = [x, up] + [line(v) for v in (n1g, n1b, mk, mv, mr, w, reward, n2g, n2b, ck, cr, mine_a, mine_f)]
    weights, saved = forward_block(nd, nt, shards, vectors, seqs, rows, 32, 2)
    whole_k, whole_v, whole_r, whole_o, whole_fr, whole_fk, whole_fv = weights
    first, before, gated, chan_rec, chan_keys, g_values, gate, recept, middle, diff2, kb, vb, yb, mb, ab, bb = saved
    keys2, values2 = chan_keys.reshape(2 * rows, dim), g_values.reshape(2 * rows, dim)
    hidden = jnp.maximum(into(keys2, whole_fk), 0.0)
    squared = jnp.square(hidden).astype(jnp.bfloat16)
    g_hidden = (into(values2, whole_fv) * 2.0 * hidden).astype(jnp.bfloat16)
    grad_fv = weight_grad(squared, values2)
    grad_fk = weight_grad(g_hidden, keys2)
    part_values = outof(squared, whole_fv).reshape(2, rows, dim)
    part_keys = outof(g_hidden, whole_fk).reshape(2, rows, dim)

    top = 16
    vec_rows = top + -(-4 * seqs // 8) * 8
    operands = [grad_fk, grad_fv, whole_k, whole_v, whole_r, whole_o, whole_fr, part_values, part_keys, diff2,
                middle, x, up, first, before, gated, chan_rec, gate, recept, kb, vb, yb, mb, ab, bb]
    operands += [line(v) for v in (n1g, mk, mv, mr, w, reward, n2g, ck, cr)]
    got = backward_block(nd, nt, head, fk.shape[1], operands, vec_rows, top, seqs, (5 * head + 2 * fk.shape[1]) // 26, 2)
    out_k, out_v, out_r, out_o, out_fr, out_fk, out_fv, result, tokens_grad, vectors = got[:10]
    slots = vectors[top:top + 4 * seqs].reshape(4, seqs, dim)
    prevs = slots[:2]
    states = lax.dynamic_slice_in_dim(slots[2:], tp * head, head, 2)
    grad_num, grad_den = states[0], states[1]
    grad_top = grad_num * num + grad_den * den
    return (result, tokens_grad, grad_num, grad_den, grad_top, prevs[0], prevs[1],
            vectors[0], vectors[1], vectors[2], vectors[3], vectors[4], vectors[5], vectors[6],
            out_k, out_v, out_r, out_o, vectors[7], vectors[8], vectors[9], vectors[10], out_fk, out_fv, out_fr)


def solution(mesh):
    nd, nt = mesh.shape["dp"], mesh.shape["tensor"]
    rows, both, lead, one = P(("dp", "tensor"), None), P("dp", "tensor"), P("dp", None), P()
    return jax.shard_map(
        functools.partial(local, nd, nt),
        mesh=mesh,
        in_specs=(rows, both, both, both, lead, lead) + (one,) * 7 + (both,) * 4 + (one,) * 4 + (both,) * 3 + (rows,),
        out_specs=(rows, rows, both, both, both, lead, lead) + (one,) * 7 + (both,) * 4 + (one,) * 4 + (both,) * 3,
        check_vma=False,
    )
```

```python
import functools

import jax
import jax.numpy as jnp
from jax import lax
from jax.experimental import pallas as pl
from jax.experimental.pallas import tpu as pltpu
from jax.sharding import PartitionSpec as P

EPS = 1e-05
STEP = 16
NEG = -1e30


def dot_nt(x, y):
    return lax.dot_general(x, y, (((1,), (1,)), ((), ())), preferred_element_type=jnp.float32)


def dot_nn(x, y):
    return lax.dot_general(x, y, (((1,), (0,)), ((), ())), preferred_element_type=jnp.float32)


def dot_tn(x, y):
    return lax.dot_general(x, y, (((0,), (0,)), ((), ())), preferred_element_type=jnp.float32)


LANES = 128
VMEM = pl.BlockSpec(memory_space=pltpu.VMEM)


def scan_groups(width):
    blocks = width // LANES
    size = 4 if blocks % 4 == 0 else 1
    return [range(g, g + size) for g in range(0, blocks, size)]


def lane(c):
    return slice(c * LANES, (c + 1) * LANES)


MESH = pl.DeviceIdType.MESH
HBM = pl.BlockSpec(memory_space=pltpu.HBM)


def place(nd, nz):
    d = lax.axis_index("dp")
    t = lax.axis_index("tensor")
    return d, t // 4, lax.rem(t // 2, 2), lax.rem(t, 2)


def spot(d, z, y, x):
    return (d, z * 4 + y * 2 + x)


def partners(nd, nz, d, z, y, x):
    out = [spot(lax.rem(d + i, nd), z, y, x) for i in range(1, nd)]
    out += [spot(d, lax.rem(z + i, nz), y, x) for i in range(1, nz)]
    return out + [spot(d, z, 1 - y, x), spot(d, z, y, 1 - x)]


def meet(others):
    barrier = pltpu.get_barrier_semaphore()
    for other in others:
        pl.semaphore_signal(barrier, inc=1, device_id=other, device_id_type=MESH)
    pl.semaphore_wait(barrier, len(others))


def send(src, dst, send_sem, recv_sem, to):
    return pltpu.make_async_remote_copy(src_ref=src, dst_ref=dst, send_sem=send_sem, recv_sem=recv_sem, device_id=to, device_id_type=MESH)


def rowwise_norm(x):
    center = x - jnp.mean(x, axis=-1, keepdims=True)
    return center * lax.rsqrt(jnp.mean(center * center, axis=-1, keepdims=True) + EPS)


def scan_ends(kb, vb, w_ref, sm, sa, sb, width, chunks):
    for group in scan_groups(width):
        m = [jnp.full((chunks, LANES), NEG, jnp.float32) for _ in group]
        a = [jnp.zeros((chunks, LANES), jnp.float32) for _ in group]
        b = [jnp.zeros((chunks, LANES), jnp.float32) for _ in group]
        for j in range(STEP):
            at = pl.ds(j, chunks, stride=STEP)
            for i, c in enumerate(group):
                k = kb[c, at, :]
                mw = m[i] - w_ref[:, lane(c)]
                m[i] = jnp.maximum(mw, k)
                keep = jnp.exp(mw - m[i])
                take = jnp.exp(k - m[i])
                a[i] = keep * a[i] + take * vb[c, at, :]
                b[i] = keep * b[i] + take
        for i, c in enumerate(group):
            sm[:, lane(c)] = m[i]
            sa[:, lane(c)] = a[i]
            sb[:, lane(c)] = b[i]


def join(m, a, b, decay, me, ae, be):
    mw = m - decay
    mn = jnp.maximum(mw, me)
    keep = jnp.exp(mw - mn)
    take = jnp.exp(me - mn)
    return mn, keep * a + take * ae, keep * b + take * be


def scan_rows(kb, vb, yb, mb, ab, bb, w_ref, u_ref, sm, sa, sb, width, chunks):
    for group in scan_groups(width):
        m = [sm[:, lane(c)] for c in group]
        a = [sa[:, lane(c)] for c in group]
        b = [sb[:, lane(c)] for c in group]
        for j in range(STEP):
            at = pl.ds(j, chunks, stride=STEP)
            for i, c in enumerate(group):
                k = kb[c, at, :]
                v = vb[c, at, :]
                mb[c, at, :] = m[i]
                ab[c, at, :] = a[i]
                bb[c, at, :] = b[i]
                uk = u_ref[:, lane(c)] + k
                p = jnp.maximum(m[i], uk)
                alpha = jnp.exp(m[i] - p)
                beta = jnp.exp(uk - p)
                yb[c, at, :] = (alpha * a[i] + beta * v) / (alpha * b[i] + beta)
                m[i], a[i], b[i] = step_state(m[i], a[i], b[i], w_ref[:, lane(c)], k, v)


def step_state(m, a, b, w, k, v):
    mw = m - w
    mn = jnp.maximum(mw, k)
    keep = jnp.exp(mw - mn)
    take = jnp.exp(k - mn)
    return mn, keep * a + take * v, keep * b + take


def forward_body(nd, nz, seqs, pieces, lag, count, *refs):
    given, refs = refs[:count], refs[count:]
    num, den, top_, prevs_a, prevs_f = refs[:5]
    refs = refs[5:]
    x_ref, up, n1g, n1b, mk, mv, mr, fading, u_ref, n2g, n2b, ck, cr = refs[:13]
    count += 1
    outs, refs = refs[13:13 + count], refs[13 + count:]
    homes = refs[:16]
    (key_in, value_in, recept_in, wbuf, sbuf, init, sm, sa, sb, halo, xs, xr, second,
     first, before, gated, chan_rec, chan_keys, g_values, gate, r_ref, middle, diff2, kb, vb, yb, mb, ab, bb,
     states, raw_k, raw_v, turned_k, turned_v, w_ref, prev_a, prev_f,
     loc, zs, zr, as_, ar, bs, br, ds, dr, hs, hr, es, er, ws, ps, pr, os) = refs[16:]
    ins = (states,) + tuple(given[:5]) + (turned_k, turned_v)
    made = (first, before, gated, chan_rec, chan_keys, g_values, gate, r_ref, middle, diff2, kb, vb, yb, mb, ab, bb)
    d, z, y, x = place(nd, nz)
    rows, dim = x_ref.shape
    part = dim // nd
    chunks = rows // STEP
    nt = 4 * nz
    span = nt // seqs
    t = lax.axis_index("tensor")
    seq = t // span
    pos = lax.rem(t, span)
    f32 = jnp.float32

    def mate(i):
        return (d, seq * span + lax.rem(pos + i, span))

    meet(partners(nd, nz, d, z, y, x) + [mate(i) for i in range(1, span)])

    def cell(a, source_d, source_z, source_y, source_x, at, n):
        if half_of(a):
            return outs[a].at[source_d, source_z, source_y, at:at + n]
        return outs[a].at[source_d, source_z, source_y, source_x, at:at + n]

    def half_of(a):
        return a >= 6

    def by_y_first(p):
        a = pieces[p][0]
        return a in (0, 4, 5) or half_of(a) or p % 2 == 0

    def leave(i):
        home = homes[i].at[x] if i in (4, 5) else homes[i]
        return pltpu.make_async_copy(made[i], home, os.at[i])

    def bring_raw(i):
        return pltpu.make_async_copy(given[5 + i], (raw_k, raw_v)[i], ws.at[3 + i])

    bring_raw(0).start()
    bring_raw(1).start()
    w_ref[...] = jnp.exp(fading[...])
    for src, dst in ((prevs_a, prev_a), (prevs_f, prev_f)):
        got = src[0:1, :].astype(f32)
        for s in range(1, seqs):
            got = jnp.where(seq == s, src[s:s + 1, :].astype(f32), got)
        dst[...] = got
    states[...] = jnp.zeros(states.shape, f32)
    for s in range(seqs):
        for j, src in enumerate((num, den, top_)):
            states[3 * s + j:3 * s + j + 1, :src.shape[1]] = src[s:s + 1, :]

    def turn(i):
        bring_raw(i).wait()
        (turned_k, turned_v)[i][...] = (raw_k, raw_v)[i][...].T

    def own(p):
        a, at, n = pieces[p]
        return pltpu.make_async_copy(ins[a].at[at:at + n], cell(a, d, z, y, x, at, n), loc.at[p])

    def along_z(p, i, source):
        a, at, n = pieces[p]
        return send(ins[a].at[at:at + n], cell(a, d, source, y, x, at, n), zs.at[p, i - 1], zr.at[p, i - 1],
                    spot(d, lax.rem(z + i, nz), y, x))

    every = slice(None)

    def first_pair(p, mine):
        a, at, n = pieces[p]
        if by_y_first(p):
            block = cell(a, d, every, y if mine else 1 - y, x, at, n)
            to = spot(d, z, 1 - y, x)
        else:
            block = cell(a, d, every, y, x if mine else 1 - x, at, n)
            to = spot(d, z, y, 1 - x)
        return send(block, block, as_.at[p], ar.at[p], to)

    def second_pair(p, mine):
        a, at, n = pieces[p]
        if by_y_first(p):
            block = cell(a, d, every, every, x if mine else 1 - x, at, n)
            to = spot(d, z, y, 1 - x)
        else:
            block = cell(a, d, every, y if mine else 1 - y, every, at, n)
            to = spot(d, z, 1 - y, x)
        return send(block, block, bs.at[p], br.at[p], to)

    def along_d(p, i, source):
        a, at, n = pieces[p]
        block = cell(a, source, every, every, every, at, n)
        return send(block, block, ds.at[p, i - 1], dr.at[p, i - 1], spot(lax.rem(d + i, nd), z, y, x))

    total = len(pieces)
    arrived = set()

    def gather_step(step):
        p = step
        if p < total:
            own(p).start()
            for i in range(1, nz):
                along_z(p, i, z).start()
        p = step - lag[0]
        if 0 <= p < total:
            own(p).wait()
            for i in range(1, nz):
                along_z(p, i, lax.rem(z - i + nz, nz)).wait_recv()
            first_pair(p, True).start()
        p = step - lag[1]
        if 0 <= p < total:
            first_pair(p, False).wait_recv()
            if half_of(pieces[p][0]):
                for i in range(1, nd):
                    along_d(p, i, d).start()
            else:
                second_pair(p, True).start()
        p = step - lag[2]
        if 0 <= p < total and not half_of(pieces[p][0]):
            second_pair(p, False).wait_recv()
            for i in range(1, nd):
                along_d(p, i, d).start()

    def have(array):
        for p in range(total):
            if pieces[p][0] == array and p not in arrived:
                arrived.add(p)
                for i in range(1, nd):
                    along_d(p, i, lax.rem(d - i + nd, nd)).wait_recv()

    def fetch(array, slot):
        return pltpu.make_async_copy(outs[array], wbuf.at[slot], ws.at[slot])

    def norm_first():
        @pl.loop(0, rows // 32)
        def _(i):
            at = pl.ds(pl.multiple_of(i * 32, 32), 32)
            first[at, :] = (rowwise_norm(x_ref[at, :]) * n1g[...] + n1b[...]).astype(jnp.bfloat16)
        pass_last(first, 0, 1).start()

    def pass_last(rows_ref, slot, to):
        return send(rows_ref.at[rows - 16:rows], halo.at[slot], hs.at[slot], hr.at[slot], mate(to))

    def shifted(rows_ref, slot, prev, cols):
        now = rows_ref[:, cols].astype(f32)
        edge = jnp.where(pos == 0, prev[:, cols], halo[slot, :, cols].astype(f32)[15:16, :])
        top = lax.broadcasted_iota(jnp.int32, now.shape, 0) == 0
        return now, jnp.where(top, edge, pltpu.roll(now, 1, 0))

    def mix_first():
        pass_last(first, 0, 1).wait()

        @pl.loop(0, dim // LANES)
        def _(c):
            cols = pl.ds(pl.multiple_of(c * LANES, LANES), LANES)
            now, old = shifted(first, 0, prev_a, cols)
            before[:, cols] = old.astype(jnp.bfloat16)
            for mix, dst in ((mk, key_in), (mv, value_in), (mr, recept_in)):
                dst[:, cols] = (now * mix[:, cols] + old * (1.0 - mix[:, cols])).astype(jnp.bfloat16)
        leave(0).start()
        leave(1).start()

    def project(array, slot, left, store):
        def run():
            fetch(array, slot).wait()
            wide = min(256, dim)
            weights = wbuf.at[slot].reshape(nd, dim, part)
            for n in range(dim // wide):
                acc = dot_nt(left[:, :part], weights[0, n * wide:(n + 1) * wide])
                for e in range(1, nd):
                    acc = acc + dot_nt(left[:, e * part:(e + 1) * part], weights[e, n * wide:(n + 1) * wide])
                store(n, wide, acc)
        return run

    def into_blocks(dst):
        def store(n, wide, acc):
            for q in range(wide // LANES):
                dst[n * (wide // LANES) + q] = acc[:, lane(q)]
        return store

    def into_rows(n, wide, acc):
        r_ref[:, n * wide:(n + 1) * wide] = acc

    def get_kv():
        have(1)
        fetch(1, 0).start()
        have(2)
        fetch(2, 1).start()

    def get_r():
        have(3)
        fetch(3, 0).start()
        have(0)
        copy = pltpu.make_async_copy(outs[0].at[d], sbuf, ws.at[2])
        copy.start()
        copy.wait()
        head = dim // nt
        per = LANES // head
        for c in range(dim // LANES):
            cells = []
            for q in range(per):
                b = c * per + q
                cells.append(sbuf[b // 4, (b // 2) % 2, b % 2][:, :head])
            init[:, lane(c)] = jnp.concatenate(cells, axis=1)

    def get_o():
        have(4)
        fetch(4, 1).start()

    def initial(j):
        got = init[j:j + 1, :]
        for s in range(1, seqs):
            got = jnp.where(seq == s, init[3 * s + j:3 * s + j + 1, :], got)
        return got

    def share(i):
        return send(xs, xr.at[i - 1], es.at[i - 1], er.at[i - 1], mate(i))

    def summarize():
        scan_ends(kb, vb, w_ref, sm, sa, sb, dim, chunks)
        lead = pos == 0
        m = jnp.where(lead, initial(2), NEG)
        a = jnp.where(lead, initial(0), 0.0)
        b = jnp.where(lead, initial(1), 0.0)
        decay = float(STEP) * w_ref[...]
        for s in range(chunks):
            m, a, b = join(m, a, b, decay, sm[s:s + 1, :], sa[s:s + 1, :], sb[s:s + 1, :])
        xs[0:1, :] = a
        xs[1:2, :] = b
        xs[2:3, :] = m
        xs[3:8, :] = jnp.zeros((5, dim), f32)
        for i in range(1, span):
            share(i).start()

    def carry_in():
        for i in range(1, span):
            share(i).wait()
        m = jnp.where(pos == 0, initial(2), NEG)
        a = jnp.where(pos == 0, initial(0), 0.0)
        b = jnp.where(pos == 0, initial(1), 0.0)
        decay = float(rows) * w_ref[...]
        for i in range(span - 1, 0, -1):
            on = i <= pos
            mn, an, bn = join(m, a, b, decay, xr[i - 1, 2:3, :], xr[i - 1, 0:1, :], xr[i - 1, 1:2, :])
            m, a, b = jnp.where(on, mn, m), jnp.where(on, an, a), jnp.where(on, bn, b)
        decay = float(STEP) * w_ref[...]
        for s in range(chunks):
            me, ae, be = sm[s:s + 1, :], sa[s:s + 1, :], sb[s:s + 1, :]
            sm[s:s + 1, :] = m
            sa[s:s + 1, :] = a
            sb[s:s + 1, :] = b
            m, a, b = join(m, a, b, decay, me, ae, be)

    def scan():
        scan_rows(kb, vb, yb, mb, ab, bb, w_ref, u_ref, sm, sa, sb, dim, chunks)
        for c in range(dim // LANES):
            gated[:, lane(c)] = (jax.nn.sigmoid(r_ref[:, lane(c)]) * yb[c]).astype(jnp.bfloat16)
        for i in (2, 7, 10, 11, 12, 13, 14, 15):
            leave(i).start()

    def attend_out():
        fetch(4, 1).wait()
        weights = wbuf.at[1].reshape(nd, dim, part)
        wide = min(256, part)
        for e in range(nd):
            for n in range(part // wide):
                at = slice(e * part + n * wide, e * part + (n + 1) * wide)
                middle[:, at] = x_ref[:, at] + dot_nn(gated[...], weights[e, :, n * wide:(n + 1) * wide])
        leave(8).start()

    def norm_second():
        @pl.loop(0, rows // 32)
        def _(i):
            at = pl.ds(pl.multiple_of(i * 32, 32), 32)
            second[at, :] = (rowwise_norm(middle[at, :]) * n2g[...] + n2b[...]).astype(jnp.bfloat16)
        pass_last(second, 1, 1).start()

    def mix_second():
        pass_last(second, 1, 1).wait()

        @pl.loop(0, dim // LANES)
        def _(c):
            cols = pl.ds(pl.multiple_of(c * LANES, LANES), LANES)
            now, old = shifted(second, 1, prev_f, cols)
            diff2[:, cols] = now - old
            chan_keys[:, cols] = (now * ck[:, cols] + old * (1.0 - ck[:, cols])).astype(jnp.bfloat16)
            chan_rec[:, cols] = (now * cr[:, cols] + old * (1.0 - cr[:, cols])).astype(jnp.bfloat16)
        pair_up(0, x).start()
        for i in (3, 4, 9):
            leave(i).start()

    def pair_up(slot, source):
        return send(made[4 + slot], homes[4 + slot].at[source], ps.at[slot], pr.at[slot], spot(d, z, y, 1 - x))

    def get_fr():
        have(5)
        fetch(5, 0).start()

    def gate_rows(n, wide, acc):
        at = slice(n * wide, (n + 1) * wide)
        got = jax.nn.sigmoid(acc)
        gate[:, at] = got
        g_values[:, at] = (up[:, at] * got).astype(jnp.bfloat16)

    def values_grad():
        project(5, 0, chan_rec, gate_rows)()
        pair_up(1, x).start()
        for i in (5, 6):
            leave(i).start()

    steps = total + lag[2]
    gather_step(0)
    gather_step(1)
    norm_first()
    gather_step(2)
    turn(0)
    turn(1)
    mix_first()
    def due(array):
        return 1 + max(p for p in range(total) if pieces[p][0] == array) + lag[2]

    ready = max(due(1), due(2))
    for s in range(3, ready):
        gather_step(s)
    work = [get_kv, project(1, 0, key_in, into_blocks(kb)), project(2, 1, value_in, into_blocks(vb)), get_r, get_o, summarize,
            project(3, 0, recept_in, into_rows), carry_in, scan, get_fr, attend_out, norm_second, mix_second, values_grad]
    last = {3: max(due(3), due(0)), 4: due(4), 9: due(5)}
    at = ready
    for i, piece in enumerate(work):
        while at < min(steps, max(last.get(i, 0), ready + i)):
            gather_step(at)
            at += 1
        piece()
    while at < steps:
        gather_step(at)
        at += 1
    for a in range(count):
        have(a)
    for p in range(total):
        for i in range(1, nz):
            along_z(p, i, z).wait_send()
        first_pair(p, True).wait_send()
        if not half_of(pieces[p][0]):
            second_pair(p, True).wait_send()
        for i in range(1, nd):
            along_d(p, i, d).wait_send()
    for slot in range(2):
        pair_up(slot, x).wait_send()
        pair_up(slot, 1 - x).wait_recv()
    for i in range(16):
        leave(i).wait()


def forward_block(nd, nt, given, small, vectors, seqs, rows, unit, lag, mixing=1):
    nz = nt // 4
    span = nt // seqs
    dim = given[0].shape[0] * nt
    part = dim // nd
    bf16 = jnp.bfloat16
    shards = [jax.ShapeDtypeStruct((-(-3 * seqs // 8) * 8, LANES), jnp.float32)] + list(given[:5])
    shards += [jax.ShapeDtypeStruct((g.shape[1], g.shape[0]), bf16) for g in given[5:]]
    pieces = []
    for a, s in enumerate(shards):
        size = min(unit[a >= 6], s.shape[0])
        pieces += [(a, at, size) for at in range(0, s.shape[0], size)]
    early = [p for p in pieces if p[0] in (1, 2)] + [p for p in pieces if p[0] in (3, 0)]
    later = [p for p in pieces if p[0] in (4, 5)]
    halves = [p for a, b in zip([p for p in pieces if p[0] == 6], [p for p in pieces if p[0] == 7]) for p in (a, b)]
    pieces = early
    while later or halves:
        pieces, later, halves = pieces + later[:1] + halves[:mixing], later[1:], halves[mixing:]
    n = len(pieces)
    dma = pltpu.SemaphoreType.DMA
    bf, f32 = jnp.bfloat16, jnp.float32
    low = jax.ShapeDtypeStruct((rows, dim), bf)
    full = jax.ShapeDtypeStruct((rows, dim), f32)
    twice = jax.ShapeDtypeStruct((2, rows, dim), bf)
    block = jax.ShapeDtypeStruct((dim // LANES, rows, LANES), f32)
    chunks = rows // STEP
    per = shards[1].shape[0]
    got = pl.pallas_call(
        functools.partial(forward_body, nd, nz, seqs, pieces, lag, len(given)),
        out_shape=tuple(jax.ShapeDtypeStruct(((nd, nz, 2, 2) if a < 6 else (nd, nz, 2)) + s.shape, s.dtype) for a, s in enumerate(shards))
        + (low,) * 4 + (twice,) * 2 + (full,) * 4 + (block,) * 6,
        in_specs=[HBM] * len(given) + [VMEM] * (5 + len(vectors)),
        out_specs=[HBM] * len(shards) + [HBM] * 16,
        scratch_shapes=[pltpu.VMEM((rows, dim), bf)] * 3
        + [pltpu.VMEM((2, nd, nz, 2, 2, per, part), bf), pltpu.VMEM((nz, 2, 2) + shards[0].shape, f32), pltpu.VMEM((shards[0].shape[0], dim), f32)]
        + [pltpu.VMEM((chunks, dim), f32)] * 3
        + [pltpu.VMEM((2, 16, dim), bf), pltpu.VMEM((8, dim), f32), pltpu.VMEM((span - 1, 8, dim), f32), pltpu.VMEM((rows, dim), bf)]
        + [pltpu.VMEM((rows, dim), bf)] * 6 + [pltpu.VMEM((rows, dim), f32)] * 4 + [pltpu.VMEM(block.shape, f32)] * 6
        + [pltpu.VMEM(shards[0].shape, f32)] + [pltpu.VMEM(g.shape, bf) for g in given[5:]] + [pltpu.VMEM(s.shape, bf) for s in shards[6:]]
        + [pltpu.VMEM((1, dim), f32)] * 3
        + [dma((n,)), dma((n, nz - 1)), dma((n, nz - 1)), dma((n,)), dma((n,)), dma((n,)), dma((n,)),
           dma((n, nd - 1)), dma((n, nd - 1)), dma((2,)), dma((2,)), dma((span - 1,)), dma((span - 1,)), dma((5,)), dma((2,)), dma((2,)), dma((16,))],
        compiler_params=pltpu.CompilerParams(collective_id=0, has_side_effects=True, vmem_limit_bytes=60 * 2**20),
        name="forward_block",
    )(*given, *small, *vectors)
    weights = [o.reshape(nd, -1, s.shape[1]) for o, s in zip(got[1:len(shards)], shards[1:])]
    return weights, got[len(shards):]


def channel_body(nd, nz, keys_in, grads_in, fk_in, fv_in, values, part_keys, gfk, gfv,
                 fk, fv, squared, hidden_grad, stage, pout, pin, ls, gs, ps, pr):
    d, z, y, x = place(nd, nz)
    part, width = fk.shape[2], fk.shape[1]
    rows2, dim = keys_in.shape
    rows = rows2 // 2
    f32, bf = jnp.float32, jnp.bfloat16
    count = ls.shape[1]
    size = width // count
    wide = min(256, size)

    def bring(i, b):
        src, dst = ((fk_in, fk), (fv_in, fv))[i]
        return pltpu.make_async_copy(src.at[:, b * size:(b + 1) * size], dst.at[:, b * size:(b + 1) * size], ls.at[i, b])

    for b in range(count):
        bring(0, b).start()
        bring(1, b).start()
    meet([spot(d, z, y, 1 - x)])
    for b in range(count):
        bring(0, b).wait()
        bring(1, b).wait()
        for n in range(size // wide):
            at = slice(b * size + n * wide, b * size + (n + 1) * wide)
            hid = dot_nt(keys_in[:, :part], fk[0, at])
            back = dot_nt(grads_in[:, :part], fv[0, at])
            for e in range(1, nd):
                hid = hid + dot_nt(keys_in[:, e * part:(e + 1) * part], fk[e, at])
                back = back + dot_nt(grads_in[:, e * part:(e + 1) * part], fv[e, at])
            hid = jnp.maximum(hid, 0.0)
            squared[:, at] = (hid * hid).astype(bf)
            hidden_grad[:, at] = (back * 2.0 * hid).astype(bf)
    mine = pl.ds(pl.multiple_of(x * rows, rows), rows)
    theirs = pl.ds(pl.multiple_of((1 - x) * rows, rows), rows)
    step = min(256, part)

    def product(left, at_rows, whole, store):
        for e in range(nd):
            for n in range(part // step):
                store(slice(e * part + n * step, e * part + (n + 1) * step),
                      dot_nn(left[at_rows, :], whole[e, :, n * step:(n + 1) * step]))

    def put_out(at, got):
        pout[:, at] = got.astype(bf)

    def put_values(at, got):
        values[:, at] = got

    def put_theirs(at, got):
        part_keys[1 - x, :, at] = got

    def put_mine(at, got):
        part_keys[x, :, at] = got

    product(squared, theirs, fv, put_out)
    swap = send(pout, pin, ps.at[0], pr.at[0], spot(d, z, y, 1 - x))
    swap.start()
    product(squared, mine, fv, put_values)
    product(hidden_grad, theirs, fk, put_theirs)
    product(hidden_grad, mine, fk, put_mine)
    broad = min(512, dim)
    busy = [None, None]
    turn = 0
    for left, right, dst in ((squared, grads_in, gfv), (hidden_grad, keys_in, gfk)):
        for b in range(count):
            if busy[turn] is not None:
                busy[turn].wait()
            for n in range(size // wide):
                at = slice(b * size + n * wide, b * size + (n + 1) * wide)
                for m in range(dim // broad):
                    stage[turn, n * wide:(n + 1) * wide, m * broad:(m + 1) * broad] = dot_tn(
                        left[:, at], right[:, m * broad:(m + 1) * broad]).astype(bf)
            busy[turn] = pltpu.make_async_copy(stage.at[turn], dst.at[b * size:(b + 1) * size], gs.at[turn])
            busy[turn].start()
            turn = 1 - turn
    swap.wait()
    for c in range(dim // LANES):
        values[:, lane(c)] = values[:, lane(c)] + pin[:, lane(c)].astype(f32)
    for copy in busy:
        copy.wait()


def channel_block(nd, nt, keys, grads, fk, fv):
    rows2, dim = keys.shape
    rows = rows2 // 2
    width, part = fk.shape[1], fk.shape[2]
    bf, f32 = jnp.bfloat16, jnp.float32
    count = 4
    dma = pltpu.SemaphoreType.DMA
    square = jax.ShapeDtypeStruct((width, dim), bf)
    return pl.pallas_call(
        functools.partial(channel_body, nd, nt // 4),
        out_shape=(jax.ShapeDtypeStruct((rows, dim), f32), jax.ShapeDtypeStruct((2, rows, dim), f32), square, square),
        in_specs=[VMEM, VMEM, HBM, HBM],
        out_specs=[VMEM, VMEM, HBM, HBM],
        scratch_shapes=[pltpu.VMEM((nd, width, part), bf), pltpu.VMEM((nd, width, part), bf), pltpu.VMEM((rows2, width), bf),
                        pltpu.VMEM((rows2, width), bf), pltpu.VMEM((2, width // count, dim), bf), pltpu.VMEM((rows, dim), bf),
                        pltpu.VMEM((rows, dim), bf), dma((2, count)), dma((2,)), dma((1,)), dma((1,))],
        compiler_params=pltpu.CompilerParams(collective_id=2, has_side_effects=True, vmem_limit_bytes=60 * 2**20),
        name="channel_block",
    )(keys, grads, fk, fv)


def carry_rows(r_ref, gg, kb, yb, mb, bb, w_ref, u_ref, gyb, ca, cb, lc, width, chunks):
    for c in range(width // LANES):
        gyb[c] = gg[:, lane(c)] * jax.nn.sigmoid(r_ref[:, lane(c)])
    for group in scan_groups(width):
        ga = [jnp.zeros((chunks, LANES), jnp.float32) for _ in group]
        gb = [jnp.zeros((chunks, LANES), jnp.float32) for _ in group]
        end = [None for _ in group]
        for j in reversed(range(STEP)):
            at = pl.ds(j, chunks, stride=STEP)
            for i, c in enumerate(group):
                w = w_ref[:, lane(c)]
                k = kb[c, at, :]
                m = mb[c, at, :]
                uk = u_ref[:, lane(c)] + k
                p = jnp.maximum(m, uk)
                alpha = jnp.exp(m - p)
                gn = gyb[c, at, :] / (alpha * bb[c, at, :] + jnp.exp(uk - p))
                gd = -gn * yb[c, at, :]
                mw = m - w
                mn = jnp.maximum(mw, k)
                if j == STEP - 1:
                    end[i] = mn
                keep = jnp.exp(mw - mn)
                ga[i] = alpha * gn + keep * ga[i]
                gb[i] = alpha * gd + keep * gb[i]
                if j == 0:
                    lc[:, lane(c)] = m - float(STEP) * w - end[i]
        for i, c in enumerate(group):
            ca[:, lane(c)] = ga[i]
            cb[:, lane(c)] = gb[i]


def back_rows(kb, vb, yb, mb, ab, bb, gyb, w_ref, u_ref, ta, tb, fk, fv, vec, width, chunks):
    for group in scan_groups(width):
        ga = [ta[:, lane(c)] for c in group]
        gb = [tb[:, lane(c)] for c in group]
        gu = [jnp.zeros((chunks, LANES), jnp.float32) for _ in group]
        gw = [jnp.zeros((chunks, LANES), jnp.float32) for _ in group]
        for j in reversed(range(STEP)):
            at = pl.ds(j, chunks, stride=STEP)
            for i, c in enumerate(group):
                k = kb[c, at, :]
                v = vb[c, at, :]
                m = mb[c, at, :]
                uk = u_ref[:, lane(c)] + k
                p = jnp.maximum(m, uk)
                alpha = jnp.exp(m - p)
                beta = jnp.exp(uk - p)
                b = bb[c, at, :]
                gn = gyb[c, at, :] / (alpha * b + beta)
                gd = -gn * yb[c, at, :]
                mw = m - w_ref[:, lane(c)]
                mn = jnp.maximum(mw, k)
                keep = jnp.exp(mw - mn)
                take = jnp.exp(k - mn)
                now = beta * (gn * v + gd)
                fv[c, at, :] = beta * gn + take * ga[i]
                fk[c, at, :] = now + take * (ga[i] * v + gb[i])
                gu[i] = gu[i] + now
                gw[i] = gw[i] + keep * (ga[i] * ab[c, at, :] + gb[i] * b)
                ga[i] = alpha * gn + keep * ga[i]
                gb[i] = alpha * gd + keep * gb[i]
        for i, c in enumerate(group):
            vec[0:1, lane(c)] = -jnp.sum(gw[i], axis=0, keepdims=True) * w_ref[:, lane(c)]
            vec[1:2, lane(c)] = jnp.sum(gu[i], axis=0, keepdims=True)


def backward_body(nd, nz, seqs, chunks_of, nf, rc, part, lag, *refs):
    gfk, gfv, wk, wv, wr, wo, wfr, keys_in, diff_in = refs[:9]
    homes = refs[9:25]
    n1g, mk, mv, mr, fading, u_ref, n2g, ck, cr = refs[25:34]
    (outk, outv, outr, outo, outfr, outfk, outfv, result, tok, vout_a, vout_b, gfr, go, gk, gv, gr, landf, landa) = refs[34:52]
    (ownf, owna, slots, raf, raa, rba, rzf, rza, pout, pin, t0, t2, t3, t4, l0, l1, l2, l3, l4, wbuf, ca, cb, lc, ta, tb, xs, xr, hs_buf, hr_buf,
     w_ref, vec_a, vec_b, got_a, got_b, gstage, *more) = refs[52:]
    values_ref, middle, x_ref, up, first, before, gated, chan_rec, gate, r_ref, kb, vb, yb, mb, ab, bb = held = more[:16]
    loc, ds, dr, cs, as_, ar, bs, br, zs, zr, vs, vr, hs, hr, es, er, ws, gs, ps, pr, os = more[16:]
    grads = [gfv, gfk, gfr, go, gk, gv, gr]
    outs = [outfv, outfk, outfr, outo, outk, outv, outr]
    d, z, y, x = place(nd, nz)
    rows, dim = x_ref.shape
    chunks = rows // STEP
    nt = 4 * nz
    span = nt // seqs
    t = lax.axis_index("tensor")
    seq = t // span
    pos = lax.rem(t, span)
    f32, bf = jnp.float32, jnp.bfloat16
    total = len(chunks_of)
    top_a, top_b = 6, 5

    def mate(i):
        return (d, seq * span + lax.rem(pos + i, span))

    def load_block(src, dst, c, sem):
        return pltpu.make_async_copy(src.at[:, c * LANES:(c + 1) * LANES], dst.at[c], sem.at[c])

    blocks = dim // LANES

    def load_all(src, dst, i):
        for c in range(blocks):
            load_block(src, dst, c, ws.at[i]).start()

    def wait_all(src, dst, i):
        for c in range(blocks):
            load_block(src, dst, c, ws.at[i]).wait()

    def enter(i):
        return pltpu.make_async_copy(homes[i], held[i], os.at[i])

    def inside(*which):
        for i in which:
            enter(i).wait()

    load_all(keys_in.at[1 - x], t4, 1)
    for i in (0, 8, 1, 3, 7, 9, 10, 12, 13, 15, 6, 11, 14, 4, 5, 2):
        enter(i).start()
    meet(partners(nd, nz, d, z, y, x) + [mate(i) for i in range(1, span)])

    def half_of(c):
        return chunks_of[c][0] < 2

    rank = [sum(1 for e in range(c) if half_of(e) == half_of(c)) for c in range(total)]

    def mine_of(c):
        return ownf.at[rank[c]] if half_of(c) else owna.at[rank[c]]

    def slab(c, source):
        a, at = chunks_of[c]
        lanes = pl.ds(pl.multiple_of(source * part, part), part)
        if half_of(c):
            g = grads[a].reshape(nz, 2, grads[a].shape[0] // (2 * nz), dim)
            return g.at[:, :, at:at + 2 * rc, lanes]
        g = grads[a].reshape(nz, 2, 2, grads[a].shape[0] // nt, dim)
        return g.at[:, :, :, at:at + rc, lanes]

    def load(c):
        return pltpu.make_async_copy(slab(c, d), mine_of(c), loc.at[c])

    def landing(c, i):
        return (landf if half_of(c) else landa).at[i - 1, rank[c]]

    def slot_of(c, i):
        full = slots.at[c % 2, i - 1]
        return full.reshape(nz, 2, 2 * rc, part) if half_of(c) else full

    def along_d(c, i):
        to = lax.rem(d + i, nd)
        return send(slab(c, to), landing(c, i), ds.at[i - 1, c], dr.at[i - 1, c], spot(to, z, y, x))

    def bring(c, i):
        return pltpu.make_async_copy(landing(c, i), slot_of(c, i), cs.at[c % 2, i - 1])

    def by_x_first(c):
        return not half_of(c) and (chunks_of[c][0] < 4 or rank[c] % 2 == 0)

    def got_first(c):
        return (raf if half_of(c) else raa).at[rank[c]]

    def first_pair(c):
        own = mine_of(c)
        if half_of(c):
            return send(own.at[:, 1 - y], got_first(c), as_.at[c], ar.at[c], spot(d, z, 1 - y, x))
        if by_x_first(c):
            return send(own.at[:, :, 1 - x], got_first(c), as_.at[c], ar.at[c], spot(d, z, y, 1 - x))
        return send(own.at[:, 1 - y], got_first(c), as_.at[c], ar.at[c], spot(d, z, 1 - y, x))

    def second_pair(c):
        own, dst = mine_of(c), rba.at[rank[c]]
        if by_x_first(c):
            return send(own.at[:, 1 - y, x], dst, bs.at[c], br.at[c], spot(d, z, 1 - y, x))
        return send(own.at[:, y, 1 - x], dst, bs.at[c], br.at[c], spot(d, z, y, 1 - x))

    def got_z(c, i):
        return (rzf if half_of(c) else rza).at[i - 1, rank[c]]

    def along_z(c, i):
        own = mine_of(c)
        to = lax.rem(z + i, nz)
        return send(own.at[to, y] if half_of(c) else own.at[to, y, x], got_z(c, i), zs.at[i - 1, c], zr.at[i - 1, c], spot(d, to, y, x))

    def add_into(dst, at, *terms):
        if len(terms) == 1:
            dst[at] = dst[at] + terms[0][0][terms[0][1]]
            return
        acc = dst[at].astype(f32)
        for src, place_at in terms:
            acc = acc + src[place_at].astype(f32)
        dst[at] = acc.astype(bf)

    def scatter_step(step):
        c = step
        if c < total:
            load(c).start()
            for i in range(1, nd):
                along_d(c, i).start()
        c = step - 2
        if 0 <= c < total:
            for i in range(1, nd):
                along_d(c, i).wait_recv()
                bring(c, i).start()
        c = step - 3
        if 0 <= c < total:
            load(c).wait()
            for i in range(1, nd):
                bring(c, i).wait()
            own = mine_of(c)

            @pl.loop(0, nz)
            def _(b):
                for q in range(2 if half_of(c) else 4):
                    at = (b, q) if half_of(c) else (b, q // 2, q % 2)
                    add_into(own, at, *[(slot_of(c, i), at) for i in range(1, nd)])
            first_pair(c).start()
        c = step - 3 - lag
        if 0 <= c < total:
            first_pair(c).wait_recv()
            own, got = mine_of(c), got_first(c)

            @pl.loop(0, nz)
            def _(b):
                if half_of(c):
                    add_into(own, (b, y), (got, (b,)))
                else:
                    for q in range(2):
                        add_into(own, (b, q, x) if by_x_first(c) else (b, y, q), (got, (b, q)))
            if half_of(c):
                for i in range(1, nz):
                    along_z(c, i).start()
            else:
                second_pair(c).start()
        c = step - 3 - 2 * lag
        if 0 <= c < total:
            if half_of(c):
                finish(c)
            else:
                second_pair(c).wait_recv()
                own, got = mine_of(c), rba.at[rank[c]]

                @pl.loop(0, nz)
                def _(b):
                    add_into(own, (b, y, x), (got, (b,)))
                for i in range(1, nz):
                    along_z(c, i).start()
        c = step - 3 - 3 * lag
        if 0 <= c < total and not half_of(c):
            finish(c)

    def finish(c):
        for i in range(1, nz):
            along_z(c, i).wait_recv()
        own = mine_of(c)
        acc = (own[z, y] if half_of(c) else own[z, y, x]).astype(f32)
        for i in range(1, nz):
            acc = acc + got_z(c, i)[...].astype(f32)
        a, at = chunks_of[c]
        if half_of(c):
            outs[a][:, at:at + acc.shape[0]] = acc.T
        else:
            outs[a][at:at + acc.shape[0], :] = acc

    steps = total + 3 + 3 * lag

    def vector_sums(vec, top, bufs, base, out):
        vd, v1, vx, v2, vy, v3, vz = bufs

        def link(i, src, dst, to):
            return send(src, dst, vs.at[base + i], vr.at[base + i], to)

        def vec_d(i):
            return link(i - 1, vec, vd.at[d], spot(lax.rem(d + i, nd), z, y, x))

        def vec_x():
            return link(nd - 1, v1, vx, spot(d, z, y, 1 - x))

        def vec_y():
            return link(nd, v2, vy, spot(d, z, 1 - y, x))

        def vec_z(i):
            return link(nd + i, v3, vz.at[z], spot(d, lax.rem(z + i, nz), y, x))

        def start():
            vd[d] = vec[...]
            for i in range(1, nd):
                vec_d(i).start()

        def over_x():
            for i in range(1, nd):
                vec_d(i).wait()
            acc = vd[0]
            for i in range(1, nd):
                acc = acc + vd[i]
            row = lax.broadcasted_iota(jnp.int32, acc.shape, 0)
            v1[...] = jnp.where(row < top, acc, vec[...])
            vec_x().start()

        def over_y():
            vec_x().wait()
            v2[...] = v1[...] + vx[...]
            vec_y().start()

        def over_z():
            vec_y().wait()
            v3[...] = v2[...] + vy[...]
            vz[z] = v3[...]
            for i in range(1, nz):
                vec_z(i).start()

        def finish_sum():
            for i in range(1, nz):
                vec_z(i).wait()
            acc = vz[0]
            for i in range(1, nz):
                acc = acc + vz[i]
            out[...] = acc

        return [start, over_x, over_y, over_z, finish_sum]

    sums_a = vector_sums(vec_a, top_a, got_a, 0, vout_a)
    sums_b = vector_sums(vec_b, top_b, got_b, nd + nz, vout_b)

    lead = pos == 0

    def keep_lead(vec, start, row):
        for s in range(seqs):
            at = start + s
            vec[at:at + 1, :] = jnp.where(jnp.logical_and(lead, seq == s), row, 0.0)

    def pass_first(slot):
        return send(hs_buf.at[slot], hr_buf.at[slot], hs.at[slot], hr.at[slot], mate(span - 1))

    def pulled(back, slot, cols):
        edge = jnp.where(pos == span - 1, 0.0, hr_buf[slot, 0:1, cols])
        last = lax.broadcasted_iota(jnp.int32, back.shape, 0) == rows - 1
        return jnp.where(last, edge, pltpu.roll(back, rows - 1, 0))

    def partial():
        return send(pout, pin, ps.at[0], pr.at[0], spot(d, z, y, 1 - x))

    def send_partials():
        wait_all(keys_in.at[1 - x], t4, 1)

        @pl.loop(0, blocks)
        def _(c):
            pout[c] = t4[c].astype(bf)
        partial().start()
        load_all(keys_in.at[x], t2, 1)
        load_all(diff_in, t4, 2)
        w_ref[...] = jnp.exp(fading[...])
        vec_a[...] = jnp.zeros(vec_a.shape, f32)
        vec_b[...] = jnp.zeros(vec_b.shape, f32)

    def block_result():
        fetch(wfr).start()
        inside(0, 8, 1, 3)

        @pl.loop(0, blocks)
        def _(c):
            cols = pl.ds(pl.multiple_of(c * LANES, LANES), LANES)
            values, open_ = values_ref[:, cols], gate[:, cols]
            result[:, cols] = middle[:, cols] + open_ * values
            l0[:, cols] = (up[:, cols] * values * open_ * (1.0 - open_)).astype(bf)

    def recept_grad():
        inside(7)
        weight_grad(l0, chan_rec, gfr)

    def recept_input():
        fetch(wfr).wait()
        for e in range(nd):
            for n in range(part // wide):
                got = dot_nn(l0[...], weights[e, :, n * wide:(n + 1) * wide])
                for q in range(wide // LANES):
                    t3[(e * part + n * wide) // LANES + q] = got[:, lane(q)]

    def start_second():
        wait_all(keys_in.at[x], t2, 1)
        wait_all(diff_in, t4, 2)
        partial().wait()
        for c in range(blocks):
            t2[c] = t2[c] + pin[c].astype(f32)
        for c in range(blocks):
            hs_buf[0, :, lane(c)] = t2[c, 0:8, :] * (1.0 - ck[:, lane(c)]) + t3[c, 0:8, :] * (1.0 - cr[:, lane(c)])
        pass_first(0).start()
        keep_lead(vec_a, top_a, hs_buf[0, 0:1, :])

        @pl.loop(0, blocks)
        def _(c):
            cols = pl.ds(pl.multiple_of(c * LANES, LANES), LANES)
            vec_a[4:5, cols] = jnp.sum(t2[c] * t4[c], axis=0, keepdims=True)
            vec_a[5:6, cols] = jnp.sum(t3[c] * t4[c], axis=0, keepdims=True)

    def second_grad():
        pass_first(0).wait()

        @pl.loop(0, blocks)
        def _(c):
            cols = pl.ds(pl.multiple_of(c * LANES, LANES), LANES)
            key, rec = t2[c], t3[c]
            back = key * (1.0 - ck[:, cols]) + rec * (1.0 - cr[:, cols])
            t0[:, cols] = key * ck[:, cols] + rec * cr[:, cols] + pulled(back, 0, cols)

    def norm_grad(src, gain, base, dst, vec, row, low):
        @pl.loop(0, rows // 32)
        def _(i):
            at = pl.ds(pl.multiple_of(i * 32, 32), 32)
            raw = src[at, :]
            center = raw - jnp.mean(raw, axis=-1, keepdims=True)
            scale = lax.rsqrt(jnp.mean(center * center, axis=-1, keepdims=True) + EPS)
            s = center * scale
            g = t0[at, :]
            q = g * gain[...]
            out = base[at, :] + (q - jnp.mean(q, axis=-1, keepdims=True) - s * jnp.mean(q * s, axis=-1, keepdims=True)) * scale
            dst[at, :] = out
            if low is not None:
                low[at, :] = out.astype(bf)
            vec[row:row + 1, :] += jnp.sum(g * s, axis=0, keepdims=True)
            vec[row + 1:row + 2, :] += jnp.sum(g, axis=0, keepdims=True)

    def norm_second_grad():
        fetch(wo).start()
        norm_grad(middle, n2g, up, tok, vec_a, 2, l0)

    def fetch(src):
        return pltpu.make_async_copy(src, wbuf, gs.at[2])

    weights = wbuf
    wide = min(256, part)

    def gated_grad():
        fetch(wo).wait()
        for n in range(dim // wide):
            acc = dot_nt(l0[:, :part], weights[0, n * wide:(n + 1) * wide])
            for e in range(1, nd):
                acc = acc + dot_nt(l0[:, e * part:(e + 1) * part], weights[e, n * wide:(n + 1) * wide])
            t0[:, n * wide:(n + 1) * wide] = acc

    busy = [None, None]
    half = dim // 2
    broad = min(512, dim)

    def settle(h):
        if busy[h] is not None:
            busy[h].wait()
            busy[h] = None

    def weight_grad(cols_ref, ins_ref, dst):
        for h in range(2):
            settle(h)
            for n in range(half // wide):
                at = h * half + n * wide
                for m in range(dim // broad):
                    gstage[h, n * wide:(n + 1) * wide, m * broad:(m + 1) * broad] = dot_tn(
                        cols_ref[:, at:at + wide], ins_ref[:, m * broad:(m + 1) * broad]).astype(bf)
            busy[h] = pltpu.make_async_copy(gstage.at[h], dst.at[h * half:(h + 1) * half], gs.at[h])
            busy[h].start()

    def share(i):
        return send(xs, xr.at[i - 1], es.at[i - 1], er.at[i - 1], mate(i))

    def chain(ga, gb, keep_ends):
        for s in reversed(range(chunks)):
            if keep_ends:
                ta[s:s + 1, :] = ga
                tb[s:s + 1, :] = gb
            keep = jnp.exp(lc[s:s + 1, :])
            ga = ca[s:s + 1, :] + keep * ga
            gb = cb[s:s + 1, :] + keep * gb
        return ga, gb

    def carry_out():
        inside(9, 10, 12, 13, 15)
        carry_rows(r_ref, t0, kb, yb, mb, bb, w_ref, u_ref, t2, ca, cb, lc, dim, chunks)
        zero = jnp.zeros((1, dim), f32)
        ga, gb = chain(zero, zero, False)
        lg = lc[0:1, :]
        for s in range(1, chunks):
            lg = lg + lc[s:s + 1, :]
        xs[0:1, :] = ga
        xs[1:2, :] = gb
        xs[2:3, :] = lg
        xs[3:8, :] = jnp.zeros((5, dim), f32)
        for i in range(1, span):
            share(i).start()

    def scan_back():
        inside(11, 14)
        for i in range(1, span):
            share(i).wait()
        ga, gb = jnp.zeros((1, dim), f32), jnp.zeros((1, dim), f32)
        for i in range(span - 1, 0, -1):
            on = pos + i < span
            slot = span - i - 1
            keep = jnp.exp(xr[slot, 2:3, :])
            ga = jnp.where(on, xr[slot, 0:1, :] + keep * ga, ga)
            gb = jnp.where(on, xr[slot, 1:2, :] + keep * gb, gb)
        ga, gb = chain(ga, gb, True)
        keep_lead(vec_a, top_a + seqs, ga)
        keep_lead(vec_a, top_a + 2 * seqs, gb)
        back_rows(kb, vb, yb, mb, ab, bb, t2, w_ref, u_ref, ta, tb, t3, t4, vec_a, dim, chunks)

    def round_grads():
        inside(4, 5, 2)
        for c in range(blocks):
            l1[:, lane(c)] = t3[c].astype(bf)
            l2[:, lane(c)] = t4[c].astype(bf)
            sig = jax.nn.sigmoid(r_ref[:, lane(c)])
            l3[:, lane(c)] = (t0[:, lane(c)] * yb[c] * sig * (1.0 - sig)).astype(bf)

    def mixed_in(mix):
        for c in range(blocks):
            l4[:, lane(c)] = (first[:, lane(c)].astype(f32) * mix[:, lane(c)]
                              + before[:, lane(c)].astype(f32) * (1.0 - mix[:, lane(c)])).astype(bf)

    def grad_of(mix, cols_ref, dst):
        def run():
            mixed_in(mix)
            weight_grad(cols_ref, l4, dst)
        return run

    def input_grad(whole, low, mix, row, initial):
        def run():
            fetch(whole).start()
            fetch(whole).wait()
            for e in range(nd):
                for n in range(part // wide):
                    at = e * part + n * wide
                    got = dot_nn(low[...], weights[e, :, n * wide:(n + 1) * wide])
                    for q in range(wide // LANES):
                        c = at // LANES + q
                        g = got[:, lane(q)]
                        diff = first[:, lane(c)].astype(f32) - before[:, lane(c)].astype(f32)
                        vec_b[row:row + 1, lane(c)] = jnp.sum(g * diff, axis=0, keepdims=True)
                        stay, back = g * mix[:, lane(c)], g * (1.0 - mix[:, lane(c)])
                        t3[c] = stay if initial else t3[c] + stay
                        t4[c] = back if initial else t4[c] + back
        return run

    def start_first():
        for c in range(blocks):
            hs_buf[1, :, lane(c)] = t4[c, 0:8, :]
        pass_first(1).start()
        keep_lead(vec_b, top_b, hs_buf[1, 0:1, :])

    def first_grad():
        pass_first(1).wait()

        @pl.loop(0, blocks)
        def _(c):
            cols = pl.ds(pl.multiple_of(c * LANES, LANES), LANES)
            t0[:, cols] = t3[c] + pulled(t4[c], 1, cols)
        norm_grad(x_ref, n1g, tok, tok, vec_b, 0, None)

    def out_grad():
        inside(6)
        weight_grad(gated, l0, go)

    first_of = [min(c for c in range(total) if chunks_of[c][0] == a) for a in range(7)]
    plan = [(send_partials, None), (block_result, None), (recept_grad, 2), (recept_input, None), (start_second, None), (second_grad, None),
            (norm_second_grad, None), (gated_grad, None), (carry_out, None), (out_grad, 3), (scan_back, None), (round_grads, None),
            (grad_of(mk, l1, gk), 4), (grad_of(mv, l2, gv), 5), (grad_of(mr, l3, gr), 6),
            (input_grad(wk, l1, mk, 2, True), None), (input_grad(wv, l2, mv, 3, False), None), (input_grad(wr, l3, mr, 4, False), None),
            (start_first, None), (first_grad, None)]
    pace = [2, 2, 3, 4, 4, 5, 6, 7, 7, 8, 9, 10, 12, 13, 14, 15, 17, 19, 20, 21]
    beside = {12: sums_a[0], 13: sums_a[1], 14: sums_a[2], 15: sums_a[3], 17: sums_a[4]}
    at, done = 0, set()

    def advance(goal):
        nonlocal at
        while at < goal:
            if at < total and chunks_of[at][0] >= 2:
                a = chunks_of[at][0]
                if a not in done:
                    return
                if at == first_of[a]:
                    settle(0)
                    settle(1)
            scatter_step(at)
            at += 1

    for i, ((piece, array), goal) in enumerate(zip(plan, pace)):
        advance(goal)
        piece()
        if i in beside:
            beside[i]()
        if array is not None:
            done.add(array)
    tail = 0
    while at < steps or tail < 10:
        if tail < 10 and tail % 2 == 0:
            sums_b[tail // 2]()
        tail += 1
        advance(min(steps, at + 1))
    settle(0)
    settle(1)
    for c in range(total):
        for i in range(1, nd):
            along_d(c, i).wait_send()
        first_pair(c).wait_send()
        if not half_of(c):
            second_pair(c).wait_send()
        for i in range(1, nz):
            along_z(c, i).wait_send()


def backward_block(nd, nt, head, wide_head, operands, seqs, rc, lag):
    nz = nt // 4
    span = nt // seqs
    rows, dim = operands[9].shape
    part = dim // nd
    chunks_of = []
    for a, cl in enumerate((wide_head, wide_head, head, head, head, head, head)):
        size = rc if a > 1 else 2 * rc
        chunks_of += [(a, at) for at in range(0, cl, size)]
    early = [c for c in chunks_of if c[0] < 2]
    middle = [c for c in chunks_of if c[0] in (2, 3)]
    late = [c for c in chunks_of if c[0] > 3]
    chunks_of, early = early[:-len(middle)], early[-len(middle):]
    for a, b in zip(middle, early):
        chunks_of += [a, b]
    chunks_of += late
    n = len(chunks_of)
    nf = sum(1 for c in chunks_of if c[0] < 2)
    na = n - nf
    chunks = rows // STEP
    dma = pltpu.SemaphoreType.DMA
    bf, f32 = jnp.bfloat16, jnp.float32

    def vv(*shape):
        return pltpu.VMEM(shape, f32)

    def lv(*shape):
        return pltpu.VMEM(shape, bf)

    def shard(*shape):
        return jax.ShapeDtypeStruct(shape, f32)

    square = jax.ShapeDtypeStruct((dim, dim), bf)
    vec_a, vec_b = (-(-(6 + 3 * seqs) // 8) * 8, dim), (-(-(5 + seqs) // 8) * 8, dim)
    blocks = dim // LANES
    held = operands[9:25]
    full = jax.ShapeDtypeStruct((rows, dim), f32)
    return pl.pallas_call(
        functools.partial(backward_body, nd, nz, seqs, chunks_of, nf, rc, part, lag),
        out_shape=(shard(head, part),) * 5 + (shard(part, wide_head),) * 2 + (full, full, jax.ShapeDtypeStruct(vec_a, f32), jax.ShapeDtypeStruct(vec_b, f32)) + (square,) * 5
        + (jax.ShapeDtypeStruct((nd - 1, nf, nz, 2, 2 * rc, part), bf), jax.ShapeDtypeStruct((nd - 1, na, nz, 2, 2, rc, part), bf)),
        in_specs=[HBM] * 25 + [VMEM] * 9,
        out_specs=[VMEM] * 11 + [HBM] * 7,
        scratch_shapes=[lv(nf, nz, 2, 2 * rc, part), lv(na, nz, 2, 2, rc, part), lv(2, nd - 1, nz, 2, 2, rc, part),
                        lv(nf, nz, 2 * rc, part), lv(na, nz, 2, rc, part), lv(na, nz, rc, part),
                        lv(nz - 1, nf, 2 * rc, part), lv(nz - 1, na, rc, part), lv(blocks, rows, LANES), lv(blocks, rows, LANES),
                        vv(rows, dim)] + [vv(blocks, rows, LANES)] * 3 + [lv(rows, dim)] * 5
        + [lv(nd, dim, part)] + [vv(chunks, dim)] * 5 + [vv(8, dim), vv(span - 1, 8, dim), vv(2, 8, dim), vv(2, 8, dim)]
        + [vv(1, dim), vv(*vec_a), vv(*vec_b)] + [[vv(nd, *s)] + [vv(*s)] * 5 + [vv(nz, *s)] for s in (vec_a, vec_b)] + [lv(2, dim // 2, dim)]
        + [pltpu.VMEM(o.shape, o.dtype) for o in held]
        + [dma((n,)), dma((nd - 1, n)), dma((nd - 1, n)), dma((2, nd - 1)), dma((n,)), dma((n,)), dma((n,)), dma((n,)),
           dma((nz - 1, n)), dma((nz - 1, n)), dma((2 * (nd + nz),)), dma((2 * (nd + nz),)), dma((2,)), dma((2,)),
           dma((span - 1,)), dma((span - 1,)), dma((3, blocks)), dma((3,)), dma((1,)), dma((1,)), dma((16,))],
        compiler_params=pltpu.CompilerParams(collective_id=1, has_side_effects=True, vmem_limit_bytes=60 * 2**20),
        name="backward_block",
    )(*operands)


def finish_body(nt, seqs, *refs):
    given, outs = refs[:13], refs[13:22]
    held, ls, ss = refs[38:51], refs[51], refs[52]
    vec_a, vec_b, num, den = held[9:]

    def enter(i):
        return pltpu.make_async_copy(given[i], held[i], ls.at[i])

    def leave(i):
        return pltpu.make_async_copy(held[i], outs[i], ss.at[i])

    for i in (9, 10, 11, 12, 7, 8, 5, 6, 0, 1, 2, 3, 4):
        enter(i).start()
    for i in range(13):
        enter(i).wait()
        if i < 9:
            leave(i).start()
    g_num, g_den, g_top, prev_t, prev_c = refs[22:27]
    lines = refs[27:38]
    for out, (vec, row) in zip(lines, ((vec_b, 0), (vec_b, 1), (vec_a, 0), (vec_a, 1), (vec_b, 2), (vec_b, 3), (vec_b, 4),
                                       (vec_a, 2), (vec_a, 3), (vec_a, 4), (vec_a, 5))):
        out[...] = vec[row, :]
    prev_c[...] = vec_a[6:6 + seqs, :]
    prev_t[...] = vec_b[5:5 + seqs, :]
    head = num.shape[1]
    per = LANES // head
    t = lax.axis_index("tensor")
    cols = pl.ds(pl.multiple_of((t // per) * LANES, LANES), LANES)

    def own_columns(at):
        block = vec_a[at:at + seqs, cols]
        got = block[:, :head]
        for q in range(1, per):
            got = jnp.where(lax.rem(t, per) == q, block[:, q * head:(q + 1) * head], got)
        return got

    a, b = own_columns(6 + seqs), own_columns(6 + 2 * seqs)
    g_num[...] = a
    g_den[...] = b
    g_top[...] = a * num[...] + b * den[...]
    for i in range(9):
        leave(i).wait()


def finish_block(nt, seqs, big, vec_a, vec_b, num, den):
    dim = vec_a.shape[1]

    def like(o):
        return jax.ShapeDtypeStruct(o.shape, o.dtype)

    pair = jax.ShapeDtypeStruct((seqs, dim), jnp.float32)
    return pl.pallas_call(
        functools.partial(finish_body, nt, seqs),
        out_shape=tuple(like(o) for o in big) + (like(num),) * 3 + (pair,) * 2 + (jax.ShapeDtypeStruct((dim,), jnp.float32),) * 11,
        in_specs=[HBM] * 13,
        out_specs=[HBM] * 9 + [VMEM] * 16,
        scratch_shapes=[pltpu.VMEM(o.shape, o.dtype) for o in (*big, vec_a, vec_b, num, den)]
        + [pltpu.SemaphoreType.DMA((13,)), pltpu.SemaphoreType.DMA((9,))],
        compiler_params=pltpu.CompilerParams(vmem_limit_bytes=60 * 2**20),
        name="finish_block",
    )(*big, vec_a, vec_b, num, den)


def local(nd, nt, x, num, den, top, prev_a, prev_f, n1g, n1b, fading, reward, mk, mv, mr, wk, wv, wr, wo, n2g, n2b, ck, cr,
          fk, fv, fr, up):
    rows, dim = x.shape
    seqs = prev_a.shape[0]
    head = num.shape[1]

    def line(v):
        return v.astype(jnp.float32).reshape(1, dim)

    given = [s.T for s in (wk, wv, wr, wo, fr)] + [fk, fv]
    vectors = [x, up] + [line(v) for v in (n1g, n1b, mk, mv, mr, fading, reward, n2g, n2b, ck, cr)]
    weights, saved = forward_block(nd, nt, given, [num, den, top, prev_a, prev_f], vectors, seqs, rows, (32, 32), (2, 4, 6))
    whole_k, whole_v, whole_r, whole_o, whole_fr, whole_fk, whole_fv = weights
    first, before, gated, chan_rec, chan_keys, g_values, gate, recept, middle, diff2, kb, vb, yb, mb, ab, bb = saved
    keys2, values2 = chan_keys.reshape(2 * rows, dim), g_values.reshape(2 * rows, dim)
    values, part_keys, grad_fk, grad_fv = channel_block(nd, nt, keys2, values2, whole_fk, whole_fv)

    operands = [grad_fk, grad_fv, whole_k, whole_v, whole_r, whole_o, whole_fr, part_keys, diff2,
                values, middle, x, up, first, before, gated, chan_rec, gate, recept, kb, vb, yb, mb, ab, bb]
    operands += [line(v) for v in (n1g, mk, mv, mr, fading, reward, n2g, ck, cr)]
    got = backward_block(nd, nt, head, fk.shape[1], operands, seqs, (5 * head + 2 * fk.shape[1]) // 26, 2)
    done = finish_block(nt, seqs, got[:9], got[9], got[10], num, den)
    out_k, out_v, out_r, out_o, out_fr = [o.T for o in done[:5]]
    out_fk, out_fv, result, tokens_grad = done[5:9]
    grad_num, grad_den, grad_top, prev_t, prev_c = done[9:14]
    vectors = done[14:]
    return (result, tokens_grad, grad_num, grad_den, grad_top, prev_t, prev_c,
            vectors[0], vectors[1], vectors[2], vectors[3], vectors[4], vectors[5], vectors[6],
            out_k, out_v, out_r, out_o, vectors[7], vectors[8], vectors[9], vectors[10], out_fk, out_fv, out_fr)


def solution(mesh):
    nd, nt = mesh.shape["dp"], mesh.shape["tensor"]
    rows, both, lead, one = P(("dp", "tensor"), None), P("dp", "tensor"), P("dp", None), P()
    return jax.shard_map(
        functools.partial(local, nd, nt),
        mesh=mesh,
        in_specs=(rows, both, both, both, lead, lead) + (one,) * 7 + (both,) * 4 + (one,) * 4 + (both,) * 3 + (rows,),
        out_specs=(rows, rows, both, both, both, lead, lead) + (one,) * 7 + (both,) * 4 + (one,) * 4 + (both,) * 3,
        check_vma=False,
    )
```

```python
import functools

import jax
import jax.numpy as jnp
from jax import lax
from jax.experimental import pallas as pl
from jax.experimental.pallas import tpu as pltpu
from jax.sharding import PartitionSpec as P

EPS = 1e-05
STEP = 16
NEG = -1e30


def dot_nt(x, y):
    return lax.dot_general(x, y, (((1,), (1,)), ((), ())), preferred_element_type=jnp.float32)


def dot_nn(x, y):
    return lax.dot_general(x, y, (((1,), (0,)), ((), ())), preferred_element_type=jnp.float32)


def dot_tn(x, y):
    return lax.dot_general(x, y, (((0,), (0,)), ((), ())), preferred_element_type=jnp.float32)


LANES = 128
VMEM = pl.BlockSpec(memory_space=pltpu.VMEM)


def scan_groups(width):
    blocks = width // LANES
    size = 4 if blocks % 4 == 0 else 1
    return [range(g, g + size) for g in range(0, blocks, size)]


def lane(c):
    return slice(c * LANES, (c + 1) * LANES)


MESH = pl.DeviceIdType.MESH
HBM = pl.BlockSpec(memory_space=pltpu.HBM)


def place(nd, nz):
    d = lax.axis_index("dp")
    t = lax.axis_index("tensor")
    return d, t // 4, lax.rem(t // 2, 2), lax.rem(t, 2)


def spot(d, z, y, x):
    return (d, z * 4 + y * 2 + x)


def partners(nd, nz, d, z, y, x):
    out = [spot(lax.rem(d + i, nd), z, y, x) for i in range(1, nd)]
    out += [spot(d, lax.rem(z + i, nz), y, x) for i in range(1, nz)]
    return out + [spot(d, z, 1 - y, x), spot(d, z, y, 1 - x)]


def meet(others):
    barrier = pltpu.get_barrier_semaphore()
    for other in others:
        pl.semaphore_signal(barrier, inc=1, device_id=other, device_id_type=MESH)
    pl.semaphore_wait(barrier, len(others))


def send(src, dst, send_sem, recv_sem, to):
    return pltpu.make_async_remote_copy(src_ref=src, dst_ref=dst, send_sem=send_sem, recv_sem=recv_sem, device_id=to, device_id_type=MESH)


def rowwise_norm(x):
    center = x - jnp.mean(x, axis=-1, keepdims=True)
    return center * lax.rsqrt(jnp.mean(center * center, axis=-1, keepdims=True) + EPS)


def scan_ends(kb, vb, w_ref, sm, sa, sb, width, chunks):
    for group in scan_groups(width):
        m = [jnp.full((chunks, LANES), NEG, jnp.float32) for _ in group]
        a = [jnp.zeros((chunks, LANES), jnp.float32) for _ in group]
        b = [jnp.zeros((chunks, LANES), jnp.float32) for _ in group]
        for j in range(STEP):
            at = pl.ds(j, chunks, stride=STEP)
            for i, c in enumerate(group):
                k = kb[c, at, :]
                mw = m[i] - w_ref[:, lane(c)]
                m[i] = jnp.maximum(mw, k)
                keep = jnp.exp(mw - m[i])
                take = jnp.exp(k - m[i])
                a[i] = keep * a[i] + take * vb[c, at, :]
                b[i] = keep * b[i] + take
        for i, c in enumerate(group):
            sm[:, lane(c)] = m[i]
            sa[:, lane(c)] = a[i]
            sb[:, lane(c)] = b[i]


def join(m, a, b, decay, me, ae, be):
    mw = m - decay
    mn = jnp.maximum(mw, me)
    keep = jnp.exp(mw - mn)
    take = jnp.exp(me - mn)
    return mn, keep * a + take * ae, keep * b + take * be


def scan_rows(kb, vb, yb, mb, ab, bb, w_ref, u_ref, sm, sa, sb, width, chunks):
    for group in scan_groups(width):
        m = [sm[:, lane(c)] for c in group]
        a = [sa[:, lane(c)] for c in group]
        b = [sb[:, lane(c)] for c in group]
        for j in range(STEP):
            at = pl.ds(j, chunks, stride=STEP)
            for i, c in enumerate(group):
                k = kb[c, at, :]
                v = vb[c, at, :]
                mb[c, at, :] = m[i]
                ab[c, at, :] = a[i]
                bb[c, at, :] = b[i]
                uk = u_ref[:, lane(c)] + k
                p = jnp.maximum(m[i], uk)
                alpha = jnp.exp(m[i] - p)
                beta = jnp.exp(uk - p)
                yb[c, at, :] = (alpha * a[i] + beta * v) / (alpha * b[i] + beta)
                m[i], a[i], b[i] = step_state(m[i], a[i], b[i], w_ref[:, lane(c)], k, v)


def step_state(m, a, b, w, k, v):
    mw = m - w
    mn = jnp.maximum(mw, k)
    keep = jnp.exp(mw - mn)
    take = jnp.exp(k - mn)
    return mn, keep * a + take * v, keep * b + take


def forward_body(nd, nz, seqs, pieces, lag, count, *refs):
    given, refs = refs[:count], refs[count:]
    num, den, top_, prevs_a, prevs_f = refs[:5]
    refs = refs[5:]
    x_ref, up, n1g, n1b, mk, mv, mr, fading, u_ref, n2g, n2b, ck, cr = refs[:13]
    count += 1
    outs, refs = refs[13:13 + count], refs[13 + count:]
    homes = refs[:16]
    (key_in, value_in, recept_in, wbuf, sbuf, init, sm, sa, sb, halo, xs, xr, second,
     first, before, gated, chan_rec, chan_keys, g_values, gate, r_ref, middle, diff2, kb, vb, yb, mb, ab, bb,
     states, raw_k, raw_v, turned_k, turned_v, w_ref, prev_a, prev_f,
     loc, zs, zr, as_, ar, bs, br, ds, dr, hs, hr, es, er, ws, ps, pr, os) = refs[16:]
    ins = (states,) + tuple(given[:5]) + (turned_k, turned_v)
    made = (first, before, gated, chan_rec, chan_keys, g_values, gate, r_ref, middle, diff2, kb, vb, yb, mb, ab, bb)
    d, z, y, x = place(nd, nz)
    rows, dim = x_ref.shape
    part = dim // nd
    chunks = rows // STEP
    nt = 4 * nz
    span = nt // seqs
    t = lax.axis_index("tensor")
    seq = t // span
    pos = lax.rem(t, span)
    f32 = jnp.float32

    def mate(i):
        return (d, seq * span + lax.rem(pos + i, span))

    meet(partners(nd, nz, d, z, y, x) + [mate(i) for i in range(1, span)])

    def cell(a, source_d, source_z, source_y, source_x, at, n):
        if half_of(a):
            return outs[a].at[source_d, source_z, source_y, at:at + n]
        return outs[a].at[source_d, source_z, source_y, source_x, at:at + n]

    def half_of(a):
        return a >= 6

    def by_y_first(p):
        a = pieces[p][0]
        return a in (0, 4, 5) or half_of(a) or p % 2 == 0

    def leave(i):
        home = homes[i].at[x] if i in (4, 5) else homes[i]
        return pltpu.make_async_copy(made[i], home, os.at[i])

    def bring_raw(i):
        return pltpu.make_async_copy(given[5 + i], (raw_k, raw_v)[i], ws.at[3 + i])

    bring_raw(0).start()
    bring_raw(1).start()
    w_ref[...] = jnp.exp(fading[...])
    for src, dst in ((prevs_a, prev_a), (prevs_f, prev_f)):
        got = src[0:1, :].astype(f32)
        for s in range(1, seqs):
            got = jnp.where(seq == s, src[s:s + 1, :].astype(f32), got)
        dst[...] = got
    states[...] = jnp.zeros(states.shape, f32)
    for s in range(seqs):
        for j, src in enumerate((num, den, top_)):
            states[3 * s + j:3 * s + j + 1, :src.shape[1]] = src[s:s + 1, :]

    def turn(i):
        bring_raw(i).wait()
        (turned_k, turned_v)[i][...] = (raw_k, raw_v)[i][...].T

    def own(p):
        a, at, n = pieces[p]
        return pltpu.make_async_copy(ins[a].at[at:at + n], cell(a, d, z, y, x, at, n), loc.at[p])

    def along_z(p, i, source):
        a, at, n = pieces[p]
        return send(ins[a].at[at:at + n], cell(a, d, source, y, x, at, n), zs.at[p, i - 1], zr.at[p, i - 1],
                    spot(d, lax.rem(z + i, nz), y, x))

    every = slice(None)

    def first_pair(p, mine):
        a, at, n = pieces[p]
        if by_y_first(p):
            block = cell(a, d, every, y if mine else 1 - y, x, at, n)
            to = spot(d, z, 1 - y, x)
        else:
            block = cell(a, d, every, y, x if mine else 1 - x, at, n)
            to = spot(d, z, y, 1 - x)
        return send(block, block, as_.at[p], ar.at[p], to)

    def second_pair(p, mine):
        a, at, n = pieces[p]
        if by_y_first(p):
            block = cell(a, d, every, every, x if mine else 1 - x, at, n)
            to = spot(d, z, y, 1 - x)
        else:
            block = cell(a, d, every, y if mine else 1 - y, every, at, n)
            to = spot(d, z, 1 - y, x)
        return send(block, block, bs.at[p], br.at[p], to)

    def along_d(p, i, source):
        a, at, n = pieces[p]
        block = cell(a, source, every, every, every, at, n)
        return send(block, block, ds.at[p, i - 1], dr.at[p, i - 1], spot(lax.rem(d + i, nd), z, y, x))

    total = len(pieces)
    arrived = set()

    def gather_step(step):
        p = step
        if p < total:
            own(p).start()
            for i in range(1, nz):
                along_z(p, i, z).start()
        p = step - lag[0]
        if 0 <= p < total:
            own(p).wait()
            for i in range(1, nz):
                along_z(p, i, lax.rem(z - i + nz, nz)).wait_recv()
            first_pair(p, True).start()
        p = step - lag[1]
        if 0 <= p < total:
            first_pair(p, False).wait_recv()
            if half_of(pieces[p][0]):
                for i in range(1, nd):
                    along_d(p, i, d).start()
            else:
                second_pair(p, True).start()
        p = step - lag[2]
        if 0 <= p < total and not half_of(pieces[p][0]):
            second_pair(p, False).wait_recv()
            for i in range(1, nd):
                along_d(p, i, d).start()

    def have(array):
        for p in range(total):
            if pieces[p][0] == array and p not in arrived:
                arrived.add(p)
                for i in range(1, nd):
                    along_d(p, i, lax.rem(d - i + nd, nd)).wait_recv()

    def fetch(array, slot):
        return pltpu.make_async_copy(outs[array], wbuf.at[slot], ws.at[slot])

    def norm_first():
        @pl.loop(0, rows // 32)
        def _(i):
            at = pl.ds(pl.multiple_of(i * 32, 32), 32)
            first[at, :] = (rowwise_norm(x_ref[at, :]) * n1g[...] + n1b[...]).astype(jnp.bfloat16)
        pass_last(first, 0, 1).start()

    def pass_last(rows_ref, slot, to):
        return send(rows_ref.at[rows - 16:rows], halo.at[slot], hs.at[slot], hr.at[slot], mate(to))

    def shifted(rows_ref, slot, prev, cols):
        now = rows_ref[:, cols].astype(f32)
        edge = jnp.where(pos == 0, prev[:, cols], halo[slot, :, cols].astype(f32)[15:16, :])
        top = lax.broadcasted_iota(jnp.int32, now.shape, 0) == 0
        return now, jnp.where(top, edge, pltpu.roll(now, 1, 0))

    def mix_first():
        pass_last(first, 0, 1).wait()

        @pl.loop(0, dim // LANES)
        def _(c):
            cols = pl.ds(pl.multiple_of(c * LANES, LANES), LANES)
            now, old = shifted(first, 0, prev_a, cols)
            before[:, cols] = old.astype(jnp.bfloat16)
            for mix, dst in ((mk, key_in), (mv, value_in), (mr, recept_in)):
                dst[:, cols] = (now * mix[:, cols] + old * (1.0 - mix[:, cols])).astype(jnp.bfloat16)
        leave(0).start()
        leave(1).start()

    def project(array, slot, left, store):
        def run():
            fetch(array, slot).wait()
            wide = min(256, dim)
            weights = wbuf.at[slot].reshape(nd, dim, part)
            for n in range(dim // wide):
                acc = dot_nt(left[:, :part], weights[0, n * wide:(n + 1) * wide])
                for e in range(1, nd):
                    acc = acc + dot_nt(left[:, e * part:(e + 1) * part], weights[e, n * wide:(n + 1) * wide])
                store(n, wide, acc)
        return run

    def into_blocks(dst):
        def store(n, wide, acc):
            for q in range(wide // LANES):
                dst[n * (wide // LANES) + q] = acc[:, lane(q)]
        return store

    def into_rows(n, wide, acc):
        r_ref[:, n * wide:(n + 1) * wide] = acc

    def get_kv():
        have(1)
        fetch(1, 0).start()
        have(2)
        fetch(2, 1).start()

    def get_r():
        have(3)
        fetch(3, 0).start()
        have(0)
        copy = pltpu.make_async_copy(outs[0].at[d], sbuf, ws.at[2])
        copy.start()
        copy.wait()
        head = dim // nt
        per = LANES // head
        for c in range(dim // LANES):
            cells = []
            for q in range(per):
                b = c * per + q
                cells.append(sbuf[b // 4, (b // 2) % 2, b % 2][:, :head])
            init[:, lane(c)] = jnp.concatenate(cells, axis=1)

    def get_o():
        have(4)
        fetch(4, 1).start()

    def initial(j):
        got = init[j:j + 1, :]
        for s in range(1, seqs):
            got = jnp.where(seq == s, init[3 * s + j:3 * s + j + 1, :], got)
        return got

    def share(i):
        return send(xs, xr.at[i - 1], es.at[i - 1], er.at[i - 1], mate(i))

    def summarize():
        scan_ends(kb, vb, w_ref, sm, sa, sb, dim, chunks)
        lead = pos == 0
        m = jnp.where(lead, initial(2), NEG)
        a = jnp.where(lead, initial(0), 0.0)
        b = jnp.where(lead, initial(1), 0.0)
        decay = float(STEP) * w_ref[...]
        for s in range(chunks):
            m, a, b = join(m, a, b, decay, sm[s:s + 1, :], sa[s:s + 1, :], sb[s:s + 1, :])
        xs[0:1, :] = a
        xs[1:2, :] = b
        xs[2:3, :] = m
        xs[3:8, :] = jnp.zeros((5, dim), f32)
        for i in range(1, span):
            share(i).start()

    def carry_in():
        for i in range(1, span):
            share(i).wait()
        m = jnp.where(pos == 0, initial(2), NEG)
        a = jnp.where(pos == 0, initial(0), 0.0)
        b = jnp.where(pos == 0, initial(1), 0.0)
        decay = float(rows) * w_ref[...]
        for i in range(span - 1, 0, -1):
            on = i <= pos
            mn, an, bn = join(m, a, b, decay, xr[i - 1, 2:3, :], xr[i - 1, 0:1, :], xr[i - 1, 1:2, :])
            m, a, b = jnp.where(on, mn, m), jnp.where(on, an, a), jnp.where(on, bn, b)
        decay = float(STEP) * w_ref[...]
        for s in range(chunks):
            me, ae, be = sm[s:s + 1, :], sa[s:s + 1, :], sb[s:s + 1, :]
            sm[s:s + 1, :] = m
            sa[s:s + 1, :] = a
            sb[s:s + 1, :] = b
            m, a, b = join(m, a, b, decay, me, ae, be)

    def scan():
        scan_rows(kb, vb, yb, mb, ab, bb, w_ref, u_ref, sm, sa, sb, dim, chunks)
        for c in range(dim // LANES):
            gated[:, lane(c)] = (jax.nn.sigmoid(r_ref[:, lane(c)]) * yb[c]).astype(jnp.bfloat16)
        for i in (2, 7, 10, 11, 12, 13, 14, 15):
            leave(i).start()

    def attend_out():
        fetch(4, 1).wait()
        weights = wbuf.at[1].reshape(nd, dim, part)
        wide = min(256, part)
        for e in range(nd):
            for n in range(part // wide):
                at = slice(e * part + n * wide, e * part + (n + 1) * wide)
                middle[:, at] = x_ref[:, at] + dot_nn(gated[...], weights[e, :, n * wide:(n + 1) * wide])
        leave(8).start()

    def norm_second():
        @pl.loop(0, rows // 32)
        def _(i):
            at = pl.ds(pl.multiple_of(i * 32, 32), 32)
            second[at, :] = (rowwise_norm(middle[at, :]) * n2g[...] + n2b[...]).astype(jnp.bfloat16)
        pass_last(second, 1, 1).start()

    def mix_second():
        pass_last(second, 1, 1).wait()

        @pl.loop(0, dim // LANES)
        def _(c):
            cols = pl.ds(pl.multiple_of(c * LANES, LANES), LANES)
            now, old = shifted(second, 1, prev_f, cols)
            diff2[:, cols] = now - old
            chan_keys[:, cols] = (now * ck[:, cols] + old * (1.0 - ck[:, cols])).astype(jnp.bfloat16)
            chan_rec[:, cols] = (now * cr[:, cols] + old * (1.0 - cr[:, cols])).astype(jnp.bfloat16)
        pair_up(0, x).start()
        for i in (3, 4, 9):
            leave(i).start()

    def pair_up(slot, source):
        return send(made[4 + slot], homes[4 + slot].at[source], ps.at[slot], pr.at[slot], spot(d, z, y, 1 - x))

    def get_fr():
        have(5)
        fetch(5, 0).start()

    def gate_rows(n, wide, acc):
        at = slice(n * wide, (n + 1) * wide)
        got = jax.nn.sigmoid(acc)
        gate[:, at] = got
        g_values[:, at] = (up[:, at] * got).astype(jnp.bfloat16)

    def values_grad():
        project(5, 0, chan_rec, gate_rows)()
        pair_up(1, x).start()
        for i in (5, 6):
            leave(i).start()

    steps = total + lag[2]
    gather_step(0)
    gather_step(1)
    norm_first()
    gather_step(2)
    turn(0)
    turn(1)
    mix_first()
    def due(array):
        return 1 + max(p for p in range(total) if pieces[p][0] == array) + lag[2]

    ready = max(due(1), due(2))
    for s in range(3, ready):
        gather_step(s)
    work = [get_kv, project(1, 0, key_in, into_blocks(kb)), project(2, 1, value_in, into_blocks(vb)), get_r, get_o, summarize,
            project(3, 0, recept_in, into_rows), carry_in, scan, get_fr, attend_out, norm_second, mix_second, values_grad]
    last = {3: max(due(3), due(0)), 4: due(4), 9: due(5)}
    at = ready
    for i, piece in enumerate(work):
        while at < min(steps, max(last.get(i, 0), ready + i)):
            gather_step(at)
            at += 1
        piece()
    while at < steps:
        gather_step(at)
        at += 1
    for a in range(count):
        have(a)
    for p in range(total):
        for i in range(1, nz):
            along_z(p, i, z).wait_send()
        first_pair(p, True).wait_send()
        if not half_of(pieces[p][0]):
            second_pair(p, True).wait_send()
        for i in range(1, nd):
            along_d(p, i, d).wait_send()
    for slot in range(2):
        pair_up(slot, x).wait_send()
        pair_up(slot, 1 - x).wait_recv()
    for i in range(16):
        leave(i).wait()


def forward_block(nd, nt, given, small, vectors, seqs, rows, unit, lag, mixing=1):
    nz = nt // 4
    span = nt // seqs
    dim = given[0].shape[0] * nt
    part = dim // nd
    bf16 = jnp.bfloat16
    shards = [jax.ShapeDtypeStruct((-(-3 * seqs // 8) * 8, LANES), jnp.float32)] + list(given[:5])
    shards += [jax.ShapeDtypeStruct((g.shape[1], g.shape[0]), bf16) for g in given[5:]]
    pieces = []
    for a, s in enumerate(shards):
        size = min(unit[a >= 6], s.shape[0])
        pieces += [(a, at, size) for at in range(0, s.shape[0], size)]
    early = [p for p in pieces if p[0] in (1, 2)] + [p for p in pieces if p[0] in (3, 0)]
    later = [p for p in pieces if p[0] in (4, 5)]
    halves = [p for a, b in zip([p for p in pieces if p[0] == 6], [p for p in pieces if p[0] == 7]) for p in (a, b)]
    pieces = early
    while later or halves:
        pieces, later, halves = pieces + later[:1] + halves[:mixing], later[1:], halves[mixing:]
    n = len(pieces)
    dma = pltpu.SemaphoreType.DMA
    bf, f32 = jnp.bfloat16, jnp.float32
    low = jax.ShapeDtypeStruct((rows, dim), bf)
    full = jax.ShapeDtypeStruct((rows, dim), f32)
    twice = jax.ShapeDtypeStruct((2, rows, dim), bf)
    block = jax.ShapeDtypeStruct((dim // LANES, rows, LANES), f32)
    chunks = rows // STEP
    per = shards[1].shape[0]
    got = pl.pallas_call(
        functools.partial(forward_body, nd, nz, seqs, pieces, lag, len(given)),
        out_shape=tuple(jax.ShapeDtypeStruct(((nd, nz, 2, 2) if a < 6 else (nd, nz, 2)) + s.shape, s.dtype) for a, s in enumerate(shards))
        + (low,) * 4 + (twice,) * 2 + (full,) * 4 + (block,) * 6,
        in_specs=[HBM] * len(given) + [VMEM] * (5 + len(vectors)),
        out_specs=[HBM] * len(shards) + [HBM] * 16,
        scratch_shapes=[pltpu.VMEM((rows, dim), bf)] * 3
        + [pltpu.VMEM((2, nd, nz, 2, 2, per, part), bf), pltpu.VMEM((nz, 2, 2) + shards[0].shape, f32), pltpu.VMEM((shards[0].shape[0], dim), f32)]
        + [pltpu.VMEM((chunks, dim), f32)] * 3
        + [pltpu.VMEM((2, 16, dim), bf), pltpu.VMEM((8, dim), f32), pltpu.VMEM((span - 1, 8, dim), f32), pltpu.VMEM((rows, dim), bf)]
        + [pltpu.VMEM((rows, dim), bf)] * 6 + [pltpu.VMEM((rows, dim), f32)] * 4 + [pltpu.VMEM(block.shape, f32)] * 6
        + [pltpu.VMEM(shards[0].shape, f32)] + [pltpu.VMEM(g.shape, bf) for g in given[5:]] + [pltpu.VMEM(s.shape, bf) for s in shards[6:]]
        + [pltpu.VMEM((1, dim), f32)] * 3
        + [dma((n,)), dma((n, nz - 1)), dma((n, nz - 1)), dma((n,)), dma((n,)), dma((n,)), dma((n,)),
           dma((n, nd - 1)), dma((n, nd - 1)), dma((2,)), dma((2,)), dma((span - 1,)), dma((span - 1,)), dma((5,)), dma((2,)), dma((2,)), dma((16,))],
        compiler_params=pltpu.CompilerParams(collective_id=0, has_side_effects=True, vmem_limit_bytes=60 * 2**20),
        name="forward_block",
    )(*given, *small, *vectors)
    weights = [o.reshape(nd, -1, s.shape[1]) for o, s in zip(got[1:len(shards)], shards[1:])]
    return weights, got[len(shards):]


def channel_body(nd, nz, keys_in, grads_in, fk_in, fv_in, values, part_keys, gfk, gfv,
                 fk, fv, squared, hidden_grad, stage, pout, pin, ls, gs, ps, pr):
    d, z, y, x = place(nd, nz)
    part, width = fk.shape[2], fk.shape[1]
    rows2, dim = keys_in.shape
    rows = rows2 // 2
    f32, bf = jnp.float32, jnp.bfloat16
    count = ls.shape[1]
    size = width // count
    wide = min(256, size)

    def bring(i, b):
        src, dst = ((fk_in, fk), (fv_in, fv))[i]
        return pltpu.make_async_copy(src.at[:, b * size:(b + 1) * size], dst.at[:, b * size:(b + 1) * size], ls.at[i, b])

    for b in range(count):
        bring(0, b).start()
        bring(1, b).start()
    meet([spot(d, z, y, 1 - x)])
    for b in range(count):
        bring(0, b).wait()
        bring(1, b).wait()
        for n in range(size // wide):
            at = slice(b * size + n * wide, b * size + (n + 1) * wide)
            hid = dot_nt(keys_in[:, :part], fk[0, at])
            back = dot_nt(grads_in[:, :part], fv[0, at])
            for e in range(1, nd):
                hid = hid + dot_nt(keys_in[:, e * part:(e + 1) * part], fk[e, at])
                back = back + dot_nt(grads_in[:, e * part:(e + 1) * part], fv[e, at])
            hid = jnp.maximum(hid, 0.0)
            squared[:, at] = (hid * hid).astype(bf)
            hidden_grad[:, at] = (back * 2.0 * hid).astype(bf)
    mine = pl.ds(pl.multiple_of(x * rows, rows), rows)
    theirs = pl.ds(pl.multiple_of((1 - x) * rows, rows), rows)
    step = min(256, part)

    def product(left, at_rows, whole, store):
        for e in range(nd):
            for n in range(part // step):
                store(slice(e * part + n * step, e * part + (n + 1) * step),
                      dot_nn(left[at_rows, :], whole[e, :, n * step:(n + 1) * step]))

    def put_out(at, got):
        pout[:, at] = got.astype(bf)

    def put_values(at, got):
        values[:, at] = got

    def put_theirs(at, got):
        part_keys[1 - x, :, at] = got

    def put_mine(at, got):
        part_keys[x, :, at] = got

    product(squared, theirs, fv, put_out)
    swap = send(pout, pin, ps.at[0], pr.at[0], spot(d, z, y, 1 - x))
    swap.start()
    product(squared, mine, fv, put_values)
    product(hidden_grad, theirs, fk, put_theirs)
    product(hidden_grad, mine, fk, put_mine)
    broad = min(512, dim)
    busy = [None, None]
    turn = 0
    for left, right, dst in ((squared, grads_in, gfv), (hidden_grad, keys_in, gfk)):
        for b in range(count):
            if busy[turn] is not None:
                busy[turn].wait()
            for n in range(size // wide):
                at = slice(b * size + n * wide, b * size + (n + 1) * wide)
                for m in range(dim // broad):
                    stage[turn, n * wide:(n + 1) * wide, m * broad:(m + 1) * broad] = dot_tn(
                        left[:, at], right[:, m * broad:(m + 1) * broad]).astype(bf)
            busy[turn] = pltpu.make_async_copy(stage.at[turn], dst.at[b * size:(b + 1) * size], gs.at[turn])
            busy[turn].start()
            turn = 1 - turn
    swap.wait()
    for c in range(dim // LANES):
        values[:, lane(c)] = values[:, lane(c)] + pin[:, lane(c)].astype(f32)
    for copy in busy:
        copy.wait()


def channel_block(nd, nt, keys, grads, fk, fv):
    rows2, dim = keys.shape
    rows = rows2 // 2
    width, part = fk.shape[1], fk.shape[2]
    bf, f32 = jnp.bfloat16, jnp.float32
    count = 4
    dma = pltpu.SemaphoreType.DMA
    square = jax.ShapeDtypeStruct((width, dim), bf)
    return pl.pallas_call(
        functools.partial(channel_body, nd, nt // 4),
        out_shape=(jax.ShapeDtypeStruct((rows, dim), f32), jax.ShapeDtypeStruct((2, rows, dim), f32), square, square),
        in_specs=[VMEM, VMEM, HBM, HBM],
        out_specs=[VMEM, VMEM, HBM, HBM],
        scratch_shapes=[pltpu.VMEM((nd, width, part), bf), pltpu.VMEM((nd, width, part), bf), pltpu.VMEM((rows2, width), bf),
                        pltpu.VMEM((rows2, width), bf), pltpu.VMEM((2, width // count, dim), bf), pltpu.VMEM((rows, dim), bf),
                        pltpu.VMEM((rows, dim), bf), dma((2, count)), dma((2,)), dma((1,)), dma((1,))],
        compiler_params=pltpu.CompilerParams(collective_id=2, has_side_effects=True, vmem_limit_bytes=60 * 2**20),
        name="channel_block",
    )(keys, grads, fk, fv)


def carry_rows(r_ref, gg, kb, yb, mb, bb, w_ref, u_ref, gyb, ca, cb, lc, width, chunks):
    for c in range(width // LANES):
        gyb[c] = gg[:, lane(c)] * jax.nn.sigmoid(r_ref[:, lane(c)])
    for group in scan_groups(width):
        ga = [jnp.zeros((chunks, LANES), jnp.float32) for _ in group]
        gb = [jnp.zeros((chunks, LANES), jnp.float32) for _ in group]
        end = [None for _ in group]
        for j in reversed(range(STEP)):
            at = pl.ds(j, chunks, stride=STEP)
            for i, c in enumerate(group):
                w = w_ref[:, lane(c)]
                k = kb[c, at, :]
                m = mb[c, at, :]
                uk = u_ref[:, lane(c)] + k
                p = jnp.maximum(m, uk)
                alpha = jnp.exp(m - p)
                gn = gyb[c, at, :] / (alpha * bb[c, at, :] + jnp.exp(uk - p))
                gd = -gn * yb[c, at, :]
                mw = m - w
                mn = jnp.maximum(mw, k)
                if j == STEP - 1:
                    end[i] = mn
                keep = jnp.exp(mw - mn)
                ga[i] = alpha * gn + keep * ga[i]
                gb[i] = alpha * gd + keep * gb[i]
                if j == 0:
                    lc[:, lane(c)] = m - float(STEP) * w - end[i]
        for i, c in enumerate(group):
            ca[:, lane(c)] = ga[i]
            cb[:, lane(c)] = gb[i]


def back_rows(kb, vb, yb, mb, ab, bb, gyb, w_ref, u_ref, ta, tb, fk, fv, vec, width, chunks):
    for group in scan_groups(width):
        ga = [ta[:, lane(c)] for c in group]
        gb = [tb[:, lane(c)] for c in group]
        gu = [jnp.zeros((chunks, LANES), jnp.float32) for _ in group]
        gw = [jnp.zeros((chunks, LANES), jnp.float32) for _ in group]
        for j in reversed(range(STEP)):
            at = pl.ds(j, chunks, stride=STEP)
            for i, c in enumerate(group):
                k = kb[c, at, :]
                v = vb[c, at, :]
                m = mb[c, at, :]
                uk = u_ref[:, lane(c)] + k
                p = jnp.maximum(m, uk)
                alpha = jnp.exp(m - p)
                beta = jnp.exp(uk - p)
                b = bb[c, at, :]
                gn = gyb[c, at, :] / (alpha * b + beta)
                gd = -gn * yb[c, at, :]
                mw = m - w_ref[:, lane(c)]
                mn = jnp.maximum(mw, k)
                keep = jnp.exp(mw - mn)
                take = jnp.exp(k - mn)
                now = beta * (gn * v + gd)
                fv[c, at, :] = beta * gn + take * ga[i]
                fk[c, at, :] = now + take * (ga[i] * v + gb[i])
                gu[i] = gu[i] + now
                gw[i] = gw[i] + keep * (ga[i] * ab[c, at, :] + gb[i] * b)
                ga[i] = alpha * gn + keep * ga[i]
                gb[i] = alpha * gd + keep * gb[i]
        for i, c in enumerate(group):
            vec[0:1, lane(c)] = -jnp.sum(gw[i], axis=0, keepdims=True) * w_ref[:, lane(c)]
            vec[1:2, lane(c)] = jnp.sum(gu[i], axis=0, keepdims=True)


def backward_body(nd, nz, seqs, chunks_of, nf, rc, part, lag, *refs):
    gfk, gfv, wk, wv, wr, wo, wfr, keys_in, diff_in = refs[:9]
    homes = refs[9:25]
    n1g, mk, mv, mr, fading, u_ref, n2g, ck, cr = refs[25:34]
    (outk, outv, outr, outo, outfr, outfk, outfv, result, tok, vout_a, vout_b, gfr, go, gk, gv, gr, landf, landa) = refs[34:52]
    (ownf, owna, slots, raf, raa, rba, rzf, rza, pout, pin, t0, t2, t3, t4, l0, l1, l2, l3, l4, wbuf, ca, cb, lc, ta, tb, xs, xr, hs_buf, hr_buf,
     w_ref, vec_a, vec_b, got_a, got_b, gstage, *more) = refs[52:]
    values_ref, middle, x_ref, up, first, before, gated, chan_rec, gate, r_ref, kb, vb, yb, mb, ab, bb = held = more[:16]
    loc, ds, dr, cs, as_, ar, bs, br, zs, zr, vs, vr, hs, hr, es, er, ws, gs, ps, pr, os = more[16:]
    grads = [gfv, gfk, gfr, go, gk, gv, gr]
    outs = [outfv, outfk, outfr, outo, outk, outv, outr]
    d, z, y, x = place(nd, nz)
    rows, dim = x_ref.shape
    chunks = rows // STEP
    nt = 4 * nz
    span = nt // seqs
    t = lax.axis_index("tensor")
    seq = t // span
    pos = lax.rem(t, span)
    f32, bf = jnp.float32, jnp.bfloat16
    total = len(chunks_of)
    top_a, top_b = 6, 5

    def mate(i):
        return (d, seq * span + lax.rem(pos + i, span))

    def load_block(src, dst, c, sem):
        return pltpu.make_async_copy(src.at[:, c * LANES:(c + 1) * LANES], dst.at[c], sem.at[c])

    blocks = dim // LANES

    def load_all(src, dst, i):
        for c in range(blocks):
            load_block(src, dst, c, ws.at[i]).start()

    def wait_all(src, dst, i):
        for c in range(blocks):
            load_block(src, dst, c, ws.at[i]).wait()

    def enter(i):
        return pltpu.make_async_copy(homes[i], held[i], os.at[i])

    def inside(*which):
        for i in which:
            enter(i).wait()

    load_all(keys_in.at[1 - x], t4, 1)
    for i in (0, 8, 1, 3, 7, 9, 10, 12, 13, 15, 6, 11, 14, 4, 5, 2):
        enter(i).start()
    meet(partners(nd, nz, d, z, y, x) + [mate(i) for i in range(1, span)])

    def half_of(c):
        return chunks_of[c][0] < 2

    rank = [sum(1 for e in range(c) if half_of(e) == half_of(c)) for c in range(total)]

    def mine_of(c):
        return ownf.at[rank[c]] if half_of(c) else owna.at[rank[c]]

    def slab(c, source):
        a, at = chunks_of[c]
        lanes = pl.ds(pl.multiple_of(source * part, part), part)
        if half_of(c):
            g = grads[a].reshape(nz, 2, grads[a].shape[0] // (2 * nz), dim)
            return g.at[:, :, at:at + 2 * rc, lanes]
        g = grads[a].reshape(nz, 2, 2, grads[a].shape[0] // nt, dim)
        return g.at[:, :, :, at:at + rc, lanes]

    def load(c):
        return pltpu.make_async_copy(slab(c, d), mine_of(c), loc.at[c])

    def landing(c, i):
        return (landf if half_of(c) else landa).at[i - 1, rank[c]]

    def slot_of(c, i):
        full = slots.at[c % 2, i - 1]
        return full.reshape(nz, 2, 2 * rc, part) if half_of(c) else full

    def along_d(c, i):
        to = lax.rem(d + i, nd)
        return send(slab(c, to), landing(c, i), ds.at[i - 1, c], dr.at[i - 1, c], spot(to, z, y, x))

    def bring(c, i):
        return pltpu.make_async_copy(landing(c, i), slot_of(c, i), cs.at[c % 2, i - 1])

    def by_x_first(c):
        return not half_of(c) and (chunks_of[c][0] < 4 or rank[c] % 2 == 0)

    def got_first(c):
        return (raf if half_of(c) else raa).at[rank[c]]

    def first_pair(c):
        own = mine_of(c)
        if half_of(c):
            return send(own.at[:, 1 - y], got_first(c), as_.at[c], ar.at[c], spot(d, z, 1 - y, x))
        if by_x_first(c):
            return send(own.at[:, :, 1 - x], got_first(c), as_.at[c], ar.at[c], spot(d, z, y, 1 - x))
        return send(own.at[:, 1 - y], got_first(c), as_.at[c], ar.at[c], spot(d, z, 1 - y, x))

    def second_pair(c):
        own, dst = mine_of(c), rba.at[rank[c]]
        if by_x_first(c):
            return send(own.at[:, 1 - y, x], dst, bs.at[c], br.at[c], spot(d, z, 1 - y, x))
        return send(own.at[:, y, 1 - x], dst, bs.at[c], br.at[c], spot(d, z, y, 1 - x))

    def got_z(c, i):
        return (rzf if half_of(c) else rza).at[i - 1, rank[c]]

    def along_z(c, i):
        own = mine_of(c)
        to = lax.rem(z + i, nz)
        return send(own.at[to, y] if half_of(c) else own.at[to, y, x], got_z(c, i), zs.at[i - 1, c], zr.at[i - 1, c], spot(d, to, y, x))

    def add_into(dst, at, *terms):
        if len(terms) == 1:
            dst[at] = dst[at] + terms[0][0][terms[0][1]]
            return
        acc = dst[at].astype(f32)
        for src, place_at in terms:
            acc = acc + src[place_at].astype(f32)
        dst[at] = acc.astype(bf)

    def scatter_step(step):
        c = step
        if c < total:
            load(c).start()
            for i in range(1, nd):
                along_d(c, i).start()
        c = step - 2
        if 0 <= c < total:
            for i in range(1, nd):
                along_d(c, i).wait_recv()
                bring(c, i).start()
        c = step - 3
        if 0 <= c < total:
            load(c).wait()
            for i in range(1, nd):
                bring(c, i).wait()
            own = mine_of(c)

            @pl.loop(0, nz)
            def _(b):
                for q in range(2 if half_of(c) else 4):
                    at = (b, q) if half_of(c) else (b, q // 2, q % 2)
                    add_into(own, at, *[(slot_of(c, i), at) for i in range(1, nd)])
            first_pair(c).start()
        c = step - 3 - lag
        if 0 <= c < total:
            first_pair(c).wait_recv()
            own, got = mine_of(c), got_first(c)

            @pl.loop(0, nz)
            def _(b):
                if half_of(c):
                    add_into(own, (b, y), (got, (b,)))
                else:
                    for q in range(2):
                        add_into(own, (b, q, x) if by_x_first(c) else (b, y, q), (got, (b, q)))
            if half_of(c):
                for i in range(1, nz):
                    along_z(c, i).start()
            else:
                second_pair(c).start()
        c = step - 3 - 2 * lag
        if 0 <= c < total:
            if half_of(c):
                finish(c)
            else:
                second_pair(c).wait_recv()
                own, got = mine_of(c), rba.at[rank[c]]

                @pl.loop(0, nz)
                def _(b):
                    add_into(own, (b, y, x), (got, (b,)))
                for i in range(1, nz):
                    along_z(c, i).start()
        c = step - 3 - 3 * lag
        if 0 <= c < total and not half_of(c):
            finish(c)

    def finish(c):
        for i in range(1, nz):
            along_z(c, i).wait_recv()
        own = mine_of(c)
        acc = (own[z, y] if half_of(c) else own[z, y, x]).astype(f32)
        for i in range(1, nz):
            acc = acc + got_z(c, i)[...].astype(f32)
        a, at = chunks_of[c]
        if half_of(c):
            outs[a][:, at:at + acc.shape[0]] = acc.T
        else:
            outs[a][at:at + acc.shape[0], :] = acc

    steps = total + 3 + 3 * lag

    def vector_sums(vec, top, bufs, base, out):
        vd, v1, vx, v2, vy, v3, vz = bufs

        def link(i, src, dst, to):
            return send(src, dst, vs.at[base + i], vr.at[base + i], to)

        def vec_d(i):
            return link(i - 1, vec, vd.at[d], spot(lax.rem(d + i, nd), z, y, x))

        def vec_x():
            return link(nd - 1, v1, vx, spot(d, z, y, 1 - x))

        def vec_y():
            return link(nd, v2, vy, spot(d, z, 1 - y, x))

        def vec_z(i):
            return link(nd + i, v3, vz.at[z], spot(d, lax.rem(z + i, nz), y, x))

        def start():
            vd[d] = vec[...]
            for i in range(1, nd):
                vec_d(i).start()

        def over_x():
            for i in range(1, nd):
                vec_d(i).wait()
            acc = vd[0]
            for i in range(1, nd):
                acc = acc + vd[i]
            row = lax.broadcasted_iota(jnp.int32, acc.shape, 0)
            v1[...] = jnp.where(row < top, acc, vec[...])
            vec_x().start()

        def over_y():
            vec_x().wait()
            v2[...] = v1[...] + vx[...]
            vec_y().start()

        def over_z():
            vec_y().wait()
            v3[...] = v2[...] + vy[...]
            vz[z] = v3[...]
            for i in range(1, nz):
                vec_z(i).start()

        def finish_sum():
            for i in range(1, nz):
                vec_z(i).wait()
            acc = vz[0]
            for i in range(1, nz):
                acc = acc + vz[i]
            out[...] = acc

        return [start, over_x, over_y, over_z, finish_sum]

    sums_a = vector_sums(vec_a, top_a, got_a, 0, vout_a)
    sums_b = vector_sums(vec_b, top_b, got_b, nd + nz, vout_b)

    lead = pos == 0

    def keep_lead(vec, start, row):
        for s in range(seqs):
            at = start + s
            vec[at:at + 1, :] = jnp.where(jnp.logical_and(lead, seq == s), row, 0.0)

    def pass_first(slot):
        return send(hs_buf.at[slot], hr_buf.at[slot], hs.at[slot], hr.at[slot], mate(span - 1))

    def pulled(back, slot, cols):
        edge = jnp.where(pos == span - 1, 0.0, hr_buf[slot, 0:1, cols])
        last = lax.broadcasted_iota(jnp.int32, back.shape, 0) == rows - 1
        return jnp.where(last, edge, pltpu.roll(back, rows - 1, 0))

    def partial():
        return send(pout, pin, ps.at[0], pr.at[0], spot(d, z, y, 1 - x))

    def send_partials():
        wait_all(keys_in.at[1 - x], t4, 1)

        @pl.loop(0, blocks)
        def _(c):
            pout[c] = t4[c].astype(bf)
        partial().start()
        load_all(keys_in.at[x], t2, 1)
        load_all(diff_in, t4, 2)
        w_ref[...] = jnp.exp(fading[...])
        vec_a[...] = jnp.zeros(vec_a.shape, f32)
        vec_b[...] = jnp.zeros(vec_b.shape, f32)

    def block_result():
        fetch(wfr).start()
        inside(0, 8, 1, 3)

        @pl.loop(0, blocks)
        def _(c):
            cols = pl.ds(pl.multiple_of(c * LANES, LANES), LANES)
            values, open_ = values_ref[:, cols], gate[:, cols]
            result[:, cols] = middle[:, cols] + open_ * values
            l0[:, cols] = (up[:, cols] * values * open_ * (1.0 - open_)).astype(bf)

    def recept_grad():
        inside(7)
        weight_grad(l0, chan_rec, gfr)

    def recept_input():
        fetch(wfr).wait()
        for e in range(nd):
            for n in range(part // wide):
                got = dot_nn(l0[...], weights[e, :, n * wide:(n + 1) * wide])
                for q in range(wide // LANES):
                    t3[(e * part + n * wide) // LANES + q] = got[:, lane(q)]

    def start_second():
        wait_all(keys_in.at[x], t2, 1)
        wait_all(diff_in, t4, 2)
        partial().wait()
        for c in range(blocks):
            t2[c] = t2[c] + pin[c].astype(f32)
        for c in range(blocks):
            hs_buf[0, :, lane(c)] = t2[c, 0:8, :] * (1.0 - ck[:, lane(c)]) + t3[c, 0:8, :] * (1.0 - cr[:, lane(c)])
        pass_first(0).start()
        keep_lead(vec_a, top_a, hs_buf[0, 0:1, :])

        @pl.loop(0, blocks)
        def _(c):
            cols = pl.ds(pl.multiple_of(c * LANES, LANES), LANES)
            vec_a[4:5, cols] = jnp.sum(t2[c] * t4[c], axis=0, keepdims=True)
            vec_a[5:6, cols] = jnp.sum(t3[c] * t4[c], axis=0, keepdims=True)

    def second_grad():
        pass_first(0).wait()

        @pl.loop(0, blocks)
        def _(c):
            cols = pl.ds(pl.multiple_of(c * LANES, LANES), LANES)
            key, rec = t2[c], t3[c]
            back = key * (1.0 - ck[:, cols]) + rec * (1.0 - cr[:, cols])
            t0[:, cols] = key * ck[:, cols] + rec * cr[:, cols] + pulled(back, 0, cols)

    def norm_grad(src, gain, base, dst, vec, row, low):
        @pl.loop(0, rows // 32)
        def _(i):
            at = pl.ds(pl.multiple_of(i * 32, 32), 32)
            raw = src[at, :]
            center = raw - jnp.mean(raw, axis=-1, keepdims=True)
            scale = lax.rsqrt(jnp.mean(center * center, axis=-1, keepdims=True) + EPS)
            s = center * scale
            g = t0[at, :]
            q = g * gain[...]
            out = base[at, :] + (q - jnp.mean(q, axis=-1, keepdims=True) - s * jnp.mean(q * s, axis=-1, keepdims=True)) * scale
            dst[at, :] = out
            if low is not None:
                low[at, :] = out.astype(bf)
            vec[row:row + 1, :] += jnp.sum(g * s, axis=0, keepdims=True)
            vec[row + 1:row + 2, :] += jnp.sum(g, axis=0, keepdims=True)

    def norm_second_grad():
        fetch(wo).start()
        norm_grad(middle, n2g, up, tok, vec_a, 2, l0)

    def fetch(src):
        return pltpu.make_async_copy(src, wbuf, gs.at[2])

    weights = wbuf
    wide = min(256, part)

    def gated_grad():
        fetch(wo).wait()
        for n in range(dim // wide):
            acc = dot_nt(l0[:, :part], weights[0, n * wide:(n + 1) * wide])
            for e in range(1, nd):
                acc = acc + dot_nt(l0[:, e * part:(e + 1) * part], weights[e, n * wide:(n + 1) * wide])
            t0[:, n * wide:(n + 1) * wide] = acc

    busy = [None, None]
    half = dim // 2
    broad = min(512, dim)

    def settle(h):
        if busy[h] is not None:
            busy[h].wait()
            busy[h] = None

    def weight_grad(cols_ref, ins_ref, dst):
        for h in range(2):
            settle(h)
            for n in range(half // wide):
                at = h * half + n * wide
                for m in range(dim // broad):
                    gstage[h, n * wide:(n + 1) * wide, m * broad:(m + 1) * broad] = dot_tn(
                        cols_ref[:, at:at + wide], ins_ref[:, m * broad:(m + 1) * broad]).astype(bf)
            busy[h] = pltpu.make_async_copy(gstage.at[h], dst.at[h * half:(h + 1) * half], gs.at[h])
            busy[h].start()

    def share(i):
        return send(xs, xr.at[i - 1], es.at[i - 1], er.at[i - 1], mate(i))

    def chain(ga, gb, keep_ends):
        for s in reversed(range(chunks)):
            if keep_ends:
                ta[s:s + 1, :] = ga
                tb[s:s + 1, :] = gb
            keep = jnp.exp(lc[s:s + 1, :])
            ga = ca[s:s + 1, :] + keep * ga
            gb = cb[s:s + 1, :] + keep * gb
        return ga, gb

    def carry_out():
        inside(9, 10, 12, 13, 15)
        carry_rows(r_ref, t0, kb, yb, mb, bb, w_ref, u_ref, t2, ca, cb, lc, dim, chunks)
        zero = jnp.zeros((1, dim), f32)
        ga, gb = chain(zero, zero, False)
        lg = lc[0:1, :]
        for s in range(1, chunks):
            lg = lg + lc[s:s + 1, :]
        xs[0:1, :] = ga
        xs[1:2, :] = gb
        xs[2:3, :] = lg
        xs[3:8, :] = jnp.zeros((5, dim), f32)
        for i in range(1, span):
            share(i).start()

    def scan_back():
        inside(11, 14)
        for i in range(1, span):
            share(i).wait()
        ga, gb = jnp.zeros((1, dim), f32), jnp.zeros((1, dim), f32)
        for i in range(span - 1, 0, -1):
            on = pos + i < span
            slot = span - i - 1
            keep = jnp.exp(xr[slot, 2:3, :])
            ga = jnp.where(on, xr[slot, 0:1, :] + keep * ga, ga)
            gb = jnp.where(on, xr[slot, 1:2, :] + keep * gb, gb)
        ga, gb = chain(ga, gb, True)
        keep_lead(vec_a, top_a + seqs, ga)
        keep_lead(vec_a, top_a + 2 * seqs, gb)
        back_rows(kb, vb, yb, mb, ab, bb, t2, w_ref, u_ref, ta, tb, t3, t4, vec_a, dim, chunks)

    def round_grads():
        inside(4, 5, 2)
        for c in range(blocks):
            l1[:, lane(c)] = t3[c].astype(bf)
            l2[:, lane(c)] = t4[c].astype(bf)
            sig = jax.nn.sigmoid(r_ref[:, lane(c)])
            l3[:, lane(c)] = (t0[:, lane(c)] * yb[c] * sig * (1.0 - sig)).astype(bf)

    def mixed_in(mix):
        for c in range(blocks):
            l4[:, lane(c)] = (first[:, lane(c)].astype(f32) * mix[:, lane(c)]
                              + before[:, lane(c)].astype(f32) * (1.0 - mix[:, lane(c)])).astype(bf)

    def grad_of(mix, cols_ref, dst):
        def run():
            mixed_in(mix)
            weight_grad(cols_ref, l4, dst)
        return run

    def input_grad(whole, low, mix, row, initial):
        def run():
            fetch(whole).start()
            fetch(whole).wait()
            for e in range(nd):
                for n in range(part // wide):
                    at = e * part + n * wide
                    got = dot_nn(low[...], weights[e, :, n * wide:(n + 1) * wide])
                    for q in range(wide // LANES):
                        c = at // LANES + q
                        g = got[:, lane(q)]
                        diff = first[:, lane(c)].astype(f32) - before[:, lane(c)].astype(f32)
                        vec_b[row:row + 1, lane(c)] = jnp.sum(g * diff, axis=0, keepdims=True)
                        stay, back = g * mix[:, lane(c)], g * (1.0 - mix[:, lane(c)])
                        t3[c] = stay if initial else t3[c] + stay
                        t4[c] = back if initial else t4[c] + back
        return run

    def start_first():
        for c in range(blocks):
            hs_buf[1, :, lane(c)] = t4[c, 0:8, :]
        pass_first(1).start()
        keep_lead(vec_b, top_b, hs_buf[1, 0:1, :])

    def first_grad():
        pass_first(1).wait()

        @pl.loop(0, blocks)
        def _(c):
            cols = pl.ds(pl.multiple_of(c * LANES, LANES), LANES)
            t0[:, cols] = t3[c] + pulled(t4[c], 1, cols)
        norm_grad(x_ref, n1g, tok, tok, vec_b, 0, None)

    def out_grad():
        inside(6)
        weight_grad(gated, l0, go)

    first_of = [min(c for c in range(total) if chunks_of[c][0] == a) for a in range(7)]
    plan = [(send_partials, None), (block_result, None), (recept_grad, 2), (recept_input, None), (start_second, None), (second_grad, None),
            (norm_second_grad, None), (gated_grad, None), (carry_out, None), (out_grad, 3), (scan_back, None), (round_grads, None),
            (grad_of(mk, l1, gk), 4), (grad_of(mv, l2, gv), 5), (grad_of(mr, l3, gr), 6),
            (input_grad(wk, l1, mk, 2, True), None), (input_grad(wv, l2, mv, 3, False), None), (input_grad(wr, l3, mr, 4, False), None),
            (start_first, None), (first_grad, None)]
    pace = [3, 4, 5, 6, 7, 8, 8, 9, 9, 9, 10, 12, 12, 13, 15, 17, 19, 20, 21, 22]
    beside = {12: sums_a[0], 13: sums_a[1], 14: sums_a[2], 15: sums_a[3], 17: sums_a[4]}
    at, done = 0, set()

    def advance(goal):
        nonlocal at
        while at < goal:
            if at < total and chunks_of[at][0] >= 2:
                a = chunks_of[at][0]
                if a not in done:
                    return
                if at == first_of[a]:
                    settle(0)
                    settle(1)
            scatter_step(at)
            at += 1

    for i, ((piece, array), goal) in enumerate(zip(plan, pace)):
        advance(goal)
        piece()
        if i in beside:
            beside[i]()
        if array is not None:
            done.add(array)
    tail = 0
    while at < steps or tail < len(sums_b):
        if tail < len(sums_b):
            sums_b[tail]()
        tail += 1
        advance(min(steps, at + 1))
    settle(0)
    settle(1)
    for c in range(total):
        for i in range(1, nd):
            along_d(c, i).wait_send()
        first_pair(c).wait_send()
        if not half_of(c):
            second_pair(c).wait_send()
        for i in range(1, nz):
            along_z(c, i).wait_send()


def backward_block(nd, nt, head, wide_head, operands, seqs, rc, lag):
    nz = nt // 4
    span = nt // seqs
    rows, dim = operands[9].shape
    part = dim // nd
    chunks_of = []
    for a, cl in enumerate((wide_head, wide_head, head, head, head, head, head)):
        size = rc if a > 1 else 2 * rc
        chunks_of += [(a, at) for at in range(0, cl, size)]
    early = [c for c in chunks_of if c[0] < 2]
    middle = [c for c in chunks_of if c[0] in (2, 3)]
    late = [c for c in chunks_of if c[0] > 3]
    split = len(early) - len(middle) + 1
    chunks_of, early = early[:split], early[split:]
    for i, a in enumerate(middle):
        chunks_of += [a] + early[i:i + 1]
    chunks_of += late
    n = len(chunks_of)
    nf = sum(1 for c in chunks_of if c[0] < 2)
    na = n - nf
    chunks = rows // STEP
    dma = pltpu.SemaphoreType.DMA
    bf, f32 = jnp.bfloat16, jnp.float32

    def vv(*shape):
        return pltpu.VMEM(shape, f32)

    def lv(*shape):
        return pltpu.VMEM(shape, bf)

    def shard(*shape):
        return jax.ShapeDtypeStruct(shape, f32)

    square = jax.ShapeDtypeStruct((dim, dim), bf)
    vec_a, vec_b = (-(-(6 + 3 * seqs) // 8) * 8, dim), (-(-(5 + seqs) // 8) * 8, dim)
    blocks = dim // LANES
    held = operands[9:25]
    full = jax.ShapeDtypeStruct((rows, dim), f32)
    return pl.pallas_call(
        functools.partial(backward_body, nd, nz, seqs, chunks_of, nf, rc, part, lag),
        out_shape=(shard(head, part),) * 5 + (shard(part, wide_head),) * 2 + (full, full, jax.ShapeDtypeStruct(vec_a, f32), jax.ShapeDtypeStruct(vec_b, f32)) + (square,) * 5
        + (jax.ShapeDtypeStruct((nd - 1, nf, nz, 2, 2 * rc, part), bf), jax.ShapeDtypeStruct((nd - 1, na, nz, 2, 2, rc, part), bf)),
        in_specs=[HBM] * 25 + [VMEM] * 9,
        out_specs=[VMEM] * 11 + [HBM] * 7,
        scratch_shapes=[lv(nf, nz, 2, 2 * rc, part), lv(na, nz, 2, 2, rc, part), lv(2, nd - 1, nz, 2, 2, rc, part),
                        lv(nf, nz, 2 * rc, part), lv(na, nz, 2, rc, part), lv(na, nz, rc, part),
                        lv(nz - 1, nf, 2 * rc, part), lv(nz - 1, na, rc, part), lv(blocks, rows, LANES), lv(blocks, rows, LANES),
                        vv(rows, dim)] + [vv(blocks, rows, LANES)] * 3 + [lv(rows, dim)] * 5
        + [lv(nd, dim, part)] + [vv(chunks, dim)] * 5 + [vv(8, dim), vv(span - 1, 8, dim), vv(2, 8, dim), vv(2, 8, dim)]
        + [vv(1, dim), vv(*vec_a), vv(*vec_b)] + [[vv(nd, *s)] + [vv(*s)] * 5 + [vv(nz, *s)] for s in (vec_a, vec_b)] + [lv(2, dim // 2, dim)]
        + [pltpu.VMEM(o.shape, o.dtype) for o in held]
        + [dma((n,)), dma((nd - 1, n)), dma((nd - 1, n)), dma((2, nd - 1)), dma((n,)), dma((n,)), dma((n,)), dma((n,)),
           dma((nz - 1, n)), dma((nz - 1, n)), dma((2 * (nd + nz),)), dma((2 * (nd + nz),)), dma((2,)), dma((2,)),
           dma((span - 1,)), dma((span - 1,)), dma((3, blocks)), dma((3,)), dma((1,)), dma((1,)), dma((16,))],
        compiler_params=pltpu.CompilerParams(collective_id=1, has_side_effects=True, vmem_limit_bytes=60 * 2**20),
        name="backward_block",
    )(*operands)


def finish_body(nt, seqs, *refs):
    given, outs = refs[:13], refs[13:22]
    held, ls, ss = refs[38:51], refs[51], refs[52]
    vec_a, vec_b, num, den = held[9:]

    def enter(i):
        return pltpu.make_async_copy(given[i], held[i], ls.at[i])

    def leave(i):
        return pltpu.make_async_copy(held[i], outs[i], ss.at[i])

    for i in (9, 10, 11, 12, 7, 8, 5, 6, 0, 1, 2, 3, 4):
        enter(i).start()
    for i in range(13):
        enter(i).wait()
        if i < 9:
            leave(i).start()
    g_num, g_den, g_top, prev_t, prev_c = refs[22:27]
    lines = refs[27:38]
    for out, (vec, row) in zip(lines, ((vec_b, 0), (vec_b, 1), (vec_a, 0), (vec_a, 1), (vec_b, 2), (vec_b, 3), (vec_b, 4),
                                       (vec_a, 2), (vec_a, 3), (vec_a, 4), (vec_a, 5))):
        out[...] = vec[row, :]
    prev_c[...] = vec_a[6:6 + seqs, :]
    prev_t[...] = vec_b[5:5 + seqs, :]
    head = num.shape[1]
    per = LANES // head
    t = lax.axis_index("tensor")
    cols = pl.ds(pl.multiple_of((t // per) * LANES, LANES), LANES)

    def own_columns(at):
        block = vec_a[at:at + seqs, cols]
        got = block[:, :head]
        for q in range(1, per):
            got = jnp.where(lax.rem(t, per) == q, block[:, q * head:(q + 1) * head], got)
        return got

    a, b = own_columns(6 + seqs), own_columns(6 + 2 * seqs)
    g_num[...] = a
    g_den[...] = b
    g_top[...] = a * num[...] + b * den[...]
    for i in range(9):
        leave(i).wait()


def finish_block(nt, seqs, big, vec_a, vec_b, num, den):
    dim = vec_a.shape[1]

    def like(o):
        return jax.ShapeDtypeStruct(o.shape, o.dtype)

    pair = jax.ShapeDtypeStruct((seqs, dim), jnp.float32)
    return pl.pallas_call(
        functools.partial(finish_body, nt, seqs),
        out_shape=tuple(like(o) for o in big) + (like(num),) * 3 + (pair,) * 2 + (jax.ShapeDtypeStruct((dim,), jnp.float32),) * 11,
        in_specs=[HBM] * 13,
        out_specs=[HBM] * 9 + [VMEM] * 16,
        scratch_shapes=[pltpu.VMEM(o.shape, o.dtype) for o in (*big, vec_a, vec_b, num, den)]
        + [pltpu.SemaphoreType.DMA((13,)), pltpu.SemaphoreType.DMA((9,))],
        compiler_params=pltpu.CompilerParams(vmem_limit_bytes=60 * 2**20),
        name="finish_block",
    )(*big, vec_a, vec_b, num, den)


def local(nd, nt, x, num, den, top, prev_a, prev_f, n1g, n1b, fading, reward, mk, mv, mr, wk, wv, wr, wo, n2g, n2b, ck, cr,
          fk, fv, fr, up):
    rows, dim = x.shape
    seqs = prev_a.shape[0]
    head = num.shape[1]

    def line(v):
        return v.astype(jnp.float32).reshape(1, dim)

    given = [s.T for s in (wk, wv, wr, wo, fr)] + [fk, fv]
    vectors = [x, up] + [line(v) for v in (n1g, n1b, mk, mv, mr, fading, reward, n2g, n2b, ck, cr)]
    weights, saved = forward_block(nd, nt, given, [num, den, top, prev_a, prev_f], vectors, seqs, rows, (32, 32), (3, 6, 9))
    whole_k, whole_v, whole_r, whole_o, whole_fr, whole_fk, whole_fv = weights
    first, before, gated, chan_rec, chan_keys, g_values, gate, recept, middle, diff2, kb, vb, yb, mb, ab, bb = saved
    keys2, values2 = chan_keys.reshape(2 * rows, dim), g_values.reshape(2 * rows, dim)
    values, part_keys, grad_fk, grad_fv = channel_block(nd, nt, keys2, values2, whole_fk, whole_fv)

    operands = [grad_fk, grad_fv, whole_k, whole_v, whole_r, whole_o, whole_fr, part_keys, diff2,
                values, middle, x, up, first, before, gated, chan_rec, gate, recept, kb, vb, yb, mb, ab, bb]
    operands += [line(v) for v in (n1g, mk, mv, mr, fading, reward, n2g, ck, cr)]
    got = backward_block(nd, nt, head, fk.shape[1], operands, seqs, (5 * head + 2 * fk.shape[1]) // 26, 2)
    done = finish_block(nt, seqs, got[:9], got[9], got[10], num, den)
    out_k, out_v, out_r, out_o, out_fr = [o.T for o in done[:5]]
    out_fk, out_fv, result, tokens_grad = done[5:9]
    grad_num, grad_den, grad_top, prev_t, prev_c = done[9:14]
    vectors = done[14:]
    return (result, tokens_grad, grad_num, grad_den, grad_top, prev_t, prev_c,
            vectors[0], vectors[1], vectors[2], vectors[3], vectors[4], vectors[5], vectors[6],
            out_k, out_v, out_r, out_o, vectors[7], vectors[8], vectors[9], vectors[10], out_fk, out_fv, out_fr)


def solution(mesh):
    nd, nt = mesh.shape["dp"], mesh.shape["tensor"]
    rows, both, lead, one = P(("dp", "tensor"), None), P("dp", "tensor"), P("dp", None), P()
    return jax.shard_map(
        functools.partial(local, nd, nt),
        mesh=mesh,
        in_specs=(rows, both, both, both, lead, lead) + (one,) * 7 + (both,) * 4 + (one,) * 4 + (both,) * 3 + (rows,),
        out_specs=(rows, rows, both, both, both, lead, lead) + (one,) * 7 + (both,) * 4 + (one,) * 4 + (both,) * 3,
        check_vma=False,
    )
```

```python
import functools

import jax
import jax.numpy as jnp
from jax import lax
from jax.experimental import pallas as pl
from jax.experimental.pallas import tpu as pltpu
from jax.sharding import PartitionSpec as P

EPS = 1e-05
STEP = 16
NEG = -1e30


def dot_nt(x, y):
    return lax.dot_general(x, y, (((1,), (1,)), ((), ())), preferred_element_type=jnp.float32)


def dot_nn(x, y):
    return lax.dot_general(x, y, (((1,), (0,)), ((), ())), preferred_element_type=jnp.float32)


def dot_tn(x, y):
    return lax.dot_general(x, y, (((0,), (0,)), ((), ())), preferred_element_type=jnp.float32)


LANES = 128
VMEM = pl.BlockSpec(memory_space=pltpu.VMEM)


def scan_groups(width):
    blocks = width // LANES
    size = 4 if blocks % 4 == 0 else 1
    return [range(g, g + size) for g in range(0, blocks, size)]


def lane(c):
    return slice(c * LANES, (c + 1) * LANES)


MESH = pl.DeviceIdType.MESH
HBM = pl.BlockSpec(memory_space=pltpu.HBM)


def place(nd, nz):
    d = lax.axis_index("dp")
    t = lax.axis_index("tensor")
    return d, t // 4, lax.rem(t // 2, 2), lax.rem(t, 2)


def spot(d, z, y, x):
    return (d, z * 4 + y * 2 + x)


def partners(nd, nz, d, z, y, x):
    out = [spot(lax.rem(d + i, nd), z, y, x) for i in range(1, nd)]
    out += [spot(d, lax.rem(z + i, nz), y, x) for i in range(1, nz)]
    return out + [spot(d, z, 1 - y, x), spot(d, z, y, 1 - x)]


def meet(others):
    barrier = pltpu.get_barrier_semaphore()
    for other in others:
        pl.semaphore_signal(barrier, inc=1, device_id=other, device_id_type=MESH)
    pl.semaphore_wait(barrier, len(others))


def send(src, dst, send_sem, recv_sem, to):
    return pltpu.make_async_remote_copy(src_ref=src, dst_ref=dst, send_sem=send_sem, recv_sem=recv_sem, device_id=to, device_id_type=MESH)


def rowwise_norm(x):
    center = x - jnp.mean(x, axis=-1, keepdims=True)
    return center * lax.rsqrt(jnp.mean(center * center, axis=-1, keepdims=True) + EPS)


def scan_ends(kb, vb, w_ref, sm, sa, sb, width, chunks):
    for group in scan_groups(width):
        m = [jnp.full((chunks, LANES), NEG, jnp.float32) for _ in group]
        a = [jnp.zeros((chunks, LANES), jnp.float32) for _ in group]
        b = [jnp.zeros((chunks, LANES), jnp.float32) for _ in group]
        for j in range(STEP):
            at = pl.ds(j, chunks, stride=STEP)
            for i, c in enumerate(group):
                k = kb[c, at, :]
                mw = m[i] - w_ref[:, lane(c)]
                m[i] = jnp.maximum(mw, k)
                keep = jnp.exp(mw - m[i])
                take = jnp.exp(k - m[i])
                a[i] = keep * a[i] + take * vb[c, at, :]
                b[i] = keep * b[i] + take
        for i, c in enumerate(group):
            sm[:, lane(c)] = m[i]
            sa[:, lane(c)] = a[i]
            sb[:, lane(c)] = b[i]


def join(m, a, b, decay, me, ae, be):
    mw = m - decay
    mn = jnp.maximum(mw, me)
    keep = jnp.exp(mw - mn)
    take = jnp.exp(me - mn)
    return mn, keep * a + take * ae, keep * b + take * be


def scan_rows(kb, vb, yb, mb, ab, bb, w_ref, u_ref, sm, sa, sb, width, chunks):
    for group in scan_groups(width):
        m = [sm[:, lane(c)] for c in group]
        a = [sa[:, lane(c)] for c in group]
        b = [sb[:, lane(c)] for c in group]
        for j in range(STEP):
            at = pl.ds(j, chunks, stride=STEP)
            for i, c in enumerate(group):
                k = kb[c, at, :]
                v = vb[c, at, :]
                mb[c, at, :] = m[i]
                ab[c, at, :] = a[i]
                bb[c, at, :] = b[i]
                uk = u_ref[:, lane(c)] + k
                p = jnp.maximum(m[i], uk)
                alpha = jnp.exp(m[i] - p)
                beta = jnp.exp(uk - p)
                yb[c, at, :] = (alpha * a[i] + beta * v) / (alpha * b[i] + beta)
                m[i], a[i], b[i] = step_state(m[i], a[i], b[i], w_ref[:, lane(c)], k, v)


def step_state(m, a, b, w, k, v):
    mw = m - w
    mn = jnp.maximum(mw, k)
    keep = jnp.exp(mw - mn)
    take = jnp.exp(k - mn)
    return mn, keep * a + take * v, keep * b + take


def forward_body(nd, nz, seqs, pieces, lag, count, *refs):
    given, refs = refs[:count], refs[count:]
    num, den, top_, prevs_a, prevs_f = refs[:5]
    refs = refs[5:]
    x_ref, up, n1g, n1b, mk, mv, mr, fading, u_ref, n2g, n2b, ck, cr = refs[:13]
    count += 1
    outs, refs = refs[13:13 + count], refs[13 + count:]
    homes = refs[:16]
    (key_in, value_in, recept_in, wbuf, sbuf, init, sm, sa, sb, halo, xs, xr, second,
     first, before, gated, chan_rec, chan_keys, g_values, gate, r_ref, middle, diff2, kb, vb, yb, mb, ab, bb,
     states, raw_k, raw_v, turned_k, turned_v, w_ref, prev_a, prev_f,
     loc, zs, zr, as_, ar, bs, br, ds, dr, hs, hr, es, er, ws, ps, pr, os) = refs[16:]
    ins = (states,) + tuple(given[:5]) + (turned_k, turned_v)
    made = (first, before, gated, chan_rec, chan_keys, g_values, gate, r_ref, middle, diff2, kb, vb, yb, mb, ab, bb)
    d, z, y, x = place(nd, nz)
    rows, dim = x_ref.shape
    part = dim // nd
    chunks = rows // STEP
    nt = 4 * nz
    span = nt // seqs
    t = lax.axis_index("tensor")
    seq = t // span
    pos = lax.rem(t, span)
    f32 = jnp.float32

    def mate(i):
        return (d, seq * span + lax.rem(pos + i, span))

    meet(partners(nd, nz, d, z, y, x) + [mate(i) for i in range(1, span)])

    def cell(a, source_d, source_z, source_y, source_x, at, n):
        if half_of(a):
            return outs[a].at[source_d, source_z, source_y, at:at + n]
        return outs[a].at[source_d, source_z, source_y, source_x, at:at + n]

    def half_of(a):
        return a >= 6

    def by_y_first(p):
        a = pieces[p][0]
        return a in (0, 4, 5) or half_of(a) or p % 2 == 0

    def leave(i):
        home = homes[i].at[x] if i in (4, 5) else homes[i]
        return pltpu.make_async_copy(made[i], home, os.at[i])

    def bring_raw(i):
        return pltpu.make_async_copy(given[5 + i], (raw_k, raw_v)[i], ws.at[3 + i])

    bring_raw(0).start()
    bring_raw(1).start()
    w_ref[...] = jnp.exp(fading[...])
    for src, dst in ((prevs_a, prev_a), (prevs_f, prev_f)):
        got = src[0:1, :].astype(f32)
        for s in range(1, seqs):
            got = jnp.where(seq == s, src[s:s + 1, :].astype(f32), got)
        dst[...] = got
    states[...] = jnp.zeros(states.shape, f32)
    for s in range(seqs):
        for j, src in enumerate((num, den, top_)):
            states[3 * s + j:3 * s + j + 1, :src.shape[1]] = src[s:s + 1, :]

    def turn(i):
        bring_raw(i).wait()
        (turned_k, turned_v)[i][...] = (raw_k, raw_v)[i][...].T

    def own(p):
        a, at, n = pieces[p]
        return pltpu.make_async_copy(ins[a].at[at:at + n], cell(a, d, z, y, x, at, n), loc.at[p])

    def along_z(p, i, source):
        a, at, n = pieces[p]
        return send(ins[a].at[at:at + n], cell(a, d, source, y, x, at, n), zs.at[p, i - 1], zr.at[p, i - 1],
                    spot(d, lax.rem(z + i, nz), y, x))

    every = slice(None)

    def first_pair(p, mine):
        a, at, n = pieces[p]
        if by_y_first(p):
            block = cell(a, d, every, y if mine else 1 - y, x, at, n)
            to = spot(d, z, 1 - y, x)
        else:
            block = cell(a, d, every, y, x if mine else 1 - x, at, n)
            to = spot(d, z, y, 1 - x)
        return send(block, block, as_.at[p], ar.at[p], to)

    def second_pair(p, mine):
        a, at, n = pieces[p]
        if by_y_first(p):
            block = cell(a, d, every, every, x if mine else 1 - x, at, n)
            to = spot(d, z, y, 1 - x)
        else:
            block = cell(a, d, every, y if mine else 1 - y, every, at, n)
            to = spot(d, z, 1 - y, x)
        return send(block, block, bs.at[p], br.at[p], to)

    def along_d(p, i, source):
        a, at, n = pieces[p]
        block = cell(a, source, every, every, every, at, n)
        return send(block, block, ds.at[p, i - 1], dr.at[p, i - 1], spot(lax.rem(d + i, nd), z, y, x))

    total = len(pieces)
    arrived = set()

    def gather_step(step):
        p = step
        if p < total:
            own(p).start()
            for i in range(1, nz):
                along_z(p, i, z).start()
        p = step - lag[0]
        if 0 <= p < total:
            own(p).wait()
            for i in range(1, nz):
                along_z(p, i, lax.rem(z - i + nz, nz)).wait_recv()
            first_pair(p, True).start()
        p = step - lag[1]
        if 0 <= p < total:
            first_pair(p, False).wait_recv()
            if half_of(pieces[p][0]):
                for i in range(1, nd):
                    along_d(p, i, d).start()
            else:
                second_pair(p, True).start()
        p = step - lag[2]
        if 0 <= p < total and not half_of(pieces[p][0]):
            second_pair(p, False).wait_recv()
            for i in range(1, nd):
                along_d(p, i, d).start()

    def have(array):
        for p in range(total):
            if pieces[p][0] == array and p not in arrived:
                arrived.add(p)
                for i in range(1, nd):
                    along_d(p, i, lax.rem(d - i + nd, nd)).wait_recv()

    def fetch(array, slot):
        return pltpu.make_async_copy(outs[array], wbuf.at[slot], ws.at[slot])

    def norm_first():
        @pl.loop(0, rows // 32)
        def _(i):
            at = pl.ds(pl.multiple_of(i * 32, 32), 32)
            first[at, :] = (rowwise_norm(x_ref[at, :]) * n1g[...] + n1b[...]).astype(jnp.bfloat16)
        pass_last(first, 0, 1).start()

    def pass_last(rows_ref, slot, to):
        return send(rows_ref.at[rows - 16:rows], halo.at[slot], hs.at[slot], hr.at[slot], mate(to))

    def shifted(rows_ref, slot, prev, cols):
        now = rows_ref[:, cols].astype(f32)
        edge = jnp.where(pos == 0, prev[:, cols], halo[slot, :, cols].astype(f32)[15:16, :])
        top = lax.broadcasted_iota(jnp.int32, now.shape, 0) == 0
        return now, jnp.where(top, edge, pltpu.roll(now, 1, 0))

    def mix_first():
        pass_last(first, 0, 1).wait()

        @pl.loop(0, dim // LANES)
        def _(c):
            cols = pl.ds(pl.multiple_of(c * LANES, LANES), LANES)
            now, old = shifted(first, 0, prev_a, cols)
            before[:, cols] = old.astype(jnp.bfloat16)
            for mix, dst in ((mk, key_in), (mv, value_in), (mr, recept_in)):
                dst[:, cols] = (now * mix[:, cols] + old * (1.0 - mix[:, cols])).astype(jnp.bfloat16)
        leave(0).start()
        leave(1).start()

    def project(array, slot, left, store):
        def run():
            fetch(array, slot).wait()
            wide = min(256, dim)
            weights = wbuf.at[slot].reshape(nd, dim, part)
            for n in range(dim // wide):
                acc = dot_nt(left[:, :part], weights[0, n * wide:(n + 1) * wide])
                for e in range(1, nd):
                    acc = acc + dot_nt(left[:, e * part:(e + 1) * part], weights[e, n * wide:(n + 1) * wide])
                store(n, wide, acc)
        return run

    def into_blocks(dst):
        def store(n, wide, acc):
            for q in range(wide // LANES):
                dst[n * (wide // LANES) + q] = acc[:, lane(q)]
        return store

    def into_rows(n, wide, acc):
        r_ref[:, n * wide:(n + 1) * wide] = acc

    def get_kv():
        have(1)
        fetch(1, 0).start()
        have(2)
        fetch(2, 1).start()

    def get_r():
        have(3)
        fetch(3, 0).start()
        have(0)
        copy = pltpu.make_async_copy(outs[0].at[d], sbuf, ws.at[2])
        copy.start()
        copy.wait()
        head = dim // nt
        per = LANES // head
        for c in range(dim // LANES):
            cells = []
            for q in range(per):
                b = c * per + q
                cells.append(sbuf[b // 4, (b // 2) % 2, b % 2][:, :head])
            init[:, lane(c)] = jnp.concatenate(cells, axis=1)

    def get_o():
        have(4)
        fetch(4, 1).start()

    def initial(j):
        got = init[j:j + 1, :]
        for s in range(1, seqs):
            got = jnp.where(seq == s, init[3 * s + j:3 * s + j + 1, :], got)
        return got

    def share(i):
        return send(xs, xr.at[i - 1], es.at[i - 1], er.at[i - 1], mate(i))

    def summarize():
        scan_ends(kb, vb, w_ref, sm, sa, sb, dim, chunks)
        lead = pos == 0
        m = jnp.where(lead, initial(2), NEG)
        a = jnp.where(lead, initial(0), 0.0)
        b = jnp.where(lead, initial(1), 0.0)
        decay = float(STEP) * w_ref[...]
        for s in range(chunks):
            m, a, b = join(m, a, b, decay, sm[s:s + 1, :], sa[s:s + 1, :], sb[s:s + 1, :])
        xs[0:1, :] = a
        xs[1:2, :] = b
        xs[2:3, :] = m
        xs[3:8, :] = jnp.zeros((5, dim), f32)
        for i in range(1, span):
            share(i).start()

    def carry_in():
        for i in range(1, span):
            share(i).wait()
        m = jnp.where(pos == 0, initial(2), NEG)
        a = jnp.where(pos == 0, initial(0), 0.0)
        b = jnp.where(pos == 0, initial(1), 0.0)
        decay = float(rows) * w_ref[...]
        for i in range(span - 1, 0, -1):
            on = i <= pos
            mn, an, bn = join(m, a, b, decay, xr[i - 1, 2:3, :], xr[i - 1, 0:1, :], xr[i - 1, 1:2, :])
            m, a, b = jnp.where(on, mn, m), jnp.where(on, an, a), jnp.where(on, bn, b)
        decay = float(STEP) * w_ref[...]
        for s in range(chunks):
            me, ae, be = sm[s:s + 1, :], sa[s:s + 1, :], sb[s:s + 1, :]
            sm[s:s + 1, :] = m
            sa[s:s + 1, :] = a
            sb[s:s + 1, :] = b
            m, a, b = join(m, a, b, decay, me, ae, be)

    def scan():
        scan_rows(kb, vb, yb, mb, ab, bb, w_ref, u_ref, sm, sa, sb, dim, chunks)
        for c in range(dim // LANES):
            gated[:, lane(c)] = (jax.nn.sigmoid(r_ref[:, lane(c)]) * yb[c]).astype(jnp.bfloat16)
        for i in (2, 7, 10, 11, 12, 13, 14, 15):
            leave(i).start()

    def attend_out():
        fetch(4, 1).wait()
        weights = wbuf.at[1].reshape(nd, dim, part)
        wide = min(256, part)
        for e in range(nd):
            for n in range(part // wide):
                at = slice(e * part + n * wide, e * part + (n + 1) * wide)
                middle[:, at] = x_ref[:, at] + dot_nn(gated[...], weights[e, :, n * wide:(n + 1) * wide])
        leave(8).start()

    def norm_second():
        @pl.loop(0, rows // 32)
        def _(i):
            at = pl.ds(pl.multiple_of(i * 32, 32), 32)
            second[at, :] = (rowwise_norm(middle[at, :]) * n2g[...] + n2b[...]).astype(jnp.bfloat16)
        pass_last(second, 1, 1).start()

    def mix_second():
        pass_last(second, 1, 1).wait()

        @pl.loop(0, dim // LANES)
        def _(c):
            cols = pl.ds(pl.multiple_of(c * LANES, LANES), LANES)
            now, old = shifted(second, 1, prev_f, cols)
            diff2[:, cols] = now - old
            chan_keys[:, cols] = (now * ck[:, cols] + old * (1.0 - ck[:, cols])).astype(jnp.bfloat16)
            chan_rec[:, cols] = (now * cr[:, cols] + old * (1.0 - cr[:, cols])).astype(jnp.bfloat16)
        pair_up(0, x).start()
        for i in (3, 4, 9):
            leave(i).start()

    def pair_up(slot, source):
        return send(made[4 + slot], homes[4 + slot].at[source], ps.at[slot], pr.at[slot], spot(d, z, y, 1 - x))

    def get_fr():
        have(5)
        fetch(5, 0).start()

    def gate_rows(n, wide, acc):
        at = slice(n * wide, (n + 1) * wide)
        got = jax.nn.sigmoid(acc)
        gate[:, at] = got
        g_values[:, at] = (up[:, at] * got).astype(jnp.bfloat16)

    def values_grad():
        project(5, 0, chan_rec, gate_rows)()
        pair_up(1, x).start()
        for i in (5, 6):
            leave(i).start()

    steps = total + lag[2]
    gather_step(0)
    gather_step(1)
    norm_first()
    gather_step(2)
    turn(0)
    turn(1)
    mix_first()
    def due(array):
        return 1 + max(p for p in range(total) if pieces[p][0] == array) + lag[2]

    ready = max(due(1), due(2))
    for s in range(3, ready):
        gather_step(s)
    work = [get_kv, project(1, 0, key_in, into_blocks(kb)), project(2, 1, value_in, into_blocks(vb)), get_r, get_o, summarize,
            project(3, 0, recept_in, into_rows), carry_in, scan, get_fr, attend_out, norm_second, mix_second, values_grad]
    last = {3: max(due(3), due(0)), 4: due(4), 9: due(5)}
    at = ready
    for i, piece in enumerate(work):
        while at < min(steps, max(last.get(i, 0), ready + i)):
            gather_step(at)
            at += 1
        piece()
    while at < steps:
        gather_step(at)
        at += 1
    for a in range(count):
        have(a)
    for p in range(total):
        for i in range(1, nz):
            along_z(p, i, z).wait_send()
        first_pair(p, True).wait_send()
        if not half_of(pieces[p][0]):
            second_pair(p, True).wait_send()
        for i in range(1, nd):
            along_d(p, i, d).wait_send()
    for slot in range(2):
        pair_up(slot, x).wait_send()
        pair_up(slot, 1 - x).wait_recv()
    for i in range(16):
        leave(i).wait()


def forward_block(nd, nt, given, small, vectors, seqs, rows, unit, lag, mixing=1):
    nz = nt // 4
    span = nt // seqs
    dim = given[0].shape[0] * nt
    part = dim // nd
    bf16 = jnp.bfloat16
    shards = [jax.ShapeDtypeStruct((-(-3 * seqs // 8) * 8, LANES), jnp.float32)] + list(given[:5])
    shards += [jax.ShapeDtypeStruct((g.shape[1], g.shape[0]), bf16) for g in given[5:]]
    pieces = []
    for a, s in enumerate(shards):
        size = min(unit[a >= 6], s.shape[0])
        pieces += [(a, at, size) for at in range(0, s.shape[0], size)]
    early = [p for p in pieces if p[0] in (1, 2)] + [p for p in pieces if p[0] in (3, 0)]
    later = [p for p in pieces if p[0] in (4, 5)]
    halves = [p for a, b in zip([p for p in pieces if p[0] == 6], [p for p in pieces if p[0] == 7]) for p in (a, b)]
    pieces = early
    while later or halves:
        pieces, later, halves = pieces + later[:1] + halves[:mixing], later[1:], halves[mixing:]
    n = len(pieces)
    dma = pltpu.SemaphoreType.DMA
    bf, f32 = jnp.bfloat16, jnp.float32
    low = jax.ShapeDtypeStruct((rows, dim), bf)
    full = jax.ShapeDtypeStruct((rows, dim), f32)
    twice = jax.ShapeDtypeStruct((2, rows, dim), bf)
    block = jax.ShapeDtypeStruct((dim // LANES, rows, LANES), f32)
    chunks = rows // STEP
    per = shards[1].shape[0]
    got = pl.pallas_call(
        functools.partial(forward_body, nd, nz, seqs, pieces, lag, len(given)),
        out_shape=tuple(jax.ShapeDtypeStruct(((nd, nz, 2, 2) if a < 6 else (nd, nz, 2)) + s.shape, s.dtype) for a, s in enumerate(shards))
        + (low,) * 4 + (twice,) * 2 + (full,) * 4 + (block,) * 6,
        in_specs=[HBM] * len(given) + [VMEM] * (5 + len(vectors)),
        out_specs=[HBM] * len(shards) + [HBM] * 16,
        scratch_shapes=[pltpu.VMEM((rows, dim), bf)] * 3
        + [pltpu.VMEM((2, nd, nz, 2, 2, per, part), bf), pltpu.VMEM((nz, 2, 2) + shards[0].shape, f32), pltpu.VMEM((shards[0].shape[0], dim), f32)]
        + [pltpu.VMEM((chunks, dim), f32)] * 3
        + [pltpu.VMEM((2, 16, dim), bf), pltpu.VMEM((8, dim), f32), pltpu.VMEM((span - 1, 8, dim), f32), pltpu.VMEM((rows, dim), bf)]
        + [pltpu.VMEM((rows, dim), bf)] * 6 + [pltpu.VMEM((rows, dim), f32)] * 4 + [pltpu.VMEM(block.shape, f32)] * 6
        + [pltpu.VMEM(shards[0].shape, f32)] + [pltpu.VMEM(g.shape, bf) for g in given[5:]] + [pltpu.VMEM(s.shape, bf) for s in shards[6:]]
        + [pltpu.VMEM((1, dim), f32)] * 3
        + [dma((n,)), dma((n, nz - 1)), dma((n, nz - 1)), dma((n,)), dma((n,)), dma((n,)), dma((n,)),
           dma((n, nd - 1)), dma((n, nd - 1)), dma((2,)), dma((2,)), dma((span - 1,)), dma((span - 1,)), dma((5,)), dma((2,)), dma((2,)), dma((16,))],
        compiler_params=pltpu.CompilerParams(collective_id=0, has_side_effects=True, vmem_limit_bytes=60 * 2**20),
        name="forward_block",
    )(*given, *small, *vectors)
    weights = [o.reshape(nd, -1, s.shape[1]) for o, s in zip(got[1:len(shards)], shards[1:])]
    return weights, got[len(shards):]


def channel_body(nd, nz, keys_home, grads_home, fk_in, fv_in, values, keys_out, gfk, gfv,
                 keys_in, grads_in, part_keys, fk, fv, squared, hidden_grad, stage, pout, pin, ls, gs, ps, pr, ks):
    d, z, y, x = place(nd, nz)
    part, width = fk.shape[2], fk.shape[1]
    rows2, dim = keys_in.shape
    rows = rows2 // 2
    f32, bf = jnp.float32, jnp.bfloat16
    count = ls.shape[1]
    size = width // count
    wide = min(256, size)

    def bring(i, b):
        src, dst = ((fk_in, fk), (fv_in, fv))[i]
        return pltpu.make_async_copy(src.at[:, b * size:(b + 1) * size], dst.at[:, b * size:(b + 1) * size], ls.at[i, b])

    keys_load = pltpu.make_async_copy(keys_home, keys_in, ks.at[0])
    grads_load = pltpu.make_async_copy(grads_home, grads_in, ks.at[1])
    keys_load.start()
    grads_load.start()
    for b in range(count):
        bring(0, b).start()
        bring(1, b).start()
    barrier = pltpu.get_barrier_semaphore()
    pl.semaphore_signal(barrier, inc=1, device_id=spot(d, z, y, 1 - x), device_id_type=MESH)
    keys_load.wait()
    grads_load.wait()
    for b in range(count):
        bring(0, b).wait()
        bring(1, b).wait()
        for n in range(size // wide):
            at = slice(b * size + n * wide, b * size + (n + 1) * wide)
            hid = dot_nt(keys_in[:, :part], fk[0, at])
            back = dot_nt(grads_in[:, :part], fv[0, at])
            for e in range(1, nd):
                hid = hid + dot_nt(keys_in[:, e * part:(e + 1) * part], fk[e, at])
                back = back + dot_nt(grads_in[:, e * part:(e + 1) * part], fv[e, at])
            hid = jnp.maximum(hid, 0.0)
            squared[:, at] = (hid * hid).astype(bf)
            hidden_grad[:, at] = (back * 2.0 * hid).astype(bf)
    mine = pl.ds(pl.multiple_of(x * rows, rows), rows)
    theirs = pl.ds(pl.multiple_of((1 - x) * rows, rows), rows)
    step = min(256, part)

    def product(left, at_rows, whole, store):
        for e in range(nd):
            for n in range(part // step):
                store(slice(e * part + n * step, e * part + (n + 1) * step),
                      dot_nn(left[at_rows, :], whole[e, :, n * step:(n + 1) * step]))

    def put_out(at, got):
        pout[:, at] = got.astype(bf)

    def put_values(at, got):
        values[:, at] = got

    def put_theirs(at, got):
        part_keys[1 - x, :, at] = got

    def put_mine(at, got):
        part_keys[x, :, at] = got

    product(squared, theirs, fv, put_out)
    swap = send(pout, pin, ps.at[0], pr.at[0], spot(d, z, y, 1 - x))
    pl.semaphore_wait(barrier, 1)
    swap.start()
    product(squared, mine, fv, put_values)
    product(hidden_grad, theirs, fk, put_theirs)
    product(hidden_grad, mine, fk, put_mine)
    keys_leave = pltpu.make_async_copy(part_keys, keys_out, ks.at[2])
    keys_leave.start()
    broad = min(512, dim)
    busy = [None, None]
    turn = 0
    for left, right, dst in ((squared, grads_in, gfv), (hidden_grad, keys_in, gfk)):
        for b in range(count):
            if busy[turn] is not None:
                busy[turn].wait()
            for n in range(size // wide):
                at = slice(b * size + n * wide, b * size + (n + 1) * wide)
                for m in range(dim // broad):
                    stage[turn, n * wide:(n + 1) * wide, m * broad:(m + 1) * broad] = dot_tn(
                        left[:, at], right[:, m * broad:(m + 1) * broad]).astype(bf)
            busy[turn] = pltpu.make_async_copy(stage.at[turn], dst.at[b * size:(b + 1) * size], gs.at[turn])
            busy[turn].start()
            turn = 1 - turn
    swap.wait()
    for c in range(dim // LANES):
        values[:, lane(c)] = values[:, lane(c)] + pin[:, lane(c)].astype(f32)
    keys_leave.wait()
    for copy in busy:
        copy.wait()


def channel_block(nd, nt, keys, grads, fk, fv):
    rows2, dim = keys.shape
    rows = rows2 // 2
    width, part = fk.shape[1], fk.shape[2]
    bf, f32 = jnp.bfloat16, jnp.float32
    count = 4
    dma = pltpu.SemaphoreType.DMA
    square = jax.ShapeDtypeStruct((width, dim), bf)
    return pl.pallas_call(
        functools.partial(channel_body, nd, nt // 4),
        out_shape=(jax.ShapeDtypeStruct((rows, dim), f32), jax.ShapeDtypeStruct((2, rows, dim), f32), square, square),
        in_specs=[HBM] * 4,
        out_specs=[VMEM, HBM, HBM, HBM],
        scratch_shapes=[pltpu.VMEM((rows2, dim), bf), pltpu.VMEM((rows2, dim), bf), pltpu.VMEM((2, rows, dim), f32), pltpu.VMEM((nd, width, part), bf), pltpu.VMEM((nd, width, part), bf), pltpu.VMEM((rows2, width), bf),
                        pltpu.VMEM((rows2, width), bf), pltpu.VMEM((2, width // count, dim), bf), pltpu.VMEM((rows, dim), bf),
                        pltpu.VMEM((rows, dim), bf), dma((2, count)), dma((2,)), dma((1,)), dma((1,)), dma((3,))],
        compiler_params=pltpu.CompilerParams(collective_id=2, has_side_effects=True, vmem_limit_bytes=60 * 2**20),
        name="channel_block",
    )(keys, grads, fk, fv)


def carry_rows(r_ref, gg, kb, yb, mb, bb, w_ref, u_ref, gyb, ca, cb, lc, width, chunks):
    for c in range(width // LANES):
        gyb[c] = gg[:, lane(c)] * jax.nn.sigmoid(r_ref[:, lane(c)])
    for group in scan_groups(width):
        ga = [jnp.zeros((chunks, LANES), jnp.float32) for _ in group]
        gb = [jnp.zeros((chunks, LANES), jnp.float32) for _ in group]
        end = [None for _ in group]
        for j in reversed(range(STEP)):
            at = pl.ds(j, chunks, stride=STEP)
            for i, c in enumerate(group):
                w = w_ref[:, lane(c)]
                k = kb[c, at, :]
                m = mb[c, at, :]
                uk = u_ref[:, lane(c)] + k
                p = jnp.maximum(m, uk)
                alpha = jnp.exp(m - p)
                gn = gyb[c, at, :] / (alpha * bb[c, at, :] + jnp.exp(uk - p))
                gd = -gn * yb[c, at, :]
                mw = m - w
                mn = jnp.maximum(mw, k)
                if j == STEP - 1:
                    end[i] = mn
                keep = jnp.exp(mw - mn)
                ga[i] = alpha * gn + keep * ga[i]
                gb[i] = alpha * gd + keep * gb[i]
                if j == 0:
                    lc[:, lane(c)] = m - float(STEP) * w - end[i]
        for i, c in enumerate(group):
            ca[:, lane(c)] = ga[i]
            cb[:, lane(c)] = gb[i]


def back_rows(kb, vb, yb, mb, ab, bb, gyb, w_ref, u_ref, ta, tb, fk, fv, vec, width, chunks):
    for group in scan_groups(width):
        ga = [ta[:, lane(c)] for c in group]
        gb = [tb[:, lane(c)] for c in group]
        gu = [jnp.zeros((chunks, LANES), jnp.float32) for _ in group]
        gw = [jnp.zeros((chunks, LANES), jnp.float32) for _ in group]
        for j in reversed(range(STEP)):
            at = pl.ds(j, chunks, stride=STEP)
            for i, c in enumerate(group):
                k = kb[c, at, :]
                v = vb[c, at, :]
                m = mb[c, at, :]
                uk = u_ref[:, lane(c)] + k
                p = jnp.maximum(m, uk)
                alpha = jnp.exp(m - p)
                beta = jnp.exp(uk - p)
                b = bb[c, at, :]
                gn = gyb[c, at, :] / (alpha * b + beta)
                gd = -gn * yb[c, at, :]
                mw = m - w_ref[:, lane(c)]
                mn = jnp.maximum(mw, k)
                keep = jnp.exp(mw - mn)
                take = jnp.exp(k - mn)
                now = beta * (gn * v + gd)
                fv[c, at, :] = beta * gn + take * ga[i]
                fk[c, at, :] = now + take * (ga[i] * v + gb[i])
                gu[i] = gu[i] + now
                gw[i] = gw[i] + keep * (ga[i] * ab[c, at, :] + gb[i] * b)
                ga[i] = alpha * gn + keep * ga[i]
                gb[i] = alpha * gd + keep * gb[i]
        for i, c in enumerate(group):
            vec[0:1, lane(c)] = -jnp.sum(gw[i], axis=0, keepdims=True) * w_ref[:, lane(c)]
            vec[1:2, lane(c)] = jnp.sum(gu[i], axis=0, keepdims=True)


def backward_body(nd, nz, seqs, chunks_of, nf, rc, part, lag, *refs):
    gfk, gfv, wk, wv, wr, wo, wfr, keys_in, diff_in = refs[:9]
    homes = refs[9:25]
    n1g, mk, mv, mr, fading, u_ref, n2g, ck, cr = refs[25:34]
    leaving = refs[34:43]
    (vout_a, vout_b, gfr, go, gk, gv, gr, landf, landa) = refs[43:52]
    (ownf, owna, slots, raf, raa, rba, rzf, rza, pout, pin, t0, t2, t3, t4, l0, l1, l2, l3, l4, wbuf, ca, cb, lc, ta, tb, xs, xr, hs_buf, hr_buf,
     w_ref, vec_a, vec_b, got_a, got_b, gstage, *more) = refs[52:]
    values_ref, middle, x_ref, up, first, before, gated, chan_rec, gate, r_ref, kb, vb, yb, mb, ab, bb = held = more[:16]
    outk, outv, outr, outo, outfr, outfk, outfv, result, tok = kept = more[16:25]
    loc, ds, dr, cs, as_, ar, bs, br, zs, zr, vs, vr, hs, hr, es, er, ws, gs, ps, pr, os, ts = more[25:]
    grads = [gfv, gfk, gfr, go, gk, gv, gr]
    outs = [outfv, outfk, outfr, outo, outk, outv, outr]
    d, z, y, x = place(nd, nz)
    rows, dim = x_ref.shape
    chunks = rows // STEP
    nt = 4 * nz
    span = nt // seqs
    t = lax.axis_index("tensor")
    seq = t // span
    pos = lax.rem(t, span)
    f32, bf = jnp.float32, jnp.bfloat16
    total = len(chunks_of)
    top_a, top_b = 6, 5

    def mate(i):
        return (d, seq * span + lax.rem(pos + i, span))

    def load_block(src, dst, c, sem):
        return pltpu.make_async_copy(src.at[:, c * LANES:(c + 1) * LANES], dst.at[c], sem.at[c])

    blocks = dim // LANES

    def load_all(src, dst, i):
        for c in range(blocks):
            load_block(src, dst, c, ws.at[i]).start()

    def wait_all(src, dst, i):
        for c in range(blocks):
            load_block(src, dst, c, ws.at[i]).wait()

    def enter(i):
        return pltpu.make_async_copy(homes[i], held[i], os.at[i])

    def leave(i):
        return pltpu.make_async_copy(kept[i], leaving[i], ts.at[i])

    def inside(*which):
        for i in which:
            enter(i).wait()

    load_all(keys_in.at[1 - x], t4, 1)
    for i in (0, 8, 1, 3, 7, 9, 10, 12, 13, 15, 6, 11, 14, 4, 5, 2):
        enter(i).start()
    meet(partners(nd, nz, d, z, y, x) + [mate(i) for i in range(1, span)])

    def half_of(c):
        return chunks_of[c][0] < 2

    rank = [sum(1 for e in range(c) if half_of(e) == half_of(c)) for c in range(total)]

    def mine_of(c):
        return ownf.at[rank[c]] if half_of(c) else owna.at[rank[c]]

    def slab(c, source):
        a, at = chunks_of[c]
        lanes = pl.ds(pl.multiple_of(source * part, part), part)
        if half_of(c):
            g = grads[a].reshape(nz, 2, grads[a].shape[0] // (2 * nz), dim)
            return g.at[:, :, at:at + 2 * rc, lanes]
        g = grads[a].reshape(nz, 2, 2, grads[a].shape[0] // nt, dim)
        return g.at[:, :, :, at:at + rc, lanes]

    def load(c):
        return pltpu.make_async_copy(slab(c, d), mine_of(c), loc.at[c])

    def landing(c, i):
        return (landf if half_of(c) else landa).at[i - 1, rank[c]]

    def slot_of(c, i):
        full = slots.at[c % 2, i - 1]
        return full.reshape(nz, 2, 2 * rc, part) if half_of(c) else full

    def along_d(c, i):
        to = lax.rem(d + i, nd)
        return send(slab(c, to), landing(c, i), ds.at[i - 1, c], dr.at[i - 1, c], spot(to, z, y, x))

    def bring(c, i):
        return pltpu.make_async_copy(landing(c, i), slot_of(c, i), cs.at[c % 2, i - 1])

    def by_x_first(c):
        return not half_of(c) and (chunks_of[c][0] < 4 or rank[c] % 2 == 0)

    def got_first(c):
        return (raf if half_of(c) else raa).at[rank[c]]

    def first_pair(c):
        own = mine_of(c)
        if half_of(c):
            return send(own.at[:, 1 - y], got_first(c), as_.at[c], ar.at[c], spot(d, z, 1 - y, x))
        if by_x_first(c):
            return send(own.at[:, :, 1 - x], got_first(c), as_.at[c], ar.at[c], spot(d, z, y, 1 - x))
        return send(own.at[:, 1 - y], got_first(c), as_.at[c], ar.at[c], spot(d, z, 1 - y, x))

    def second_pair(c):
        own, dst = mine_of(c), rba.at[rank[c]]
        if by_x_first(c):
            return send(own.at[:, 1 - y, x], dst, bs.at[c], br.at[c], spot(d, z, 1 - y, x))
        return send(own.at[:, y, 1 - x], dst, bs.at[c], br.at[c], spot(d, z, y, 1 - x))

    def got_z(c, i):
        return (rzf if half_of(c) else rza).at[i - 1, rank[c]]

    def along_z(c, i):
        own = mine_of(c)
        to = lax.rem(z + i, nz)
        return send(own.at[to, y] if half_of(c) else own.at[to, y, x], got_z(c, i), zs.at[i - 1, c], zr.at[i - 1, c], spot(d, to, y, x))

    def add_into(dst, at, *terms):
        if len(terms) == 1:
            dst[at] = dst[at] + terms[0][0][terms[0][1]]
            return
        acc = dst[at].astype(f32)
        for src, place_at in terms:
            acc = acc + src[place_at].astype(f32)
        dst[at] = acc.astype(bf)

    def scatter_step(step):
        c = step
        if c < total:
            load(c).start()
            for i in range(1, nd):
                along_d(c, i).start()
        c = step - 2
        if 0 <= c < total:
            for i in range(1, nd):
                along_d(c, i).wait_recv()
                bring(c, i).start()
        c = step - 3
        if 0 <= c < total:
            load(c).wait()
            for i in range(1, nd):
                bring(c, i).wait()
            own = mine_of(c)

            @pl.loop(0, nz)
            def _(b):
                for q in range(2 if half_of(c) else 4):
                    at = (b, q) if half_of(c) else (b, q // 2, q % 2)
                    add_into(own, at, *[(slot_of(c, i), at) for i in range(1, nd)])
            first_pair(c).start()
        c = step - 3 - lag
        if 0 <= c < total:
            first_pair(c).wait_recv()
            own, got = mine_of(c), got_first(c)

            @pl.loop(0, nz)
            def _(b):
                if half_of(c):
                    add_into(own, (b, y), (got, (b,)))
                else:
                    for q in range(2):
                        add_into(own, (b, q, x) if by_x_first(c) else (b, y, q), (got, (b, q)))
            if half_of(c):
                for i in range(1, nz):
                    along_z(c, i).start()
            else:
                second_pair(c).start()
        c = step - 3 - 2 * lag
        if 0 <= c < total:
            if half_of(c):
                finish(c)
            else:
                second_pair(c).wait_recv()
                own, got = mine_of(c), rba.at[rank[c]]

                @pl.loop(0, nz)
                def _(b):
                    add_into(own, (b, y, x), (got, (b,)))
                for i in range(1, nz):
                    along_z(c, i).start()
        c = step - 3 - 3 * lag
        if 0 <= c < total and not half_of(c):
            finish(c)

    def finish(c):
        for i in range(1, nz):
            along_z(c, i).wait_recv()
        own = mine_of(c)
        acc = (own[z, y] if half_of(c) else own[z, y, x]).astype(f32)
        for i in range(1, nz):
            acc = acc + got_z(c, i)[...].astype(f32)
        a, at = chunks_of[c]
        if half_of(c):
            outs[a][:, at:at + acc.shape[0]] = acc.T
        else:
            outs[a][at:at + acc.shape[0], :] = acc
        if c == max(e for e in range(total) if chunks_of[e][0] == a):
            leave((6, 5, 4, 3, 0, 1, 2)[a]).start()

    steps = total + 3 + 3 * lag

    def vector_sums(vec, top, bufs, base, out):
        vd, v1, vx, v2, vy, v3, vz = bufs

        def link(i, src, dst, to):
            return send(src, dst, vs.at[base + i], vr.at[base + i], to)

        def vec_d(i):
            return link(i - 1, vec, vd.at[d], spot(lax.rem(d + i, nd), z, y, x))

        def vec_x():
            return link(nd - 1, v1, vx, spot(d, z, y, 1 - x))

        def vec_y():
            return link(nd, v2, vy, spot(d, z, 1 - y, x))

        def vec_z(i):
            return link(nd + i, v3, vz.at[z], spot(d, lax.rem(z + i, nz), y, x))

        def start():
            vd[d] = vec[...]
            for i in range(1, nd):
                vec_d(i).start()

        def over_x():
            for i in range(1, nd):
                vec_d(i).wait()
            acc = vd[0]
            for i in range(1, nd):
                acc = acc + vd[i]
            row = lax.broadcasted_iota(jnp.int32, acc.shape, 0)
            v1[...] = jnp.where(row < top, acc, vec[...])
            vec_x().start()

        def over_y():
            vec_x().wait()
            v2[...] = v1[...] + vx[...]
            vec_y().start()

        def over_z():
            vec_y().wait()
            v3[...] = v2[...] + vy[...]
            vz[z] = v3[...]
            for i in range(1, nz):
                vec_z(i).start()

        def finish_sum():
            for i in range(1, nz):
                vec_z(i).wait()
            acc = vz[0]
            for i in range(1, nz):
                acc = acc + vz[i]
            out[...] = acc

        return [start, over_x, over_y, over_z, finish_sum]

    sums_a = vector_sums(vec_a, top_a, got_a, 0, vout_a)
    sums_b = vector_sums(vec_b, top_b, got_b, nd + nz, vout_b)

    lead = pos == 0

    def keep_lead(vec, start, row):
        for s in range(seqs):
            at = start + s
            vec[at:at + 1, :] = jnp.where(jnp.logical_and(lead, seq == s), row, 0.0)

    def pass_first(slot):
        return send(hs_buf.at[slot], hr_buf.at[slot], hs.at[slot], hr.at[slot], mate(span - 1))

    def pulled(back, slot, cols):
        edge = jnp.where(pos == span - 1, 0.0, hr_buf[slot, 0:1, cols])
        last = lax.broadcasted_iota(jnp.int32, back.shape, 0) == rows - 1
        return jnp.where(last, edge, pltpu.roll(back, rows - 1, 0))

    def partial():
        return send(pout, pin, ps.at[0], pr.at[0], spot(d, z, y, 1 - x))

    def send_partials():
        wait_all(keys_in.at[1 - x], t4, 1)

        @pl.loop(0, blocks)
        def _(c):
            pout[c] = t4[c].astype(bf)
        partial().start()
        load_all(keys_in.at[x], t2, 1)
        load_all(diff_in, t4, 2)
        w_ref[...] = jnp.exp(fading[...])
        vec_a[...] = jnp.zeros(vec_a.shape, f32)
        vec_b[...] = jnp.zeros(vec_b.shape, f32)

    def block_result():
        fetch(wfr).start()
        inside(0, 8, 1, 3)

        @pl.loop(0, blocks)
        def _(c):
            cols = pl.ds(pl.multiple_of(c * LANES, LANES), LANES)
            values, open_ = values_ref[:, cols], gate[:, cols]
            result[:, cols] = middle[:, cols] + open_ * values
            l0[:, cols] = (up[:, cols] * values * open_ * (1.0 - open_)).astype(bf)
        leave(7).start()

    def recept_grad():
        inside(7)
        weight_grad(l0, chan_rec, gfr)

    def recept_input():
        fetch(wfr).wait()
        for e in range(nd):
            for n in range(part // wide):
                got = dot_nn(l0[...], weights[e, :, n * wide:(n + 1) * wide])
                for q in range(wide // LANES):
                    t3[(e * part + n * wide) // LANES + q] = got[:, lane(q)]

    def start_second():
        wait_all(keys_in.at[x], t2, 1)
        wait_all(diff_in, t4, 2)
        partial().wait()
        for c in range(blocks):
            t2[c] = t2[c] + pin[c].astype(f32)
        for c in range(blocks):
            hs_buf[0, :, lane(c)] = t2[c, 0:8, :] * (1.0 - ck[:, lane(c)]) + t3[c, 0:8, :] * (1.0 - cr[:, lane(c)])
        pass_first(0).start()
        keep_lead(vec_a, top_a, hs_buf[0, 0:1, :])

        @pl.loop(0, blocks)
        def _(c):
            cols = pl.ds(pl.multiple_of(c * LANES, LANES), LANES)
            vec_a[4:5, cols] = jnp.sum(t2[c] * t4[c], axis=0, keepdims=True)
            vec_a[5:6, cols] = jnp.sum(t3[c] * t4[c], axis=0, keepdims=True)

    def second_grad():
        pass_first(0).wait()

        @pl.loop(0, blocks)
        def _(c):
            cols = pl.ds(pl.multiple_of(c * LANES, LANES), LANES)
            key, rec = t2[c], t3[c]
            back = key * (1.0 - ck[:, cols]) + rec * (1.0 - cr[:, cols])
            t0[:, cols] = key * ck[:, cols] + rec * cr[:, cols] + pulled(back, 0, cols)

    def norm_grad(src, gain, base, dst, vec, row, low):
        @pl.loop(0, rows // 32)
        def _(i):
            at = pl.ds(pl.multiple_of(i * 32, 32), 32)
            raw = src[at, :]
            center = raw - jnp.mean(raw, axis=-1, keepdims=True)
            scale = lax.rsqrt(jnp.mean(center * center, axis=-1, keepdims=True) + EPS)
            s = center * scale
            g = t0[at, :]
            q = g * gain[...]
            out = base[at, :] + (q - jnp.mean(q, axis=-1, keepdims=True) - s * jnp.mean(q * s, axis=-1, keepdims=True)) * scale
            dst[at, :] = out
            if low is not None:
                low[at, :] = out.astype(bf)
            vec[row:row + 1, :] += jnp.sum(g * s, axis=0, keepdims=True)
            vec[row + 1:row + 2, :] += jnp.sum(g, axis=0, keepdims=True)

    def norm_second_grad():
        fetch(wo).start()
        norm_grad(middle, n2g, up, tok, vec_a, 2, l0)

    def fetch(src):
        return pltpu.make_async_copy(src, wbuf, gs.at[2])

    weights = wbuf
    wide = min(256, part)

    def gated_grad():
        fetch(wo).wait()
        for n in range(dim // wide):
            acc = dot_nt(l0[:, :part], weights[0, n * wide:(n + 1) * wide])
            for e in range(1, nd):
                acc = acc + dot_nt(l0[:, e * part:(e + 1) * part], weights[e, n * wide:(n + 1) * wide])
            t0[:, n * wide:(n + 1) * wide] = acc

    busy = [None, None]
    half = dim // 2
    broad = min(512, dim)

    def settle(h):
        if busy[h] is not None:
            busy[h].wait()
            busy[h] = None

    def weight_grad(cols_ref, ins_ref, dst):
        for h in range(2):
            settle(h)
            for n in range(half // wide):
                at = h * half + n * wide
                for m in range(dim // broad):
                    gstage[h, n * wide:(n + 1) * wide, m * broad:(m + 1) * broad] = dot_tn(
                        cols_ref[:, at:at + wide], ins_ref[:, m * broad:(m + 1) * broad]).astype(bf)
            busy[h] = pltpu.make_async_copy(gstage.at[h], dst.at[h * half:(h + 1) * half], gs.at[h])
            busy[h].start()

    def share(i):
        return send(xs, xr.at[i - 1], es.at[i - 1], er.at[i - 1], mate(i))

    def chain(ga, gb, keep_ends):
        for s in reversed(range(chunks)):
            if keep_ends:
                ta[s:s + 1, :] = ga
                tb[s:s + 1, :] = gb
            keep = jnp.exp(lc[s:s + 1, :])
            ga = ca[s:s + 1, :] + keep * ga
            gb = cb[s:s + 1, :] + keep * gb
        return ga, gb

    def carry_out():
        inside(9, 10, 12, 13, 15)
        carry_rows(r_ref, t0, kb, yb, mb, bb, w_ref, u_ref, t2, ca, cb, lc, dim, chunks)
        zero = jnp.zeros((1, dim), f32)
        ga, gb = chain(zero, zero, False)
        lg = lc[0:1, :]
        for s in range(1, chunks):
            lg = lg + lc[s:s + 1, :]
        xs[0:1, :] = ga
        xs[1:2, :] = gb
        xs[2:3, :] = lg
        xs[3:8, :] = jnp.zeros((5, dim), f32)
        for i in range(1, span):
            share(i).start()

    def scan_back():
        inside(11, 14)
        for i in range(1, span):
            share(i).wait()
        ga, gb = jnp.zeros((1, dim), f32), jnp.zeros((1, dim), f32)
        for i in range(span - 1, 0, -1):
            on = pos + i < span
            slot = span - i - 1
            keep = jnp.exp(xr[slot, 2:3, :])
            ga = jnp.where(on, xr[slot, 0:1, :] + keep * ga, ga)
            gb = jnp.where(on, xr[slot, 1:2, :] + keep * gb, gb)
        ga, gb = chain(ga, gb, True)
        keep_lead(vec_a, top_a + seqs, ga)
        keep_lead(vec_a, top_a + 2 * seqs, gb)
        back_rows(kb, vb, yb, mb, ab, bb, t2, w_ref, u_ref, ta, tb, t3, t4, vec_a, dim, chunks)

    def round_grads():
        inside(4, 5, 2)
        for c in range(blocks):
            l1[:, lane(c)] = t3[c].astype(bf)
            l2[:, lane(c)] = t4[c].astype(bf)
            sig = jax.nn.sigmoid(r_ref[:, lane(c)])
            l3[:, lane(c)] = (t0[:, lane(c)] * yb[c] * sig * (1.0 - sig)).astype(bf)

    def mixed_in(mix):
        for c in range(blocks):
            l4[:, lane(c)] = (first[:, lane(c)].astype(f32) * mix[:, lane(c)]
                              + before[:, lane(c)].astype(f32) * (1.0 - mix[:, lane(c)])).astype(bf)

    def grad_of(mix, cols_ref, dst):
        def run():
            mixed_in(mix)
            weight_grad(cols_ref, l4, dst)
        return run

    def input_grad(whole, low, mix, row, initial):
        def run():
            fetch(whole).start()
            fetch(whole).wait()
            for e in range(nd):
                for n in range(part // wide):
                    at = e * part + n * wide
                    got = dot_nn(low[...], weights[e, :, n * wide:(n + 1) * wide])
                    for q in range(wide // LANES):
                        c = at // LANES + q
                        g = got[:, lane(q)]
                        diff = first[:, lane(c)].astype(f32) - before[:, lane(c)].astype(f32)
                        vec_b[row:row + 1, lane(c)] = jnp.sum(g * diff, axis=0, keepdims=True)
                        stay, back = g * mix[:, lane(c)], g * (1.0 - mix[:, lane(c)])
                        t3[c] = stay if initial else t3[c] + stay
                        t4[c] = back if initial else t4[c] + back
        return run

    def start_first():
        for c in range(blocks):
            hs_buf[1, :, lane(c)] = t4[c, 0:8, :]
        pass_first(1).start()
        keep_lead(vec_b, top_b, hs_buf[1, 0:1, :])

    def first_grad():
        pass_first(1).wait()

        @pl.loop(0, blocks)
        def _(c):
            cols = pl.ds(pl.multiple_of(c * LANES, LANES), LANES)
            t0[:, cols] = t3[c] + pulled(t4[c], 1, cols)
        norm_grad(x_ref, n1g, tok, tok, vec_b, 0, None)
        leave(8).start()

    def out_grad():
        inside(6)
        weight_grad(gated, l0, go)

    first_of = [min(c for c in range(total) if chunks_of[c][0] == a) for a in range(7)]
    plan = [(send_partials, None), (block_result, None), (recept_grad, 2), (recept_input, None), (start_second, None), (second_grad, None),
            (norm_second_grad, None), (gated_grad, None), (carry_out, None), (out_grad, 3), (scan_back, None), (round_grads, None),
            (grad_of(mk, l1, gk), 4), (grad_of(mv, l2, gv), 5), (grad_of(mr, l3, gr), 6),
            (input_grad(wk, l1, mk, 2, True), None), (input_grad(wv, l2, mv, 3, False), None), (input_grad(wr, l3, mr, 4, False), None),
            (start_first, None), (first_grad, None)]
    pace = [3, 4, 5, 6, 7, 8, 8, 9, 9, 9, 10, 12, 12, 13, 15, 17, 19, 20, 21, 22]
    beside = {12: sums_a[0], 13: sums_a[1], 14: sums_a[2], 15: sums_a[3], 17: sums_a[4]}
    at, done = 0, set()

    def advance(goal):
        nonlocal at
        while at < goal:
            if at < total and chunks_of[at][0] >= 2:
                a = chunks_of[at][0]
                if a not in done:
                    return
                if at == first_of[a]:
                    settle(0)
                    settle(1)
            scatter_step(at)
            at += 1

    for i, ((piece, array), goal) in enumerate(zip(plan, pace)):
        advance(goal)
        piece()
        if i in beside:
            beside[i]()
        if array is not None:
            done.add(array)
    tail = 0
    while at < steps or tail < len(sums_b):
        if tail < len(sums_b):
            sums_b[tail]()
        tail += 1
        advance(min(steps, at + 1))
    settle(0)
    settle(1)
    for i in range(9):
        leave(i).wait()
    for c in range(total):
        for i in range(1, nd):
            along_d(c, i).wait_send()
        first_pair(c).wait_send()
        if not half_of(c):
            second_pair(c).wait_send()
        for i in range(1, nz):
            along_z(c, i).wait_send()


def backward_block(nd, nt, head, wide_head, operands, seqs, rc, lag):
    nz = nt // 4
    span = nt // seqs
    rows, dim = operands[9].shape
    part = dim // nd
    chunks_of = []
    for a, cl in enumerate((wide_head, wide_head, head, head, head, head, head)):
        size = rc if a > 1 else 2 * rc
        chunks_of += [(a, at) for at in range(0, cl, size)]
    early = [c for c in chunks_of if c[0] < 2]
    middle = [c for c in chunks_of if c[0] in (2, 3)]
    late = [c for c in chunks_of if c[0] > 3]
    split = len(early) - len(middle) + 1
    chunks_of, early = early[:split], early[split:]
    for i, a in enumerate(middle):
        chunks_of += [a] + early[i:i + 1]
    chunks_of += late
    n = len(chunks_of)
    nf = sum(1 for c in chunks_of if c[0] < 2)
    na = n - nf
    chunks = rows // STEP
    dma = pltpu.SemaphoreType.DMA
    bf, f32 = jnp.bfloat16, jnp.float32

    def vv(*shape):
        return pltpu.VMEM(shape, f32)

    def lv(*shape):
        return pltpu.VMEM(shape, bf)

    def shard(*shape):
        return jax.ShapeDtypeStruct(shape, f32)

    square = jax.ShapeDtypeStruct((dim, dim), bf)
    vec_a, vec_b = (-(-(6 + 3 * seqs) // 8) * 8, dim), (-(-(5 + seqs) // 8) * 8, dim)
    blocks = dim // LANES
    held = operands[9:25]
    full = jax.ShapeDtypeStruct((rows, dim), f32)
    return pl.pallas_call(
        functools.partial(backward_body, nd, nz, seqs, chunks_of, nf, rc, part, lag),
        out_shape=(shard(head, part),) * 5 + (shard(part, wide_head),) * 2 + (full, full, jax.ShapeDtypeStruct(vec_a, f32), jax.ShapeDtypeStruct(vec_b, f32)) + (square,) * 5
        + (jax.ShapeDtypeStruct((nd - 1, nf, nz, 2, 2 * rc, part), bf), jax.ShapeDtypeStruct((nd - 1, na, nz, 2, 2, rc, part), bf)),
        in_specs=[HBM] * 25 + [VMEM] * 9,
        out_specs=[HBM] * 9 + [VMEM] * 2 + [HBM] * 7,
        scratch_shapes=[lv(nf, nz, 2, 2 * rc, part), lv(na, nz, 2, 2, rc, part), lv(2, nd - 1, nz, 2, 2, rc, part),
                        lv(nf, nz, 2 * rc, part), lv(na, nz, 2, rc, part), lv(na, nz, rc, part),
                        lv(nz - 1, nf, 2 * rc, part), lv(nz - 1, na, rc, part), lv(blocks, rows, LANES), lv(blocks, rows, LANES),
                        vv(rows, dim)] + [vv(blocks, rows, LANES)] * 3 + [lv(rows, dim)] * 5
        + [lv(nd, dim, part)] + [vv(chunks, dim)] * 5 + [vv(8, dim), vv(span - 1, 8, dim), vv(2, 8, dim), vv(2, 8, dim)]
        + [vv(1, dim), vv(*vec_a), vv(*vec_b)] + [[vv(nd, *s)] + [vv(*s)] * 5 + [vv(nz, *s)] for s in (vec_a, vec_b)] + [lv(2, dim // 2, dim)]
        + [pltpu.VMEM(o.shape, o.dtype) for o in held]
        + [vv(head, part)] * 5 + [vv(part, wide_head)] * 2 + [vv(rows, dim)] * 2
        + [dma((n,)), dma((nd - 1, n)), dma((nd - 1, n)), dma((2, nd - 1)), dma((n,)), dma((n,)), dma((n,)), dma((n,)),
           dma((nz - 1, n)), dma((nz - 1, n)), dma((2 * (nd + nz),)), dma((2 * (nd + nz),)), dma((2,)), dma((2,)),
           dma((span - 1,)), dma((span - 1,)), dma((3, blocks)), dma((3,)), dma((1,)), dma((1,)), dma((16,)), dma((9,))],
        compiler_params=pltpu.CompilerParams(collective_id=1, has_side_effects=True, vmem_limit_bytes=60 * 2**20),
        name="backward_block",
    )(*operands)


def finish_body(nt, seqs, *refs):
    given, outs = refs[:13], refs[13:22]
    held, ls, ss = refs[38:51], refs[51], refs[52]
    vec_a, vec_b, num, den = held[9:]

    def enter(i):
        return pltpu.make_async_copy(given[i], held[i], ls.at[i])

    def leave(i):
        return pltpu.make_async_copy(held[i], outs[i], ss.at[i])

    for i in (9, 10, 11, 12, 7, 8, 5, 6, 0, 1, 2, 3, 4):
        enter(i).start()
    for i in range(13):
        enter(i).wait()
        if i < 9:
            leave(i).start()
    g_num, g_den, g_top, prev_t, prev_c = refs[22:27]
    lines = refs[27:38]
    for out, (vec, row) in zip(lines, ((vec_b, 0), (vec_b, 1), (vec_a, 0), (vec_a, 1), (vec_b, 2), (vec_b, 3), (vec_b, 4),
                                       (vec_a, 2), (vec_a, 3), (vec_a, 4), (vec_a, 5))):
        out[...] = vec[row, :]
    prev_c[...] = vec_a[6:6 + seqs, :]
    prev_t[...] = vec_b[5:5 + seqs, :]
    head = num.shape[1]
    per = LANES // head
    t = lax.axis_index("tensor")
    cols = pl.ds(pl.multiple_of((t // per) * LANES, LANES), LANES)

    def own_columns(at):
        block = vec_a[at:at + seqs, cols]
        got = block[:, :head]
        for q in range(1, per):
            got = jnp.where(lax.rem(t, per) == q, block[:, q * head:(q + 1) * head], got)
        return got

    a, b = own_columns(6 + seqs), own_columns(6 + 2 * seqs)
    g_num[...] = a
    g_den[...] = b
    g_top[...] = a * num[...] + b * den[...]
    for i in range(9):
        leave(i).wait()


def finish_block(nt, seqs, big, vec_a, vec_b, num, den):
    dim = vec_a.shape[1]

    def like(o):
        return jax.ShapeDtypeStruct(o.shape, o.dtype)

    pair = jax.ShapeDtypeStruct((seqs, dim), jnp.float32)
    return pl.pallas_call(
        functools.partial(finish_body, nt, seqs),
        out_shape=tuple(like(o) for o in big) + (like(num),) * 3 + (pair,) * 2 + (jax.ShapeDtypeStruct((dim,), jnp.float32),) * 11,
        in_specs=[HBM] * 13,
        out_specs=[HBM] * 9 + [VMEM] * 16,
        scratch_shapes=[pltpu.VMEM(o.shape, o.dtype) for o in (*big, vec_a, vec_b, num, den)]
        + [pltpu.SemaphoreType.DMA((13,)), pltpu.SemaphoreType.DMA((9,))],
        compiler_params=pltpu.CompilerParams(vmem_limit_bytes=60 * 2**20),
        name="finish_block",
    )(*big, vec_a, vec_b, num, den)


def local(nd, nt, x, num, den, top, prev_a, prev_f, n1g, n1b, fading, reward, mk, mv, mr, wk, wv, wr, wo, n2g, n2b, ck, cr,
          fk, fv, fr, up):
    rows, dim = x.shape
    seqs = prev_a.shape[0]
    head = num.shape[1]

    def line(v):
        return v.astype(jnp.float32).reshape(1, dim)

    given = [s.T for s in (wk, wv, wr, wo, fr)] + [fk, fv]
    vectors = [x, up] + [line(v) for v in (n1g, n1b, mk, mv, mr, fading, reward, n2g, n2b, ck, cr)]
    weights, saved = forward_block(nd, nt, given, [num, den, top, prev_a, prev_f], vectors, seqs, rows, (32, 32), (3, 6, 9))
    whole_k, whole_v, whole_r, whole_o, whole_fr, whole_fk, whole_fv = weights
    first, before, gated, chan_rec, chan_keys, g_values, gate, recept, middle, diff2, kb, vb, yb, mb, ab, bb = saved
    keys2, values2 = chan_keys.reshape(2 * rows, dim), g_values.reshape(2 * rows, dim)
    values, part_keys, grad_fk, grad_fv = channel_block(nd, nt, keys2, values2, whole_fk, whole_fv)

    operands = [grad_fk, grad_fv, whole_k, whole_v, whole_r, whole_o, whole_fr, part_keys, diff2,
                values, middle, x, up, first, before, gated, chan_rec, gate, recept, kb, vb, yb, mb, ab, bb]
    operands += [line(v) for v in (n1g, mk, mv, mr, fading, reward, n2g, ck, cr)]
    got = backward_block(nd, nt, head, fk.shape[1], operands, seqs, (5 * head + 2 * fk.shape[1]) // 26, 2)
    done = finish_block(nt, seqs, got[:9], got[9], got[10], num, den)
    out_k, out_v, out_r, out_o, out_fr = [o.T for o in done[:5]]
    out_fk, out_fv, result, tokens_grad = done[5:9]
    grad_num, grad_den, grad_top, prev_t, prev_c = done[9:14]
    vectors = done[14:]
    return (result, tokens_grad, grad_num, grad_den, grad_top, prev_t, prev_c,
            vectors[0], vectors[1], vectors[2], vectors[3], vectors[4], vectors[5], vectors[6],
            out_k, out_v, out_r, out_o, vectors[7], vectors[8], vectors[9], vectors[10], out_fk, out_fv, out_fr)


def solution(mesh):
    nd, nt = mesh.shape["dp"], mesh.shape["tensor"]
    rows, both, lead, one = P(("dp", "tensor"), None), P("dp", "tensor"), P("dp", None), P()
    return jax.shard_map(
        functools.partial(local, nd, nt),
        mesh=mesh,
        in_specs=(rows, both, both, both, lead, lead) + (one,) * 7 + (both,) * 4 + (one,) * 4 + (both,) * 3 + (rows,),
        out_specs=(rows, rows, both, both, both, lead, lead) + (one,) * 7 + (both,) * 4 + (one,) * 4 + (both,) * 3,
        check_vma=False,
    )
```
